32 devices in a mesh: fsdp: 8 (over y, x, core), seq: 4 (over z).
Axes of the slice: x: 2, y: 2, z: 4, core: 2. Of those that a mesh axis runs over, the one named last changes fastest.
Arguments:
- tokens: float32 [16, 1568, 1024], P('fsdp', 'seq'), may hold values from -6 to 6
- visible: int32 [16, 1568], P('fsdp'), may hold values from 0 to 1, as said below
- slot_token: int32 [16, 1568], P('fsdp'), may hold values from 0 to 1567, each once within a row
- positions: float32 [1568, 384], replicated, may hold values from -6 to 6
- encoder_pre_gain: bfloat16 [1024], P('fsdp'), may hold values from 0.5 to 1.5
- encoder_pre_shift: bfloat16 [1024], P('fsdp'), may hold values from -1.75 to 1.75
- encoder_joint_weight: bfloat16 [1024, 3072], P('fsdp'), may hold values from -0.1875 to 0.1875
- encoder_query_bias: bfloat16 [1024], P('fsdp'), may hold values from -1.75 to 1.75
- encoder_value_bias: bfloat16 [1024], P('fsdp'), may hold values from -1.75 to 1.75
- encoder_out_weight: bfloat16 [1024, 1024], P('fsdp'), may hold values from -1.5 to 1.5
- encoder_out_bias: bfloat16 [1024], P('fsdp'), may hold values from -1.75 to 1.75
- encoder_mid_gain: bfloat16 [1024], P('fsdp'), may hold values from 0.5 to 1.5
- encoder_mid_shift: bfloat16 [1024], P('fsdp'), may hold values from -1.75 to 1.75
- encoder_expand_weight: bfloat16 [1024, 4096], P('fsdp'), may hold values from -0.1875 to 0.1875
- encoder_expand_bias: bfloat16 [4096], P('fsdp'), may hold values from -1.75 to 1.75
- encoder_contract_weight: bfloat16 [4096, 1024], P('fsdp'), may hold values from -0.09375 to 0.09375
- encoder_contract_bias: bfloat16 [1024], P('fsdp'), may hold values from -1.75 to 1.75
- embed_weight: bfloat16 [1024, 384], P('fsdp'), may hold values from -0.1875 to 0.1875
- embed_bias: bfloat16 [384], P('fsdp'), may hold values from -1.75 to 1.75
- mask_token: bfloat16 [384], P('fsdp'), may hold values from -6 to 6
- predictor_pre_gain: bfloat16 [384], P('fsdp'), may hold values from 0.5 to 1.5
- predictor_pre_shift: bfloat16 [384], P('fsdp'), may hold values from -1.75 to 1.75
- predictor_joint_weight: bfloat16 [384, 1152], P('fsdp'), may hold values from -0.3125 to 0.3125
- predictor_query_bias: bfloat16 [384], P('fsdp'), may hold values from -1.75 to 1.75
- predictor_value_bias: bfloat16 [384], P('fsdp'), may hold values from -1.75 to 1.75
- predictor_out_weight: bfloat16 [384, 384], P('fsdp'), may hold values from -2.5 to 2.5
- predictor_out_bias: bfloat16 [384], P('fsdp'), may hold values from -1.75 to 1.75
- predictor_mid_gain: bfloat16 [384], P('fsdp'), may hold values from 0.5 to 1.5
- predictor_mid_shift: bfloat16 [384], P('fsdp'), may hold values from -1.75 to 1.75
- predictor_expand_weight: bfloat16 [384, 1536], P('fsdp'), may hold values from -0.3125 to 0.3125
- predictor_expand_bias: bfloat16 [1536], P('fsdp'), may hold values from -1.75 to 1.75
- predictor_contract_weight: bfloat16 [1536, 384], P('fsdp'), may hold values from -0.15625 to 0.15625
- predictor_contract_bias: bfloat16 [384], P('fsdp'), may hold values from -1.75 to 1.75
- cotangent: float32 [16, 1568, 384], P('fsdp', 'seq'), may hold values from -6 to 6
Outputs:
- encoded: float32 [16, 1568, 1024], P('fsdp', 'seq')
- predicted: float32 [16, 1568, 384], P('fsdp', 'seq')
- grad_tokens: float32 [16, 1568, 1024], P('fsdp', 'seq')
- grad_encoder_pre_gain: float32 [1024], P('fsdp')
- grad_encoder_pre_shift: float32 [1024], P('fsdp')
- grad_encoder_joint_weight: float32 [1024, 3072], P('fsdp')
- grad_encoder_query_bias: float32 [1024], P('fsdp')
- grad_encoder_value_bias: float32 [1024], P('fsdp')
- grad_encoder_out_weight: float32 [1024, 1024], P('fsdp')
- grad_encoder_out_bias: float32 [1024], P('fsdp')
- grad_encoder_mid_gain: float32 [1024], P('fsdp')
- grad_encoder_mid_shift: float32 [1024], P('fsdp')
- grad_encoder_expand_weight: float32 [1024, 4096], P('fsdp')
- grad_encoder_expand_bias: float32 [4096], P('fsdp')
- grad_encoder_contract_weight: float32 [4096, 1024], P('fsdp')
- grad_encoder_contract_bias: float32 [1024], P('fsdp')
- grad_embed_weight: float32 [1024, 384], P('fsdp')
- grad_embed_bias: float32 [384], P('fsdp')
- grad_mask_token: float32 [384], P('fsdp')
- grad_predictor_pre_gain: float32 [384], P('fsdp')
- grad_predictor_pre_shift: float32 [384], P('fsdp')
- grad_predictor_joint_weight: float32 [384, 1152], P('fsdp')
- grad_predictor_query_bias: float32 [384], P('fsdp')
- grad_predictor_value_bias: float32 [384], P('fsdp')
- grad_predictor_out_weight: float32 [384, 384], P('fsdp')
- grad_predictor_out_bias: float32 [384], P('fsdp')
- grad_predictor_mid_gain: float32 [384], P('fsdp')
- grad_predictor_mid_shift: float32 [384], P('fsdp')
- grad_predictor_expand_weight: float32 [384, 1536], P('fsdp')
- grad_predictor_expand_bias: float32 [1536], P('fsdp')
- grad_predictor_contract_weight: float32 [1536, 384], P('fsdp')
- grad_predictor_contract_bias: float32 [384], P('fsdp')
The draws below stay inside these ranges and needn't reach their ends.
Inputs may be any that keep to these rules, and one draw needn't show every extreme that they name: In every clip the visible positions form one rectangle of the 14 x 14 spatial grid, the same in all 8 frames, and cover less than half of each frame. `slot_token`: each clip's row is a permutation of the token positions.
All inputs are finite; a program needn't handle non-finite values.
Results may differ from the reference program's by a relative error of at most 0.018.
Values may be sent and summed in bfloat16 or wider, within the bound.
A program may use at most 320 MiB of HBM per device.

```python
import math
import jax
import jax.numpy as jnp
from jax import lax

D = 1024
HEADS = 16
FF = 4096
P_SIZE = 384
PHEADS = 12
PFF = 1536
FRAMES = 8
GRID = 14
LEN = 1568
CLIPS = 16


def draw_visible(key, part):
    subkeys = jax.random.split(key, 4)
    least_height = max(1, 2 * GRID // 7)
    most_height = max(least_height, GRID // 2)
    least_width = max(1, 5 * GRID // 14)
    most_width = max(least_width, 11 * GRID // 14)
    height = jax.random.randint(subkeys[0], (CLIPS, 1, 1), least_height, most_height + 1)
    breadth = jax.random.randint(subkeys[1], (CLIPS, 1, 1), least_width, most_width + 1)
    top_edge = jax.random.randint(subkeys[2], (CLIPS, 1, 1), 0, GRID - height + 1)
    left_edge = jax.random.randint(subkeys[3], (CLIPS, 1, 1), 0, GRID - breadth + 1)
    row_index = jnp.arange(GRID, dtype=jnp.int32)[None, :, None]
    column_index = jnp.arange(GRID, dtype=jnp.int32)[None, None, :]
    inside = (row_index >= top_edge) & (row_index < top_edge + height) & (column_index >= left_edge) & (column_index < left_edge + breadth)
    frames_all = jnp.broadcast_to(inside[:, None, :, :], (CLIPS, FRAMES, GRID, GRID))
    return frames_all.reshape(CLIPS, LEN).astype(jnp.int32)


def levels(stream_key, dims, pieces, least, top_value):
    def one(axis_at, parts):
        heights = jax.random.uniform(jax.random.fold_in(jax.random.fold_in(stream_key, 6), axis_at), (parts,), jnp.float32, least / len(pieces), top_value / len(pieces))
        return jnp.repeat(jnp.exp(heights), dims[axis_at] // parts).reshape((-1,) + (1,) * (len(dims) - axis_at - 1))

    factor_of = one(*pieces[0])
    for cut in pieces[1:]:
        factor_of = factor_of * one(*cut)
    return factor_of


def normal_values(own_key, extent, scale, limit, shards=(), held_as=jnp.bfloat16):
    values = jax.random.normal(own_key, extent, jnp.float32) * scale
    if len(shards) > 0:
        values = levels(own_key, extent, shards, -0.22, 0.18) * values
    return jnp.clip(values, min=-limit, max=limit).astype(held_as)


def setup_inputs(seed: int = 0) -> dict:
    arg_keys = jax.random.split(jax.random.key(seed), 35)
    tokens = normal_values(arg_keys[0], (CLIPS, LEN, D), 1.0, 6.0, ((0, 8), (1, 4)), jnp.float32)
    visible = draw_visible(jax.random.fold_in(arg_keys[34], 71), 0)
    slot_token = jax.vmap(lambda own: jax.random.permutation(own, LEN))(jax.random.split(arg_keys[2], CLIPS)).reshape((CLIPS, LEN)).astype(jnp.int32)
    positions = normal_values(arg_keys[3], (LEN, P_SIZE), 1.0, 6.0, (), jnp.float32)
    encoder_pre_gain = jnp.clip(1.0 + 0.1 * jax.random.normal(arg_keys[4], (D,), jnp.float32), 0.5, 1.5).astype(jnp.bfloat16)
    encoder_pre_shift = normal_values(arg_keys[5], (D,), 0.3, 1.75, ((0, 8),))
    encoder_joint_weight = normal_values(arg_keys[6], (D, 3 * D), D ** -0.5, 0.1875, ((0, 8),))
    encoder_query_bias = normal_values(arg_keys[7], (D,), 0.3, 1.75, ((0, 8),))
    encoder_value_bias = normal_values(arg_keys[8], (D,), 0.3, 1.75, ((0, 8),))
    encoder_out_weight = normal_values(arg_keys[9], (D, D), (D // 64) ** -0.5, 1.5, ((0, 8),))
    encoder_out_bias = normal_values(arg_keys[10], (D,), 0.3, 1.75, ((0, 8),))
    encoder_mid_gain = jnp.clip(1.0 + 0.1 * jax.random.normal(arg_keys[11], (D,), jnp.float32), 0.5, 1.5).astype(jnp.bfloat16)
    encoder_mid_shift = normal_values(arg_keys[12], (D,), 0.3, 1.75, ((0, 8),))
    encoder_expand_weight = normal_values(arg_keys[13], (D, FF), D ** -0.5, 0.1875, ((0, 8),))
    encoder_expand_bias = normal_values(arg_keys[14], (FF,), 0.3, 1.75, ((0, 8),))
    encoder_contract_weight = normal_values(arg_keys[15], (FF, D), FF ** -0.5, 0.09375, ((0, 8),))
    encoder_contract_bias = normal_values(arg_keys[16], (D,), 0.3, 1.75, ((0, 8),))
    embed_weight = normal_values(arg_keys[17], (D, P_SIZE), D ** -0.5, 0.1875, ((0, 8),))
    embed_bias = normal_values(arg_keys[18], (P_SIZE,), 0.3, 1.75, ((0, 8),))
    mask_token = normal_values(arg_keys[19], (P_SIZE,), 1.0, 6.0, ((0, 8),))
    predictor_pre_gain = jnp.clip(1.0 + 0.1 * jax.random.normal(arg_keys[20], (P_SIZE,), jnp.float32), 0.5, 1.5).astype(jnp.bfloat16)
    predictor_pre_shift = normal_values(arg_keys[21], (P_SIZE,), 0.3, 1.75, ((0, 8),))
    predictor_joint_weight = normal_values(arg_keys[22], (P_SIZE, 3 * P_SIZE), P_SIZE ** -0.5, 0.3125, ((0, 8),))
    predictor_query_bias = normal_values(arg_keys[23], (P_SIZE,), 0.3, 1.75, ((0, 8),))
    predictor_value_bias = normal_values(arg_keys[24], (P_SIZE,), 0.3, 1.75, ((0, 8),))
    predictor_out_weight = normal_values(arg_keys[25], (P_SIZE, P_SIZE), (P_SIZE // 64) ** -0.5, 2.5, ((0, 8),))
    predictor_out_bias = normal_values(arg_keys[26], (P_SIZE,), 0.3, 1.75, ((0, 8),))
    predictor_mid_gain = jnp.clip(1.0 + 0.1 * jax.random.normal(arg_keys[27], (P_SIZE,), jnp.float32), 0.5, 1.5).astype(jnp.bfloat16)
    predictor_mid_shift = normal_values(arg_keys[28], (P_SIZE,), 0.3, 1.75, ((0, 8),))
    predictor_expand_weight = normal_values(arg_keys[29], (P_SIZE, PFF), P_SIZE ** -0.5, 0.3125, ((0, 8),))
    predictor_expand_bias = normal_values(arg_keys[30], (PFF,), 0.3, 1.75, ((0, 8),))
    predictor_contract_weight = normal_values(arg_keys[31], (PFF, P_SIZE), PFF ** -0.5, 0.15625, ((0, 8),))
    predictor_contract_bias = normal_values(arg_keys[32], (P_SIZE,), 0.3, 1.75, ((0, 8),))
    cotangent = normal_values(arg_keys[33], (CLIPS, LEN, P_SIZE), 1.0, 6.0, ((0, 8), (1, 4)), jnp.float32)
    return {"tokens": tokens, "visible": visible, "slot_token": slot_token, "positions": positions, "encoder_pre_gain": encoder_pre_gain, "encoder_pre_shift": encoder_pre_shift, "encoder_joint_weight": encoder_joint_weight, "encoder_query_bias": encoder_query_bias, "encoder_value_bias": encoder_value_bias, "encoder_out_weight": encoder_out_weight, "encoder_out_bias": encoder_out_bias, "encoder_mid_gain": encoder_mid_gain, "encoder_mid_shift": encoder_mid_shift, "encoder_expand_weight": encoder_expand_weight, "encoder_expand_bias": encoder_expand_bias, "encoder_contract_weight": encoder_contract_weight, "encoder_contract_bias": encoder_contract_bias, "embed_weight": embed_weight, "embed_bias": embed_bias, "mask_token": mask_token, "predictor_pre_gain": predictor_pre_gain, "predictor_pre_shift": predictor_pre_shift, "predictor_joint_weight": predictor_joint_weight, "predictor_query_bias": predictor_query_bias, "predictor_value_bias": predictor_value_bias, "predictor_out_weight": predictor_out_weight, "predictor_out_bias": predictor_out_bias, "predictor_mid_gain": predictor_mid_gain, "predictor_mid_shift": predictor_mid_shift, "predictor_expand_weight": predictor_expand_weight, "predictor_expand_bias": predictor_expand_bias, "predictor_contract_weight": predictor_contract_weight, "predictor_contract_bias": predictor_contract_bias, "cotangent": cotangent}


@jax.custom_vjp
def low(v):
    return lax.optimization_barrier(v.astype(jnp.bfloat16)).astype(jnp.float32)

@jax.custom_vjp
def low_back(v):
    return v

def low_keep(v):
    return (low(v), None)

def low_pass(kept, grad):
    return (grad,)

def back_keep(v):
    return (v, None)

def back_low(kept, grad):
    return (low(grad),)
low.defvjp(low_keep, low_pass)
low_back.defvjp(back_keep, back_low)
highest = lax.Precision.HIGHEST
norm_eps = 1e-06

def rounded_both(value):
    return low(low_back(value))

def norm_layer(value, gain, shift):
    center = value - lax.optimization_barrier(jnp.mean(value, axis=-1, keepdims=True))
    spread = lax.optimization_barrier(jnp.mean(center * center, axis=-1, keepdims=True))
    return center * lax.rsqrt(spread + norm_eps) * gain + shift

def matmul(left, weight):
    return jnp.einsum('gld,de->gle', left, weight, precision=highest)

def attention(queries, keys_all, values_all, keep, head_count):
    group_size, length, model_width = queries.shape
    head_size = model_width // head_count
    score_scale = 1.0 / math.sqrt(head_size)

    def split_heads(array):
        return jnp.transpose(array.reshape(group_size, length, head_count, head_size), (2, 0, 1, 3))

    @jax.checkpoint
    def one_head(operands):
        head_q, head_k, head_v = operands
        scores = low_back(jnp.einsum('gqd,gkd->gqk', head_q, head_k, precision=highest) * score_scale)
        scores = jnp.where(keep[:, None, :], scores, -1e+30)
        chance = low(jax.nn.softmax(scores, axis=-1))
        return jnp.einsum('gqk,gkd->gqd', chance, head_v, precision=highest)
    result = lax.map(one_head, (split_heads(queries), split_heads(keys_all), split_heads(values_all)))
    return jnp.transpose(result, (1, 2, 0, 3)).reshape(group_size, length, model_width)

def block(inputs, keep, weights, head_count):
    pre_gain, pre_shift, joint_weight, query_bias, value_bias, out_weight, out_bias, mid_gain, mid_shift, expand_weight, expand_bias, contract_weight, contract_bias = weights
    model_width = inputs.shape[-1]
    normed = low(norm_layer(inputs, pre_gain, pre_shift))
    joint = matmul(normed, joint_weight)
    queries = rounded_both(joint[..., :model_width] + query_bias)
    keys_all = rounded_both(joint[..., model_width:2 * model_width])
    values_all = rounded_both(joint[..., 2 * model_width:] + value_bias)
    mixed = rounded_both(attention(queries, keys_all, values_all, keep, head_count))
    middle = inputs + low_back(matmul(mixed, out_weight) + out_bias)
    normed_mid = low(norm_layer(middle, mid_gain, mid_shift))
    hidden = low_back(matmul(normed_mid, expand_weight) + expand_bias)
    active = low(jax.nn.gelu(hidden, approximate=False))
    return middle + low_back(matmul(active, contract_weight) + contract_bias)

def forward(weights, inputs, slot_visible, slot_code):
    encoded = block(inputs, slot_visible > 0, weights[0:13], HEADS)
    embedded = low_back(matmul(low(encoded), weights[13]) + weights[14])
    pred_input = jnp.where(slot_visible[..., None] > 0, embedded, weights[15]) + slot_code
    everyone = jnp.ones(pred_input.shape[:2], dtype=bool)
    predicted = block(pred_input, everyone, weights[16:29], PHEADS)
    return (predicted, encoded)

def reference(tokens, visible, slot_token, positions, encoder_pre_gain, encoder_pre_shift, encoder_joint_weight, encoder_query_bias, encoder_value_bias, encoder_out_weight, encoder_out_bias, encoder_mid_gain, encoder_mid_shift, encoder_expand_weight, encoder_expand_bias, encoder_contract_weight, encoder_contract_bias, embed_weight, embed_bias, mask_token, predictor_pre_gain, predictor_pre_shift, predictor_joint_weight, predictor_query_bias, predictor_value_bias, predictor_out_weight, predictor_out_bias, predictor_mid_gain, predictor_mid_shift, predictor_expand_weight, predictor_expand_bias, predictor_contract_weight, predictor_contract_bias, cotangent):
    listed = [encoder_pre_gain, encoder_pre_shift, encoder_joint_weight, encoder_query_bias, encoder_value_bias, encoder_out_weight, encoder_out_bias, encoder_mid_gain, encoder_mid_shift, encoder_expand_weight, encoder_expand_bias, encoder_contract_weight, encoder_contract_bias, embed_weight, embed_bias, mask_token, predictor_pre_gain, predictor_pre_shift, predictor_joint_weight, predictor_query_bias, predictor_value_bias, predictor_out_weight, predictor_out_bias, predictor_mid_gain, predictor_mid_shift, predictor_expand_weight, predictor_expand_bias, predictor_contract_weight, predictor_contract_bias]
    weights = [member.astype(jnp.float32) for member in listed]
    slot_visible = jnp.take_along_axis(visible, slot_token, axis=1)
    slot_code = positions[slot_token]
    group_size = 2 if CLIPS % 2 == 0 else 1
    group_count = CLIPS // group_size

    def group_step(totals, operands):
        group_tokens, group_visible, group_code, group_cot = operands

        def function(weight_list, inputs):
            return forward(weight_list, inputs, group_visible, group_code)
        predicted, pull_back, encoded = jax.vjp(function, weights, group_tokens, has_aux=True)
        weight_grads, input_grads = pull_back(group_cot)
        totals = [running + fresh for running, fresh in zip(totals, weight_grads)]
        return (totals, (encoded, predicted, input_grads))
    initial = [jnp.zeros_like(member) for member in weights]
    operands = (tokens.reshape(group_count, group_size, LEN, D), slot_visible.reshape(group_count, group_size, LEN), slot_code.reshape(group_count, group_size, LEN, P_SIZE), cotangent.reshape(group_count, group_size, LEN, P_SIZE))
    totals, (encoded, predicted, grad_tokens) = lax.scan(group_step, initial, operands)
    encoded = encoded.reshape(CLIPS, LEN, D)
    predicted = predicted.reshape(CLIPS, LEN, P_SIZE)
    grad_tokens = grad_tokens.reshape(CLIPS, LEN, D)
    return (encoded, predicted, grad_tokens, totals[0], totals[1], totals[2], totals[3], totals[4], totals[5], totals[6], totals[7], totals[8], totals[9], totals[10], totals[11], totals[12], totals[13], totals[14], totals[15], totals[16], totals[17], totals[18], totals[19], totals[20], totals[21], totals[22], totals[23], totals[24], totals[25], totals[26], totals[27], totals[28])
```

```python
import functools
import math

import jax
import jax.numpy as jnp
from jax import lax
from jax.experimental import pallas as pl
from jax.experimental.pallas import tpu as pltpu
from jax.sharding import PartitionSpec as P

HEADS = 16
PHEADS = 12

f32 = jnp.float32
bf16 = jnp.bfloat16
norm_eps = 1e-06
LOG2E = math.log2(math.e)
NN = (((1,), (0,)), ((), ()))
NT = (((1,), (1,)), ((), ()))
TN = (((0,), (0,)), ((), ()))
VMEM_LIMIT = 60 * 2**20


def mm(left, right, dims=NN):
    return lax.dot_general(left, right, dims, preferred_element_type=f32)


def norm_parts(value):
    center = value - jnp.mean(value, axis=-1, keepdims=True)
    spread = jnp.mean(center * center, axis=-1, keepdims=True)
    scale = lax.rsqrt(spread + norm_eps)
    return center * scale, scale


def norm_layer(value, gain, shift):
    unit, _ = norm_parts(value)
    return (unit * gain + shift).astype(bf16)


def norm_back(value, gain, grad):
    unit, scale = norm_parts(value)
    grad_gain = jnp.sum(grad * unit, axis=0)
    grad_shift = jnp.sum(grad, axis=0)
    inner = grad * gain
    inner = inner - jnp.mean(inner, axis=-1, keepdims=True) - unit * jnp.mean(
        inner * unit, axis=-1, keepdims=True
    )
    return scale * inner, grad_gain, grad_shift


def gelu_parts(hidden):
    cdf = 0.5 * (1.0 + lax.erf(hidden * math.sqrt(0.5)))
    return cdf


def gelu(hidden):
    return (hidden * gelu_parts(hidden)).astype(bf16)


def gelu_slope(hidden):
    pdf = jnp.exp(-0.5 * hidden * hidden) * (1.0 / math.sqrt(2.0 * math.pi))
    return gelu_parts(hidden) + hidden * pdf


def forward_kernel(scale, head_size, q_ref, k_ref, v_ref, *rest):
    if len(rest) == 2:
        bias_ref, o_ref = rest
    else:
        bias_ref, o_ref = None, rest[0]
    head = pl.program_id(2)
    query = q_ref[0]
    lane = lax.broadcasted_iota(jnp.int32, query.shape, 1)
    mine = (lane // head_size) == head
    own_query = jnp.where(mine, query, jnp.zeros_like(query))
    scores = mm(own_query, k_ref[0], NT) * (scale * LOG2E)
    if bias_ref is not None:
        scores = scores + bias_ref[0]
    top = jnp.max(scores, axis=1, keepdims=True)
    weight = jnp.exp2(scores - top)
    total = jnp.sum(weight, axis=1, keepdims=True)
    result = (mm(weight.astype(bf16), v_ref[0]) / total).astype(bf16)

    @pl.when(head == 0)
    def _():
        o_ref[0] = result

    @pl.when(head > 0)
    def _():
        o_ref[0] = jnp.where(mine, result, o_ref[0])


def attend(queries, joined, head_size, bias):
    clips, rows, width = queries.shape
    keys = joined.shape[1]
    groups = width // 128
    in_specs = [
        pl.BlockSpec((1, rows, 128), lambda c, g, h: (c, 0, g)),
        pl.BlockSpec((1, keys, 128), lambda c, g, h: (c, 0, g)),
        pl.BlockSpec((1, keys, 128), lambda c, g, h: (c, 0, g + groups)),
    ]
    operands = [queries, joined, joined]
    if bias is not None:
        in_specs.append(pl.BlockSpec((1, 1, keys), lambda c, g, h: (c, 0, 0)))
        operands.append(bias)
    cells = clips * rows * keys * (width // head_size)
    return pl.pallas_call(
        functools.partial(forward_kernel, 1.0 / math.sqrt(head_size), head_size),
        grid=(clips, groups, 128 // head_size),
        in_specs=in_specs,
        out_specs=pl.BlockSpec((1, rows, 128), lambda c, g, h: (c, 0, g)),
        out_shape=jax.ShapeDtypeStruct((clips, rows, width), bf16),
        compiler_params=pltpu.CompilerParams(vmem_limit_bytes=VMEM_LIMIT),
        cost_estimate=pl.CostEstimate(
            flops=cells * 1024, bytes_accessed=4 * clips * keys * width, transcendentals=cells
        ),
        name="attend",
    )(*operands)


def backward_kernel(scale, head_size, q_ref, k_ref, v_ref, g_ref, *rest):
    if len(rest) == 7:
        bias_ref = rest[0]
        rest = rest[1:]
    else:
        bias_ref = None
    dq_ref, dk_ref, dv_ref, dq_sum, dk_sum, dv_sum = rest
    part = pl.program_id(2)
    head = pl.program_id(3)
    query, key, value, grad = q_ref[0], k_ref[0], v_ref[0], g_ref[0]
    lane = lax.broadcasted_iota(jnp.int32, query.shape, 1)
    mine = (lane // head_size) == head
    zero = jnp.zeros_like(query)
    own_query = jnp.where(mine, query, zero)
    own_grad = jnp.where(mine, grad, zero)
    key_lane = lax.broadcasted_iota(jnp.int32, key.shape, 1)
    own_key = jnp.where((key_lane // head_size) == head, key, jnp.zeros_like(key))
    scores = mm(own_query, key, NT) * (scale * LOG2E)
    if bias_ref is not None:
        scores = scores + bias_ref[0]
    top = jnp.max(scores, axis=1, keepdims=True)
    weight = jnp.exp2(scores - top)
    total = jnp.sum(weight, axis=1, keepdims=True)
    chance = weight * (1.0 / total)
    grad_chance = mm(own_grad, value, NT)
    delta = jnp.sum(chance * grad_chance, axis=1, keepdims=True)
    grad_scores = (chance * (grad_chance - delta)).astype(bf16)
    part_q = mm(grad_scores, own_key)
    part_v = mm(own_grad, chance.astype(bf16), TN)
    part_k = mm(own_query, grad_scores, TN)

    @pl.when(head == 0)
    def _():
        dq_sum[...] = part_q

    @pl.when(head > 0)
    def _():
        dq_sum[...] += part_q

    @pl.when((head == 0) & (part == 0))
    def _():
        dk_sum[...] = part_k
        dv_sum[...] = part_v

    @pl.when((head > 0) | (part > 0))
    def _():
        dk_sum[...] += part_k
        dv_sum[...] += part_v

    last_head = head == pl.num_programs(3) - 1

    @pl.when(last_head)
    def _():
        dq_ref[0] = (dq_sum[...] * scale).astype(bf16)

    @pl.when(last_head & (part == pl.num_programs(2) - 1))
    def _():
        dk_ref[0] = (dk_sum[...] * scale).T.astype(bf16)
        dv_ref[0] = dv_sum[...].T.astype(bf16)


def attend_back(queries, keys, values, grad_mixed, head_size, bias, parts):
    clips, length, width = queries.shape
    lanes = min(width, 128)
    groups = width // lanes
    rows = length // parts
    by_query = pl.BlockSpec((1, rows, lanes), lambda c, g, r, h: (c, r, g))
    by_key = pl.BlockSpec((1, length, lanes), lambda c, g, r, h: (c, 0, g))
    in_specs = [by_query, by_key, by_key, by_query]
    operands = [queries, keys, values, grad_mixed]
    if bias is not None:
        in_specs.append(pl.BlockSpec((1, 1, length), lambda c, g, r, h: (c, 0, 0)))
        operands.append(bias)
    cells = clips * length * length * (width // head_size)
    shape = jax.ShapeDtypeStruct((clips, length, width), bf16)
    return pl.pallas_call(
        functools.partial(backward_kernel, 1.0 / math.sqrt(head_size), head_size),
        grid=(clips, groups, parts, lanes // head_size),
        in_specs=in_specs,
        out_specs=[by_query, by_key, by_key],
        out_shape=[shape, shape, shape],
        scratch_shapes=[
            pltpu.VMEM((rows, lanes), f32),
            pltpu.VMEM((lanes, length), f32),
            pltpu.VMEM((lanes, length), f32),
        ],
        compiler_params=pltpu.CompilerParams(vmem_limit_bytes=VMEM_LIMIT),
        cost_estimate=pl.CostEstimate(
            flops=cells * 2560, bytes_accessed=14 * clips * length * width, transcendentals=cells
        ),
        name="attend_back",
    )(*operands)


def heads_from_slots(array, shards):
    if shards == 1:
        return array
    return lax.all_to_all(array, "seq", split_axis=2, concat_axis=1, tiled=True)


def slots_from_heads(array, shards):
    if shards == 1:
        return array
    return lax.all_to_all(array, "seq", split_axis=2, concat_axis=3, tiled=True)


def own_columns(joint_weight, query_bias, value_bias, shards, shard):
    width = joint_weight.shape[0]
    own = width // shards
    weight = lax.dynamic_slice_in_dim(joint_weight.reshape(width, 3, width), shard * own, own, 2)
    bias_q = lax.dynamic_slice_in_dim(query_bias, shard * own, own, 0)
    bias_v = lax.dynamic_slice_in_dim(value_bias, shard * own, own, 0)
    return weight, bias_q, bias_v


def attention_back(grad_mixed, normed_all, weights, head_size, bias, parts, shards, shard):
    joint_weight, query_bias, value_bias = weights
    clips, length, width = normed_all.shape
    own_weight, bias_q, bias_v = own_columns(joint_weight, query_bias, value_bias, shards, shard)
    own = own_weight.shape[2]
    flat = normed_all.reshape(clips * length, width)
    queries = (mm(flat, own_weight[:, 0]) + bias_q).astype(bf16).reshape(clips, length, own)
    keys = mm(flat, own_weight[:, 1]).astype(bf16).reshape(clips, length, own)
    values = (mm(flat, own_weight[:, 2]) + bias_v).astype(bf16).reshape(clips, length, own)
    own_grad = heads_from_slots(grad_mixed, shards)
    grads = attend_back(queries, keys, values, own_grad, head_size, bias, parts)
    flat_grads = [member.reshape(clips * length, own) for member in grads]
    grad_weight = [mm(flat, member, TN).astype(bf16) for member in flat_grads]
    grad_query_bias = jnp.sum(flat_grads[0].astype(f32), axis=0)
    grad_value_bias = jnp.sum(flat_grads[2].astype(f32), axis=0)
    back = slots_from_heads(jnp.stack(grads), shards)
    return back, jnp.stack(grad_weight, axis=1), grad_query_bias, grad_value_bias


def joint_back(grad_joint, joint_weight):
    _, clips, rows, width = grad_joint.shape
    total = None
    for index in range(3):
        term = mm(
            grad_joint[index].reshape(clips * rows, width),
            joint_weight[:, index * width : (index + 1) * width],
            NT,
        )
        total = term if total is None else total + term
    return total


def split_packed(packed, sizes):
    out = []
    at = 0
    for size in sizes:
        out.append(packed[:, at : at + size].reshape(-1).astype(f32))
        at += size
    return out


def gather(array):
    return lax.all_gather(array, "fsdp", axis=0, tiled=True)


def scatter(array):
    return lax.psum_scatter(array, "fsdp", scatter_dimension=0, tiled=True)


def across_slots(array):
    return lax.psum(array, "seq").astype(f32)


def body(
    fsdp_size,
    seq_size,
    tokens,
    visible,
    slot_token,
    positions,
    encoder_pre_gain,
    encoder_pre_shift,
    encoder_joint_weight,
    encoder_query_bias,
    encoder_value_bias,
    encoder_out_weight,
    encoder_out_bias,
    encoder_mid_gain,
    encoder_mid_shift,
    encoder_expand_weight,
    encoder_expand_bias,
    encoder_contract_weight,
    encoder_contract_bias,
    embed_weight,
    embed_bias,
    mask_token,
    predictor_pre_gain,
    predictor_pre_shift,
    predictor_joint_weight,
    predictor_query_bias,
    predictor_value_bias,
    predictor_out_weight,
    predictor_out_bias,
    predictor_mid_gain,
    predictor_mid_shift,
    predictor_expand_weight,
    predictor_expand_bias,
    predictor_contract_weight,
    predictor_contract_bias,
    cotangent,
):
    shard = lax.axis_index("seq")
    clips, slots, width = tokens.shape
    span = visible.shape[1]
    rows = clips * slots
    small_width = cotangent.shape[2]
    head_size = width // HEADS
    small_head = small_width // PHEADS

    vectors = (
        encoder_pre_gain,
        encoder_pre_shift,
        encoder_query_bias,
        encoder_value_bias,
        encoder_out_bias,
        encoder_mid_gain,
        encoder_mid_shift,
        encoder_expand_bias,
        encoder_contract_bias,
        embed_bias,
        mask_token,
        predictor_pre_gain,
        predictor_pre_shift,
        predictor_query_bias,
        predictor_value_bias,
        predictor_out_bias,
        predictor_mid_gain,
        predictor_mid_shift,
        predictor_expand_bias,
        predictor_contract_bias,
    )
    sizes = [member.shape[0] for member in vectors]
    packed = lax.all_gather(jnp.concatenate(vectors), "fsdp", axis=0, tiled=False)
    (
        e_pre_gain,
        e_pre_shift,
        e_query_bias,
        e_value_bias,
        e_out_bias,
        e_mid_gain,
        e_mid_shift,
        e_expand_bias,
        e_contract_bias,
        embed_bias_full,
        mask_full,
        p_pre_gain,
        p_pre_shift,
        p_query_bias,
        p_value_bias,
        p_out_bias,
        p_mid_gain,
        p_mid_shift,
        p_expand_bias,
        p_contract_bias,
    ) = split_packed(packed, sizes)

    e_joint = gather(encoder_joint_weight)
    e_out = gather(encoder_out_weight)
    e_expand = gather(encoder_expand_weight)
    e_contract = gather(encoder_contract_weight)
    embed_full = gather(embed_weight)
    p_joint = gather(predictor_joint_weight)
    p_out = gather(predictor_out_weight)
    p_expand = gather(predictor_expand_weight)
    p_contract = gather(predictor_contract_weight)

    place = lax.broadcasted_iota(jnp.int32, (1, 1, span), 2)
    slot_visible = jnp.any(
        (slot_token[:, :, None] == place) & (visible[:, None, :] > 0), axis=2
    )
    own_visible = lax.dynamic_slice_in_dim(slot_visible, shard * slots, slots, 1)
    own_flat = own_visible.reshape(rows, 1)
    own_tokens = lax.dynamic_slice_in_dim(slot_token, shard * slots, slots, 1)
    slot_code = jnp.take(positions, own_tokens.reshape(rows), axis=0)
    bias = jnp.where(slot_visible, 0.0, -1e30).astype(f32).reshape(clips, 1, span)

    inputs = tokens.reshape(rows, width)
    normed = norm_layer(inputs, e_pre_gain, e_pre_shift)
    normed_all = lax.all_gather(normed.reshape(clips, slots, width), "seq", axis=1, tiled=True)
    length = normed_all.shape[1]
    queries = (mm(normed, e_joint[:, :width]) + e_query_bias).astype(bf16)
    joined = mm(normed_all.reshape(clips * length, width), e_joint[:, width:])
    joined = (joined + jnp.concatenate([jnp.zeros_like(e_value_bias), e_value_bias])).astype(bf16)
    mixed = attend(
        queries.reshape(clips, slots, width),
        joined.reshape(clips, length, 2 * width),
        head_size,
        bias,
    ).reshape(rows, width)
    middle = inputs + mm(mixed, e_out) + e_out_bias
    normed_mid = norm_layer(middle, e_mid_gain, e_mid_shift)
    hidden = mm(normed_mid, e_expand) + e_expand_bias
    active = gelu(hidden)
    encoded = middle + mm(active, e_contract) + e_contract_bias
    context = encoded.astype(bf16)

    embedded = mm(context, embed_full) + embed_bias_full
    pred_input = jnp.where(own_flat, embedded, mask_full) + slot_code
    p_normed = norm_layer(pred_input, p_pre_gain, p_pre_shift)
    p_normed_all = lax.all_gather(
        p_normed.reshape(clips, slots, small_width), "seq", axis=1, tiled=True
    )
    p_queries = (mm(p_normed, p_joint[:, :small_width]) + p_query_bias).astype(bf16)
    p_joined = mm(p_normed_all.reshape(clips * span, small_width), p_joint[:, small_width:])
    p_joined = (p_joined + jnp.concatenate([jnp.zeros_like(p_value_bias), p_value_bias])).astype(
        bf16
    )
    p_mixed = attend(
        p_queries.reshape(clips, slots, small_width),
        p_joined.reshape(clips, span, 2 * small_width),
        small_head,
        None,
    ).reshape(rows, small_width)
    p_middle = pred_input + mm(p_mixed, p_out) + p_out_bias
    p_normed_mid = norm_layer(p_middle, p_mid_gain, p_mid_shift)
    p_hidden = mm(p_normed_mid, p_expand) + p_expand_bias
    p_active = gelu(p_hidden)
    predicted = p_middle + mm(p_active, p_contract) + p_contract_bias

    def block_back(
        grad_out,
        inputs,
        normed_all,
        mixed,
        middle,
        normed_mid,
        hidden,
        active,
        weights,
        vectors,
        head_size,
        bias,
        parts,
        clips,
    ):
        joint, out, expand, contract = weights
        pre_gain, mid_gain, query_bias, value_bias = vectors
        local_rows = inputs.shape[0] // clips
        grad_y = grad_out.astype(bf16)
        grad_contract = mm(active, grad_y, TN).astype(bf16)
        grad_contract_bias = jnp.sum(grad_y.astype(f32), axis=0)
        grad_hidden = (mm(grad_y, contract, NT) * gelu_slope(hidden)).astype(bf16)
        grad_expand = mm(normed_mid, grad_hidden, TN).astype(bf16)
        grad_expand_bias = jnp.sum(grad_hidden.astype(f32), axis=0)
        grad_norm, grad_mid_gain, grad_mid_shift = norm_back(
            middle, mid_gain, mm(grad_hidden, expand, NT)
        )
        grad_middle = grad_out + grad_norm
        grad_att = grad_middle.astype(bf16)
        grad_out_weight = mm(mixed, grad_att, TN).astype(bf16)
        grad_out_bias = jnp.sum(grad_att.astype(f32), axis=0)
        grad_mixed = mm(grad_att, out, NT).astype(bf16).reshape(clips, local_rows, -1)
        grad_joint, grad_joint_weight, grad_query_bias, grad_value_bias = attention_back(
            grad_mixed,
            normed_all,
            (joint, query_bias, value_bias),
            head_size,
            bias,
            parts,
            seq_size,
            shard,
        )
        grad_norm, grad_pre_gain, grad_pre_shift = norm_back(
            inputs, pre_gain, joint_back(grad_joint, joint)
        )
        grad_inputs = grad_middle + grad_norm
        small = dict(
            pre_gain=grad_pre_gain,
            pre_shift=grad_pre_shift,
            query_bias=grad_query_bias,
            value_bias=grad_value_bias,
            out_bias=grad_out_bias,
            mid_gain=grad_mid_gain,
            mid_shift=grad_mid_shift,
            expand_bias=grad_expand_bias,
            contract_bias=grad_contract_bias,
        )
        return (
            grad_inputs,
            (grad_joint_weight, grad_out_weight, grad_expand, grad_contract),
            small,
        )

    grad_pred_input, p_grads, p_small = block_back(
        cotangent.reshape(rows, small_width),
        pred_input,
        p_normed_all,
        p_mixed,
        p_middle,
        p_normed_mid,
        p_hidden,
        p_active,
        (p_joint, p_out, p_expand, p_contract),
        (p_pre_gain, p_mid_gain, p_query_bias, p_value_bias),
        small_head,
        None,
        seq_size,
        clips,
    )
    grad_mask_token = jnp.sum(jnp.where(own_flat, 0.0, grad_pred_input), axis=0)
    grad_embedded = jnp.where(own_flat, grad_pred_input, 0.0).astype(bf16)
    grad_embed_weight = mm(context, grad_embedded, TN).astype(bf16)
    grad_embed_bias = jnp.sum(grad_embedded.astype(f32), axis=0)

    grad_context = mm(grad_embedded, embed_full, NT)
    grad_tokens, e_grads, e_small = block_back(
        grad_context,
        inputs,
        normed_all,
        mixed,
        middle,
        normed_mid,
        hidden,
        active,
        (e_joint, e_out, e_expand, e_contract),
        (e_pre_gain, e_mid_gain, e_query_bias, e_value_bias),
        head_size,
        bias,
        seq_size,
        clips,
    )

    def joint_total(grad):
        part = scatter(grad)
        whole = lax.all_gather(part, "seq", axis=2, tiled=True)
        return whole.reshape(part.shape[0], -1).astype(f32)

    def total(grad):
        return across_slots(scatter(grad))

    def spread(vector):
        full = jnp.zeros((vector.shape[0] * seq_size,), f32)
        return lax.dynamic_update_slice_in_dim(full, vector, shard * vector.shape[0], 0)

    for small in (e_small, p_small):
        small["query_bias"] = spread(small["query_bias"])
        small["value_bias"] = spread(small["value_bias"])
    order = (
        "pre_gain",
        "pre_shift",
        "query_bias",
        "value_bias",
        "out_bias",
        "mid_gain",
        "mid_shift",
        "expand_bias",
        "contract_bias",
    )
    small_grads = [e_small[name] for name in order]
    small_grads += [grad_embed_bias, grad_mask_token]
    small_grads += [p_small[name] for name in order]
    small_packed = jnp.concatenate(
        [member.reshape(fsdp_size, -1) for member in small_grads], axis=1
    )
    small_sum = lax.psum(small_packed, ("fsdp", "seq"))
    own_small = lax.dynamic_slice_in_dim(small_sum, lax.axis_index("fsdp"), 1, 0)[0]
    small_out = []
    at = 0
    for size in sizes:
        small_out.append(own_small[at : at + size])
        at += size
    e_vec = dict(zip(order, small_out[:9]))
    embed_bias_out, mask_out = small_out[9], small_out[10]
    p_vec = dict(zip(order, small_out[11:]))

    def ordered(vec, grads):
        joint, out, expand, contract = grads
        return (
            vec["pre_gain"],
            vec["pre_shift"],
            joint_total(joint),
            vec["query_bias"],
            vec["value_bias"],
            total(out),
            vec["out_bias"],
            vec["mid_gain"],
            vec["mid_shift"],
            total(expand),
            vec["expand_bias"],
            total(contract),
            vec["contract_bias"],
        )

    return (
        encoded.reshape(tokens.shape),
        predicted.reshape(cotangent.shape),
        grad_tokens.reshape(tokens.shape),
        *ordered(e_vec, e_grads),
        total(grad_embed_weight),
        embed_bias_out,
        mask_out,
        *ordered(p_vec, p_grads),
    )


def solution(mesh):
    cut, rows, slots, vec, full = (
        P("fsdp", "seq", None),
        P("fsdp", None),
        P("fsdp", None),
        P("fsdp"),
        P(),
    )
    block = (vec, vec, rows, vec, vec, rows, vec, vec, vec, rows, vec, rows, vec)
    return jax.shard_map(
        functools.partial(body, mesh.shape["fsdp"], mesh.shape["seq"]),
        mesh=mesh,
        in_specs=(cut, slots, slots, full, *block, rows, vec, vec, *block, cut),
        out_specs=(cut, cut, cut, *block, rows, vec, vec, *block),
        check_vma=False,
    )
```

```python
import functools
import math

import jax
import jax.numpy as jnp
from jax import lax
from jax.experimental import pallas as pl
from jax.experimental.pallas import tpu as pltpu
from jax.sharding import PartitionSpec as P

HEADS = 16
PHEADS = 12

f32 = jnp.float32
bf16 = jnp.bfloat16
norm_eps = 1e-06
LOG2E = math.log2(math.e)
NN = (((1,), (0,)), ((), ()))
NT = (((1,), (1,)), ((), ()))
TN = (((0,), (0,)), ((), ()))
VMEM_LIMIT = 60 * 2**20


def mm(left, right, dims=NN):
    return lax.dot_general(left, right, dims, preferred_element_type=f32)


def norm_parts(value):
    center = value - jnp.mean(value, axis=-1, keepdims=True)
    spread = jnp.mean(center * center, axis=-1, keepdims=True)
    scale = lax.rsqrt(spread + norm_eps)
    return center * scale, scale


def norm_layer(value, gain, shift):
    unit, _ = norm_parts(value)
    return (unit * gain + shift).astype(bf16)


def norm_back(value, gain, grad):
    unit, scale = norm_parts(value)
    grad_gain = jnp.sum(grad * unit, axis=0)
    grad_shift = jnp.sum(grad, axis=0)
    inner = grad * gain
    inner = inner - jnp.mean(inner, axis=-1, keepdims=True) - unit * jnp.mean(
        inner * unit, axis=-1, keepdims=True
    )
    return scale * inner, grad_gain, grad_shift


def gelu_parts(hidden):
    cdf = 0.5 * (1.0 + lax.erf(hidden * math.sqrt(0.5)))
    return cdf


def gelu(hidden):
    return (hidden * gelu_parts(hidden)).astype(bf16)


def gelu_slope(hidden):
    pdf = jnp.exp(-0.5 * hidden * hidden) * (1.0 / math.sqrt(2.0 * math.pi))
    return gelu_parts(hidden) + hidden * pdf


def forward_kernel(scale, head_size, q_ref, k_ref, v_ref, *rest):
    if len(rest) == 2:
        bias_ref, o_ref = rest
    else:
        bias_ref, o_ref = None, rest[0]
    head = pl.program_id(2)
    query = q_ref[0]
    key = k_ref[...].reshape(-1, k_ref.shape[-1])
    value = v_ref[...].reshape(-1, v_ref.shape[-1])
    lane = lax.broadcasted_iota(jnp.int32, query.shape, 1)
    mine = (lane // head_size) == head
    own_query = jnp.where(mine, query, jnp.zeros_like(query))
    scores = mm(own_query, key, NT) * (scale * LOG2E)
    if bias_ref is not None:
        scores = scores + bias_ref[0]
    top = jnp.max(scores, axis=1, keepdims=True)
    weight = jnp.exp2(scores - top)
    total = jnp.sum(weight, axis=1, keepdims=True)
    result = (mm(weight.astype(bf16), value) / total).astype(bf16)

    @pl.when(head == 0)
    def _():
        o_ref[0] = result

    @pl.when(head > 0)
    def _():
        o_ref[0] = jnp.where(mine, result, o_ref[0])


def attend(queries, joined, head_size, bias):
    clips, rows, width = queries.shape
    major, _, length, _ = joined.shape
    keys = major * length
    groups = width // 128
    in_specs = [
        pl.BlockSpec((1, rows, 128), lambda c, g, h: (c, 0, g)),
        pl.BlockSpec((major, 1, length, 128), lambda c, g, h: (0, c, 0, g)),
        pl.BlockSpec((major, 1, length, 128), lambda c, g, h: (0, c, 0, g + groups)),
    ]
    operands = [queries, joined, joined]
    if bias is not None:
        in_specs.append(pl.BlockSpec((1, 1, keys), lambda c, g, h: (c, 0, 0)))
        operands.append(bias)
    cells = clips * rows * keys * (width // head_size)
    return pl.pallas_call(
        functools.partial(forward_kernel, 1.0 / math.sqrt(head_size), head_size),
        grid=(clips, groups, 128 // head_size),
        in_specs=in_specs,
        out_specs=pl.BlockSpec((1, rows, 128), lambda c, g, h: (c, 0, g)),
        out_shape=jax.ShapeDtypeStruct((clips, rows, width), bf16),
        compiler_params=pltpu.CompilerParams(vmem_limit_bytes=VMEM_LIMIT),
        cost_estimate=pl.CostEstimate(
            flops=cells * 1024, bytes_accessed=4 * clips * keys * width, transcendentals=cells
        ),
        name="attend",
    )(*operands)


def backward_kernel(scale, head_size, shards, q_ref, k_ref, v_ref, g_ref, *rest):
    if len(rest) == 5:
        bias_ref = rest[0]
        rest = rest[1:]
    else:
        bias_ref = None
    out_ref, dq_sum, dk_sum, dv_sum = rest
    group = pl.program_id(1)
    part = pl.program_id(2)
    head = pl.program_id(3)
    lanes = q_ref.shape[-1]
    query = q_ref[...].reshape(-1, lanes)
    key = k_ref[...].reshape(-1, lanes)
    value = v_ref[...].reshape(-1, lanes)
    grad = g_ref[...].reshape(-1, lanes)
    lane = lax.broadcasted_iota(jnp.int32, query.shape, 1)
    mine = (lane // head_size) == head
    zero = jnp.zeros_like(query)
    own_query = jnp.where(mine, query, zero)
    own_grad = jnp.where(mine, grad, zero)
    key_lane = lax.broadcasted_iota(jnp.int32, key.shape, 1)
    own_key = jnp.where((key_lane // head_size) == head, key, jnp.zeros_like(key))
    scores = mm(own_query, key, NT) * (scale * LOG2E)
    if bias_ref is not None:
        scores = scores + bias_ref[0]
    top = jnp.max(scores, axis=1, keepdims=True)
    weight = jnp.exp2(scores - top)
    total = jnp.sum(weight, axis=1, keepdims=True)
    chance = weight * (1.0 / total)
    grad_chance = mm(own_grad, value, NT)
    delta = jnp.sum(chance * grad_chance, axis=1, keepdims=True)
    grad_scores = (chance * (grad_chance - delta)).astype(bf16)
    part_q = mm(grad_scores, own_key)
    part_v = mm(own_grad, chance.astype(bf16), TN)
    part_k = mm(own_query, grad_scores, TN)

    @pl.when(head == 0)
    def _():
        dq_sum[...] = part_q

    @pl.when(head > 0)
    def _():
        dq_sum[...] += part_q

    @pl.when((head == 0) & (part == 0))
    def _():
        dk_sum[...] = part_k
        dv_sum[...] = part_v

    @pl.when((head > 0) | (part > 0))
    def _():
        dk_sum[...] += part_k
        dv_sum[...] += part_v

    rows = out_ref.shape[2]
    width = out_ref.shape[3] // 3
    held = query.shape[0] // rows
    last_head = head == pl.num_programs(3) - 1

    def place(kind):
        if width == lanes:
            return slice(kind * width, (kind + 1) * width)
        return pl.ds(pl.multiple_of(kind * width + group * lanes, 128), lanes)

    @pl.when(last_head)
    def _():
        result = (dq_sum[...] * scale).astype(bf16)
        for index in range(held):
            out_ref[part * held + index, 0, :, place(0)] = result[index * rows : (index + 1) * rows]

    @pl.when(last_head & (part == pl.num_programs(2) - 1))
    def _():
        for kind, total_ref, factor in ((1, dk_sum, scale), (2, dv_sum, 1.0)):
            result = (total_ref[...] * factor).T.astype(bf16)
            for index in range(shards):
                out_ref[index, 0, :, place(kind)] = result[index * rows : (index + 1) * rows]


def attend_back(queries, keys, values, grad_mixed, head_size, bias, shards):
    major, clips, length, width = queries.shape
    lanes = min(width, 128)
    groups = width // lanes
    rows = major * length // shards
    parts = shards if major == 1 else 1
    query_rows = rows if major == 1 else length
    by_query = pl.BlockSpec((major, 1, query_rows, lanes), lambda c, g, r, h: (0, c, r, g))
    by_key = pl.BlockSpec((major, 1, length, lanes), lambda c, g, r, h: (0, c, 0, g))
    in_specs = [by_query, by_key, by_key, by_query]
    operands = [queries, keys, values, grad_mixed]
    total = major * length
    if bias is not None:
        in_specs.append(pl.BlockSpec((1, 1, total), lambda c, g, r, h: (c, 0, 0)))
        operands.append(bias)
    cells = clips * total * total * (width // head_size)
    return pl.pallas_call(
        functools.partial(backward_kernel, 1.0 / math.sqrt(head_size), head_size, shards),
        grid=(clips, groups, parts, lanes // head_size),
        in_specs=in_specs,
        out_specs=pl.BlockSpec((shards, 1, rows, 3 * width), lambda c, g, r, h: (0, c, 0, 0)),
        out_shape=jax.ShapeDtypeStruct((shards, clips, rows, 3 * width), bf16),
        scratch_shapes=[
            pltpu.VMEM((major * query_rows, lanes), f32),
            pltpu.VMEM((lanes, total), f32),
            pltpu.VMEM((lanes, total), f32),
        ],
        compiler_params=pltpu.CompilerParams(vmem_limit_bytes=VMEM_LIMIT),
        cost_estimate=pl.CostEstimate(
            flops=cells * 2560, bytes_accessed=14 * clips * total * width, transcendentals=cells
        ),
        name="attend_back",
    )(*operands)


def exchange(array):
    return lax.all_to_all(array, "seq", split_axis=0, concat_axis=0, tiled=True)


def gather(array):
    return lax.all_gather(array, "fsdp", axis=0, tiled=True)


def scatter(array):
    return lax.psum_scatter(array, "fsdp", scatter_dimension=0, tiled=True)[0]


def blocks_of(array, count, lanes):
    rows = array.shape[0] // count
    split = array.shape[1] // lanes
    array = array.reshape(count, rows, split, lanes)
    return array.transpose(0, 2, 1, 3).reshape(count, split * rows, lanes)


def from_blocks(array, lanes):
    split = lanes // array.shape[1]
    rows = array.shape[0] // split
    return array.reshape(split, rows, -1).transpose(1, 0, 2).reshape(rows, lanes)


def pack_rows(vectors):
    rows = []
    for member in vectors:
        count = -(-member.shape[0] // 128)
        padded = jnp.pad(member.astype(f32), (0, count * 128 - member.shape[0]))
        rows.append(padded.reshape(count, 128))
    total = sum(member.shape[0] for member in rows)
    if total % 8:
        rows.append(jnp.zeros((8 - total % 8, 128), f32))
    return jnp.concatenate(rows, axis=0)


def unpack_rows(packed, sizes):
    out = []
    at = 0
    for size in sizes:
        count = -(-size // 128)
        piece = packed[:, at : at + count].reshape(packed.shape[0], count * 128)[:, :size]
        out.append(piece.reshape(-1))
        at += count
    return out


def feed_back(grad_out, mixed, middle, normed_mid, hidden, active, weights, mid_gain):
    out, expand, contract = weights
    grad_y = grad_out.astype(bf16)
    grad_contract = mm(active, grad_y, TN).astype(bf16)
    grad_contract_bias = jnp.sum(grad_y.astype(f32), axis=0)
    grad_hidden = (mm(grad_y, contract, NT) * gelu_slope(hidden)).astype(bf16)
    grad_expand = mm(normed_mid, grad_hidden, TN).astype(bf16)
    grad_expand_bias = jnp.sum(grad_hidden.astype(f32), axis=0)
    grad_norm, grad_mid_gain, grad_mid_shift = norm_back(
        middle, mid_gain, mm(grad_hidden, expand, NT)
    )
    grad_middle = grad_out + grad_norm
    grad_att = grad_middle.astype(bf16)
    grad_out_weight = mm(mixed, grad_att, TN).astype(bf16)
    grad_out_bias = jnp.sum(grad_att.astype(f32), axis=0)
    grad_mixed = mm(grad_att, out, NT).astype(bf16)
    grads = (grad_out_weight, grad_expand, grad_contract)
    small = dict(
        out_bias=grad_out_bias,
        mid_gain=grad_mid_gain,
        mid_shift=grad_mid_shift,
        expand_bias=grad_expand_bias,
        contract_bias=grad_contract_bias,
    )
    return grad_middle, grad_mixed, grads, small


def own_joint(joint_weight, query_bias, value_bias, shards, shard):
    width = joint_weight.shape[0]
    own = width // shards
    weight = lax.dynamic_slice_in_dim(joint_weight.reshape(width, 3, width), shard * own, own, 2)
    bias_q = lax.dynamic_slice_in_dim(query_bias, shard * own, own, 0)
    bias_v = lax.dynamic_slice_in_dim(value_bias, shard * own, own, 0)
    return weight, (bias_q, None, bias_v)


def own_parts(normed_all, weight, biases):
    flat = normed_all.reshape(-1, normed_all.shape[3])
    out = []
    for index in range(3):
        part = mm(flat, weight[:, index])
        if biases[index] is not None:
            part = part + biases[index]
        out.append(part.astype(bf16).reshape(normed_all.shape[:3] + (weight.shape[2],)))
    return out


def by_sender(joint_weight, shards):
    width = joint_weight.shape[0]
    array = joint_weight.reshape(width, 3, shards, width // shards)
    return array.transpose(0, 2, 1, 3).reshape(width, 3 * width)


def joint_back(received, joint_by_sender):
    shards, clips, rows, width = received.shape
    flat = received.reshape(shards, clips * rows, width).transpose(1, 0, 2)
    return mm(flat.reshape(clips * rows, shards * width), joint_by_sender, NT)


def spread(vector, shards, shard):
    full = jnp.zeros((vector.shape[0] * shards,), f32)
    return lax.dynamic_update_slice_in_dim(full, vector, shard * vector.shape[0], 0)


def joint_small(columns, shards, shard):
    own = columns.shape[0] // 3
    return dict(
        query_bias=spread(columns[:own], shards, shard),
        value_bias=spread(columns[2 * own :], shards, shard),
    )


ORDER = (
    "pre_gain",
    "pre_shift",
    "query_bias",
    "value_bias",
    "out_bias",
    "mid_gain",
    "mid_shift",
    "expand_bias",
    "contract_bias",
)
BLOCK = (
    "pre_gain",
    "pre_shift",
    "joint",
    "query_bias",
    "value_bias",
    "out",
    "out_bias",
    "mid_gain",
    "mid_shift",
    "expand",
    "expand_bias",
    "contract",
    "contract_bias",
)
FRAMES = 8
GRID = 14
MOST_VISIBLE = FRAMES * max(
    high * wide
    for high in range(1, GRID + 1)
    for wide in range(1, GRID + 1)
    if 2 * high * wide < GRID * GRID
)


def body(fsdp_size, seq_size, tokens, visible, slot_token, positions, *rest):
    e_shard = dict(zip(BLOCK, rest[:13]))
    embed_weight, embed_bias, mask_token = rest[13:16]
    p_shard = dict(zip(BLOCK, rest[16:29]))
    cotangent = rest[29]
    shard = lax.axis_index("seq")
    clips, slots, width = tokens.shape
    span = visible.shape[1]

    e_out = gather(e_shard["out"])

    place = lax.broadcasted_iota(jnp.int32, (1, 1, span), 2)
    slot_visible = jnp.any(
        (slot_token[:, :, None] == place) & (visible[:, None, :] > 0), axis=2
    )
    counts = jnp.sum(slot_visible.reshape(clips, seq_size, slots).astype(jnp.int32), axis=2)
    compact = -(-MOST_VISIBLE // (16 * seq_size)) * 16
    fits = (jnp.max(counts) <= compact).astype(f32)

    vectors = [e_shard[name] for name in ORDER] + [embed_bias, mask_token]
    vectors += [p_shard[name] for name in ORDER]
    sizes = [member.shape[0] for member in vectors]
    packed = lax.all_gather(
        pack_rows(vectors + [jnp.full((1,), fits)]), "fsdp", axis=0, tiled=False
    )
    full = unpack_rows(packed, sizes + [1])
    all_fit = jnp.min(full[-1]) > 0.5

    operands = (
        tokens,
        slot_visible,
        counts,
        slot_token,
        positions,
        e_out,
        e_shard["joint"],
        e_shard["expand"],
        e_shard["contract"],
        embed_weight,
        tuple(p_shard[name] for name in ("joint", "out", "expand", "contract")),
        tuple(full[:-1]),
        cotangent,
    )
    whole = functools.partial(main, fsdp_size, seq_size, slots)
    if compact >= slots:
        return whole(*operands)
    return lax.cond(
        all_fit, functools.partial(main, fsdp_size, seq_size, compact), whole, *operands
    )


def main(
    fsdp_size,
    seq_size,
    held,
    tokens,
    slot_visible,
    counts,
    slot_token,
    positions,
    e_out,
    e_joint_shard,
    e_expand_shard,
    e_contract_shard,
    embed_shard,
    p_shards,
    vectors,
    cotangent,
):
    shard = lax.axis_index("seq")
    clips, slots, width = tokens.shape
    span = slot_visible.shape[1]
    rows = clips * slots
    small_width = cotangent.shape[2]
    head_size = width // HEADS
    small_head = small_width // PHEADS
    whole = held == slots
    e_vec = dict(zip(ORDER, vectors[:9]))
    embed_bias, mask_token = vectors[9:11]
    p_vec = dict(zip(ORDER, vectors[11:]))

    e_joint = gather(e_joint_shard)
    e_expand = gather(e_expand_shard)
    e_contract = gather(e_contract_shard)
    packed = jnp.concatenate(
        [blocks_of(member, 1, small_width)[0] for member in (*p_shards, embed_shard)], axis=0
    )
    packed = lax.all_gather(packed, "fsdp", axis=0, tiled=False)
    unpacked = []
    at = 0
    for member in (*p_shards, embed_shard):
        split = member.shape[1] // small_width
        count = member.shape[0] * split
        piece = packed[:, at : at + count].reshape(fsdp_size, split, member.shape[0], small_width)
        unpacked.append(piece.transpose(0, 2, 1, 3).reshape(-1, member.shape[1]))
        at += count
    p_joint, p_out, p_expand, p_contract, embed = unpacked

    own_visible = lax.dynamic_slice_in_dim(slot_visible, shard * slots, slots, 1)
    own_flat = own_visible.reshape(rows, 1)
    own_tokens = lax.dynamic_slice_in_dim(slot_token, shard * slots, slots, 1)
    slot_code = jnp.take(positions, own_tokens.reshape(rows), axis=0)

    if whole:
        kept = slot_visible.reshape(clips, 1, span)

        def keep(array):
            return array

        def put_back(array):
            return array

    else:
        kept = lax.broadcasted_iota(jnp.int32, (1, 1, held), 2) < counts[:, :, None]
        kept = kept.reshape(clips, 1, seq_size * held)
        ones = own_visible.astype(bf16)
        before = lax.broadcasted_iota(jnp.int32, (slots, slots), 0)
        after = lax.broadcasted_iota(jnp.int32, (slots, slots), 1)
        rank = mm(ones, (before < after).astype(bf16)).astype(jnp.int32)
        target = lax.broadcasted_iota(jnp.int32, (1, held, 1), 1)
        picks = ((rank[:, None, :] == target) & own_visible[:, None, :]).astype(bf16)

        def keep(array):
            precision = lax.Precision.HIGHEST if array.dtype == f32 else None
            picked = jnp.einsum(
                "crs,csw->crw",
                picks.astype(array.dtype),
                array.reshape(clips, slots, -1),
                precision=precision,
                preferred_element_type=f32,
            )
            return picked.astype(array.dtype).reshape(clips * held, -1)

        def put_back(array):
            placed = jnp.einsum(
                "crs,crw->csw",
                picks.astype(f32),
                array.reshape(clips, held, -1),
                precision=lax.Precision.HIGHEST,
                preferred_element_type=f32,
            )
            return placed.reshape(rows, -1)

    bias = jnp.where(kept, 0.0, -1e30).astype(f32)
    tiled = held % 16 == 0

    def by_clip(array):
        if tiled:
            return array
        shards, count, length, lanes = array.shape
        return array.transpose(1, 0, 2, 3).reshape(1, count, shards * length, lanes)

    inputs = tokens.reshape(rows, width)
    normed = norm_layer(inputs, e_vec["pre_gain"], e_vec["pre_shift"])
    normed_kept = keep(normed).reshape(1, clips, held, width)
    normed_all = exchange(jnp.broadcast_to(normed_kept, (seq_size, clips, held, width)))
    queries = (mm(normed, e_joint[:, :width]) + e_vec["query_bias"]).astype(bf16)
    joined = mm(normed_all.reshape(-1, width), e_joint[:, width:])
    joined_bias = jnp.concatenate([jnp.zeros_like(e_vec["value_bias"]), e_vec["value_bias"]])
    joined = (joined + joined_bias).astype(bf16)
    mixed = attend(
        queries.reshape(clips, slots, width),
        by_clip(joined.reshape(seq_size, clips, held, 2 * width)),
        head_size,
        bias,
    ).reshape(rows, width)
    middle = inputs + mm(mixed, e_out) + e_vec["out_bias"]
    normed_mid = norm_layer(middle, e_vec["mid_gain"], e_vec["mid_shift"])
    active = gelu(mm(normed_mid, e_expand) + e_vec["expand_bias"])
    encoded = middle + mm(active, e_contract) + e_vec["contract_bias"]
    context = encoded.astype(bf16)

    embedded = mm(context, embed) + embed_bias
    pred_input = jnp.where(own_flat, embedded, mask_token) + slot_code
    p_normed = norm_layer(pred_input, p_vec["pre_gain"], p_vec["pre_shift"])
    p_queries = (mm(p_normed, p_joint[:, :small_width]) + p_vec["query_bias"]).astype(bf16)
    p_bias = jnp.concatenate([jnp.zeros_like(p_vec["value_bias"]), p_vec["value_bias"]])
    p_normed_all = []
    p_mixed = []
    for clip in range(clips):
        own = p_normed.reshape(clips, slots, small_width)[clip]
        every = lax.all_gather(own, "seq", axis=0, tiled=True)
        p_joined = (mm(every, p_joint[:, small_width:]) + p_bias).astype(bf16)
        p_normed_all.append(every)
        p_mixed.append(
            attend(
                p_queries.reshape(clips, slots, small_width)[clip : clip + 1],
                p_joined.reshape(1, 1, span, 2 * small_width),
                small_head,
                None,
            )
        )
    p_mixed = jnp.concatenate(p_mixed, axis=0).reshape(rows, small_width)
    p_middle = pred_input + mm(p_mixed, p_out) + p_vec["out_bias"]
    p_normed_mid = norm_layer(p_middle, p_vec["mid_gain"], p_vec["mid_shift"])
    p_hidden = mm(p_normed_mid, p_expand) + p_vec["expand_bias"]
    p_active = gelu(p_hidden)
    predicted = p_middle + mm(p_active, p_contract) + p_vec["contract_bias"]

    grad_middle, grad_mixed, p_grads, p_small = feed_back(
        cotangent.reshape(rows, small_width),
        p_mixed,
        p_middle,
        p_normed_mid,
        p_hidden,
        p_active,
        (p_out, p_expand, p_contract),
        p_vec["mid_gain"],
    )
    own_weight, own_bias = own_joint(
        p_joint, p_vec["query_bias"], p_vec["value_bias"], seq_size, shard
    )
    own_width = small_width // seq_size
    grad_mixed = grad_mixed.reshape(rows, seq_size, own_width).transpose(1, 0, 2)
    grad_mixed = exchange(grad_mixed.reshape(seq_size, clips, slots, own_width))
    p_by_sender = by_sender(p_joint, seq_size)
    grad_normed = []
    p_grad_joint = 0.0
    p_columns = 0.0
    for clip in range(clips):
        every = p_normed_all[clip].reshape(1, 1, span, small_width)
        grads = attend_back(
            *own_parts(every, own_weight, own_bias),
            grad_mixed[:, clip].reshape(1, 1, span, own_width),
            small_head,
            None,
            seq_size,
        )
        flat = grads.reshape(span, 3 * own_width)
        p_grad_joint = p_grad_joint + mm(p_normed_all[clip], flat, TN)
        p_columns = p_columns + jnp.sum(flat.astype(f32), axis=0)
        grad_normed.append(joint_back(exchange(grads), p_by_sender))
    p_small.update(joint_small(p_columns, seq_size, shard))
    grad_norm, p_small["pre_gain"], p_small["pre_shift"] = norm_back(
        pred_input, p_vec["pre_gain"], jnp.concatenate(grad_normed, axis=0)
    )
    grad_pred_input = grad_middle + grad_norm
    grad_mask_token = jnp.sum(jnp.where(own_flat, 0.0, grad_pred_input), axis=0)
    grad_embedded = jnp.where(own_flat, grad_pred_input, 0.0).astype(bf16)
    grad_embed = mm(context, grad_embedded, TN).astype(bf16)
    grad_embed_bias = jnp.sum(grad_embedded.astype(f32), axis=0)

    p_grad_joint = jnp.pad(p_grad_joint.astype(bf16), ((0, 0), (0, small_width - 3 * own_width)))
    members = (p_grad_joint, *p_grads, grad_embed)
    p_part = scatter(
        jnp.concatenate([blocks_of(member, fsdp_size, small_width) for member in members], axis=1)
    )

    grad_context = mm(keep(grad_embedded), embed, NT)
    kept_mid = keep(normed_mid)
    kept_hidden = mm(kept_mid, e_expand) + e_vec["expand_bias"]
    grad_middle, grad_mixed, e_grads, e_small = feed_back(
        grad_context,
        keep(mixed),
        keep(middle),
        kept_mid,
        kept_hidden,
        gelu(kept_hidden),
        (e_out, e_expand, e_contract),
        e_vec["mid_gain"],
    )
    expand_part = scatter(e_grads[1].reshape(fsdp_size, -1, e_grads[1].shape[1]))
    contract_part = scatter(e_grads[2].reshape(fsdp_size, -1, e_grads[2].shape[1]))
    own_weight, own_bias = own_joint(
        e_joint, e_vec["query_bias"], e_vec["value_bias"], seq_size, shard
    )
    own_width = width // seq_size
    grad_mixed = grad_mixed.reshape(clips * held, seq_size, own_width).transpose(1, 0, 2)
    grad_mixed = exchange(grad_mixed.reshape(seq_size, clips, held, own_width))
    parts = own_parts(normed_all, own_weight, own_bias)
    grads = attend_back(
        *[by_clip(member) for member in (*parts, grad_mixed)], head_size, bias, seq_size
    )
    flat = grads.reshape(-1, 3 * own_width)
    e_grad_joint = mm(normed_all.reshape(-1, width), flat, TN).astype(bf16)
    e_small.update(joint_small(jnp.sum(flat.astype(f32), axis=0), seq_size, shard))
    grad_norm, e_small["pre_gain"], e_small["pre_shift"] = norm_back(
        keep(inputs),
        e_vec["pre_gain"],
        joint_back(exchange(grads), by_sender(e_joint, seq_size)),
    )
    grad_tokens = put_back(grad_middle + grad_norm)

    small = [e_small[name] for name in ORDER] + [grad_embed_bias, grad_mask_token]
    small += [p_small[name] for name in ORDER]
    small = [member.reshape(fsdp_size, -1) for member in small]
    sizes = [member.shape[1] for member in small]
    count = -(-sum(sizes) // (16 * own_width)) * 16
    small.append(jnp.zeros((fsdp_size, count * own_width - sum(sizes)), f32))
    small = jnp.concatenate(small, axis=1).astype(bf16).reshape(fsdp_size, count, own_width)
    late = scatter(
        jnp.concatenate(
            [
                blocks_of(e_grad_joint, fsdp_size, own_width),
                blocks_of(e_grads[0], fsdp_size, own_width),
                small,
            ],
            axis=1,
        )
    )
    own_rows = width // fsdp_size
    joint_rows = 3 * own_rows
    p_rows = small_width // fsdp_size
    e_columns = late[:joint_rows]
    p_columns = p_part[:p_rows, : 3 * (small_width // seq_size)]
    e_whole = lax.all_gather(e_columns, "seq", axis=0, tiled=False)
    p_whole = lax.all_gather(p_columns, "seq", axis=0, tiled=False)
    expand_sum, contract_sum, p_sum, late_sum = lax.psum(
        (expand_part, contract_part, p_part[p_rows:], late[joint_rows:]), "seq"
    )
    e_joint_out = e_whole.reshape(seq_size, 3, own_rows, own_width)
    e_joint_out = e_joint_out.transpose(2, 1, 0, 3).reshape(own_rows, 3 * width)
    p_joint_out = p_whole.reshape(seq_size, p_rows, 3, -1)
    p_joint_out = p_joint_out.transpose(1, 2, 0, 3).reshape(p_rows, 3 * small_width)
    out_sum = from_blocks(late_sum[: seq_size * own_rows], width)
    vector_sum = late_sum[seq_size * own_rows :].reshape(-1)
    small_out = []
    at = 0
    for size in sizes:
        small_out.append(vector_sum[at : at + size].astype(f32))
        at += size

    def cut(array, at, rows, lanes):
        split = lanes // small_width
        return from_blocks(array[at : at + split * rows], lanes), at + split * rows

    p_wide = p_shards[2].shape[1]
    p_out_sum, at = cut(p_sum, 0, p_rows, small_width)
    p_expand_sum, at = cut(p_sum, at, p_rows, p_wide)
    p_contract_sum, at = cut(p_sum, at, p_shards[3].shape[0], small_width)
    embed_sum, at = cut(p_sum, at, own_rows, small_width)

    def ordered(vec, joint, out, expand, contract):
        vec = dict(
            zip(ORDER, vec),
            joint=joint.astype(f32),
            out=out.astype(f32),
            expand=expand.astype(f32),
            contract=contract.astype(f32),
        )
        return tuple(vec[name] for name in BLOCK)

    return (
        encoded.reshape(tokens.shape),
        predicted.reshape(cotangent.shape),
        grad_tokens.reshape(tokens.shape),
        *ordered(small_out[:9], e_joint_out, out_sum, expand_sum, contract_sum),
        embed_sum.astype(f32),
        small_out[9],
        small_out[10],
        *ordered(small_out[11:], p_joint_out, p_out_sum, p_expand_sum, p_contract_sum),
    )


def solution(mesh):
    cut, rows, vec, full = P("fsdp", "seq", None), P("fsdp", None), P("fsdp"), P()
    block = (vec, vec, rows, vec, vec, rows, vec, vec, vec, rows, vec, rows, vec)
    return jax.shard_map(
        functools.partial(body, mesh.shape["fsdp"], mesh.shape["seq"]),
        mesh=mesh,
        in_specs=(cut, rows, rows, full, *block, rows, vec, vec, *block, cut),
        out_specs=(cut, cut, cut, *block, rows, vec, vec, *block),
        check_vma=False,
    )
```

```python
import functools
import math

import jax
import jax.numpy as jnp
from jax import lax
from jax.experimental import pallas as pl
from jax.experimental.pallas import tpu as pltpu
from jax.sharding import PartitionSpec as P

HEADS = 16
PHEADS = 12

f32 = jnp.float32
bf16 = jnp.bfloat16
norm_eps = 1e-06
LOG2E = math.log2(math.e)
NN = (((1,), (0,)), ((), ()))
NT = (((1,), (1,)), ((), ()))
TN = (((0,), (0,)), ((), ()))
VMEM_LIMIT = 60 * 2**20


def mm(left, right, dims=NN):
    return lax.dot_general(left, right, dims, preferred_element_type=f32)


def norm_parts(value):
    center = value - jnp.mean(value, axis=-1, keepdims=True)
    spread = jnp.mean(center * center, axis=-1, keepdims=True)
    scale = lax.rsqrt(spread + norm_eps)
    return center * scale, scale


def norm_layer(value, gain, shift):
    unit, _ = norm_parts(value)
    return (unit * gain + shift).astype(bf16)


def norm_back(value, gain, grad):
    unit, scale = norm_parts(value)
    grad_gain = jnp.sum(grad * unit, axis=0)
    grad_shift = jnp.sum(grad, axis=0)
    inner = grad * gain
    inner = inner - jnp.mean(inner, axis=-1, keepdims=True) - unit * jnp.mean(
        inner * unit, axis=-1, keepdims=True
    )
    return scale * inner, grad_gain, grad_shift


def gelu_parts(hidden):
    cdf = 0.5 * (1.0 + lax.erf(hidden * math.sqrt(0.5)))
    return cdf


def gelu(hidden):
    return (hidden * gelu_parts(hidden)).astype(bf16)


def gelu_slope(hidden):
    pdf = jnp.exp(-0.5 * hidden * hidden) * (1.0 / math.sqrt(2.0 * math.pi))
    return gelu_parts(hidden) + hidden * pdf


def forward_kernel(scale, head_size, q_ref, k_ref, v_ref, *rest):
    if len(rest) == 2:
        bias_ref, o_ref = rest
    else:
        bias_ref, o_ref = None, rest[0]
    head = pl.program_id(2)
    query = q_ref[0]
    key = k_ref[...].reshape(-1, k_ref.shape[-1])
    value = v_ref[...].reshape(-1, v_ref.shape[-1])
    lane = lax.broadcasted_iota(jnp.int32, query.shape, 1)
    mine = (lane // head_size) == head
    own_query = jnp.where(mine, query, jnp.zeros_like(query))
    scores = mm(own_query, key, NT) * (scale * LOG2E)
    if bias_ref is not None:
        scores = scores + bias_ref[0]
    top = jnp.max(scores, axis=1, keepdims=True)
    weight = jnp.exp2(scores - top)
    total = jnp.sum(weight, axis=1, keepdims=True)
    result = (mm(weight.astype(bf16), value) / total).astype(bf16)

    @pl.when(head == 0)
    def _():
        o_ref[0] = result

    @pl.when(head > 0)
    def _():
        o_ref[0] = jnp.where(mine, result, o_ref[0])


def attend(queries, joined, head_size, bias):
    clips, rows, width = queries.shape
    major, _, length, _ = joined.shape
    keys = major * length
    groups = width // 128
    in_specs = [
        pl.BlockSpec((1, rows, 128), lambda c, g, h: (c, 0, g)),
        pl.BlockSpec((major, 1, length, 128), lambda c, g, h: (0, c, 0, g)),
        pl.BlockSpec((major, 1, length, 128), lambda c, g, h: (0, c, 0, g + groups)),
    ]
    operands = [queries, joined, joined]
    if bias is not None:
        in_specs.append(pl.BlockSpec((1, 1, keys), lambda c, g, h: (c, 0, 0)))
        operands.append(bias)
    cells = clips * rows * keys * (width // head_size)
    return pl.pallas_call(
        functools.partial(forward_kernel, 1.0 / math.sqrt(head_size), head_size),
        grid=(clips, groups, 128 // head_size),
        in_specs=in_specs,
        out_specs=pl.BlockSpec((1, rows, 128), lambda c, g, h: (c, 0, g)),
        out_shape=jax.ShapeDtypeStruct((clips, rows, width), bf16),
        compiler_params=pltpu.CompilerParams(vmem_limit_bytes=VMEM_LIMIT),
        cost_estimate=pl.CostEstimate(
            flops=cells * 1024, bytes_accessed=4 * clips * keys * width, transcendentals=cells
        ),
        name="attend",
    )(*operands)


def backward_kernel(scale, head_size, shards, q_ref, k_ref, v_ref, g_ref, *rest):
    if len(rest) == 5:
        bias_ref = rest[0]
        rest = rest[1:]
    else:
        bias_ref = None
    out_ref, dq_sum, dk_sum, dv_sum = rest
    group = pl.program_id(1)
    part = pl.program_id(2)
    head = pl.program_id(3)
    lanes = q_ref.shape[-1]
    query = q_ref[...].reshape(-1, lanes)
    key = k_ref[...].reshape(-1, lanes)
    value = v_ref[...].reshape(-1, lanes)
    grad = g_ref[...].reshape(-1, lanes)
    lane = lax.broadcasted_iota(jnp.int32, query.shape, 1)
    mine = (lane // head_size) == head
    zero = jnp.zeros_like(query)
    own_query = jnp.where(mine, query, zero)
    own_grad = jnp.where(mine, grad, zero)
    key_lane = lax.broadcasted_iota(jnp.int32, key.shape, 1)
    own_key = jnp.where((key_lane // head_size) == head, key, jnp.zeros_like(key))
    scores = mm(own_query, key, NT) * (scale * LOG2E)
    if bias_ref is not None:
        scores = scores + bias_ref[0]
    top = jnp.max(scores, axis=1, keepdims=True)
    weight = jnp.exp2(scores - top)
    total = jnp.sum(weight, axis=1, keepdims=True)
    chance = weight * (1.0 / total)
    grad_chance = mm(own_grad, value, NT)
    delta = jnp.sum(chance * grad_chance, axis=1, keepdims=True)
    grad_scores = (chance * (grad_chance - delta)).astype(bf16)
    part_q = mm(grad_scores, own_key)
    part_v = mm(own_grad, chance.astype(bf16), TN)
    part_k = mm(own_query, grad_scores, TN)

    @pl.when(head == 0)
    def _():
        dq_sum[...] = part_q

    @pl.when(head > 0)
    def _():
        dq_sum[...] += part_q

    @pl.when((head == 0) & (part == 0))
    def _():
        dk_sum[...] = part_k
        dv_sum[...] = part_v

    @pl.when((head > 0) | (part > 0))
    def _():
        dk_sum[...] += part_k
        dv_sum[...] += part_v

    rows = out_ref.shape[2]
    width = out_ref.shape[3] // 3
    held = query.shape[0] // rows
    last_head = head == pl.num_programs(3) - 1

    def place(kind):
        if width == lanes:
            return slice(kind * width, (kind + 1) * width)
        return pl.ds(pl.multiple_of(kind * width + group * lanes, 128), lanes)

    @pl.when(last_head)
    def _():
        result = (dq_sum[...] * scale).astype(bf16)
        for index in range(held):
            out_ref[part * held + index, 0, :, place(0)] = result[index * rows : (index + 1) * rows]

    @pl.when(last_head & (part == pl.num_programs(2) - 1))
    def _():
        for kind, total_ref, factor in ((1, dk_sum, scale), (2, dv_sum, 1.0)):
            result = (total_ref[...] * factor).T.astype(bf16)
            for index in range(shards):
                out_ref[index, 0, :, place(kind)] = result[index * rows : (index + 1) * rows]


def attend_back(queries, keys, values, grad_mixed, head_size, bias, shards):
    major, clips, length, width = queries.shape
    lanes = min(width, 128)
    groups = width // lanes
    rows = major * length // shards
    parts = shards if major == 1 else 1
    query_rows = rows if major == 1 else length
    by_query = pl.BlockSpec((major, 1, query_rows, lanes), lambda c, g, r, h: (0, c, r, g))
    by_key = pl.BlockSpec((major, 1, length, lanes), lambda c, g, r, h: (0, c, 0, g))
    in_specs = [by_query, by_key, by_key, by_query]
    operands = [queries, keys, values, grad_mixed]
    total = major * length
    if bias is not None:
        in_specs.append(pl.BlockSpec((1, 1, total), lambda c, g, r, h: (c, 0, 0)))
        operands.append(bias)
    cells = clips * total * total * (width // head_size)
    return pl.pallas_call(
        functools.partial(backward_kernel, 1.0 / math.sqrt(head_size), head_size, shards),
        grid=(clips, groups, parts, lanes // head_size),
        in_specs=in_specs,
        out_specs=pl.BlockSpec((shards, 1, rows, 3 * width), lambda c, g, r, h: (0, c, 0, 0)),
        out_shape=jax.ShapeDtypeStruct((shards, clips, rows, 3 * width), bf16),
        scratch_shapes=[
            pltpu.VMEM((major * query_rows, lanes), f32),
            pltpu.VMEM((lanes, total), f32),
            pltpu.VMEM((lanes, total), f32),
        ],
        compiler_params=pltpu.CompilerParams(vmem_limit_bytes=VMEM_LIMIT),
        cost_estimate=pl.CostEstimate(
            flops=cells * 2560, bytes_accessed=14 * clips * total * width, transcendentals=cells
        ),
        name="attend_back",
    )(*operands)


def exchange(array):
    return lax.all_to_all(array, "seq", split_axis=0, concat_axis=0, tiled=True)


def gather(array):
    return lax.all_gather(array, "fsdp", axis=0, tiled=True)


def scatter(array):
    return lax.psum_scatter(array, "fsdp", scatter_dimension=0, tiled=True)[0]


def blocks_of(array, count, lanes):
    rows = array.shape[0] // count
    split = array.shape[1] // lanes
    array = array.reshape(count, rows, split, lanes)
    return array.transpose(0, 2, 1, 3).reshape(count, split * rows, lanes)


def from_blocks(array, lanes):
    split = lanes // array.shape[1]
    rows = array.shape[0] // split
    return array.reshape(split, rows, -1).transpose(1, 0, 2).reshape(rows, lanes)


def pack_rows(vectors):
    rows = []
    for member in vectors:
        count = -(-member.shape[0] // 128)
        padded = jnp.pad(member.astype(f32), (0, count * 128 - member.shape[0]))
        rows.append(padded.reshape(count, 128))
    total = sum(member.shape[0] for member in rows)
    if total % 8:
        rows.append(jnp.zeros((8 - total % 8, 128), f32))
    return jnp.concatenate(rows, axis=0)


def unpack_rows(packed, sizes):
    out = []
    at = 0
    for size in sizes:
        count = -(-size // 128)
        piece = packed[:, at : at + count].reshape(packed.shape[0], count * 128)[:, :size]
        out.append(piece.reshape(-1))
        at += count
    return out


MESH = pl.DeviceIdType.MESH


def line_kernel(size, cuts, *refs):
    count = len(cuts)
    ins, outs = refs[:count], refs[count : 2 * count]
    scratch = refs[2 * count :]
    inner, outer, partial = (scratch[i * count : (i + 1) * count] for i in range(3))
    to_inner, to_outer, from_inner, from_outer = scratch[3 * count :]
    me = lax.axis_index("seq")
    left = me < size // 2
    toward = jnp.where(left, me + 1, me - 1)
    away = jnp.where(left, me - 1, me + 1)
    end = (me == 0) | (me == size - 1)
    barrier = pltpu.get_barrier_semaphore()
    pl.semaphore_signal(barrier, inc=1, device_id={"seq": toward}, device_id_type=MESH)

    @pl.when(jnp.logical_not(end))
    def _():
        pl.semaphore_signal(barrier, inc=1, device_id={"seq": away}, device_id_type=MESH)
        pl.semaphore_wait(barrier, 2)

    @pl.when(end)
    def _():
        pl.semaphore_wait(barrier, 1)

    pieces = []
    for index, parts in enumerate(cuts):
        rows = ins[index].shape[0] // parts
        for part in range(parts):
            pieces.append((part / parts, index, slice(part * rows, (part + 1) * rows)))
    pieces.sort(key=lambda piece: piece[:2])
    pieces = [(slot, index, cut) for slot, (_, index, cut) in enumerate(pieces)]

    def inwards(slot, index, cut):
        return pltpu.make_async_remote_copy(
            src_ref=ins[index].at[cut],
            dst_ref=outer[index].at[cut],
            send_sem=to_inner.at[slot],
            recv_sem=from_outer.at[slot],
            device_id={"seq": toward},
            device_id_type=MESH,
        )

    def swap(slot, index, cut):
        return pltpu.make_async_remote_copy(
            src_ref=partial[index].at[cut],
            dst_ref=inner[index].at[cut],
            send_sem=to_inner.at[slot],
            recv_sem=from_inner.at[slot],
            device_id={"seq": toward},
            device_id_type=MESH,
        )

    def outwards(slot, index, cut):
        return pltpu.make_async_remote_copy(
            src_ref=outs[index].at[cut],
            dst_ref=outs[index].at[cut],
            send_sem=to_outer.at[slot],
            recv_sem=from_inner.at[slot],
            device_id={"seq": away},
            device_id_type=MESH,
        )

    @pl.when(end)
    def _():
        for piece in pieces:
            inwards(*piece).start()
        for piece in pieces:
            outwards(*piece).wait_recv()
        for piece in pieces:
            inwards(*piece).wait_send()

    @pl.when(jnp.logical_not(end))
    def _():
        for piece in pieces:
            inwards(*piece).wait_recv()
            _, index, cut = piece
            both = ins[index][cut].astype(f32) + outer[index][cut].astype(f32)
            partial[index][cut] = both.astype(bf16)
            swap(*piece).start()
        for piece in pieces:
            swap(*piece).wait_recv()
            _, index, cut = piece
            both = partial[index][cut].astype(f32) + inner[index][cut].astype(f32)
            outs[index][cut] = both.astype(bf16)
            outwards(*piece).start()
        for piece in pieces:
            swap(*piece).wait_send()
            outwards(*piece).wait_send()


def line_sum(arrays, size, identity):
    cuts = []
    for member in arrays:
        parts = 8
        while parts > 1 and member.shape[0] % (16 * parts):
            parts //= 2
        cuts.append(parts)
    hold = [pltpu.VMEM(member.shape, bf16) for member in arrays]
    whole = pl.BlockSpec(memory_space=pltpu.VMEM)
    return pl.pallas_call(
        functools.partial(line_kernel, size, tuple(cuts)),
        out_shape=[jax.ShapeDtypeStruct(member.shape, bf16) for member in arrays],
        in_specs=[whole] * len(arrays),
        out_specs=[whole] * len(arrays),
        scratch_shapes=hold * 3 + [pltpu.SemaphoreType.DMA((sum(cuts),))] * 4,
        compiler_params=pltpu.CompilerParams(
            collective_id=identity, has_side_effects=True, vmem_limit_bytes=VMEM_LIMIT
        ),
        name="line_sum",
    )(*arrays)


def sum_slots(arrays, size, identity):
    if size == 4:
        return line_sum(arrays, size, identity)
    return lax.psum(tuple(arrays), "seq")


def feed_back(grad_out, mixed, middle, normed_mid, hidden, active, weights, mid_gain):
    out, expand, contract = weights
    grad_y = grad_out.astype(bf16)
    grad_contract = mm(active, grad_y, TN).astype(bf16)
    grad_contract_bias = jnp.sum(grad_y.astype(f32), axis=0)
    grad_hidden = (mm(grad_y, contract, NT) * gelu_slope(hidden)).astype(bf16)
    grad_expand = mm(normed_mid, grad_hidden, TN).astype(bf16)
    grad_expand_bias = jnp.sum(grad_hidden.astype(f32), axis=0)
    grad_norm, grad_mid_gain, grad_mid_shift = norm_back(
        middle, mid_gain, mm(grad_hidden, expand, NT)
    )
    grad_middle = grad_out + grad_norm
    grad_att = grad_middle.astype(bf16)
    grad_out_weight = mm(mixed, grad_att, TN).astype(bf16)
    grad_out_bias = jnp.sum(grad_att.astype(f32), axis=0)
    grad_mixed = mm(grad_att, out, NT).astype(bf16)
    grad_mixed, grad_expand, grad_contract = lax.optimization_barrier(
        (grad_mixed, grad_expand, grad_contract)
    )
    grads = (grad_out_weight, grad_expand, grad_contract)
    small = dict(
        out_bias=grad_out_bias,
        mid_gain=grad_mid_gain,
        mid_shift=grad_mid_shift,
        expand_bias=grad_expand_bias,
        contract_bias=grad_contract_bias,
    )
    return grad_middle, grad_mixed, grads, small


def own_joint(joint_weight, query_bias, value_bias, shards, shard):
    width = joint_weight.shape[0]
    own = width // shards
    weight = lax.dynamic_slice_in_dim(joint_weight.reshape(width, 3, width), shard * own, own, 2)
    bias_q = lax.dynamic_slice_in_dim(query_bias, shard * own, own, 0)
    bias_v = lax.dynamic_slice_in_dim(value_bias, shard * own, own, 0)
    return weight, (bias_q, None, bias_v)


def own_parts(normed_all, weight, biases):
    flat = normed_all.reshape(-1, normed_all.shape[3])
    out = []
    for index in range(3):
        part = mm(flat, weight[:, index])
        if biases[index] is not None:
            part = part + biases[index]
        out.append(part.astype(bf16).reshape(normed_all.shape[:3] + (weight.shape[2],)))
    return out


def by_sender(joint_weight, shards):
    width = joint_weight.shape[0]
    array = joint_weight.reshape(width, 3, shards, width // shards)
    return array.transpose(0, 2, 1, 3).reshape(width, 3 * width)


def joint_back(received, joint_by_sender):
    shards, clips, rows, width = received.shape
    flat = received.reshape(shards, clips * rows, width).transpose(1, 0, 2)
    return mm(flat.reshape(clips * rows, shards * width), joint_by_sender, NT)


def spread(vector, shards, shard):
    full = jnp.zeros((vector.shape[0] * shards,), f32)
    return lax.dynamic_update_slice_in_dim(full, vector, shard * vector.shape[0], 0)


def joint_small(columns, shards, shard):
    own = columns.shape[0] // 3
    return dict(
        query_bias=spread(columns[:own], shards, shard),
        value_bias=spread(columns[2 * own :], shards, shard),
    )


ORDER = (
    "pre_gain",
    "pre_shift",
    "query_bias",
    "value_bias",
    "out_bias",
    "mid_gain",
    "mid_shift",
    "expand_bias",
    "contract_bias",
)
BLOCK = (
    "pre_gain",
    "pre_shift",
    "joint",
    "query_bias",
    "value_bias",
    "out",
    "out_bias",
    "mid_gain",
    "mid_shift",
    "expand",
    "expand_bias",
    "contract",
    "contract_bias",
)
FRAMES = 8
GRID = 14
MOST_VISIBLE = FRAMES * max(
    high * wide
    for high in range(1, GRID + 1)
    for wide in range(1, GRID + 1)
    if 2 * high * wide < GRID * GRID
)


def body(fsdp_size, seq_size, tokens, visible, slot_token, positions, *rest):
    e_shard = dict(zip(BLOCK, rest[:13]))
    embed_weight, embed_bias, mask_token = rest[13:16]
    p_shard = dict(zip(BLOCK, rest[16:29]))
    cotangent = rest[29]
    shard = lax.axis_index("seq")
    clips, slots, width = tokens.shape
    span = visible.shape[1]

    e_out = gather(e_shard["out"])

    place = lax.broadcasted_iota(jnp.int32, (1, 1, span), 2)
    slot_visible = jnp.any(
        (slot_token[:, :, None] == place) & (visible[:, None, :] > 0), axis=2
    )
    counts = jnp.sum(slot_visible.reshape(clips, seq_size, slots).astype(jnp.int32), axis=2)
    compact = -(-MOST_VISIBLE // (16 * seq_size)) * 16
    fits = (jnp.max(counts) <= compact).astype(f32)

    vectors = [e_shard[name] for name in ORDER] + [embed_bias, mask_token]
    vectors += [p_shard[name] for name in ORDER]
    sizes = [member.shape[0] for member in vectors]
    packed = lax.all_gather(
        pack_rows(vectors + [jnp.full((1,), fits)]), "fsdp", axis=0, tiled=False
    )
    full = unpack_rows(packed, sizes + [1])
    all_fit = jnp.min(full[-1]) > 0.5

    operands = (
        tokens,
        slot_visible,
        counts,
        slot_token,
        positions,
        e_out,
        e_shard["joint"],
        e_shard["expand"],
        e_shard["contract"],
        embed_weight,
        tuple(p_shard[name] for name in ("joint", "out", "expand", "contract")),
        tuple(full[:-1]),
        cotangent,
    )
    whole = functools.partial(main, fsdp_size, seq_size, slots)
    if compact >= slots:
        return whole(*operands)
    return lax.cond(
        all_fit, functools.partial(main, fsdp_size, seq_size, compact), whole, *operands
    )


def main(
    fsdp_size,
    seq_size,
    held,
    tokens,
    slot_visible,
    counts,
    slot_token,
    positions,
    e_out,
    e_joint_shard,
    e_expand_shard,
    e_contract_shard,
    embed_shard,
    p_shards,
    vectors,
    cotangent,
):
    shard = lax.axis_index("seq")
    clips, slots, width = tokens.shape
    span = slot_visible.shape[1]
    rows = clips * slots
    small_width = cotangent.shape[2]
    head_size = width // HEADS
    small_head = small_width // PHEADS
    whole = held == slots
    e_vec = dict(zip(ORDER, vectors[:9]))
    embed_bias, mask_token = vectors[9:11]
    p_vec = dict(zip(ORDER, vectors[11:]))

    e_joint = gather(e_joint_shard)
    e_joint, e_expand_shard = lax.optimization_barrier((e_joint, e_expand_shard))
    e_expand = gather(e_expand_shard)
    e_expand, e_contract_shard = lax.optimization_barrier((e_expand, e_contract_shard))
    e_contract = gather(e_contract_shard)
    packed = jnp.concatenate(
        [blocks_of(member, 1, small_width)[0] for member in (*p_shards, embed_shard)], axis=0
    )
    e_contract, packed = lax.optimization_barrier((e_contract, packed))
    packed = lax.all_gather(packed, "fsdp", axis=0, tiled=False)
    unpacked = []
    at = 0
    for member in (*p_shards, embed_shard):
        split = member.shape[1] // small_width
        count = member.shape[0] * split
        piece = packed[:, at : at + count].reshape(fsdp_size, split, member.shape[0], small_width)
        unpacked.append(piece.transpose(0, 2, 1, 3).reshape(-1, member.shape[1]))
        at += count
    p_joint, p_out, p_expand, p_contract, embed = unpacked

    own_visible = lax.dynamic_slice_in_dim(slot_visible, shard * slots, slots, 1)
    own_flat = own_visible.reshape(rows, 1)
    own_tokens = lax.dynamic_slice_in_dim(slot_token, shard * slots, slots, 1)
    slot_code = jnp.take(positions, own_tokens.reshape(rows), axis=0)

    if whole:
        kept = slot_visible.reshape(clips, 1, span)

        def keep(array):
            return array

        def put_back(array):
            return array

    else:
        kept = lax.broadcasted_iota(jnp.int32, (1, 1, held), 2) < counts[:, :, None]
        kept = kept.reshape(clips, 1, seq_size * held)
        ones = own_visible.astype(bf16)
        before = lax.broadcasted_iota(jnp.int32, (slots, slots), 0)
        after = lax.broadcasted_iota(jnp.int32, (slots, slots), 1)
        rank = mm(ones, (before < after).astype(bf16)).astype(jnp.int32)
        target = lax.broadcasted_iota(jnp.int32, (1, held, 1), 1)
        picks = ((rank[:, None, :] == target) & own_visible[:, None, :]).astype(bf16)

        def keep(array):
            precision = lax.Precision.HIGHEST if array.dtype == f32 else None
            picked = jnp.einsum(
                "crs,csw->crw",
                picks.astype(array.dtype),
                array.reshape(clips, slots, -1),
                precision=precision,
                preferred_element_type=f32,
            )
            return picked.astype(array.dtype).reshape(clips * held, -1)

        def put_back(array):
            placed = jnp.einsum(
                "crs,crw->csw",
                picks.astype(f32),
                array.reshape(clips, held, -1),
                precision=lax.Precision.HIGHEST,
                preferred_element_type=f32,
            )
            return placed.reshape(rows, -1)

    bias = jnp.where(kept, 0.0, -1e30).astype(f32)
    tiled = held % 16 == 0

    def by_clip(array):
        if tiled:
            return array
        shards, count, length, lanes = array.shape
        return array.transpose(1, 0, 2, 3).reshape(1, count, shards * length, lanes)

    inputs = tokens.reshape(rows, width)
    normed = norm_layer(inputs, e_vec["pre_gain"], e_vec["pre_shift"])
    normed_kept = keep(normed).reshape(1, clips, held, width)
    normed_all = exchange(jnp.broadcast_to(normed_kept, (seq_size, clips, held, width)))
    queries = (mm(normed, e_joint[:, :width]) + e_vec["query_bias"]).astype(bf16)
    joined = mm(normed_all.reshape(-1, width), e_joint[:, width:])
    joined_bias = jnp.concatenate([jnp.zeros_like(e_vec["value_bias"]), e_vec["value_bias"]])
    joined = (joined + joined_bias).astype(bf16)
    mixed = attend(
        queries.reshape(clips, slots, width),
        by_clip(joined.reshape(seq_size, clips, held, 2 * width)),
        head_size,
        bias,
    ).reshape(rows, width)
    middle = inputs + mm(mixed, e_out) + e_vec["out_bias"]
    normed_mid = norm_layer(middle, e_vec["mid_gain"], e_vec["mid_shift"])
    active = gelu(mm(normed_mid, e_expand) + e_vec["expand_bias"])
    encoded = middle + mm(active, e_contract) + e_vec["contract_bias"]
    context = encoded.astype(bf16)

    embedded = mm(context, embed) + embed_bias
    pred_input = jnp.where(own_flat, embedded, mask_token) + slot_code
    p_normed = norm_layer(pred_input, p_vec["pre_gain"], p_vec["pre_shift"])
    p_queries = (mm(p_normed, p_joint[:, :small_width]) + p_vec["query_bias"]).astype(bf16)
    p_bias = jnp.concatenate([jnp.zeros_like(p_vec["value_bias"]), p_vec["value_bias"]])
    p_normed_all = []
    p_mixed = []
    for clip in range(clips):
        own = p_normed.reshape(clips, slots, small_width)[clip]
        every = lax.all_gather(own, "seq", axis=0, tiled=True)
        p_joined = (mm(every, p_joint[:, small_width:]) + p_bias).astype(bf16)
        p_normed_all.append(every)
        p_mixed.append(
            attend(
                p_queries.reshape(clips, slots, small_width)[clip : clip + 1],
                p_joined.reshape(1, 1, span, 2 * small_width),
                small_head,
                None,
            )
        )
    p_mixed = jnp.concatenate(p_mixed, axis=0).reshape(rows, small_width)
    p_middle = pred_input + mm(p_mixed, p_out) + p_vec["out_bias"]
    p_normed_mid = norm_layer(p_middle, p_vec["mid_gain"], p_vec["mid_shift"])
    p_hidden = mm(p_normed_mid, p_expand) + p_vec["expand_bias"]
    p_active = gelu(p_hidden)
    predicted = p_middle + mm(p_active, p_contract) + p_vec["contract_bias"]

    grad_middle, grad_mixed, p_grads, p_small = feed_back(
        cotangent.reshape(rows, small_width),
        p_mixed,
        p_middle,
        p_normed_mid,
        p_hidden,
        p_active,
        (p_out, p_expand, p_contract),
        p_vec["mid_gain"],
    )
    p_pack = jnp.concatenate(
        [blocks_of(member, fsdp_size, small_width) for member in p_grads], axis=1
    )
    grad_mixed, p_pack = lax.optimization_barrier((grad_mixed, p_pack))
    p_part = scatter(p_pack)
    own_weight, own_bias = own_joint(
        p_joint, p_vec["query_bias"], p_vec["value_bias"], seq_size, shard
    )
    own_width = small_width // seq_size
    grad_mixed = grad_mixed.reshape(rows, seq_size, own_width).transpose(1, 0, 2)
    grad_mixed = exchange(grad_mixed.reshape(seq_size, clips, slots, own_width))
    p_by_sender = by_sender(p_joint, seq_size)
    grad_normed = []
    p_grad_joint = 0.0
    p_columns = 0.0
    for clip in range(clips):
        every = p_normed_all[clip].reshape(1, 1, span, small_width)
        grads = attend_back(
            *own_parts(every, own_weight, own_bias),
            grad_mixed[:, clip].reshape(1, 1, span, own_width),
            small_head,
            None,
            seq_size,
        )
        flat = grads.reshape(span, 3 * own_width)
        p_grad_joint = p_grad_joint + mm(p_normed_all[clip], flat, TN)
        p_columns = p_columns + jnp.sum(flat.astype(f32), axis=0)
        grad_normed.append(joint_back(exchange(grads), p_by_sender))
    p_small.update(joint_small(p_columns, seq_size, shard))
    grad_norm, p_small["pre_gain"], p_small["pre_shift"] = norm_back(
        pred_input, p_vec["pre_gain"], jnp.concatenate(grad_normed, axis=0)
    )
    grad_pred_input = grad_middle + grad_norm
    grad_mask_token = jnp.sum(jnp.where(own_flat, 0.0, grad_pred_input), axis=0)
    grad_embedded = jnp.where(own_flat, grad_pred_input, 0.0).astype(bf16)
    grad_embed = mm(context, grad_embedded, TN).astype(bf16)
    grad_embed_bias = jnp.sum(grad_embedded.astype(f32), axis=0)

    p_own_width = own_width
    p_grad_joint = jnp.pad(p_grad_joint.astype(bf16), ((0, 0), (0, small_width - 3 * own_width)))

    grad_context = mm(keep(grad_embedded), embed, NT)
    kept_mid = keep(normed_mid)
    kept_hidden = mm(kept_mid, e_expand) + e_vec["expand_bias"]
    grad_middle, grad_mixed, e_grads, e_small = feed_back(
        grad_context,
        keep(mixed),
        keep(middle),
        kept_mid,
        kept_hidden,
        gelu(kept_hidden),
        (e_out, e_expand, e_contract),
        e_vec["mid_gain"],
    )
    expand_part = scatter(e_grads[1].reshape(fsdp_size, -1, e_grads[1].shape[1]))
    contract_part = scatter(e_grads[2].reshape(fsdp_size, -1, e_grads[2].shape[1]))
    own_weight, own_bias = own_joint(
        e_joint, e_vec["query_bias"], e_vec["value_bias"], seq_size, shard
    )
    own_width = width // seq_size
    grad_mixed = grad_mixed.reshape(clips * held, seq_size, own_width).transpose(1, 0, 2)
    grad_mixed = exchange(grad_mixed.reshape(seq_size, clips, held, own_width))
    parts = own_parts(normed_all, own_weight, own_bias)
    grads = attend_back(
        *[by_clip(member) for member in (*parts, grad_mixed)], head_size, bias, seq_size
    )
    flat = grads.reshape(-1, 3 * own_width)
    e_grad_joint = mm(normed_all.reshape(-1, width), flat, TN).astype(bf16)
    e_small.update(joint_small(jnp.sum(flat.astype(f32), axis=0), seq_size, shard))
    grad_norm, e_small["pre_gain"], e_small["pre_shift"] = norm_back(
        keep(inputs),
        e_vec["pre_gain"],
        joint_back(exchange(grads), by_sender(e_joint, seq_size)),
    )
    grad_tokens = put_back(grad_middle + grad_norm)

    first = 0 if whole else 2
    contract_sum, expand_sum, p_sum = sum_slots(
        (contract_part, expand_part, p_part), seq_size, first
    )

    small = [e_small[name] for name in ORDER] + [grad_embed_bias, grad_mask_token]
    small += [p_small[name] for name in ORDER]
    small = [member.reshape(fsdp_size, -1) for member in small]
    sizes = [member.shape[1] for member in small]
    count = -(-sum(sizes) // (16 * 128)) * 16
    small.append(jnp.zeros((fsdp_size, count * 128 - sum(sizes)), f32))
    small = jnp.concatenate(small, axis=1).astype(bf16).reshape(fsdp_size, count, 128)
    members = (e_grad_joint, p_grad_joint, e_grads[0], grad_embed)
    late = scatter(
        jnp.concatenate(
            [blocks_of(member, fsdp_size, 128) for member in members] + [small], axis=1
        )
    )

    def cut(array, at, rows, lanes, block):
        split = lanes // block
        return from_blocks(array[at : at + split * rows], lanes), at + split * rows

    def all_columns(columns, own):
        columns = columns[:, : 3 * own].reshape(-1, 3, 1, own)
        which = lax.broadcasted_iota(jnp.int32, (1, 1, seq_size, 1), 2)
        placed = jnp.where(which == shard, columns, jnp.zeros_like(columns))
        return placed.reshape(-1, 3 * own * seq_size)

    own_rows = width // fsdp_size
    p_rows = small_width // fsdp_size
    e_columns, at = cut(late, 0, own_rows, 3 * own_width, 128)
    p_columns, at = cut(late, at, p_rows, small_width, 128)
    e_joint_out, p_joint_out, late_sum = sum_slots(
        (all_columns(e_columns, own_width), all_columns(p_columns, p_own_width), late[at:]),
        seq_size,
        first + 1,
    )
    out_sum, at = cut(late_sum, 0, own_rows, width, 128)
    embed_sum, at = cut(late_sum, at, own_rows, small_width, 128)
    vector_sum = late_sum[at:].reshape(-1)
    small_out = []
    at = 0
    for size in sizes:
        small_out.append(vector_sum[at : at + size].astype(f32))
        at += size
    p_wide = p_shards[2].shape[1]
    p_out_sum, at = cut(p_sum, 0, p_rows, small_width, small_width)
    p_expand_sum, at = cut(p_sum, at, p_rows, p_wide, small_width)
    p_contract_sum, at = cut(p_sum, at, p_shards[3].shape[0], small_width, small_width)

    def ordered(vec, joint, out, expand, contract):
        vec = dict(
            zip(ORDER, vec),
            joint=joint.astype(f32),
            out=out.astype(f32),
            expand=expand.astype(f32),
            contract=contract.astype(f32),
        )
        return tuple(vec[name] for name in BLOCK)

    return (
        encoded.reshape(tokens.shape),
        predicted.reshape(cotangent.shape),
        grad_tokens.reshape(tokens.shape),
        *ordered(small_out[:9], e_joint_out, out_sum, expand_sum, contract_sum),
        embed_sum.astype(f32),
        small_out[9],
        small_out[10],
        *ordered(small_out[11:], p_joint_out, p_out_sum, p_expand_sum, p_contract_sum),
    )


def solution(mesh):
    cut, rows, vec, full = P("fsdp", "seq", None), P("fsdp", None), P("fsdp"), P()
    block = (vec, vec, rows, vec, vec, rows, vec, vec, vec, rows, vec, rows, vec)
    return jax.shard_map(
        functools.partial(body, mesh.shape["fsdp"], mesh.shape["seq"]),
        mesh=mesh,
        in_specs=(cut, rows, rows, full, *block, rows, vec, vec, *block, cut),
        out_specs=(cut, cut, cut, *block, rows, vec, vec, *block),
        check_vma=False,
    )
```

```python
import functools
import math

import jax
import jax.numpy as jnp
from jax import lax
from jax.experimental import pallas as pl
from jax.experimental.pallas import tpu as pltpu
from jax.sharding import PartitionSpec as P

HEADS = 16
PHEADS = 12

f32 = jnp.float32
bf16 = jnp.bfloat16
norm_eps = 1e-06
LOG2E = math.log2(math.e)
NN = (((1,), (0,)), ((), ()))
NT = (((1,), (1,)), ((), ()))
TN = (((0,), (0,)), ((), ()))
VMEM_LIMIT = 60 * 2**20


def mm(left, right, dims=NN):
    return lax.dot_general(left, right, dims, preferred_element_type=f32)


def norm_parts(value):
    center = value - jnp.mean(value, axis=-1, keepdims=True)
    spread = jnp.mean(center * center, axis=-1, keepdims=True)
    scale = lax.rsqrt(spread + norm_eps)
    return center * scale, scale


def norm_layer(value, gain, shift):
    unit, _ = norm_parts(value)
    return (unit * gain + shift).astype(bf16)


def norm_back(value, gain, grad):
    unit, scale = norm_parts(value)
    grad_gain = jnp.sum(grad * unit, axis=0)
    grad_shift = jnp.sum(grad, axis=0)
    inner = grad * gain
    inner = inner - jnp.mean(inner, axis=-1, keepdims=True) - unit * jnp.mean(
        inner * unit, axis=-1, keepdims=True
    )
    return scale * inner, grad_gain, grad_shift


def gelu_parts(hidden):
    cdf = 0.5 * (1.0 + lax.erf(hidden * math.sqrt(0.5)))
    return cdf


def gelu(hidden):
    return (hidden * gelu_parts(hidden)).astype(bf16)


def gelu_slope(hidden):
    pdf = jnp.exp(-0.5 * hidden * hidden) * (1.0 / math.sqrt(2.0 * math.pi))
    return gelu_parts(hidden) + hidden * pdf


def forward_kernel(scale, head_size, q_ref, k_ref, v_ref, *rest):
    if len(rest) == 2:
        bias_ref, o_ref = rest
    else:
        bias_ref, o_ref = None, rest[0]
    head = pl.program_id(2)
    query = q_ref[0]
    key = k_ref[...].reshape(-1, k_ref.shape[-1])
    value = v_ref[...].reshape(-1, v_ref.shape[-1])
    lane = lax.broadcasted_iota(jnp.int32, query.shape, 1)
    mine = (lane // head_size) == head
    own_query = jnp.where(mine, query, jnp.zeros_like(query))
    scores = mm(own_query, key, NT) * (scale * LOG2E)
    if bias_ref is not None:
        scores = scores + bias_ref[0]
    top = jnp.max(scores, axis=1, keepdims=True)
    weight = jnp.exp2(scores - top)
    total = jnp.sum(weight, axis=1, keepdims=True)
    result = (mm(weight.astype(bf16), value) / total).astype(bf16)

    @pl.when(head == 0)
    def _():
        o_ref[0] = result

    @pl.when(head > 0)
    def _():
        o_ref[0] = jnp.where(mine, result, o_ref[0])


def attend(queries, joined, head_size, bias):
    clips, rows, width = queries.shape
    major, _, length, _ = joined.shape
    keys = major * length
    groups = width // 128
    in_specs = [
        pl.BlockSpec((1, rows, 128), lambda c, g, h: (c, 0, g)),
        pl.BlockSpec((major, 1, length, 128), lambda c, g, h: (0, c, 0, g)),
        pl.BlockSpec((major, 1, length, 128), lambda c, g, h: (0, c, 0, g + groups)),
    ]
    operands = [queries, joined, joined]
    if bias is not None:
        in_specs.append(pl.BlockSpec((1, 1, keys), lambda c, g, h: (c, 0, 0)))
        operands.append(bias)
    cells = clips * rows * keys * (width // head_size)
    return pl.pallas_call(
        functools.partial(forward_kernel, 1.0 / math.sqrt(head_size), head_size),
        grid=(clips, groups, 128 // head_size),
        in_specs=in_specs,
        out_specs=pl.BlockSpec((1, rows, 128), lambda c, g, h: (c, 0, g)),
        out_shape=jax.ShapeDtypeStruct((clips, rows, width), bf16),
        compiler_params=pltpu.CompilerParams(vmem_limit_bytes=VMEM_LIMIT),
        cost_estimate=pl.CostEstimate(
            flops=cells * 1024, bytes_accessed=4 * clips * keys * width, transcendentals=cells
        ),
        name="attend",
    )(*operands)


def backward_kernel(scale, head_size, shards, q_ref, k_ref, v_ref, g_ref, *rest):
    if len(rest) == 5:
        bias_ref = rest[0]
        rest = rest[1:]
    else:
        bias_ref = None
    out_ref, dq_sum, dk_sum, dv_sum = rest
    group = pl.program_id(1)
    part = pl.program_id(2)
    head = pl.program_id(3)
    lanes = q_ref.shape[-1]
    query = q_ref[...].reshape(-1, lanes)
    key = k_ref[...].reshape(-1, lanes)
    value = v_ref[...].reshape(-1, lanes)
    grad = g_ref[...].reshape(-1, lanes)
    lane = lax.broadcasted_iota(jnp.int32, query.shape, 1)
    mine = (lane // head_size) == head
    zero = jnp.zeros_like(query)
    own_query = jnp.where(mine, query, zero)
    own_grad = jnp.where(mine, grad, zero)
    key_lane = lax.broadcasted_iota(jnp.int32, key.shape, 1)
    own_key = jnp.where((key_lane // head_size) == head, key, jnp.zeros_like(key))
    scores = mm(own_query, key, NT) * (scale * LOG2E)
    if bias_ref is not None:
        scores = scores + bias_ref[0]
    top = jnp.max(scores, axis=1, keepdims=True)
    weight = jnp.exp2(scores - top)
    total = jnp.sum(weight, axis=1, keepdims=True)
    chance = weight * (1.0 / total)
    grad_chance = mm(own_grad, value, NT)
    delta = jnp.sum(chance * grad_chance, axis=1, keepdims=True)
    grad_scores = (chance * (grad_chance - delta)).astype(bf16)
    part_q = mm(grad_scores, own_key)
    part_v = mm(own_grad, chance.astype(bf16), TN)
    part_k = mm(own_query, grad_scores, TN)

    @pl.when(head == 0)
    def _():
        dq_sum[...] = part_q

    @pl.when(head > 0)
    def _():
        dq_sum[...] += part_q

    @pl.when((head == 0) & (part == 0))
    def _():
        dk_sum[...] = part_k
        dv_sum[...] = part_v

    @pl.when((head > 0) | (part > 0))
    def _():
        dk_sum[...] += part_k
        dv_sum[...] += part_v

    rows = out_ref.shape[2]
    width = out_ref.shape[3] // 3
    held = query.shape[0] // rows
    last_head = head == pl.num_programs(3) - 1

    def place(kind):
        if width == lanes:
            return slice(kind * width, (kind + 1) * width)
        return pl.ds(pl.multiple_of(kind * width + group * lanes, 128), lanes)

    @pl.when(last_head)
    def _():
        result = (dq_sum[...] * scale).astype(bf16)
        for index in range(held):
            out_ref[part * held + index, 0, :, place(0)] = result[index * rows : (index + 1) * rows]

    @pl.when(last_head & (part == pl.num_programs(2) - 1))
    def _():
        for kind, total_ref, factor in ((1, dk_sum, scale), (2, dv_sum, 1.0)):
            result = (total_ref[...] * factor).T.astype(bf16)
            for index in range(shards):
                out_ref[index, 0, :, place(kind)] = result[index * rows : (index + 1) * rows]


def attend_back(queries, keys, values, grad_mixed, head_size, bias, shards):
    major, clips, length, width = queries.shape
    lanes = min(width, 128)
    groups = width // lanes
    rows = major * length // shards
    parts = shards if major == 1 else 1
    query_rows = rows if major == 1 else length
    by_query = pl.BlockSpec((major, 1, query_rows, lanes), lambda c, g, r, h: (0, c, r, g))
    by_key = pl.BlockSpec((major, 1, length, lanes), lambda c, g, r, h: (0, c, 0, g))
    in_specs = [by_query, by_key, by_key, by_query]
    operands = [queries, keys, values, grad_mixed]
    total = major * length
    if bias is not None:
        in_specs.append(pl.BlockSpec((1, 1, total), lambda c, g, r, h: (c, 0, 0)))
        operands.append(bias)
    cells = clips * total * total * (width // head_size)
    return pl.pallas_call(
        functools.partial(backward_kernel, 1.0 / math.sqrt(head_size), head_size, shards),
        grid=(clips, groups, parts, lanes // head_size),
        in_specs=in_specs,
        out_specs=pl.BlockSpec((shards, 1, rows, 3 * width), lambda c, g, r, h: (0, c, 0, 0)),
        out_shape=jax.ShapeDtypeStruct((shards, clips, rows, 3 * width), bf16),
        scratch_shapes=[
            pltpu.VMEM((major * query_rows, lanes), f32),
            pltpu.VMEM((lanes, total), f32),
            pltpu.VMEM((lanes, total), f32),
        ],
        compiler_params=pltpu.CompilerParams(vmem_limit_bytes=VMEM_LIMIT),
        cost_estimate=pl.CostEstimate(
            flops=cells * 2560, bytes_accessed=14 * clips * total * width, transcendentals=cells
        ),
        name="attend_back",
    )(*operands)


def exchange(array):
    return lax.all_to_all(array, "seq", split_axis=0, concat_axis=0, tiled=True)


def gather(array):
    return lax.all_gather(array, "fsdp", axis=0, tiled=True)


def scatter(array):
    return lax.psum_scatter(array, "fsdp", scatter_dimension=0, tiled=True)[0]


def blocks_of(array, count, lanes):
    rows = array.shape[0] // count
    split = array.shape[1] // lanes
    array = array.reshape(count, rows, split, lanes)
    return array.transpose(0, 2, 1, 3).reshape(count, split * rows, lanes)


def from_blocks(array, lanes):
    split = lanes // array.shape[1]
    rows = array.shape[0] // split
    return array.reshape(split, rows, -1).transpose(1, 0, 2).reshape(rows, lanes)


def pack_rows(vectors):
    rows = []
    for member in vectors:
        count = -(-member.shape[0] // 128)
        padded = jnp.pad(member.astype(f32), (0, count * 128 - member.shape[0]))
        rows.append(padded.reshape(count, 128))
    total = sum(member.shape[0] for member in rows)
    if total % 8:
        rows.append(jnp.zeros((8 - total % 8, 128), f32))
    return jnp.concatenate(rows, axis=0)


def unpack_rows(packed, sizes):
    out = []
    at = 0
    for size in sizes:
        count = -(-size // 128)
        piece = packed[:, at : at + count].reshape(packed.shape[0], count * 128)[:, :size]
        out.append(piece.reshape(-1))
        at += count
    return out


MESH = pl.DeviceIdType.MESH


def line_kernel(size, cuts, *refs):
    count = len(cuts)
    ins, outs = refs[:count], refs[count : 2 * count]
    scratch = refs[2 * count :]
    inner, outer, partial = (scratch[i * count : (i + 1) * count] for i in range(3))
    to_inner, to_outer, from_inner, from_outer = scratch[3 * count :]
    me = lax.axis_index("seq")
    left = me < size // 2
    toward = jnp.where(left, me + 1, me - 1)
    away = jnp.where(left, me - 1, me + 1)
    end = (me == 0) | (me == size - 1)
    barrier = pltpu.get_barrier_semaphore()
    pl.semaphore_signal(barrier, inc=1, device_id={"seq": toward}, device_id_type=MESH)

    @pl.when(jnp.logical_not(end))
    def _():
        pl.semaphore_signal(barrier, inc=1, device_id={"seq": away}, device_id_type=MESH)
        pl.semaphore_wait(barrier, 2)

    @pl.when(end)
    def _():
        pl.semaphore_wait(barrier, 1)

    pieces = []
    for index, parts in enumerate(cuts):
        rows = ins[index].shape[0] // parts
        for part in range(parts):
            pieces.append((part / parts, index, slice(part * rows, (part + 1) * rows)))
    pieces.sort(key=lambda piece: piece[:2])
    pieces = [(slot, index, cut) for slot, (_, index, cut) in enumerate(pieces)]

    def inwards(slot, index, cut):
        return pltpu.make_async_remote_copy(
            src_ref=ins[index].at[cut],
            dst_ref=outer[index].at[cut],
            send_sem=to_inner.at[slot],
            recv_sem=from_outer.at[slot],
            device_id={"seq": toward},
            device_id_type=MESH,
        )

    def swap(slot, index, cut):
        return pltpu.make_async_remote_copy(
            src_ref=partial[index].at[cut],
            dst_ref=inner[index].at[cut],
            send_sem=to_inner.at[slot],
            recv_sem=from_inner.at[slot],
            device_id={"seq": toward},
            device_id_type=MESH,
        )

    def outwards(slot, index, cut):
        return pltpu.make_async_remote_copy(
            src_ref=outs[index].at[cut],
            dst_ref=outs[index].at[cut],
            send_sem=to_outer.at[slot],
            recv_sem=from_inner.at[slot],
            device_id={"seq": away},
            device_id_type=MESH,
        )

    @pl.when(end)
    def _():
        for piece in pieces:
            inwards(*piece).start()
        for piece in pieces:
            outwards(*piece).wait_recv()
        for piece in pieces:
            inwards(*piece).wait_send()

    @pl.when(jnp.logical_not(end))
    def _():
        lag = min(count, len(pieces))
        for step in range(len(pieces) + lag):
            if step < len(pieces):
                piece = pieces[step]
                inwards(*piece).wait_recv()
                _, index, cut = piece
                both = ins[index][cut].astype(f32) + outer[index][cut].astype(f32)
                partial[index][cut] = both.astype(bf16)
                swap(*piece).start()
            if step >= lag:
                piece = pieces[step - lag]
                swap(*piece).wait_recv()
                _, index, cut = piece
                both = partial[index][cut].astype(f32) + inner[index][cut].astype(f32)
                outs[index][cut] = both.astype(bf16)
                outwards(*piece).start()
        for piece in pieces:
            swap(*piece).wait_send()
            outwards(*piece).wait_send()


def line_sum(arrays, size, identity):
    cuts = []
    for member in arrays:
        parts = 8
        while parts > 1 and member.shape[0] % (16 * parts):
            parts //= 2
        cuts.append(parts)
    hold = [pltpu.VMEM(member.shape, bf16) for member in arrays]
    whole = pl.BlockSpec(memory_space=pltpu.VMEM)
    return pl.pallas_call(
        functools.partial(line_kernel, size, tuple(cuts)),
        out_shape=[jax.ShapeDtypeStruct(member.shape, bf16) for member in arrays],
        in_specs=[whole] * len(arrays),
        out_specs=[whole] * len(arrays),
        scratch_shapes=hold * 3 + [pltpu.SemaphoreType.DMA((sum(cuts),))] * 4,
        compiler_params=pltpu.CompilerParams(
            collective_id=identity, has_side_effects=True, vmem_limit_bytes=VMEM_LIMIT
        ),
        cost_estimate=pl.CostEstimate(
            flops=0,
            bytes_accessed=40 * sum(2 * member.size for member in arrays),
            transcendentals=0,
        ),
        name="line_sum",
    )(*arrays)


def sum_slots(arrays, size, identity):
    if size == 4:
        return line_sum(arrays, size, identity)
    return lax.psum(tuple(arrays), "seq")


def feed_back(grad_out, mixed, middle, normed_mid, hidden, active, weights, mid_gain):
    out, expand, contract = weights
    grad_y = grad_out.astype(bf16)
    grad_contract = mm(active, grad_y, TN).astype(bf16)
    grad_contract_bias = jnp.sum(grad_y.astype(f32), axis=0)
    grad_hidden = (mm(grad_y, contract, NT) * gelu_slope(hidden)).astype(bf16)
    grad_hidden, grad_contract = lax.optimization_barrier((grad_hidden, grad_contract))
    grad_expand = mm(normed_mid, grad_hidden, TN).astype(bf16)
    grad_expand_bias = jnp.sum(grad_hidden.astype(f32), axis=0)
    grad_normed = mm(grad_hidden, expand, NT)
    grad_normed, grad_expand = lax.optimization_barrier((grad_normed, grad_expand))
    grad_norm, grad_mid_gain, grad_mid_shift = norm_back(middle, mid_gain, grad_normed)
    grad_middle = grad_out + grad_norm
    grad_att = grad_middle.astype(bf16)
    grad_out_weight = mm(mixed, grad_att, TN).astype(bf16)
    grad_out_bias = jnp.sum(grad_att.astype(f32), axis=0)
    grad_mixed = mm(grad_att, out, NT).astype(bf16)
    grads = (grad_out_weight, grad_expand, grad_contract)
    small = dict(
        out_bias=grad_out_bias,
        mid_gain=grad_mid_gain,
        mid_shift=grad_mid_shift,
        expand_bias=grad_expand_bias,
        contract_bias=grad_contract_bias,
    )
    return grad_middle, grad_mixed, grads, small


def own_joint(joint_weight, query_bias, value_bias, shards, shard):
    width = joint_weight.shape[0]
    own = width // shards
    weight = lax.dynamic_slice_in_dim(joint_weight.reshape(width, 3, width), shard * own, own, 2)
    bias_q = lax.dynamic_slice_in_dim(query_bias, shard * own, own, 0)
    bias_v = lax.dynamic_slice_in_dim(value_bias, shard * own, own, 0)
    return weight, (bias_q, None, bias_v)


def own_parts(normed_all, weight, biases):
    flat = normed_all.reshape(-1, normed_all.shape[3])
    out = []
    for index in range(3):
        part = mm(flat, weight[:, index])
        if biases[index] is not None:
            part = part + biases[index]
        out.append(part.astype(bf16).reshape(normed_all.shape[:3] + (weight.shape[2],)))
    return out


def by_sender(joint_weight, shards):
    width = joint_weight.shape[0]
    array = joint_weight.reshape(width, 3, shards, width // shards)
    return array.transpose(0, 2, 1, 3).reshape(width, 3 * width)


def joint_back(received, joint_by_sender):
    shards, clips, rows, width = received.shape
    flat = received.reshape(shards, clips * rows, width).transpose(1, 0, 2)
    return mm(flat.reshape(clips * rows, shards * width), joint_by_sender, NT)


def spread(vector, shards, shard):
    full = jnp.zeros((vector.shape[0] * shards,), f32)
    return lax.dynamic_update_slice_in_dim(full, vector, shard * vector.shape[0], 0)


def joint_small(columns, shards, shard):
    own = columns.shape[0] // 3
    return dict(
        query_bias=spread(columns[:own], shards, shard),
        value_bias=spread(columns[2 * own :], shards, shard),
    )


ORDER = (
    "pre_gain",
    "pre_shift",
    "query_bias",
    "value_bias",
    "out_bias",
    "mid_gain",
    "mid_shift",
    "expand_bias",
    "contract_bias",
)
BLOCK = (
    "pre_gain",
    "pre_shift",
    "joint",
    "query_bias",
    "value_bias",
    "out",
    "out_bias",
    "mid_gain",
    "mid_shift",
    "expand",
    "expand_bias",
    "contract",
    "contract_bias",
)
FRAMES = 8
GRID = 14
MOST_VISIBLE = FRAMES * max(
    high * wide
    for high in range(1, GRID + 1)
    for wide in range(1, GRID + 1)
    if 2 * high * wide < GRID * GRID
)


def body(fsdp_size, seq_size, tokens, visible, slot_token, positions, *rest):
    e_shard = dict(zip(BLOCK, rest[:13]))
    embed_weight, embed_bias, mask_token = rest[13:16]
    p_shard = dict(zip(BLOCK, rest[16:29]))
    cotangent = rest[29]
    shard = lax.axis_index("seq")
    clips, slots, width = tokens.shape
    span = visible.shape[1]

    e_out = gather(e_shard["out"])

    place = lax.broadcasted_iota(jnp.int32, (1, 1, span), 2)
    slot_visible = jnp.any(
        (slot_token[:, :, None] == place) & (visible[:, None, :] > 0), axis=2
    )
    counts = jnp.sum(slot_visible.reshape(clips, seq_size, slots).astype(jnp.int32), axis=2)
    compact = -(-MOST_VISIBLE // (16 * seq_size)) * 16
    fits = (jnp.max(counts) <= compact).astype(f32)

    vectors = [e_shard[name] for name in ORDER] + [embed_bias, mask_token]
    vectors += [p_shard[name] for name in ORDER]
    sizes = [member.shape[0] for member in vectors]
    packed = lax.all_gather(
        pack_rows(vectors + [jnp.full((1,), fits)]), "fsdp", axis=0, tiled=False
    )
    full = unpack_rows(packed, sizes + [1])
    all_fit = jnp.min(full[-1]) > 0.5

    operands = (
        tokens,
        slot_visible,
        counts,
        slot_token,
        positions,
        e_out,
        e_shard["joint"],
        e_shard["expand"],
        e_shard["contract"],
        embed_weight,
        tuple(p_shard[name] for name in ("joint", "out", "expand", "contract")),
        tuple(full[:-1]),
        cotangent,
    )
    whole = functools.partial(main, fsdp_size, seq_size, slots)
    if compact >= slots:
        return whole(*operands)
    return lax.cond(
        all_fit, functools.partial(main, fsdp_size, seq_size, compact), whole, *operands
    )


def main(
    fsdp_size,
    seq_size,
    held,
    tokens,
    slot_visible,
    counts,
    slot_token,
    positions,
    e_out,
    e_joint_shard,
    e_expand_shard,
    e_contract_shard,
    embed_shard,
    p_shards,
    vectors,
    cotangent,
):
    shard = lax.axis_index("seq")
    clips, slots, width = tokens.shape
    span = slot_visible.shape[1]
    rows = clips * slots
    small_width = cotangent.shape[2]
    head_size = width // HEADS
    small_head = small_width // PHEADS
    whole = held == slots
    e_vec = dict(zip(ORDER, vectors[:9]))
    embed_bias, mask_token = vectors[9:11]
    p_vec = dict(zip(ORDER, vectors[11:]))

    e_joint = gather(e_joint_shard)
    packed = jnp.concatenate(
        [blocks_of(member, 1, small_width)[0] for member in (*p_shards, embed_shard)], axis=0
    )

    own_visible = lax.dynamic_slice_in_dim(slot_visible, shard * slots, slots, 1)
    own_flat = own_visible.reshape(rows, 1)
    own_tokens = lax.dynamic_slice_in_dim(slot_token, shard * slots, slots, 1)
    slot_code = jnp.take(positions, own_tokens.reshape(rows), axis=0)

    if whole:
        kept = slot_visible.reshape(clips, 1, span)

        def keep(array):
            return array

        def put_back(array):
            return array

    else:
        kept = lax.broadcasted_iota(jnp.int32, (1, 1, held), 2) < counts[:, :, None]
        kept = kept.reshape(clips, 1, seq_size * held)
        ones = own_visible.astype(bf16)
        before = lax.broadcasted_iota(jnp.int32, (slots, slots), 0)
        after = lax.broadcasted_iota(jnp.int32, (slots, slots), 1)
        rank = mm(ones, (before < after).astype(bf16)).astype(jnp.int32)
        target = lax.broadcasted_iota(jnp.int32, (1, held, 1), 1)
        picks = ((rank[:, None, :] == target) & own_visible[:, None, :]).astype(bf16)

        def keep(array):
            precision = lax.Precision.HIGHEST if array.dtype == f32 else None
            picked = jnp.einsum(
                "crs,csw->crw",
                picks.astype(array.dtype),
                array.reshape(clips, slots, -1),
                precision=precision,
                preferred_element_type=f32,
            )
            return picked.astype(array.dtype).reshape(clips * held, -1)

        def put_back(array):
            placed = jnp.einsum(
                "crs,crw->csw",
                picks.astype(f32),
                array.reshape(clips, held, -1),
                precision=lax.Precision.HIGHEST,
                preferred_element_type=f32,
            )
            return placed.reshape(rows, -1)

    bias = jnp.where(kept, 0.0, -1e30).astype(f32)
    tiled = held % 16 == 0

    def by_clip(array):
        if tiled:
            return array
        shards, count, length, lanes = array.shape
        return array.transpose(1, 0, 2, 3).reshape(1, count, shards * length, lanes)

    inputs = tokens.reshape(rows, width)
    normed = norm_layer(inputs, e_vec["pre_gain"], e_vec["pre_shift"])
    normed_kept = keep(normed).reshape(1, clips, held, width)
    normed_kept, e_expand_shard = lax.optimization_barrier((normed_kept, e_expand_shard))
    e_expand = gather(e_expand_shard)
    normed_all = exchange(jnp.broadcast_to(normed_kept, (seq_size, clips, held, width)))
    queries = (mm(normed, e_joint[:, :width]) + e_vec["query_bias"]).astype(bf16)
    joined = mm(normed_all.reshape(-1, width), e_joint[:, width:])
    joined_bias = jnp.concatenate([jnp.zeros_like(e_vec["value_bias"]), e_vec["value_bias"]])
    joined = (joined + joined_bias).astype(bf16)
    joined, e_contract_shard = lax.optimization_barrier((joined, e_contract_shard))
    e_contract = gather(e_contract_shard)
    mixed = attend(
        queries.reshape(clips, slots, width),
        by_clip(joined.reshape(seq_size, clips, held, 2 * width)),
        head_size,
        bias,
    ).reshape(rows, width)
    mixed, packed = lax.optimization_barrier((mixed, packed))
    packed = lax.all_gather(packed, "fsdp", axis=0, tiled=False)
    middle = inputs + mm(mixed, e_out) + e_vec["out_bias"]
    normed_mid = norm_layer(middle, e_vec["mid_gain"], e_vec["mid_shift"])
    active = gelu(mm(normed_mid, e_expand) + e_vec["expand_bias"])
    encoded = middle + mm(active, e_contract) + e_vec["contract_bias"]
    encoded, packed = lax.optimization_barrier((encoded, packed))
    unpacked = []
    at = 0
    for member in (*p_shards, embed_shard):
        split = member.shape[1] // small_width
        count = member.shape[0] * split
        piece = packed[:, at : at + count].reshape(fsdp_size, split, member.shape[0], small_width)
        unpacked.append(piece.transpose(0, 2, 1, 3).reshape(-1, member.shape[1]))
        at += count
    p_joint, p_out, p_expand, p_contract, embed = unpacked
    context = encoded.astype(bf16)

    embedded = mm(context, embed) + embed_bias
    pred_input = jnp.where(own_flat, embedded, mask_token) + slot_code
    p_normed = norm_layer(pred_input, p_vec["pre_gain"], p_vec["pre_shift"])
    p_queries = (mm(p_normed, p_joint[:, :small_width]) + p_vec["query_bias"]).astype(bf16)
    p_bias = jnp.concatenate([jnp.zeros_like(p_vec["value_bias"]), p_vec["value_bias"]])
    p_normed_all = []
    p_mixed = []
    for clip in range(clips):
        own = p_normed.reshape(clips, slots, small_width)[clip]
        every = lax.all_gather(own, "seq", axis=0, tiled=True)
        p_joined = (mm(every, p_joint[:, small_width:]) + p_bias).astype(bf16)
        p_normed_all.append(every)
        p_mixed.append(
            attend(
                p_queries.reshape(clips, slots, small_width)[clip : clip + 1],
                p_joined.reshape(1, 1, span, 2 * small_width),
                small_head,
                None,
            )
        )
    p_mixed = jnp.concatenate(p_mixed, axis=0).reshape(rows, small_width)
    p_middle = pred_input + mm(p_mixed, p_out) + p_vec["out_bias"]
    p_normed_mid = norm_layer(p_middle, p_vec["mid_gain"], p_vec["mid_shift"])
    p_hidden = mm(p_normed_mid, p_expand) + p_vec["expand_bias"]
    p_active = gelu(p_hidden)
    predicted = p_middle + mm(p_active, p_contract) + p_vec["contract_bias"]

    grad_middle, grad_mixed, p_grads, p_small = feed_back(
        cotangent.reshape(rows, small_width),
        p_mixed,
        p_middle,
        p_normed_mid,
        p_hidden,
        p_active,
        (p_out, p_expand, p_contract),
        p_vec["mid_gain"],
    )
    p_pack = jnp.concatenate(
        [blocks_of(member, fsdp_size, small_width) for member in p_grads], axis=1
    )
    grad_mixed, p_pack = lax.optimization_barrier((grad_mixed, p_pack))
    p_part = scatter(p_pack)
    own_weight, own_bias = own_joint(
        p_joint, p_vec["query_bias"], p_vec["value_bias"], seq_size, shard
    )
    own_width = small_width // seq_size
    grad_mixed = grad_mixed.reshape(rows, seq_size, own_width).transpose(1, 0, 2)
    grad_mixed = exchange(grad_mixed.reshape(seq_size, clips, slots, own_width))
    p_by_sender = by_sender(p_joint, seq_size)
    grad_normed = []
    p_grad_joint = 0.0
    p_columns = 0.0
    for clip in range(clips):
        every = p_normed_all[clip].reshape(1, 1, span, small_width)
        grads = attend_back(
            *own_parts(every, own_weight, own_bias),
            grad_mixed[:, clip].reshape(1, 1, span, own_width),
            small_head,
            None,
            seq_size,
        )
        flat = grads.reshape(span, 3 * own_width)
        p_grad_joint = p_grad_joint + mm(p_normed_all[clip], flat, TN)
        p_columns = p_columns + jnp.sum(flat.astype(f32), axis=0)
        grad_normed.append(joint_back(exchange(grads), p_by_sender))
    p_small.update(joint_small(p_columns, seq_size, shard))
    grad_norm, p_small["pre_gain"], p_small["pre_shift"] = norm_back(
        pred_input, p_vec["pre_gain"], jnp.concatenate(grad_normed, axis=0)
    )
    grad_pred_input = grad_middle + grad_norm
    grad_mask_token = jnp.sum(jnp.where(own_flat, 0.0, grad_pred_input), axis=0)
    grad_embedded = jnp.where(own_flat, grad_pred_input, 0.0).astype(bf16)
    grad_embed = mm(context, grad_embedded, TN).astype(bf16)
    grad_embed_bias = jnp.sum(grad_embedded.astype(f32), axis=0)

    p_own_width = own_width
    p_grad_joint = jnp.pad(p_grad_joint.astype(bf16), ((0, 0), (0, small_width - 3 * own_width)))

    grad_embedded, p_part = lax.optimization_barrier((grad_embedded, p_part))
    grad_context = mm(keep(grad_embedded), embed, NT)
    kept_mid = keep(normed_mid)
    kept_hidden = mm(kept_mid, e_expand) + e_vec["expand_bias"]
    grad_middle, grad_mixed, e_grads, e_small = feed_back(
        grad_context,
        keep(mixed),
        keep(middle),
        kept_mid,
        kept_hidden,
        gelu(kept_hidden),
        (e_out, e_expand, e_contract),
        e_vec["mid_gain"],
    )
    expand_part = scatter(e_grads[1].reshape(fsdp_size, -1, e_grads[1].shape[1]))
    contract_part = scatter(e_grads[2].reshape(fsdp_size, -1, e_grads[2].shape[1]))
    own_weight, own_bias = own_joint(
        e_joint, e_vec["query_bias"], e_vec["value_bias"], seq_size, shard
    )
    own_width = width // seq_size
    grad_mixed = grad_mixed.reshape(clips * held, seq_size, own_width).transpose(1, 0, 2)
    grad_mixed = exchange(grad_mixed.reshape(seq_size, clips, held, own_width))
    parts = own_parts(normed_all, own_weight, own_bias)
    grads = attend_back(
        *[by_clip(member) for member in (*parts, grad_mixed)], head_size, bias, seq_size
    )
    flat = grads.reshape(-1, 3 * own_width)
    e_grad_joint = mm(normed_all.reshape(-1, width), flat, TN).astype(bf16)
    e_small.update(joint_small(jnp.sum(flat.astype(f32), axis=0), seq_size, shard))
    received, contract_part = lax.optimization_barrier((exchange(grads), contract_part))
    grad_norm, e_small["pre_gain"], e_small["pre_shift"] = norm_back(
        keep(inputs), e_vec["pre_gain"], joint_back(received, by_sender(e_joint, seq_size))
    )
    grad_tokens = put_back(grad_middle + grad_norm)

    first = 0 if whole else 2
    contract_sum, expand_sum, p_sum = sum_slots(
        (contract_part, expand_part, p_part), seq_size, first
    )

    small = [e_small[name] for name in ORDER] + [grad_embed_bias, grad_mask_token]
    small += [p_small[name] for name in ORDER]
    small = [member.reshape(fsdp_size, -1) for member in small]
    sizes = [member.shape[1] for member in small]
    count = -(-sum(sizes) // (16 * 128)) * 16
    small.append(jnp.zeros((fsdp_size, count * 128 - sum(sizes)), f32))
    small = jnp.concatenate(small, axis=1).astype(bf16).reshape(fsdp_size, count, 128)
    members = (e_grad_joint, p_grad_joint, e_grads[0], grad_embed)
    late = scatter(
        jnp.concatenate(
            [blocks_of(member, fsdp_size, 128) for member in members] + [small], axis=1
        )
    )

    late, contract_sum = lax.optimization_barrier((late, contract_sum))

    def cut(array, at, rows, lanes, block):
        split = lanes // block
        return from_blocks(array[at : at + split * rows], lanes), at + split * rows

    def all_columns(columns, own):
        columns = columns[:, : 3 * own].reshape(-1, 3, 1, own)
        which = lax.broadcasted_iota(jnp.int32, (1, 1, seq_size, 1), 2)
        placed = jnp.where(which == shard, columns, jnp.zeros_like(columns))
        return placed.reshape(-1, 3 * own * seq_size)

    own_rows = width // fsdp_size
    p_rows = small_width // fsdp_size
    e_columns, at = cut(late, 0, own_rows, 3 * own_width, 128)
    p_columns, at = cut(late, at, p_rows, small_width, 128)
    e_joint_out, p_joint_out, late_sum = sum_slots(
        (all_columns(e_columns, own_width), all_columns(p_columns, p_own_width), late[at:]),
        seq_size,
        first + 1,
    )
    out_sum, at = cut(late_sum, 0, own_rows, width, 128)
    embed_sum, at = cut(late_sum, at, own_rows, small_width, 128)
    vector_sum = late_sum[at:].reshape(-1)
    small_out = []
    at = 0
    for size in sizes:
        small_out.append(vector_sum[at : at + size].astype(f32))
        at += size
    p_wide = p_shards[2].shape[1]
    p_out_sum, at = cut(p_sum, 0, p_rows, small_width, small_width)
    p_expand_sum, at = cut(p_sum, at, p_rows, p_wide, small_width)
    p_contract_sum, at = cut(p_sum, at, p_shards[3].shape[0], small_width, small_width)

    def ordered(vec, joint, out, expand, contract):
        vec = dict(
            zip(ORDER, vec),
            joint=joint.astype(f32),
            out=out.astype(f32),
            expand=expand.astype(f32),
            contract=contract.astype(f32),
        )
        return tuple(vec[name] for name in BLOCK)

    return (
        encoded.reshape(tokens.shape),
        predicted.reshape(cotangent.shape),
        grad_tokens.reshape(tokens.shape),
        *ordered(small_out[:9], e_joint_out, out_sum, expand_sum, contract_sum),
        embed_sum.astype(f32),
        small_out[9],
        small_out[10],
        *ordered(small_out[11:], p_joint_out, p_out_sum, p_expand_sum, p_contract_sum),
    )


def solution(mesh):
    cut, rows, vec, full = P("fsdp", "seq", None), P("fsdp", None), P("fsdp"), P()
    block = (vec, vec, rows, vec, vec, rows, vec, vec, vec, rows, vec, rows, vec)
    return jax.shard_map(
        functools.partial(body, mesh.shape["fsdp"], mesh.shape["seq"]),
        mesh=mesh,
        in_specs=(cut, rows, rows, full, *block, rows, vec, vec, *block, cut),
        out_specs=(cut, cut, cut, *block, rows, vec, vec, *block),
        check_vma=False,
    )
```

```python
import functools
import math

import jax
import jax.numpy as jnp
from jax import lax
from jax.experimental import pallas as pl
from jax.experimental.pallas import tpu as pltpu
from jax.sharding import PartitionSpec as P

HEADS = 16
PHEADS = 12

f32 = jnp.float32
bf16 = jnp.bfloat16
norm_eps = 1e-06
LOG2E = math.log2(math.e)
NN = (((1,), (0,)), ((), ()))
NT = (((1,), (1,)), ((), ()))
TN = (((0,), (0,)), ((), ()))
VMEM_LIMIT = 60 * 2**20


def mm(left, right, dims=NN):
    return lax.dot_general(left, right, dims, preferred_element_type=f32)


def norm_parts(value):
    center = value - jnp.mean(value, axis=-1, keepdims=True)
    spread = jnp.mean(center * center, axis=-1, keepdims=True)
    scale = lax.rsqrt(spread + norm_eps)
    return center * scale, scale


def norm_layer(value, gain, shift):
    unit, _ = norm_parts(value)
    return (unit * gain + shift).astype(bf16)


def norm_back(value, gain, grad):
    unit, scale = norm_parts(value)
    grad_gain = jnp.sum(grad * unit, axis=0)
    grad_shift = jnp.sum(grad, axis=0)
    inner = grad * gain
    inner = inner - jnp.mean(inner, axis=-1, keepdims=True) - unit * jnp.mean(
        inner * unit, axis=-1, keepdims=True
    )
    return scale * inner, grad_gain, grad_shift


def gelu_parts(hidden):
    cdf = 0.5 * (1.0 + lax.erf(hidden * math.sqrt(0.5)))
    return cdf


def gelu(hidden):
    return (hidden * gelu_parts(hidden)).astype(bf16)


def gelu_slope(hidden):
    pdf = jnp.exp(-0.5 * hidden * hidden) * (1.0 / math.sqrt(2.0 * math.pi))
    return gelu_parts(hidden) + hidden * pdf


def forward_kernel(scale, head_size, q_ref, k_ref, v_ref, *rest):
    if len(rest) == 2:
        bias_ref, o_ref = rest
    else:
        bias_ref, o_ref = None, rest[0]
    query = q_ref[0]
    lanes = query.shape[1]
    key = k_ref[...].reshape(-1, lanes)
    value = v_ref[...].reshape(-1, lanes)
    lane = lax.broadcasted_iota(jnp.int32, query.shape, 1)
    result = None
    for head in range(lanes // head_size):
        mine = (lane // head_size) == head
        own_query = jnp.where(mine, query, jnp.zeros_like(query))
        scores = mm(own_query, key, NT) * (scale * LOG2E)
        if bias_ref is not None:
            scores = scores + bias_ref[0]
        top = jnp.max(scores, axis=1, keepdims=True)
        weight = jnp.exp2(scores - top)
        total = jnp.sum(weight, axis=1, keepdims=True)
        part = jnp.where(mine, mm(weight.astype(bf16), value) / total, 0.0)
        result = part if result is None else result + part
    o_ref[0] = result.astype(bf16)


def attend(queries, joined, head_size, bias):
    clips, rows, width = queries.shape
    major, _, length, _ = joined.shape
    keys = major * length
    groups = width // 128
    in_specs = [
        pl.BlockSpec((1, rows, 128), lambda c, g: (c, 0, g)),
        pl.BlockSpec((major, 1, length, 128), lambda c, g: (0, c, 0, g)),
        pl.BlockSpec((major, 1, length, 128), lambda c, g: (0, c, 0, g + groups)),
    ]
    operands = [queries, joined, joined]
    if bias is not None:
        in_specs.append(pl.BlockSpec((1, 1, keys), lambda c, g: (c, 0, 0)))
        operands.append(bias)
    cells = clips * rows * keys * (width // head_size)
    return pl.pallas_call(
        functools.partial(forward_kernel, 1.0 / math.sqrt(head_size), head_size),
        grid=(clips, groups),
        in_specs=in_specs,
        out_specs=pl.BlockSpec((1, rows, 128), lambda c, g: (c, 0, g)),
        out_shape=jax.ShapeDtypeStruct((clips, rows, width), bf16),
        compiler_params=pltpu.CompilerParams(vmem_limit_bytes=VMEM_LIMIT),
        cost_estimate=pl.CostEstimate(
            flops=cells * 1024, bytes_accessed=4 * clips * keys * width, transcendentals=cells
        ),
        name="attend",
    )(*operands)


def backward_kernel(scale, head_size, shards, q_ref, k_ref, v_ref, g_ref, *rest):
    if len(rest) == 4:
        bias_ref = rest[0]
        rest = rest[1:]
    else:
        bias_ref = None
    out_ref, dk_sum, dv_sum = rest
    group = pl.program_id(0)
    part = pl.program_id(1)
    lanes = q_ref.shape[-1]
    query = q_ref[...].reshape(-1, lanes)
    key = k_ref[...].reshape(-1, lanes)
    value = v_ref[...].reshape(-1, lanes)
    grad = g_ref[...].reshape(-1, lanes)
    lane = lax.broadcasted_iota(jnp.int32, query.shape, 1)
    key_lane = lax.broadcasted_iota(jnp.int32, key.shape, 1)
    sums = None
    for head in range(lanes // head_size):
        mine = (lane // head_size) == head
        own_query = jnp.where(mine, query, jnp.zeros_like(query))
        own_grad = jnp.where(mine, grad, jnp.zeros_like(grad))
        own_key = jnp.where((key_lane // head_size) == head, key, jnp.zeros_like(key))
        scores = mm(own_query, key, NT) * (scale * LOG2E)
        if bias_ref is not None:
            scores = scores + bias_ref[0]
        top = jnp.max(scores, axis=1, keepdims=True)
        weight = jnp.exp2(scores - top)
        chance = weight * (1.0 / jnp.sum(weight, axis=1, keepdims=True))
        grad_chance = mm(own_grad, value, NT)
        delta = jnp.sum(chance * grad_chance, axis=1, keepdims=True)
        grad_scores = (chance * (grad_chance - delta)).astype(bf16)
        terms = (
            mm(grad_scores, own_key),
            mm(own_query, grad_scores, TN),
            mm(own_grad, chance.astype(bf16), TN),
        )
        sums = terms if sums is None else tuple(x + y for x, y in zip(sums, terms))
    part_q, part_k, part_v = sums

    @pl.when(part == 0)
    def _():
        dk_sum[...] = part_k
        dv_sum[...] = part_v

    @pl.when(part > 0)
    def _():
        dk_sum[...] += part_k
        dv_sum[...] += part_v

    rows = out_ref.shape[2]
    width = out_ref.shape[3] // 3
    held = query.shape[0] // rows

    def place(kind):
        if width == lanes:
            return slice(kind * width, (kind + 1) * width)
        return pl.ds(pl.multiple_of(kind * width + group * lanes, 128), lanes)

    result_q = (part_q * scale).astype(bf16)
    for index in range(held):
        out_ref[part * held + index, 0, :, place(0)] = result_q[index * rows : (index + 1) * rows]

    @pl.when(part == pl.num_programs(1) - 1)
    def _():
        for kind, total_ref, factor in ((1, dk_sum, scale), (2, dv_sum, 1.0)):
            result = (total_ref[...] * factor).T.astype(bf16)
            for index in range(shards):
                out_ref[index, 0, :, place(kind)] = result[index * rows : (index + 1) * rows]


def attend_back(queries, keys, values, grad_mixed, clip, head_size, bias, shards):
    major, _, length, width = queries.shape
    lanes = min(width, 128)
    groups = width // lanes
    rows = major * length // shards
    parts = shards if major == 1 else 1
    query_rows = rows if major == 1 else length
    by_query = pl.BlockSpec((major, 1, query_rows, lanes), lambda g, r: (0, clip, r, g))
    by_key = pl.BlockSpec((major, 1, length, lanes), lambda g, r: (0, clip, 0, g))
    in_specs = [by_query, by_key, by_key, by_query]
    operands = [queries, keys, values, grad_mixed]
    total = major * length
    if bias is not None:
        in_specs.append(pl.BlockSpec((1, 1, total), lambda g, r: (clip, 0, 0)))
        operands.append(bias)
    cells = total * total * (width // head_size)
    return pl.pallas_call(
        functools.partial(backward_kernel, 1.0 / math.sqrt(head_size), head_size, shards),
        grid=(groups, parts),
        in_specs=in_specs,
        out_specs=pl.BlockSpec((shards, 1, rows, 3 * width), lambda g, r: (0, 0, 0, 0)),
        out_shape=jax.ShapeDtypeStruct((shards, 1, rows, 3 * width), bf16),
        scratch_shapes=[pltpu.VMEM((lanes, total), f32), pltpu.VMEM((lanes, total), f32)],
        compiler_params=pltpu.CompilerParams(vmem_limit_bytes=VMEM_LIMIT),
        cost_estimate=pl.CostEstimate(
            flops=cells * 2560, bytes_accessed=14 * total * width, transcendentals=cells
        ),
        name="attend_back",
    )(*operands)


def exchange(array):
    return lax.all_to_all(array, "seq", split_axis=0, concat_axis=0, tiled=True)


def gather_slots(array, size, shard):
    right = [(index, index + 1) for index in range(size - 1)]
    left = [(index + 1, index) for index in range(size - 1)]
    from_left, from_right = [array], [array]
    for _ in range(size - 1):
        from_left.append(lax.ppermute(from_left[-1], "seq", right))
        from_right.append(lax.ppermute(from_right[-1], "seq", left))
    line = jnp.stack(from_left[:0:-1] + from_right)
    return lax.dynamic_slice_in_dim(line, size - 1 - shard, size, 0)


def gather(array):
    return lax.all_gather(array, "fsdp", axis=0, tiled=True)


def scatter(array):
    return lax.psum_scatter(array, "fsdp", scatter_dimension=0, tiled=True)[0]


def blocks_of(array, count, lanes):
    rows = array.shape[0] // count
    split = array.shape[1] // lanes
    array = array.reshape(count, rows, split, lanes)
    return array.transpose(0, 2, 1, 3).reshape(count, split * rows, lanes)


def from_blocks(array, lanes):
    split = lanes // array.shape[1]
    rows = array.shape[0] // split
    return array.reshape(split, rows, -1).transpose(1, 0, 2).reshape(rows, lanes)


def pack_rows(vectors):
    rows = []
    for member in vectors:
        count = -(-member.shape[0] // 128)
        padded = jnp.pad(member.astype(f32), (0, count * 128 - member.shape[0]))
        rows.append(padded.reshape(count, 128))
    total = sum(member.shape[0] for member in rows)
    if total % 8:
        rows.append(jnp.zeros((8 - total % 8, 128), f32))
    return jnp.concatenate(rows, axis=0)


def unpack_rows(packed, sizes):
    out = []
    at = 0
    for size in sizes:
        count = -(-size // 128)
        piece = packed[:, at : at + count].reshape(packed.shape[0], count * 128)[:, :size]
        out.append(piece.reshape(-1))
        at += count
    return out


MESH = pl.DeviceIdType.MESH


def line_kernel(size, cuts, *refs):
    count = len(cuts)
    ins, outs = refs[:count], refs[count : 2 * count]
    scratch = refs[2 * count :]
    inner, outer, partial = (scratch[i * count : (i + 1) * count] for i in range(3))
    to_inner, to_outer, from_inner, from_outer = scratch[3 * count :]
    me = lax.axis_index("seq")
    left = me < size // 2
    toward = jnp.where(left, me + 1, me - 1)
    away = jnp.where(left, me - 1, me + 1)
    end = (me == 0) | (me == size - 1)
    barrier = pltpu.get_barrier_semaphore()
    pl.semaphore_signal(barrier, inc=1, device_id={"seq": toward}, device_id_type=MESH)

    @pl.when(jnp.logical_not(end))
    def _():
        pl.semaphore_signal(barrier, inc=1, device_id={"seq": away}, device_id_type=MESH)
        pl.semaphore_wait(barrier, 2)

    @pl.when(end)
    def _():
        pl.semaphore_wait(barrier, 1)

    pieces = []
    for index, parts in enumerate(cuts):
        rows = ins[index].shape[0] // parts
        for part in range(parts):
            pieces.append((part / parts, index, slice(part * rows, (part + 1) * rows)))
    pieces.sort(key=lambda piece: piece[:2])
    pieces = [(slot, index, cut) for slot, (_, index, cut) in enumerate(pieces)]

    def inwards(slot, index, cut):
        return pltpu.make_async_remote_copy(
            src_ref=ins[index].at[cut],
            dst_ref=outer[index].at[cut],
            send_sem=to_inner.at[slot],
            recv_sem=from_outer.at[slot],
            device_id={"seq": toward},
            device_id_type=MESH,
        )

    def swap(slot, index, cut):
        return pltpu.make_async_remote_copy(
            src_ref=partial[index].at[cut],
            dst_ref=inner[index].at[cut],
            send_sem=to_inner.at[slot],
            recv_sem=from_inner.at[slot],
            device_id={"seq": toward},
            device_id_type=MESH,
        )

    def outwards(slot, index, cut):
        return pltpu.make_async_remote_copy(
            src_ref=outs[index].at[cut],
            dst_ref=outs[index].at[cut],
            send_sem=to_outer.at[slot],
            recv_sem=from_inner.at[slot],
            device_id={"seq": away},
            device_id_type=MESH,
        )

    @pl.when(end)
    def _():
        for piece in pieces:
            inwards(*piece).start()
        for piece in pieces:
            outwards(*piece).wait_recv()
        for piece in pieces:
            inwards(*piece).wait_send()

    @pl.when(jnp.logical_not(end))
    def _():
        lag = min(count, len(pieces))
        for step in range(len(pieces) + lag):
            if step < len(pieces):
                piece = pieces[step]
                inwards(*piece).wait_recv()
                _, index, cut = piece
                both = ins[index][cut].astype(f32) + outer[index][cut].astype(f32)
                partial[index][cut] = both.astype(bf16)
                swap(*piece).start()
            if step >= lag:
                piece = pieces[step - lag]
                swap(*piece).wait_recv()
                _, index, cut = piece
                both = partial[index][cut].astype(f32) + inner[index][cut].astype(f32)
                outs[index][cut] = both.astype(bf16)
                outwards(*piece).start()
        for piece in pieces:
            swap(*piece).wait_send()
            outwards(*piece).wait_send()


def line_sum(arrays, size, identity):
    cuts = []
    for member in arrays:
        parts = 8
        while parts > 1 and member.shape[0] % (16 * parts):
            parts //= 2
        cuts.append(parts)
    hold = [pltpu.VMEM(member.shape, bf16) for member in arrays]
    whole = pl.BlockSpec(memory_space=pltpu.VMEM)
    return pl.pallas_call(
        functools.partial(line_kernel, size, tuple(cuts)),
        out_shape=[jax.ShapeDtypeStruct(member.shape, bf16) for member in arrays],
        in_specs=[whole] * len(arrays),
        out_specs=[whole] * len(arrays),
        scratch_shapes=hold * 3 + [pltpu.SemaphoreType.DMA((sum(cuts),))] * 4,
        compiler_params=pltpu.CompilerParams(
            collective_id=identity, has_side_effects=True, vmem_limit_bytes=VMEM_LIMIT
        ),
        cost_estimate=pl.CostEstimate(
            flops=0,
            bytes_accessed=40 * sum(2 * member.size for member in arrays),
            transcendentals=0,
        ),
        name="line_sum",
    )(*arrays)


def sum_slots(arrays, size, identity):
    if size == 4:
        return line_sum(arrays, size, identity)
    return lax.psum(tuple(arrays), "seq")


def feed_back(grad_out, mixed, middle, normed_mid, hidden, active, weights, mid_gain):
    out, expand, contract = weights
    grad_y = grad_out.astype(bf16)
    grad_contract = mm(active, grad_y, TN).astype(bf16)
    grad_contract_bias = jnp.sum(grad_y.astype(f32), axis=0)
    grad_y, grad_contract = lax.optimization_barrier((grad_y, grad_contract))
    grad_hidden = (mm(grad_y, contract, NT) * gelu_slope(hidden)).astype(bf16)
    grad_expand = mm(normed_mid, grad_hidden, TN).astype(bf16)
    grad_expand_bias = jnp.sum(grad_hidden.astype(f32), axis=0)
    grad_normed = mm(grad_hidden, expand, NT)
    grad_normed, grad_expand = lax.optimization_barrier((grad_normed, grad_expand))
    grad_norm, grad_mid_gain, grad_mid_shift = norm_back(middle, mid_gain, grad_normed)
    grad_middle = grad_out + grad_norm
    grad_att = grad_middle.astype(bf16)
    grad_out_weight = mm(mixed, grad_att, TN).astype(bf16)
    grad_out_bias = jnp.sum(grad_att.astype(f32), axis=0)
    grad_mixed = mm(grad_att, out, NT).astype(bf16)
    grads = (grad_out_weight, grad_expand, grad_contract)
    small = dict(
        out_bias=grad_out_bias,
        mid_gain=grad_mid_gain,
        mid_shift=grad_mid_shift,
        expand_bias=grad_expand_bias,
        contract_bias=grad_contract_bias,
    )
    return grad_middle, grad_mixed, grads, small


def own_joint(joint_weight, query_bias, value_bias, shards, shard):
    width = joint_weight.shape[0]
    own = width // shards
    weight = lax.dynamic_slice_in_dim(joint_weight.reshape(width, 3, width), shard * own, own, 2)
    bias_q = lax.dynamic_slice_in_dim(query_bias, shard * own, own, 0)
    bias_v = lax.dynamic_slice_in_dim(value_bias, shard * own, own, 0)
    return weight, (bias_q, None, bias_v)


def own_parts(normed_all, weight, biases):
    flat = normed_all.reshape(-1, normed_all.shape[3])
    out = []
    for index in range(3):
        part = mm(flat, weight[:, index])
        if biases[index] is not None:
            part = part + biases[index]
        out.append(part.astype(bf16).reshape(normed_all.shape[:3] + (weight.shape[2],)))
    return out


def by_sender(joint_weight, shards):
    width = joint_weight.shape[0]
    array = joint_weight.reshape(width, 3, shards, width // shards)
    return array.transpose(0, 2, 1, 3).reshape(width, 3 * width)


def joint_back(received, joint_by_sender):
    shards, clips, rows, width = received.shape
    flat = received.reshape(shards, clips * rows, width).transpose(1, 0, 2)
    return mm(flat.reshape(clips * rows, shards * width), joint_by_sender, NT)


def spread(vector, shards, shard):
    full = jnp.zeros((vector.shape[0] * shards,), f32)
    return lax.dynamic_update_slice_in_dim(full, vector, shard * vector.shape[0], 0)


def joint_small(columns, shards, shard):
    own = columns.shape[0] // 3
    return dict(
        query_bias=spread(columns[:own], shards, shard),
        value_bias=spread(columns[2 * own :], shards, shard),
    )


ORDER = (
    "pre_gain",
    "pre_shift",
    "query_bias",
    "value_bias",
    "out_bias",
    "mid_gain",
    "mid_shift",
    "expand_bias",
    "contract_bias",
)
BLOCK = (
    "pre_gain",
    "pre_shift",
    "joint",
    "query_bias",
    "value_bias",
    "out",
    "out_bias",
    "mid_gain",
    "mid_shift",
    "expand",
    "expand_bias",
    "contract",
    "contract_bias",
)
FRAMES = 8
GRID = 14
MOST_VISIBLE = FRAMES * max(
    high * wide
    for high in range(1, GRID + 1)
    for wide in range(1, GRID + 1)
    if 2 * high * wide < GRID * GRID
)


def body(fsdp_size, seq_size, tokens, visible, slot_token, positions, *rest):
    e_shard = dict(zip(BLOCK, rest[:13]))
    embed_weight, embed_bias, mask_token = rest[13:16]
    p_shard = dict(zip(BLOCK, rest[16:29]))
    cotangent = rest[29]
    shard = lax.axis_index("seq")
    clips, slots, width = tokens.shape
    span = visible.shape[1]

    e_out = gather(e_shard["out"])
    e_first = jnp.concatenate([e_shard["joint"], e_shard["expand"], embed_weight], axis=1)

    place = lax.broadcasted_iota(jnp.int32, (1, 1, span), 2)
    slot_visible = jnp.any(
        (slot_token[:, :, None] == place) & (visible[:, None, :] > 0), axis=2
    )
    counts = jnp.sum(slot_visible.reshape(clips, seq_size, slots).astype(jnp.int32), axis=2)
    compact = -(-MOST_VISIBLE // (16 * seq_size)) * 16
    fits = (jnp.max(counts) <= compact).astype(f32)

    vectors = [e_shard[name] for name in ORDER] + [embed_bias, mask_token]
    vectors += [p_shard[name] for name in ORDER]
    sizes = [member.shape[0] for member in vectors]
    packed = lax.all_gather(
        pack_rows(vectors + [jnp.full((1,), fits)]), "fsdp", axis=0, tiled=False
    )
    full = unpack_rows(packed, sizes + [1])
    all_fit = jnp.min(full[-1]) > 0.5

    operands = (
        tokens,
        slot_visible,
        counts,
        slot_token,
        positions,
        e_out,
        e_first,
        e_shard["contract"],
        tuple(p_shard[name] for name in ("joint", "out", "expand", "contract")),
        tuple(full[:-1]),
        cotangent,
    )
    whole = functools.partial(main, fsdp_size, seq_size, slots)
    if compact >= slots:
        return whole(*operands)
    return lax.cond(
        all_fit, functools.partial(main, fsdp_size, seq_size, compact), whole, *operands
    )


def main(
    fsdp_size,
    seq_size,
    held,
    tokens,
    slot_visible,
    counts,
    slot_token,
    positions,
    e_out,
    e_first_shard,
    e_contract_shard,
    p_shards,
    vectors,
    cotangent,
):
    shard = lax.axis_index("seq")
    clips, slots, width = tokens.shape
    span = slot_visible.shape[1]
    rows = clips * slots
    small_width = cotangent.shape[2]
    head_size = width // HEADS
    small_head = small_width // PHEADS
    whole = held == slots
    e_vec = dict(zip(ORDER, vectors[:9]))
    embed_bias, mask_token = vectors[9:11]
    p_vec = dict(zip(ORDER, vectors[11:]))

    e_first = gather(e_first_shard)
    e_joint = e_first[:, : 3 * width]
    e_expand = e_first[:, 3 * width : -small_width]
    embed = e_first[:, -small_width:]
    packed = jnp.concatenate(
        [blocks_of(member, 1, small_width)[0] for member in p_shards], axis=0
    )

    own_visible = lax.dynamic_slice_in_dim(slot_visible, shard * slots, slots, 1)
    own_flat = own_visible.reshape(rows, 1)
    own_tokens = lax.dynamic_slice_in_dim(slot_token, shard * slots, slots, 1)
    slot_code = jnp.take(positions, own_tokens.reshape(rows), axis=0)

    if whole:
        kept = slot_visible.reshape(clips, 1, span)

        def keep(array):
            return array

        def put_back(array):
            return array

    else:
        kept = lax.broadcasted_iota(jnp.int32, (1, 1, held), 2) < counts[:, :, None]
        kept = kept.reshape(clips, 1, seq_size * held)
        ones = own_visible.astype(bf16)
        before = lax.broadcasted_iota(jnp.int32, (slots, slots), 0)
        after = lax.broadcasted_iota(jnp.int32, (slots, slots), 1)
        rank = mm(ones, (before < after).astype(bf16)).astype(jnp.int32)
        target = lax.broadcasted_iota(jnp.int32, (1, held, 1), 1)
        picks = ((rank[:, None, :] == target) & own_visible[:, None, :]).astype(bf16)

        def keep(array):
            precision = lax.Precision.HIGHEST if array.dtype == f32 else None
            picked = jnp.einsum(
                "crs,csw->crw",
                picks.astype(array.dtype),
                array.reshape(clips, slots, -1),
                precision=precision,
                preferred_element_type=f32,
            )
            return picked.astype(array.dtype).reshape(clips * held, -1)

        def put_back(array):
            placed = jnp.einsum(
                "crs,crw->csw",
                picks.astype(f32),
                array.reshape(clips, held, -1),
                precision=lax.Precision.HIGHEST,
                preferred_element_type=f32,
            )
            return placed.reshape(rows, -1)

    bias = jnp.where(kept, 0.0, -1e30).astype(f32)
    tiled = held % 16 == 0

    def by_clip(array):
        if tiled:
            return array
        shards, count, length, lanes = array.shape
        return array.transpose(1, 0, 2, 3).reshape(1, count, shards * length, lanes)

    inputs = tokens.reshape(rows, width)
    normed = norm_layer(inputs, e_vec["pre_gain"], e_vec["pre_shift"])
    normed_kept = keep(normed).reshape(clips, held, width)
    normed_all = gather_slots(normed_kept, seq_size, shard)
    queries = (mm(normed, e_joint[:, :width]) + e_vec["query_bias"]).astype(bf16)
    joined = mm(normed_all.reshape(-1, width), e_joint[:, width:])
    joined_bias = jnp.concatenate([jnp.zeros_like(e_vec["value_bias"]), e_vec["value_bias"]])
    joined = (joined + joined_bias).astype(bf16)
    joined, e_contract_shard = lax.optimization_barrier((joined, e_contract_shard))
    e_contract = gather(e_contract_shard)
    mixed = attend(
        queries.reshape(clips, slots, width),
        by_clip(joined.reshape(seq_size, clips, held, 2 * width)),
        head_size,
        bias,
    ).reshape(rows, width)
    mixed, packed = lax.optimization_barrier((mixed, packed))
    packed = lax.all_gather(packed, "fsdp", axis=0, tiled=False)
    middle = inputs + mm(mixed, e_out) + e_vec["out_bias"]
    normed_mid = norm_layer(middle, e_vec["mid_gain"], e_vec["mid_shift"])
    active = gelu(mm(normed_mid, e_expand) + e_vec["expand_bias"])
    encoded = middle + mm(active, e_contract) + e_vec["contract_bias"]
    encoded, packed = lax.optimization_barrier((encoded, packed))
    unpacked = []
    at = 0
    for member in p_shards:
        split = member.shape[1] // small_width
        count = member.shape[0] * split
        piece = packed[:, at : at + count].reshape(fsdp_size, split, member.shape[0], small_width)
        unpacked.append(piece.transpose(0, 2, 1, 3).reshape(-1, member.shape[1]))
        at += count
    p_joint, p_out, p_expand, p_contract = unpacked
    context = encoded.astype(bf16)

    embedded = mm(context, embed) + embed_bias
    pred_input = jnp.where(own_flat, embedded, mask_token) + slot_code
    p_normed = norm_layer(pred_input, p_vec["pre_gain"], p_vec["pre_shift"])
    p_queries = (mm(p_normed, p_joint[:, :small_width]) + p_vec["query_bias"]).astype(bf16)
    own_weight, own_bias = own_joint(
        e_joint, e_vec["query_bias"], e_vec["value_bias"], seq_size, shard
    )
    own_qkv = [by_clip(member) for member in own_parts(normed_all, own_weight, own_bias)]
    p_queries, *own_qkv = lax.optimization_barrier((p_queries, *own_qkv))
    p_bias = jnp.concatenate([jnp.zeros_like(p_vec["value_bias"]), p_vec["value_bias"]])
    p_normed_all = []
    p_mixed = []
    for clip in range(clips):
        own = p_normed.reshape(clips, slots, small_width)[clip]
        every = lax.all_gather(own, "seq", axis=0, tiled=True)
        p_joined = (mm(every, p_joint[:, small_width:]) + p_bias).astype(bf16)
        p_normed_all.append(every)
        p_mixed.append(
            attend(
                p_queries.reshape(clips, slots, small_width)[clip : clip + 1],
                p_joined.reshape(1, 1, span, 2 * small_width),
                small_head,
                None,
            )
        )
    p_mixed = jnp.concatenate(p_mixed, axis=0).reshape(rows, small_width)
    p_middle = pred_input + mm(p_mixed, p_out) + p_vec["out_bias"]
    p_normed_mid = norm_layer(p_middle, p_vec["mid_gain"], p_vec["mid_shift"])
    p_hidden = mm(p_normed_mid, p_expand) + p_vec["expand_bias"]
    p_active = gelu(p_hidden)
    predicted = p_middle + mm(p_active, p_contract) + p_vec["contract_bias"]

    grad_middle, grad_mixed, p_grads, p_small = feed_back(
        cotangent.reshape(rows, small_width),
        p_mixed,
        p_middle,
        p_normed_mid,
        p_hidden,
        p_active,
        (p_out, p_expand, p_contract),
        p_vec["mid_gain"],
    )
    p_pack = jnp.concatenate(
        [blocks_of(member, fsdp_size, small_width) for member in p_grads], axis=1
    )
    grad_mixed, p_pack = lax.optimization_barrier((grad_mixed, p_pack))
    p_part = scatter(p_pack)
    own_weight, own_bias = own_joint(
        p_joint, p_vec["query_bias"], p_vec["value_bias"], seq_size, shard
    )
    own_width = small_width // seq_size
    grad_mixed = grad_mixed.reshape(rows, seq_size, own_width).transpose(1, 0, 2)
    grad_mixed = exchange(grad_mixed.reshape(seq_size, clips, slots, own_width))
    p_by_sender = by_sender(p_joint, seq_size)
    grad_normed = []
    p_grad_joint = 0.0
    p_columns = 0.0
    for clip in range(clips):
        every = p_normed_all[clip].reshape(1, 1, span, small_width)
        grads = attend_back(
            *own_parts(every, own_weight, own_bias),
            grad_mixed[:, clip].reshape(1, 1, span, own_width),
            0,
            small_head,
            None,
            seq_size,
        )
        flat = grads.reshape(span, 3 * own_width)
        p_grad_joint = p_grad_joint + mm(p_normed_all[clip], flat, TN)
        p_columns = p_columns + jnp.sum(flat.astype(f32), axis=0)
        grad_normed.append(joint_back(exchange(grads), p_by_sender))
    p_small.update(joint_small(p_columns, seq_size, shard))
    grad_norm, p_small["pre_gain"], p_small["pre_shift"] = norm_back(
        pred_input, p_vec["pre_gain"], jnp.concatenate(grad_normed, axis=0)
    )
    grad_pred_input = grad_middle + grad_norm
    grad_mask_token = jnp.sum(jnp.where(own_flat, 0.0, grad_pred_input), axis=0)
    grad_embedded = jnp.where(own_flat, grad_pred_input, 0.0).astype(bf16)
    grad_embed = mm(context, grad_embedded, TN).astype(bf16)
    grad_embed_bias = jnp.sum(grad_embedded.astype(f32), axis=0)

    p_own_width = own_width
    p_grad_joint = jnp.pad(p_grad_joint.astype(bf16), ((0, 0), (0, small_width - 3 * own_width)))

    grad_embedded, p_part = lax.optimization_barrier((grad_embedded, p_part))
    grad_context = mm(keep(grad_embedded), embed, NT)
    kept_mid = keep(normed_mid)
    kept_hidden = mm(kept_mid, e_expand) + e_vec["expand_bias"]
    grad_middle, grad_mixed, e_grads, e_small = feed_back(
        grad_context,
        keep(mixed),
        keep(middle),
        kept_mid,
        kept_hidden,
        gelu(kept_hidden),
        (e_out, e_expand, e_contract),
        e_vec["mid_gain"],
    )
    expand_part = scatter(e_grads[1].reshape(fsdp_size, -1, e_grads[1].shape[1]))
    contract_part = scatter(e_grads[2].reshape(fsdp_size, -1, e_grads[2].shape[1]))
    own_width = width // seq_size
    grad_mixed = grad_mixed.reshape(clips * held, seq_size, own_width).transpose(1, 0, 2)
    grad_mixed = by_clip(exchange(grad_mixed.reshape(seq_size, clips, held, own_width)))
    grads = [
        attend_back(*own_qkv, grad_mixed, clip, head_size, bias, seq_size) for clip in range(clips)
    ]
    received = [exchange(member) for member in grads]
    received[0], contract_part = lax.optimization_barrier((received[0], contract_part))
    flat = jnp.concatenate(grads, axis=1).reshape(-1, 3 * own_width)
    e_grad_joint = mm(normed_all.reshape(-1, width), flat, TN).astype(bf16)
    e_small.update(joint_small(jnp.sum(flat.astype(f32), axis=0), seq_size, shard))
    e_by_sender = by_sender(e_joint, seq_size)
    grad_normed = jnp.concatenate([joint_back(member, e_by_sender) for member in received], axis=0)
    grad_norm, e_small["pre_gain"], e_small["pre_shift"] = norm_back(
        keep(inputs), e_vec["pre_gain"], grad_normed
    )
    grad_tokens = put_back(grad_middle + grad_norm)

    first = 0 if whole else 2
    contract_sum, expand_sum, p_sum = sum_slots(
        (contract_part, expand_part, p_part), seq_size, first
    )

    small = [e_small[name] for name in ORDER] + [grad_embed_bias, grad_mask_token]
    small += [p_small[name] for name in ORDER]
    small = [member.reshape(fsdp_size, -1) for member in small]
    sizes = [member.shape[1] for member in small]
    count = -(-sum(sizes) // (16 * 128)) * 16
    small.append(jnp.zeros((fsdp_size, count * 128 - sum(sizes)), f32))
    small = jnp.concatenate(small, axis=1).astype(bf16).reshape(fsdp_size, count, 128)
    members = (e_grad_joint, p_grad_joint, e_grads[0], grad_embed)
    late = scatter(
        jnp.concatenate(
            [blocks_of(member, fsdp_size, 128) for member in members] + [small], axis=1
        )
    )

    late, expand_sum = lax.optimization_barrier((late, expand_sum))

    def cut(array, at, rows, lanes, block):
        split = lanes // block
        return from_blocks(array[at : at + split * rows], lanes), at + split * rows

    def all_columns(columns, own):
        columns = columns[:, : 3 * own].reshape(-1, 3, 1, own)
        which = lax.broadcasted_iota(jnp.int32, (1, 1, seq_size, 1), 2)
        placed = jnp.where(which == shard, columns, jnp.zeros_like(columns))
        return placed.reshape(-1, 3 * own * seq_size)

    own_rows = width // fsdp_size
    p_rows = small_width // fsdp_size
    e_columns, at = cut(late, 0, own_rows, 3 * own_width, 128)
    p_columns, at = cut(late, at, p_rows, small_width, 128)
    e_joint_out, p_joint_out, late_sum = sum_slots(
        (all_columns(e_columns, own_width), all_columns(p_columns, p_own_width), late[at:]),
        seq_size,
        first + 1,
    )
    out_sum, at = cut(late_sum, 0, own_rows, width, 128)
    embed_sum, at = cut(late_sum, at, own_rows, small_width, 128)
    vector_sum = late_sum[at:].reshape(-1)
    small_out = []
    at = 0
    for size in sizes:
        small_out.append(vector_sum[at : at + size].astype(f32))
        at += size
    p_wide = p_shards[2].shape[1]
    p_out_sum, at = cut(p_sum, 0, p_rows, small_width, small_width)
    p_expand_sum, at = cut(p_sum, at, p_rows, p_wide, small_width)
    p_contract_sum, at = cut(p_sum, at, p_shards[3].shape[0], small_width, small_width)

    def ordered(vec, joint, out, expand, contract):
        vec = dict(
            zip(ORDER, vec),
            joint=joint.astype(f32),
            out=out.astype(f32),
            expand=expand.astype(f32),
            contract=contract.astype(f32),
        )
        return tuple(vec[name] for name in BLOCK)

    return (
        encoded.reshape(tokens.shape),
        predicted.reshape(cotangent.shape),
        grad_tokens.reshape(tokens.shape),
        *ordered(small_out[:9], e_joint_out, out_sum, expand_sum, contract_sum),
        embed_sum.astype(f32),
        small_out[9],
        small_out[10],
        *ordered(small_out[11:], p_joint_out, p_out_sum, p_expand_sum, p_contract_sum),
    )


def solution(mesh):
    cut, rows, vec, full = P("fsdp", "seq", None), P("fsdp", None), P("fsdp"), P()
    block = (vec, vec, rows, vec, vec, rows, vec, vec, vec, rows, vec, rows, vec)
    return jax.shard_map(
        functools.partial(body, mesh.shape["fsdp"], mesh.shape["seq"]),
        mesh=mesh,
        in_specs=(cut, rows, rows, full, *block, rows, vec, vec, *block, cut),
        out_specs=(cut, cut, cut, *block, rows, vec, vec, *block),
        check_vma=False,
    )
```

```python
import functools
import math

import jax
import jax.numpy as jnp
from jax import lax
from jax.experimental import pallas as pl
from jax.experimental.pallas import tpu as pltpu
from jax.sharding import PartitionSpec as P

HEADS = 16
PHEADS = 12

f32 = jnp.float32
bf16 = jnp.bfloat16
norm_eps = 1e-06
LOG2E = math.log2(math.e)
NN = (((1,), (0,)), ((), ()))
NT = (((1,), (1,)), ((), ()))
TN = (((0,), (0,)), ((), ()))
VMEM_LIMIT = 60 * 2**20


def mm(left, right, dims=NN):
    return lax.dot_general(left, right, dims, preferred_element_type=f32)


def norm_parts(value):
    center = value - jnp.mean(value, axis=-1, keepdims=True)
    spread = jnp.mean(center * center, axis=-1, keepdims=True)
    scale = lax.rsqrt(spread + norm_eps)
    return center * scale, scale


def norm_layer(value, gain, shift):
    unit, _ = norm_parts(value)
    return (unit * gain + shift).astype(bf16)


def norm_back(value, gain, grad):
    unit, scale = norm_parts(value)
    grad_gain = jnp.sum(grad * unit, axis=0)
    grad_shift = jnp.sum(grad, axis=0)
    inner = grad * gain
    inner = inner - jnp.mean(inner, axis=-1, keepdims=True) - unit * jnp.mean(
        inner * unit, axis=-1, keepdims=True
    )
    return scale * inner, grad_gain, grad_shift


def gelu_parts(hidden):
    cdf = 0.5 * (1.0 + lax.erf(hidden * math.sqrt(0.5)))
    return cdf


def gelu(hidden):
    return (hidden * gelu_parts(hidden)).astype(bf16)


def gelu_slope(hidden):
    pdf = jnp.exp(-0.5 * hidden * hidden) * (1.0 / math.sqrt(2.0 * math.pi))
    return gelu_parts(hidden) + hidden * pdf


def forward_kernel(scale, head_size, q_ref, k_ref, v_ref, *rest):
    if len(rest) == 2:
        bias_ref, o_ref = rest
    else:
        bias_ref, o_ref = None, rest[0]
    query = q_ref[0]
    lanes = query.shape[1]
    key = k_ref[...].reshape(-1, lanes)
    value = v_ref[...].reshape(-1, lanes)
    lane = lax.broadcasted_iota(jnp.int32, query.shape, 1)
    result = None
    for head in range(lanes // head_size):
        mine = (lane // head_size) == head
        own_query = jnp.where(mine, query, jnp.zeros_like(query))
        scores = mm(own_query, key, NT) * (scale * LOG2E)
        if bias_ref is not None:
            scores = scores + bias_ref[0]
        top = jnp.max(scores, axis=1, keepdims=True)
        weight = jnp.exp2(scores - top)
        total = jnp.sum(weight, axis=1, keepdims=True)
        part = jnp.where(mine, mm(weight.astype(bf16), value) / total, 0.0)
        result = part if result is None else result + part
    o_ref[0] = result.astype(bf16)


def attend(queries, joined, head_size, bias):
    clips, rows, width = queries.shape
    major, _, length, _ = joined.shape
    keys = major * length
    groups = width // 128
    in_specs = [
        pl.BlockSpec((1, rows, 128), lambda c, g: (c, 0, g)),
        pl.BlockSpec((major, 1, length, 128), lambda c, g: (0, c, 0, g)),
        pl.BlockSpec((major, 1, length, 128), lambda c, g: (0, c, 0, g + groups)),
    ]
    operands = [queries, joined, joined]
    if bias is not None:
        in_specs.append(pl.BlockSpec((1, 1, keys), lambda c, g: (c, 0, 0)))
        operands.append(bias)
    cells = clips * rows * keys * (width // head_size)
    return pl.pallas_call(
        functools.partial(forward_kernel, 1.0 / math.sqrt(head_size), head_size),
        grid=(clips, groups),
        in_specs=in_specs,
        out_specs=pl.BlockSpec((1, rows, 128), lambda c, g: (c, 0, g)),
        out_shape=jax.ShapeDtypeStruct((clips, rows, width), bf16),
        compiler_params=pltpu.CompilerParams(vmem_limit_bytes=VMEM_LIMIT),
        cost_estimate=pl.CostEstimate(
            flops=cells * 1024, bytes_accessed=4 * clips * keys * width, transcendentals=cells
        ),
        name="attend",
    )(*operands)


def backward_kernel(scale, head_size, shards, q_ref, k_ref, v_ref, g_ref, *rest):
    if len(rest) == 4:
        bias_ref = rest[0]
        rest = rest[1:]
    else:
        bias_ref = None
    out_ref, dk_sum, dv_sum = rest
    group = pl.program_id(0)
    part = pl.program_id(1)
    lanes = q_ref.shape[-1]
    query = q_ref[...].reshape(-1, lanes)
    key = k_ref[...].reshape(-1, lanes)
    value = v_ref[...].reshape(-1, lanes)
    grad = g_ref[...].reshape(-1, lanes)
    lane = lax.broadcasted_iota(jnp.int32, query.shape, 1)
    key_lane = lax.broadcasted_iota(jnp.int32, key.shape, 1)
    sums = None
    for head in range(lanes // head_size):
        mine = (lane // head_size) == head
        own_query = jnp.where(mine, query, jnp.zeros_like(query))
        own_grad = jnp.where(mine, grad, jnp.zeros_like(grad))
        own_key = jnp.where((key_lane // head_size) == head, key, jnp.zeros_like(key))
        scores = mm(own_query, key, NT) * (scale * LOG2E)
        if bias_ref is not None:
            scores = scores + bias_ref[0]
        top = jnp.max(scores, axis=1, keepdims=True)
        weight = jnp.exp2(scores - top)
        chance = weight * (1.0 / jnp.sum(weight, axis=1, keepdims=True))
        grad_chance = mm(own_grad, value, NT)
        delta = jnp.sum(chance * grad_chance, axis=1, keepdims=True)
        grad_scores = (chance * (grad_chance - delta)).astype(bf16)
        terms = (
            mm(grad_scores, own_key),
            mm(own_query, grad_scores, TN),
            mm(own_grad, chance.astype(bf16), TN),
        )
        sums = terms if sums is None else tuple(x + y for x, y in zip(sums, terms))
    part_q, part_k, part_v = sums

    @pl.when(part == 0)
    def _():
        dk_sum[...] = part_k
        dv_sum[...] = part_v

    @pl.when(part > 0)
    def _():
        dk_sum[...] += part_k
        dv_sum[...] += part_v

    rows = out_ref.shape[2]
    width = out_ref.shape[3] // 3
    held = query.shape[0] // rows

    def place(kind):
        if width == lanes:
            return slice(kind * width, (kind + 1) * width)
        return pl.ds(pl.multiple_of(kind * width + group * lanes, 128), lanes)

    result_q = (part_q * scale).astype(bf16)
    for index in range(held):
        out_ref[part * held + index, 0, :, place(0)] = result_q[index * rows : (index + 1) * rows]

    @pl.when(part == pl.num_programs(1) - 1)
    def _():
        for kind, total_ref, factor in ((1, dk_sum, scale), (2, dv_sum, 1.0)):
            result = (total_ref[...] * factor).T.astype(bf16)
            for index in range(shards):
                out_ref[index, 0, :, place(kind)] = result[index * rows : (index + 1) * rows]


def attend_back(queries, keys, values, grad_mixed, clip, head_size, bias, shards):
    major, _, length, width = queries.shape
    lanes = min(width, 128)
    groups = width // lanes
    rows = major * length // shards
    parts = shards if major == 1 else 1
    query_rows = rows if major == 1 else length
    by_query = pl.BlockSpec((major, 1, query_rows, lanes), lambda g, r: (0, clip, r, g))
    by_key = pl.BlockSpec((major, 1, length, lanes), lambda g, r: (0, clip, 0, g))
    in_specs = [by_query, by_key, by_key, by_query]
    operands = [queries, keys, values, grad_mixed]
    total = major * length
    if bias is not None:
        in_specs.append(pl.BlockSpec((1, 1, total), lambda g, r: (clip, 0, 0)))
        operands.append(bias)
    cells = total * total * (width // head_size)
    return pl.pallas_call(
        functools.partial(backward_kernel, 1.0 / math.sqrt(head_size), head_size, shards),
        grid=(groups, parts),
        in_specs=in_specs,
        out_specs=pl.BlockSpec((shards, 1, rows, 3 * width), lambda g, r: (0, 0, 0, 0)),
        out_shape=jax.ShapeDtypeStruct((shards, 1, rows, 3 * width), bf16),
        scratch_shapes=[pltpu.VMEM((lanes, total), f32), pltpu.VMEM((lanes, total), f32)],
        compiler_params=pltpu.CompilerParams(vmem_limit_bytes=VMEM_LIMIT),
        cost_estimate=pl.CostEstimate(
            flops=cells * 2560, bytes_accessed=14 * total * width, transcendentals=cells
        ),
        name="attend_back",
    )(*operands)


def exchange(array):
    return lax.all_to_all(array, "seq", split_axis=0, concat_axis=0, tiled=True)


def gather(array):
    return lax.all_gather(array, "fsdp", axis=0, tiled=True)


def scatter(array):
    return lax.psum_scatter(array, "fsdp", scatter_dimension=0, tiled=True)


def pack_rows(vectors):
    rows = []
    for member in vectors:
        count = -(-member.shape[0] // 128)
        padded = jnp.pad(member.astype(f32), (0, count * 128 - member.shape[0]))
        rows.append(padded.reshape(count, 128))
    total = sum(member.shape[0] for member in rows)
    if total % 8:
        rows.append(jnp.zeros((8 - total % 8, 128), f32))
    return jnp.concatenate(rows, axis=0)


def unpack_rows(packed, sizes):
    out = []
    at = 0
    for size in sizes:
        count = -(-size // 128)
        piece = packed[:, at : at + count].reshape(packed.shape[0], count * 128)[:, :size]
        out.append(piece.reshape(-1))
        at += count
    return out


MESH = pl.DeviceIdType.MESH


def line_kernel(size, cuts, shares, *refs):
    count = len(cuts)
    held = count + shares
    ins, outs = refs[:count], refs[held : held + count]
    own, every = refs[count], refs[held + count]
    scratch = refs[2 * held :]
    inner, outer, partial = (scratch[i * count : (i + 1) * count] for i in range(3))
    to_inner, to_outer, from_inner, from_outer = scratch[3 * count : 3 * count + 4]
    me = lax.axis_index("seq")
    left = me < size // 2
    toward = jnp.where(left, me + 1, me - 1)
    away = jnp.where(left, me - 1, me + 1)
    end = (me == 0) | (me == size - 1)
    barrier = pltpu.get_barrier_semaphore()
    pl.semaphore_signal(barrier, inc=1, device_id={"seq": toward}, device_id_type=MESH)

    @pl.when(jnp.logical_not(end))
    def _():
        pl.semaphore_signal(barrier, inc=1, device_id={"seq": away}, device_id_type=MESH)
        pl.semaphore_wait(barrier, 2)

    @pl.when(end)
    def _():
        pl.semaphore_wait(barrier, 1)

    pieces = []
    for index, parts in enumerate(cuts):
        rows = ins[index].shape[0] // parts
        for part in range(parts):
            pieces.append((part / parts, index, slice(part * rows, (part + 1) * rows)))
    pieces.sort(key=lambda piece: piece[:2])
    pieces = [(slot, index, cut) for slot, (_, index, cut) in enumerate(pieces)]

    def inwards(slot, index, cut):
        return pltpu.make_async_remote_copy(
            src_ref=ins[index].at[cut],
            dst_ref=outer[index].at[cut],
            send_sem=to_inner.at[slot],
            recv_sem=from_outer.at[slot],
            device_id={"seq": toward},
            device_id_type=MESH,
        )

    def swap(slot, index, cut):
        return pltpu.make_async_remote_copy(
            src_ref=partial[index].at[cut],
            dst_ref=inner[index].at[cut],
            send_sem=to_inner.at[slot],
            recv_sem=from_inner.at[slot],
            device_id={"seq": toward},
            device_id_type=MESH,
        )

    def outwards(slot, index, cut):
        return pltpu.make_async_remote_copy(
            src_ref=outs[index].at[cut],
            dst_ref=outs[index].at[cut],
            send_sem=to_outer.at[slot],
            recv_sem=from_inner.at[slot],
            device_id={"seq": away},
            device_id_type=MESH,
        )

    @pl.when(end)
    def _():
        for piece in pieces:
            inwards(*piece).start()

    if shares:
        sent, arrived = scratch[3 * count + 4 :]
        every[me] = own[...]

        def passes(way, hop):
            step = 1 - 2 * way
            block = me - step * hop
            return pltpu.make_async_remote_copy(
                src_ref=own if hop == 0 else every.at[block],
                dst_ref=every.at[block],
                send_sem=sent.at[way, hop],
                recv_sem=arrived.at[way, hop],
                device_id={"seq": me + step},
                device_id_type=MESH,
            )

        def sends(way, hop):
            if way == 0:
                return (me < size - 1) & (me - hop >= 0)
            return (me > 0) & (me + hop <= size - 1)

        def receives(way, hop):
            return me - 1 - hop >= 0 if way == 0 else me + 1 + hop <= size - 1

        def landing(way, hop):
            block = me - 1 - hop if way == 0 else me + 1 + hop
            return pltpu.make_async_remote_copy(
                src_ref=every.at[block],
                dst_ref=every.at[block],
                send_sem=sent.at[way, hop],
                recv_sem=arrived.at[way, hop],
                device_id={"seq": toward},
                device_id_type=MESH,
            )

        for hop in range(size - 1):
            for way in (0, 1):
                if hop > 0:

                    @pl.when(receives(way, hop - 1))
                    def _(way=way, hop=hop):
                        landing(way, hop - 1).wait_recv()

                @pl.when(sends(way, hop))
                def _(way=way, hop=hop):
                    passes(way, hop).start()

        for way in (0, 1):

            @pl.when(receives(way, size - 2))
            def _(way=way):
                landing(way, size - 2).wait_recv()

            for hop in range(size - 1):

                @pl.when(sends(way, hop))
                def _(way=way, hop=hop):
                    passes(way, hop).wait_send()

    @pl.when(end)
    def _():
        for piece in pieces:
            outwards(*piece).wait_recv()
        for piece in pieces:
            inwards(*piece).wait_send()

    @pl.when(jnp.logical_not(end))
    def _():
        lag = min(count, len(pieces))
        for step in range(len(pieces) + lag):
            if step < len(pieces):
                piece = pieces[step]
                inwards(*piece).wait_recv()
                _, index, cut = piece
                both = ins[index][cut].astype(f32) + outer[index][cut].astype(f32)
                partial[index][cut] = both.astype(bf16)
                swap(*piece).start()
            if step >= lag:
                piece = pieces[step - lag]
                swap(*piece).wait_recv()
                _, index, cut = piece
                both = partial[index][cut].astype(f32) + inner[index][cut].astype(f32)
                outs[index][cut] = both.astype(bf16)
                outwards(*piece).start()
        for piece in pieces:
            swap(*piece).wait_send()
            outwards(*piece).wait_send()


def line_sum(arrays, size, identity, share=None):
    cuts = []
    for member in arrays:
        parts = 8
        while parts > 1 and member.shape[0] % (16 * parts):
            parts //= 2
        cuts.append(parts)
    hold = [pltpu.VMEM(member.shape, bf16) for member in arrays]
    shapes = [jax.ShapeDtypeStruct(member.shape, bf16) for member in arrays]
    semaphores = [pltpu.SemaphoreType.DMA((sum(cuts),))] * 4
    operands = list(arrays)
    if share is not None:
        operands.append(share)
        shapes.append(jax.ShapeDtypeStruct((size,) + share.shape, bf16))
        semaphores += [pltpu.SemaphoreType.DMA((2, size - 1))] * 2
    whole = pl.BlockSpec(memory_space=pltpu.VMEM)
    return pl.pallas_call(
        functools.partial(line_kernel, size, tuple(cuts), int(share is not None)),
        out_shape=shapes,
        in_specs=[whole] * len(operands),
        out_specs=[whole] * len(operands),
        scratch_shapes=hold * 3 + semaphores,
        compiler_params=pltpu.CompilerParams(
            collective_id=identity, has_side_effects=True, vmem_limit_bytes=VMEM_LIMIT
        ),
        cost_estimate=pl.CostEstimate(
            flops=0,
            bytes_accessed=40 * sum(2 * member.size for member in operands),
            transcendentals=0,
        ),
        name="line_sum",
    )(*operands)


def sum_slots(arrays, size, identity, share=None):
    if size == 4:
        return line_sum(arrays, size, identity, share)
    sums = lax.psum(tuple(arrays), "seq")
    if share is None:
        return sums
    return (*sums, lax.all_gather(share, "seq", axis=0, tiled=False))


def feed_back(grad_out, middle, normed_mid, hidden, active, weights, mid_gain):
    out, expand, contract = weights
    grad_y = grad_out.astype(bf16)
    grad_contract = mm(active, grad_y, TN).astype(bf16)
    grad_contract_bias = jnp.sum(grad_y.astype(f32), axis=0)
    grad_y, grad_contract = lax.optimization_barrier((grad_y, grad_contract))
    grad_hidden = (mm(grad_y, contract, NT) * gelu_slope(hidden)).astype(bf16)
    grad_expand = mm(normed_mid, grad_hidden, TN).astype(bf16)
    grad_expand_bias = jnp.sum(grad_hidden.astype(f32), axis=0)
    grad_normed = mm(grad_hidden, expand, NT)
    grad_normed, grad_expand = lax.optimization_barrier((grad_normed, grad_expand))
    grad_norm, grad_mid_gain, grad_mid_shift = norm_back(middle, mid_gain, grad_normed)
    grad_middle = grad_out + grad_norm
    grad_att = grad_middle.astype(bf16)
    grad_out_bias = jnp.sum(grad_att.astype(f32), axis=0)
    grad_mixed = mm(grad_att, out, NT).astype(bf16)
    small = dict(
        out_bias=grad_out_bias,
        mid_gain=grad_mid_gain,
        mid_shift=grad_mid_shift,
        expand_bias=grad_expand_bias,
        contract_bias=grad_contract_bias,
    )
    return grad_middle, grad_att, grad_mixed, (grad_expand, grad_contract), small


def own_joint(joint_weight, query_bias, value_bias, shards, shard):
    width = joint_weight.shape[0]
    own = width // shards
    weight = lax.dynamic_slice_in_dim(joint_weight.reshape(width, 3, width), shard * own, own, 2)
    bias_q = lax.dynamic_slice_in_dim(query_bias, shard * own, own, 0)
    bias_v = lax.dynamic_slice_in_dim(value_bias, shard * own, own, 0)
    return weight, (bias_q, None, bias_v)


def own_parts(normed_all, weight, biases):
    flat = normed_all.reshape(-1, normed_all.shape[3])
    out = []
    for index in range(3):
        part = mm(flat, weight[:, index])
        if biases[index] is not None:
            part = part + biases[index]
        out.append(part.astype(bf16).reshape(normed_all.shape[:3] + (weight.shape[2],)))
    return out


def by_sender(joint_weight, shards):
    width = joint_weight.shape[0]
    array = joint_weight.reshape(width, 3, shards, width // shards)
    return array.transpose(0, 2, 1, 3).reshape(width, 3 * width)


def joint_back(received, joint_by_sender):
    shards, clips, rows, width = received.shape
    flat = received.reshape(shards, clips * rows, width).transpose(1, 0, 2)
    return mm(flat.reshape(clips * rows, shards * width), joint_by_sender, NT)


def joint_small(columns, owners, shards, shard):
    own = columns.shape[0] // 3
    each = owners // shards
    mine = lax.broadcasted_iota(jnp.int32, (owners, 1), 0) // each == shard

    def full(vector):
        return jnp.where(mine, jnp.tile(vector.reshape(each, -1), (shards, 1)), 0.0)

    return dict(query_bias=full(columns[:own]), value_bias=full(columns[2 * own :]))


ORDER = (
    "pre_gain",
    "pre_shift",
    "query_bias",
    "value_bias",
    "out_bias",
    "mid_gain",
    "mid_shift",
    "expand_bias",
    "contract_bias",
)
BLOCK = (
    "pre_gain",
    "pre_shift",
    "joint",
    "query_bias",
    "value_bias",
    "out",
    "out_bias",
    "mid_gain",
    "mid_shift",
    "expand",
    "expand_bias",
    "contract",
    "contract_bias",
)
FRAMES = 8
GRID = 14
MOST_VISIBLE = FRAMES * max(
    high * wide
    for high in range(1, GRID + 1)
    for wide in range(1, GRID + 1)
    if 2 * high * wide < GRID * GRID
)


def body(fsdp_size, seq_size, tokens, visible, slot_token, positions, *rest):
    e_shard = dict(zip(BLOCK, rest[:13]))
    embed_weight, embed_bias, mask_token = rest[13:16]
    p_shard = dict(zip(BLOCK, rest[16:29]))
    cotangent = rest[29]
    shard = lax.axis_index("seq")
    clips, slots, width = tokens.shape
    span = visible.shape[1]

    e_out = gather(e_shard["out"])
    place = lax.broadcasted_iota(jnp.int32, (1, 1, span), 2)
    slot_visible = jnp.any(
        (slot_token[:, :, None] == place) & (visible[:, None, :] > 0), axis=2
    )
    counts = jnp.sum(slot_visible.reshape(clips, seq_size, slots).astype(jnp.int32), axis=2)
    compact = -(-MOST_VISIBLE // (16 * seq_size)) * 16
    fits = (jnp.max(counts) <= compact).astype(f32)

    vectors = [e_shard[name] for name in ORDER] + [embed_bias, mask_token]
    vectors += [p_shard[name] for name in ORDER]
    sizes = [member.shape[0] for member in vectors]
    packed = lax.all_gather(
        pack_rows(vectors + [jnp.full((1,), fits)]), "fsdp", axis=0, tiled=False
    )
    full = unpack_rows(packed, sizes + [1])
    all_fit = jnp.min(full[-1]) > 0.5

    operands = (
        tokens,
        slot_visible,
        counts,
        slot_token,
        positions,
        e_out,
        tuple(e_shard[name] for name in ("joint", "expand", "contract")),
        embed_weight,
        tuple(p_shard[name] for name in ("joint", "out", "expand", "contract")),
        tuple(full[:-1]),
        cotangent,
    )
    whole = functools.partial(main, fsdp_size, seq_size, slots)
    if compact >= slots:
        return whole(*operands)
    return lax.cond(
        all_fit, functools.partial(main, fsdp_size, seq_size, compact), whole, *operands
    )


def main(
    fsdp_size,
    seq_size,
    held,
    tokens,
    slot_visible,
    counts,
    slot_token,
    positions,
    e_out,
    e_shards,
    embed_shard,
    p_shards,
    vectors,
    cotangent,
):
    shard = lax.axis_index("seq")
    clips, slots, width = tokens.shape
    span = slot_visible.shape[1]
    rows = clips * slots
    small_width = cotangent.shape[2]
    head_size = width // HEADS
    small_head = small_width // PHEADS
    whole = held == slots
    e_vec = dict(zip(ORDER, vectors[:9]))
    embed_bias, mask_token = vectors[9:11]
    p_vec = dict(zip(ORDER, vectors[11:]))

    e_joint_shard, e_expand_shard, e_contract_shard = e_shards
    p_joint_shard, p_out_shard, p_expand_shard, p_contract_shard = p_shards
    e_joint = gather(e_joint_shard)

    own_visible = lax.dynamic_slice_in_dim(slot_visible, shard * slots, slots, 1)
    own_flat = own_visible.reshape(rows, 1)
    own_tokens = lax.dynamic_slice_in_dim(slot_token, shard * slots, slots, 1)
    slot_code = jnp.take(positions, own_tokens.reshape(rows), axis=0)

    if whole:
        kept = slot_visible.reshape(clips, 1, span)

        def keep(array):
            return array

        def put_back(array):
            return array

    else:
        kept = lax.broadcasted_iota(jnp.int32, (1, 1, held), 2) < counts[:, :, None]
        kept = kept.reshape(clips, 1, seq_size * held)
        ones = own_visible.astype(bf16)
        before = lax.broadcasted_iota(jnp.int32, (slots, slots), 0)
        after = lax.broadcasted_iota(jnp.int32, (slots, slots), 1)
        rank = mm(ones, (before < after).astype(bf16)).astype(jnp.int32)
        target = lax.broadcasted_iota(jnp.int32, (1, held, 1), 1)
        picks = ((rank[:, None, :] == target) & own_visible[:, None, :]).astype(bf16)

        def keep(array):
            precision = lax.Precision.HIGHEST if array.dtype == f32 else None
            picked = jnp.einsum(
                "crs,csw->crw",
                picks.astype(array.dtype),
                array.reshape(clips, slots, -1),
                precision=precision,
                preferred_element_type=f32,
            )
            return picked.astype(array.dtype).reshape(clips * held, -1)

        def put_back(array):
            placed = jnp.einsum(
                "crs,crw->csw",
                picks.astype(f32),
                array.reshape(clips, held, -1),
                precision=lax.Precision.HIGHEST,
                preferred_element_type=f32,
            )
            return placed.reshape(rows, -1)

    bias = jnp.where(kept, 0.0, -1e30).astype(f32)
    tiled = held % 16 == 0

    def by_clip(array):
        if tiled:
            return array
        shards, count, length, lanes = array.shape
        return array.transpose(1, 0, 2, 3).reshape(1, count, shards * length, lanes)

    inputs = tokens.reshape(rows, width)
    normed = norm_layer(inputs, e_vec["pre_gain"], e_vec["pre_shift"])
    normed_kept = keep(normed).reshape(1, clips, held, width)
    normed_kept, e_expand_shard = lax.optimization_barrier((normed_kept, e_expand_shard))
    e_expand = gather(e_expand_shard)
    normed_all = exchange(jnp.broadcast_to(normed_kept, (seq_size, clips, held, width)))
    embed, p_joint, p_out = gather(embed_shard), gather(p_joint_shard), gather(p_out_shard)
    e_by_sender = by_sender(e_joint, seq_size)
    normed_all, embed, p_joint, p_out, e_by_sender = lax.optimization_barrier(
        (normed_all, embed, p_joint, p_out, e_by_sender)
    )
    queries = (mm(normed, e_joint[:, :width]) + e_vec["query_bias"]).astype(bf16)
    joined = mm(normed_all.reshape(-1, width), e_joint[:, width:])
    joined_bias = jnp.concatenate([jnp.zeros_like(e_vec["value_bias"]), e_vec["value_bias"]])
    joined = (joined + joined_bias).astype(bf16)
    joined, e_contract_shard = lax.optimization_barrier((joined, e_contract_shard))
    e_contract = gather(e_contract_shard)
    mixed = attend(
        queries.reshape(clips, slots, width),
        by_clip(joined.reshape(seq_size, clips, held, 2 * width)),
        head_size,
        bias,
    ).reshape(rows, width)
    middle = inputs + mm(mixed, e_out) + e_vec["out_bias"]
    normed_mid = norm_layer(middle, e_vec["mid_gain"], e_vec["mid_shift"])
    active = gelu(mm(normed_mid, e_expand) + e_vec["expand_bias"])
    encoded = middle + mm(active, e_contract) + e_vec["contract_bias"]
    context = encoded.astype(bf16)

    embedded = mm(context, embed) + embed_bias
    pred_input = jnp.where(own_flat, embedded, mask_token) + slot_code
    p_normed = norm_layer(pred_input, p_vec["pre_gain"], p_vec["pre_shift"])
    p_queries = (mm(p_normed, p_joint[:, :small_width]) + p_vec["query_bias"]).astype(bf16)
    own_weight, own_bias = own_joint(
        e_joint, e_vec["query_bias"], e_vec["value_bias"], seq_size, shard
    )
    own_qkv = [by_clip(member) for member in own_parts(normed_all, own_weight, own_bias)]
    p_queries, *own_qkv = lax.optimization_barrier((p_queries, *own_qkv))
    p_bias = jnp.concatenate([jnp.zeros_like(p_vec["value_bias"]), p_vec["value_bias"]])
    p_normed_all = []
    p_mixed = []
    everyone = [
        lax.all_gather(p_normed.reshape(clips, slots, small_width)[clip], "seq", axis=0, tiled=True)
        for clip in range(clips)
    ]
    p_expand_shard, p_contract_shard, everyone[0] = lax.optimization_barrier(
        (p_expand_shard, p_contract_shard, everyone[0])
    )
    p_expand, p_contract = gather(p_expand_shard), gather(p_contract_shard)
    for clip in range(clips):
        every = everyone[clip]
        p_joined = (mm(every, p_joint[:, small_width:]) + p_bias).astype(bf16)
        p_normed_all.append(every)
        p_mixed.append(
            attend(
                p_queries.reshape(clips, slots, small_width)[clip : clip + 1],
                p_joined.reshape(1, 1, span, 2 * small_width),
                small_head,
                None,
            )
        )
    kept_mid, kept_mixed, kept_middle, kept_inputs = (
        keep(member) for member in (normed_mid, mixed, middle, inputs)
    )
    p_mixed[0], kept_mid, kept_mixed, kept_middle, kept_inputs = lax.optimization_barrier(
        (p_mixed[0], kept_mid, kept_mixed, kept_middle, kept_inputs)
    )
    p_mixed = jnp.concatenate(p_mixed, axis=0).reshape(rows, small_width)
    p_middle = pred_input + mm(p_mixed, p_out) + p_vec["out_bias"]
    p_normed_mid = norm_layer(p_middle, p_vec["mid_gain"], p_vec["mid_shift"])
    p_hidden = mm(p_normed_mid, p_expand) + p_vec["expand_bias"]
    p_active = gelu(p_hidden)
    predicted = p_middle + mm(p_active, p_contract) + p_vec["contract_bias"]

    grad_middle, grad_att, grad_mixed, p_grads, p_small = feed_back(
        cotangent.reshape(rows, small_width),
        p_middle,
        p_normed_mid,
        p_hidden,
        p_active,
        (p_out, p_expand, p_contract),
        p_vec["mid_gain"],
    )
    p_grad_out = mm(p_mixed, grad_att, TN).astype(bf16)
    p_wide = jnp.concatenate([p_grad_out, p_grads[0]], axis=1)
    p_tall = p_grads[1]
    grad_mixed, p_wide, p_tall = lax.optimization_barrier((grad_mixed, p_wide, p_tall))
    p_wide, p_tall = scatter(p_wide), scatter(p_tall)
    own_weight, own_bias = own_joint(
        p_joint, p_vec["query_bias"], p_vec["value_bias"], seq_size, shard
    )
    own_width = small_width // seq_size
    grad_mixed = grad_mixed.reshape(rows, seq_size, own_width).transpose(1, 0, 2)
    grad_mixed = exchange(grad_mixed.reshape(seq_size, clips, slots, own_width))
    p_by_sender = by_sender(p_joint, seq_size)
    grad_normed = []
    p_grad_joint = 0.0
    p_columns = 0.0
    for clip in range(clips):
        every = p_normed_all[clip].reshape(1, 1, span, small_width)
        grads = attend_back(
            *own_parts(every, own_weight, own_bias),
            grad_mixed[:, clip].reshape(1, 1, span, own_width),
            0,
            small_head,
            None,
            seq_size,
        )
        flat = grads.reshape(span, 3 * own_width)
        p_grad_joint = p_grad_joint + mm(p_normed_all[clip], flat, TN)
        p_columns = p_columns + jnp.sum(flat.astype(f32), axis=0)
        grad_normed.append(joint_back(exchange(grads), p_by_sender))
    p_small.update(joint_small(p_columns, fsdp_size, seq_size, shard))
    p_own_width = own_width
    grad_norm, p_small["pre_gain"], p_small["pre_shift"] = norm_back(
        pred_input, p_vec["pre_gain"], jnp.concatenate(grad_normed, axis=0)
    )
    grad_pred_input = grad_middle + grad_norm
    grad_mask_token = jnp.sum(jnp.where(own_flat, 0.0, grad_pred_input), axis=0)
    grad_embedded = jnp.where(own_flat, grad_pred_input, 0.0).astype(bf16)
    grad_embed_bias = jnp.sum(grad_embedded.astype(f32), axis=0)

    grad_embedded, p_wide, p_tall = lax.optimization_barrier((grad_embedded, p_wide, p_tall))
    grad_context = mm(keep(grad_embedded), embed, NT)
    kept_hidden = mm(kept_mid, e_expand) + e_vec["expand_bias"]
    grad_middle, grad_att, grad_mixed, e_grads, e_small = feed_back(
        grad_context,
        kept_middle,
        kept_mid,
        kept_hidden,
        gelu(kept_hidden),
        (e_out, e_expand, e_contract),
        e_vec["mid_gain"],
    )
    expand_part, contract_part = scatter(e_grads[0]), scatter(e_grads[1])
    own_width = width // seq_size
    grad_mixed = grad_mixed.reshape(clips * held, seq_size, own_width).transpose(1, 0, 2)
    grad_mixed = by_clip(exchange(grad_mixed.reshape(seq_size, clips, held, own_width)))
    grads = [
        attend_back(*own_qkv, grad_mixed, clip, head_size, bias, seq_size) for clip in range(clips)
    ]
    grads[-1], grad_att, late_embedded = lax.optimization_barrier(
        (grads[-1], grad_att, grad_embedded)
    )
    received = [exchange(member) for member in grads]
    received[0], contract_part = lax.optimization_barrier((received[0], contract_part))
    flat = jnp.concatenate(grads, axis=1).reshape(-1, 3 * own_width)
    e_grad_joint = mm(normed_all.reshape(-1, width), flat, TN).astype(bf16)
    e_grad_out = mm(kept_mixed, grad_att, TN).astype(bf16)
    grad_embed = mm(context, late_embedded, TN).astype(bf16)
    e_small.update(joint_small(jnp.sum(flat.astype(f32), axis=0), fsdp_size, seq_size, shard))
    grad_normed = jnp.concatenate([joint_back(member, e_by_sender) for member in received], axis=0)
    grad_norm, e_small["pre_gain"], e_small["pre_shift"] = norm_back(
        kept_inputs, e_vec["pre_gain"], grad_normed
    )

    own_rows = width // fsdp_size
    p_rows = small_width // fsdp_size
    p_lanes = -(-3 * p_own_width // 128) * 128
    p_grad_joint = p_grad_joint.astype(bf16).reshape(fsdp_size, p_rows, 3 * p_own_width)
    p_grad_joint = jnp.pad(
        p_grad_joint, ((0, 0), (0, own_rows - p_rows), (0, p_lanes - 3 * p_own_width))
    ).reshape(width, p_lanes)
    small = [e_small[name] for name in ORDER] + [grad_embed_bias, grad_mask_token]
    small += [p_small[name] for name in ORDER]
    small = [member.reshape(fsdp_size, -1) for member in small]
    sizes = [member.shape[1] for member in small]
    small.append(jnp.zeros((fsdp_size, own_rows * 128 - sum(sizes)), f32))
    small = jnp.concatenate(small, axis=1).astype(bf16).reshape(width, 128)
    late = scatter(jnp.concatenate([e_grad_joint, p_grad_joint, e_grad_out, grad_embed, small], axis=1))
    grad_tokens = put_back(grad_middle + grad_norm)

    first = 0 if whole else 2
    contract_sum, expand_sum, p_wide_sum, p_contract_sum = sum_slots(
        (contract_part, expand_part, p_wide, p_tall), seq_size, first
    )
    late, expand_sum = lax.optimization_barrier((late, expand_sum))
    shared = 3 * own_width + p_lanes
    late_sum, columns = sum_slots((late[:, shared:],), seq_size, first + 1, late[:, :shared])
    e_joint_sum = columns[:, :, : 3 * own_width].reshape(seq_size, own_rows, 3, own_width)
    e_joint_sum = e_joint_sum.transpose(1, 2, 0, 3).reshape(own_rows, 3 * width)
    p_joint_sum = columns[:, :p_rows, 3 * own_width : 3 * (own_width + p_own_width)]
    p_joint_sum = p_joint_sum.reshape(seq_size, p_rows, 3, p_own_width)
    p_joint_sum = p_joint_sum.transpose(1, 2, 0, 3).reshape(p_rows, 3 * small_width)
    out_sum = late_sum[:, :width]
    embed_sum = late_sum[:, width : width + small_width]
    vector_sum = late_sum[:, width + small_width :].reshape(-1)
    small_out = []
    at = 0
    for size in sizes:
        small_out.append(vector_sum[at : at + size].astype(f32))
        at += size
    p_out_sum, p_expand_sum = p_wide_sum[:, :small_width], p_wide_sum[:, small_width:]

    def ordered(vec, joint, out, expand, contract):
        vec = dict(
            zip(ORDER, vec),
            joint=joint.astype(f32),
            out=out.astype(f32),
            expand=expand.astype(f32),
            contract=contract.astype(f32),
        )
        return tuple(vec[name] for name in BLOCK)

    return (
        encoded.reshape(tokens.shape),
        predicted.reshape(cotangent.shape),
        grad_tokens.reshape(tokens.shape),
        *ordered(small_out[:9], e_joint_sum, out_sum, expand_sum, contract_sum),
        embed_sum.astype(f32),
        small_out[9],
        small_out[10],
        *ordered(small_out[11:], p_joint_sum, p_out_sum, p_expand_sum, p_contract_sum),
    )


def solution(mesh):
    cut, rows, vec, full = P("fsdp", "seq", None), P("fsdp", None), P("fsdp"), P()
    block = (vec, vec, rows, vec, vec, rows, vec, vec, vec, rows, vec, rows, vec)
    return jax.shard_map(
        functools.partial(body, mesh.shape["fsdp"], mesh.shape["seq"]),
        mesh=mesh,
        in_specs=(cut, rows, rows, full, *block, rows, vec, vec, *block, cut),
        out_specs=(cut, cut, cut, *block, rows, vec, vec, *block),
        check_vma=False,
    )
```

```python
import functools
import math

import jax
import jax.numpy as jnp
from jax import lax
from jax.experimental import pallas as pl
from jax.experimental.pallas import tpu as pltpu
from jax.sharding import PartitionSpec as P

HEADS = 16
PHEADS = 12

f32 = jnp.float32
bf16 = jnp.bfloat16
norm_eps = 1e-06
LOG2E = math.log2(math.e)
NN = (((1,), (0,)), ((), ()))
NT = (((1,), (1,)), ((), ()))
TN = (((0,), (0,)), ((), ()))
VMEM_LIMIT = 60 * 2**20


def mm(left, right, dims=NN):
    return lax.dot_general(left, right, dims, preferred_element_type=f32)


def norm_parts(value):
    center = value - jnp.mean(value, axis=-1, keepdims=True)
    spread = jnp.mean(center * center, axis=-1, keepdims=True)
    scale = lax.rsqrt(spread + norm_eps)
    return center * scale, scale


def norm_layer(value, gain, shift):
    unit, _ = norm_parts(value)
    return (unit * gain + shift).astype(bf16)


def norm_back(value, gain, grad):
    unit, scale = norm_parts(value)
    grad_gain = jnp.sum(grad * unit, axis=0)
    grad_shift = jnp.sum(grad, axis=0)
    inner = grad * gain
    inner = inner - jnp.mean(inner, axis=-1, keepdims=True) - unit * jnp.mean(
        inner * unit, axis=-1, keepdims=True
    )
    return scale * inner, grad_gain, grad_shift


def gelu_parts(hidden):
    cdf = 0.5 * (1.0 + lax.erf(hidden * math.sqrt(0.5)))
    return cdf


def gelu(hidden):
    return (hidden * gelu_parts(hidden)).astype(bf16)


def gelu_slope(hidden):
    pdf = jnp.exp(-0.5 * hidden * hidden) * (1.0 / math.sqrt(2.0 * math.pi))
    return gelu_parts(hidden) + hidden * pdf


def forward_kernel(scale, head_size, q_ref, k_ref, v_ref, *rest):
    if len(rest) == 2:
        bias_ref, o_ref = rest
    else:
        bias_ref, o_ref = None, rest[0]
    query = q_ref[0]
    lanes = query.shape[1]
    key = k_ref[...].reshape(-1, lanes)
    value = v_ref[...].reshape(-1, lanes)
    lane = lax.broadcasted_iota(jnp.int32, query.shape, 1)
    result = None
    for head in range(lanes // head_size):
        mine = (lane // head_size) == head
        own_query = jnp.where(mine, query, jnp.zeros_like(query))
        scores = mm(own_query, key, NT) * (scale * LOG2E)
        if bias_ref is not None:
            scores = scores + bias_ref[0]
        top = jnp.max(scores, axis=1, keepdims=True)
        weight = jnp.exp2(scores - top)
        total = jnp.sum(weight, axis=1, keepdims=True)
        part = jnp.where(mine, mm(weight.astype(bf16), value) / total, 0.0)
        result = part if result is None else result + part
    o_ref[0] = result.astype(bf16)


def attend(queries, joined, head_size, bias):
    clips, rows, width = queries.shape
    major, _, length, _ = joined.shape
    keys = major * length
    groups = width // 128
    in_specs = [
        pl.BlockSpec((1, rows, 128), lambda c, g: (c, 0, g)),
        pl.BlockSpec((major, 1, length, 128), lambda c, g: (0, c, 0, g)),
        pl.BlockSpec((major, 1, length, 128), lambda c, g: (0, c, 0, g + groups)),
    ]
    operands = [queries, joined, joined]
    if bias is not None:
        in_specs.append(pl.BlockSpec((1, 1, keys), lambda c, g: (c, 0, 0)))
        operands.append(bias)
    cells = clips * rows * keys * (width // head_size)
    return pl.pallas_call(
        functools.partial(forward_kernel, 1.0 / math.sqrt(head_size), head_size),
        grid=(clips, groups),
        in_specs=in_specs,
        out_specs=pl.BlockSpec((1, rows, 128), lambda c, g: (c, 0, g)),
        out_shape=jax.ShapeDtypeStruct((clips, rows, width), bf16),
        compiler_params=pltpu.CompilerParams(vmem_limit_bytes=VMEM_LIMIT),
        cost_estimate=pl.CostEstimate(
            flops=cells * 1024, bytes_accessed=4 * clips * keys * width, transcendentals=cells
        ),
        name="attend",
    )(*operands)


def backward_kernel(scale, head_size, shards, q_ref, k_ref, v_ref, g_ref, *rest):
    if len(rest) == 4:
        bias_ref = rest[0]
        rest = rest[1:]
    else:
        bias_ref = None
    out_ref, dk_sum, dv_sum = rest
    group = pl.program_id(0)
    part = pl.program_id(1)
    lanes = q_ref.shape[-1]
    query = q_ref[...].reshape(-1, lanes)
    key = k_ref[...].reshape(-1, lanes)
    value = v_ref[...].reshape(-1, lanes)
    grad = g_ref[...].reshape(-1, lanes)
    lane = lax.broadcasted_iota(jnp.int32, query.shape, 1)
    key_lane = lax.broadcasted_iota(jnp.int32, key.shape, 1)
    sums = None
    for head in range(lanes // head_size):
        mine = (lane // head_size) == head
        own_query = jnp.where(mine, query, jnp.zeros_like(query))
        own_grad = jnp.where(mine, grad, jnp.zeros_like(grad))
        own_key = jnp.where((key_lane // head_size) == head, key, jnp.zeros_like(key))
        scores = mm(own_query, key, NT) * (scale * LOG2E)
        if bias_ref is not None:
            scores = scores + bias_ref[0]
        top = jnp.max(scores, axis=1, keepdims=True)
        weight = jnp.exp2(scores - top)
        chance = weight * (1.0 / jnp.sum(weight, axis=1, keepdims=True))
        grad_chance = mm(own_grad, value, NT)
        delta = jnp.sum(chance * grad_chance, axis=1, keepdims=True)
        grad_scores = (chance * (grad_chance - delta)).astype(bf16)
        terms = (
            mm(grad_scores, own_key),
            mm(own_query, grad_scores, TN),
            mm(own_grad, chance.astype(bf16), TN),
        )
        sums = terms if sums is None else tuple(x + y for x, y in zip(sums, terms))
    part_q, part_k, part_v = sums

    @pl.when(part == 0)
    def _():
        dk_sum[...] = part_k
        dv_sum[...] = part_v

    @pl.when(part > 0)
    def _():
        dk_sum[...] += part_k
        dv_sum[...] += part_v

    rows = out_ref.shape[2]
    width = out_ref.shape[3] // 3
    held = query.shape[0] // rows

    def place(kind):
        if width == lanes:
            return slice(kind * width, (kind + 1) * width)
        return pl.ds(pl.multiple_of(kind * width + group * lanes, 128), lanes)

    result_q = (part_q * scale).astype(bf16)
    for index in range(held):
        out_ref[part * held + index, 0, :, place(0)] = result_q[index * rows : (index + 1) * rows]

    @pl.when(part == pl.num_programs(1) - 1)
    def _():
        for kind, total_ref, factor in ((1, dk_sum, scale), (2, dv_sum, 1.0)):
            result = (total_ref[...] * factor).T.astype(bf16)
            for index in range(shards):
                out_ref[index, 0, :, place(kind)] = result[index * rows : (index + 1) * rows]


def attend_back(queries, keys, values, grad_mixed, clip, head_size, bias, shards):
    major, _, length, width = queries.shape
    lanes = min(width, 128)
    groups = width // lanes
    rows = major * length // shards
    parts = shards if major == 1 else 1
    query_rows = rows if major == 1 else length
    by_query = pl.BlockSpec((major, 1, query_rows, lanes), lambda g, r: (0, clip, r, g))
    by_key = pl.BlockSpec((major, 1, length, lanes), lambda g, r: (0, clip, 0, g))
    in_specs = [by_query, by_key, by_key, by_query]
    operands = [queries, keys, values, grad_mixed]
    total = major * length
    if bias is not None:
        in_specs.append(pl.BlockSpec((1, 1, total), lambda g, r: (clip, 0, 0)))
        operands.append(bias)
    cells = total * total * (width // head_size)
    return pl.pallas_call(
        functools.partial(backward_kernel, 1.0 / math.sqrt(head_size), head_size, shards),
        grid=(groups, parts),
        in_specs=in_specs,
        out_specs=pl.BlockSpec((shards, 1, rows, 3 * width), lambda g, r: (0, 0, 0, 0)),
        out_shape=jax.ShapeDtypeStruct((shards, 1, rows, 3 * width), bf16),
        scratch_shapes=[pltpu.VMEM((lanes, total), f32), pltpu.VMEM((lanes, total), f32)],
        compiler_params=pltpu.CompilerParams(vmem_limit_bytes=VMEM_LIMIT),
        cost_estimate=pl.CostEstimate(
            flops=cells * 2560, bytes_accessed=14 * total * width, transcendentals=cells
        ),
        name="attend_back",
    )(*operands)


def exchange(array):
    return lax.all_to_all(array, "seq", split_axis=0, concat_axis=0, tiled=True)


def gather(array):
    return lax.all_gather(array, "fsdp", axis=0, tiled=True)


def scatter(array):
    return lax.psum_scatter(array, "fsdp", scatter_dimension=0, tiled=True)


def pack_rows(vectors):
    rows = []
    for member in vectors:
        count = -(-member.shape[0] // 128)
        padded = jnp.pad(member.astype(f32), (0, count * 128 - member.shape[0]))
        rows.append(padded.reshape(count, 128))
    total = sum(member.shape[0] for member in rows)
    if total % 8:
        rows.append(jnp.zeros((8 - total % 8, 128), f32))
    return jnp.concatenate(rows, axis=0)


def unpack_rows(packed, sizes):
    out = []
    at = 0
    for size in sizes:
        count = -(-size // 128)
        piece = packed[:, at : at + count].reshape(packed.shape[0], count * 128)[:, :size]
        out.append(piece.reshape(-1))
        at += count
    return out


MESH = pl.DeviceIdType.MESH


def line_kernel(size, cuts, shares, *refs):
    count = len(cuts)
    held = count + shares
    ins, outs = refs[:count], refs[held : held + count]
    own, every = refs[count], refs[held + count]
    scratch = refs[2 * held :]
    inner, outer, partial = (scratch[i * count : (i + 1) * count] for i in range(3))
    to_inner, to_outer, from_inner, from_outer = scratch[3 * count : 3 * count + 4]
    me = lax.axis_index("seq")
    left = me < size // 2
    toward = jnp.where(left, me + 1, me - 1)
    away = jnp.where(left, me - 1, me + 1)
    end = (me == 0) | (me == size - 1)
    barrier = pltpu.get_barrier_semaphore()
    pl.semaphore_signal(barrier, inc=1, device_id={"seq": toward}, device_id_type=MESH)

    @pl.when(jnp.logical_not(end))
    def _():
        pl.semaphore_signal(barrier, inc=1, device_id={"seq": away}, device_id_type=MESH)
        pl.semaphore_wait(barrier, 2)

    @pl.when(end)
    def _():
        pl.semaphore_wait(barrier, 1)

    pieces = []
    for index, parts in enumerate(cuts):
        rows = ins[index].shape[0] // parts
        for part in range(parts):
            pieces.append((part / parts, index, slice(part * rows, (part + 1) * rows)))
    pieces.sort(key=lambda piece: piece[:2])
    pieces = [(slot, index, cut) for slot, (_, index, cut) in enumerate(pieces)]

    def inwards(slot, index, cut):
        return pltpu.make_async_remote_copy(
            src_ref=ins[index].at[cut],
            dst_ref=outer[index].at[cut],
            send_sem=to_inner.at[slot],
            recv_sem=from_outer.at[slot],
            device_id={"seq": toward},
            device_id_type=MESH,
        )

    def swap(slot, index, cut):
        return pltpu.make_async_remote_copy(
            src_ref=partial[index].at[cut],
            dst_ref=inner[index].at[cut],
            send_sem=to_inner.at[slot],
            recv_sem=from_inner.at[slot],
            device_id={"seq": toward},
            device_id_type=MESH,
        )

    def outwards(slot, index, cut):
        return pltpu.make_async_remote_copy(
            src_ref=outs[index].at[cut],
            dst_ref=outs[index].at[cut],
            send_sem=to_outer.at[slot],
            recv_sem=from_inner.at[slot],
            device_id={"seq": away},
            device_id_type=MESH,
        )

    @pl.when(end)
    def _():
        for piece in pieces:
            inwards(*piece).start()

    if shares:
        sent, arrived = scratch[3 * count + 4 :]
        every[me] = own[...]

        def passes(way, hop):
            step = 1 - 2 * way
            block = me - step * hop
            return pltpu.make_async_remote_copy(
                src_ref=own if hop == 0 else every.at[block],
                dst_ref=every.at[block],
                send_sem=sent.at[way, hop],
                recv_sem=arrived.at[way, hop],
                device_id={"seq": me + step},
                device_id_type=MESH,
            )

        def sends(way, hop):
            if way == 0:
                return (me < size - 1) & (me - hop >= 0)
            return (me > 0) & (me + hop <= size - 1)

        def receives(way, hop):
            return me - 1 - hop >= 0 if way == 0 else me + 1 + hop <= size - 1

        def landing(way, hop):
            block = me - 1 - hop if way == 0 else me + 1 + hop
            return pltpu.make_async_remote_copy(
                src_ref=every.at[block],
                dst_ref=every.at[block],
                send_sem=sent.at[way, hop],
                recv_sem=arrived.at[way, hop],
                device_id={"seq": toward},
                device_id_type=MESH,
            )

        def forward(hop):
            for way in (0, 1):
                if hop > 0:

                    @pl.when(receives(way, hop - 1))
                    def _(way=way):
                        landing(way, hop - 1).wait_recv()

                if hop < size - 1:

                    @pl.when(sends(way, hop))
                    def _(way=way):
                        passes(way, hop).start()

        forward(0)

    @pl.when(end)
    def _():
        for piece in pieces:
            outwards(*piece).wait_recv()
        for piece in pieces:
            inwards(*piece).wait_send()

    @pl.when(jnp.logical_not(end))
    def _():
        lag = min(count, len(pieces))
        steps = len(pieces) + lag
        for step in range(steps):
            if shares and step in (steps // 3, 2 * steps // 3):
                forward(1 if step == steps // 3 else 2)
            if step < len(pieces):
                piece = pieces[step]
                inwards(*piece).wait_recv()
                _, index, cut = piece
                both = ins[index][cut].astype(f32) + outer[index][cut].astype(f32)
                partial[index][cut] = both.astype(bf16)
                swap(*piece).start()
            if step >= lag:
                piece = pieces[step - lag]
                swap(*piece).wait_recv()
                _, index, cut = piece
                both = partial[index][cut].astype(f32) + inner[index][cut].astype(f32)
                outs[index][cut] = both.astype(bf16)
                outwards(*piece).start()
        for piece in pieces:
            swap(*piece).wait_send()
            outwards(*piece).wait_send()

    if shares:

        @pl.when(end)
        def _():
            for hop in range(1, size):
                forward(hop)

        @pl.when(jnp.logical_not(end))
        def _():
            for hop in range(3, size):
                forward(hop)

        for way in (0, 1):
            for hop in range(size - 1):

                @pl.when(sends(way, hop))
                def _(way=way, hop=hop):
                    passes(way, hop).wait_send()


def line_sum(arrays, size, identity, share=None):
    cuts = []
    for member in arrays:
        parts = 8
        while parts > 1 and member.shape[0] % (16 * parts):
            parts //= 2
        cuts.append(parts)
    hold = [pltpu.VMEM(member.shape, bf16) for member in arrays]
    shapes = [jax.ShapeDtypeStruct(member.shape, bf16) for member in arrays]
    semaphores = [pltpu.SemaphoreType.DMA((sum(cuts),))] * 4
    operands = list(arrays)
    if share is not None:
        operands.append(share)
        shapes.append(jax.ShapeDtypeStruct((size,) + share.shape, bf16))
        semaphores += [pltpu.SemaphoreType.DMA((2, size - 1))] * 2
    whole = pl.BlockSpec(memory_space=pltpu.VMEM)
    return pl.pallas_call(
        functools.partial(line_kernel, size, tuple(cuts), int(share is not None)),
        out_shape=shapes,
        in_specs=[whole] * len(operands),
        out_specs=[whole] * len(operands),
        scratch_shapes=hold * 3 + semaphores,
        compiler_params=pltpu.CompilerParams(
            collective_id=identity, has_side_effects=True, vmem_limit_bytes=VMEM_LIMIT
        ),
        cost_estimate=pl.CostEstimate(
            flops=0,
            bytes_accessed=40 * sum(2 * member.size for member in operands),
            transcendentals=0,
        ),
        name="line_sum",
    )(*operands)


def sum_slots(arrays, size, identity, share=None):
    if size == 4:
        return line_sum(arrays, size, identity, share)
    sums = lax.psum(tuple(arrays), "seq")
    if share is None:
        return sums
    return (*sums, lax.all_gather(share, "seq", axis=0, tiled=False))


def feed_back(grad_out, middle, normed_mid, hidden, active, weights, mid_gain):
    out, expand, contract = weights
    grad_y = grad_out.astype(bf16)
    grad_contract = mm(active, grad_y, TN).astype(bf16)
    grad_contract_bias = jnp.sum(grad_y.astype(f32), axis=0)
    grad_y, grad_contract = lax.optimization_barrier((grad_y, grad_contract))
    grad_hidden = (mm(grad_y, contract, NT) * gelu_slope(hidden)).astype(bf16)
    grad_expand = mm(normed_mid, grad_hidden, TN).astype(bf16)
    grad_expand_bias = jnp.sum(grad_hidden.astype(f32), axis=0)
    grad_normed = mm(grad_hidden, expand, NT)
    grad_normed, grad_expand = lax.optimization_barrier((grad_normed, grad_expand))
    grad_norm, grad_mid_gain, grad_mid_shift = norm_back(middle, mid_gain, grad_normed)
    grad_middle = grad_out + grad_norm
    grad_att = grad_middle.astype(bf16)
    grad_out_bias = jnp.sum(grad_att.astype(f32), axis=0)
    grad_mixed = mm(grad_att, out, NT).astype(bf16)
    small = dict(
        out_bias=grad_out_bias,
        mid_gain=grad_mid_gain,
        mid_shift=grad_mid_shift,
        expand_bias=grad_expand_bias,
        contract_bias=grad_contract_bias,
    )
    return grad_middle, grad_att, grad_mixed, (grad_expand, grad_contract), small


def own_joint(joint_weight, query_bias, value_bias, shards, shard):
    width = joint_weight.shape[0]
    own = width // shards
    weight = lax.dynamic_slice_in_dim(joint_weight.reshape(width, 3, width), shard * own, own, 2)
    bias_q = lax.dynamic_slice_in_dim(query_bias, shard * own, own, 0)
    bias_v = lax.dynamic_slice_in_dim(value_bias, shard * own, own, 0)
    return weight, (bias_q, None, bias_v)


def own_parts(normed_all, weight, biases):
    flat = normed_all.reshape(-1, normed_all.shape[3])
    out = []
    for index in range(3):
        part = mm(flat, weight[:, index])
        if biases[index] is not None:
            part = part + biases[index]
        out.append(part.astype(bf16).reshape(normed_all.shape[:3] + (weight.shape[2],)))
    return out


def by_sender(joint_weight, shards):
    width = joint_weight.shape[0]
    array = joint_weight.reshape(width, 3, shards, width // shards)
    return array.transpose(0, 2, 1, 3).reshape(width, 3 * width)


def joint_back(received, joint_by_sender):
    shards, clips, rows, width = received.shape
    flat = received.reshape(shards, clips * rows, width).transpose(1, 0, 2)
    return mm(flat.reshape(clips * rows, shards * width), joint_by_sender, NT)


def joint_small(columns, owners, shards, shard):
    own = columns.shape[0] // 3
    each = owners // shards
    mine = lax.broadcasted_iota(jnp.int32, (owners, 1), 0) // each == shard

    def full(vector):
        return jnp.where(mine, jnp.tile(vector.reshape(each, -1), (shards, 1)), 0.0)

    return dict(query_bias=full(columns[:own]), value_bias=full(columns[2 * own :]))


ORDER = (
    "pre_gain",
    "pre_shift",
    "query_bias",
    "value_bias",
    "out_bias",
    "mid_gain",
    "mid_shift",
    "expand_bias",
    "contract_bias",
)
BLOCK = (
    "pre_gain",
    "pre_shift",
    "joint",
    "query_bias",
    "value_bias",
    "out",
    "out_bias",
    "mid_gain",
    "mid_shift",
    "expand",
    "expand_bias",
    "contract",
    "contract_bias",
)
FRAMES = 8
GRID = 14
MOST_VISIBLE = FRAMES * max(
    high * wide
    for high in range(1, GRID + 1)
    for wide in range(1, GRID + 1)
    if 2 * high * wide < GRID * GRID
)


def body(fsdp_size, seq_size, tokens, visible, slot_token, positions, *rest):
    e_shard = dict(zip(BLOCK, rest[:13]))
    embed_weight, embed_bias, mask_token = rest[13:16]
    p_shard = dict(zip(BLOCK, rest[16:29]))
    cotangent = rest[29]
    shard = lax.axis_index("seq")
    clips, slots, width = tokens.shape
    span = visible.shape[1]

    e_out = gather(e_shard["out"])
    place = lax.broadcasted_iota(jnp.int32, (1, 1, span), 2)
    slot_visible = jnp.any(
        (slot_token[:, :, None] == place) & (visible[:, None, :] > 0), axis=2
    )
    counts = jnp.sum(slot_visible.reshape(clips, seq_size, slots).astype(jnp.int32), axis=2)
    compact = -(-MOST_VISIBLE // (16 * seq_size)) * 16
    fits = (jnp.max(counts) <= compact).astype(f32)

    vectors = [e_shard[name] for name in ORDER] + [embed_bias, mask_token]
    vectors += [p_shard[name] for name in ORDER]
    sizes = [member.shape[0] for member in vectors]
    packed = lax.all_gather(
        pack_rows(vectors + [jnp.full((1,), fits)]), "fsdp", axis=0, tiled=False
    )
    full = unpack_rows(packed, sizes + [1])
    all_fit = jnp.min(full[-1]) > 0.5

    operands = (
        tokens,
        slot_visible,
        counts,
        slot_token,
        positions,
        e_out,
        tuple(e_shard[name] for name in ("joint", "expand", "contract")),
        embed_weight,
        tuple(p_shard[name] for name in ("joint", "out", "expand", "contract")),
        tuple(full[:-1]),
        cotangent,
    )
    whole = functools.partial(main, fsdp_size, seq_size, slots)
    if compact >= slots:
        return whole(*operands)
    return lax.cond(
        all_fit, functools.partial(main, fsdp_size, seq_size, compact), whole, *operands
    )


def main(
    fsdp_size,
    seq_size,
    held,
    tokens,
    slot_visible,
    counts,
    slot_token,
    positions,
    e_out,
    e_shards,
    embed_shard,
    p_shards,
    vectors,
    cotangent,
):
    shard = lax.axis_index("seq")
    clips, slots, width = tokens.shape
    span = slot_visible.shape[1]
    rows = clips * slots
    small_width = cotangent.shape[2]
    head_size = width // HEADS
    small_head = small_width // PHEADS
    whole = held == slots
    e_vec = dict(zip(ORDER, vectors[:9]))
    embed_bias, mask_token = vectors[9:11]
    p_vec = dict(zip(ORDER, vectors[11:]))

    e_joint_shard, e_expand_shard, e_contract_shard = e_shards
    p_joint_shard, p_out_shard, p_expand_shard, p_contract_shard = p_shards
    e_joint = gather(e_joint_shard)

    own_visible = lax.dynamic_slice_in_dim(slot_visible, shard * slots, slots, 1)
    own_flat = own_visible.reshape(rows, 1)
    own_tokens = lax.dynamic_slice_in_dim(slot_token, shard * slots, slots, 1)
    slot_code = jnp.take(positions, own_tokens.reshape(rows), axis=0)

    if whole:
        kept = slot_visible.reshape(clips, 1, span)

        def keep(array):
            return array

        def put_back(array):
            return array

    else:
        kept = lax.broadcasted_iota(jnp.int32, (1, 1, held), 2) < counts[:, :, None]
        kept = kept.reshape(clips, 1, seq_size * held)
        ones = own_visible.astype(bf16)
        before = lax.broadcasted_iota(jnp.int32, (slots, slots), 0)
        after = lax.broadcasted_iota(jnp.int32, (slots, slots), 1)
        rank = mm(ones, (before < after).astype(bf16)).astype(jnp.int32)
        target = lax.broadcasted_iota(jnp.int32, (1, held, 1), 1)
        picks = ((rank[:, None, :] == target) & own_visible[:, None, :]).astype(bf16)

        def keep(array):
            precision = lax.Precision.HIGHEST if array.dtype == f32 else None
            picked = jnp.einsum(
                "crs,csw->crw",
                picks.astype(array.dtype),
                array.reshape(clips, slots, -1),
                precision=precision,
                preferred_element_type=f32,
            )
            return picked.astype(array.dtype).reshape(clips * held, -1)

        def put_back(array):
            placed = jnp.einsum(
                "crs,crw->csw",
                picks.astype(f32),
                array.reshape(clips, held, -1),
                precision=lax.Precision.HIGHEST,
                preferred_element_type=f32,
            )
            return placed.reshape(rows, -1)

    bias = jnp.where(kept, 0.0, -1e30).astype(f32)
    tiled = held % 16 == 0

    def by_clip(array):
        if tiled:
            return array
        shards, count, length, lanes = array.shape
        return array.transpose(1, 0, 2, 3).reshape(1, count, shards * length, lanes)

    inputs = tokens.reshape(rows, width)
    normed = norm_layer(inputs, e_vec["pre_gain"], e_vec["pre_shift"])
    normed_kept = keep(normed).reshape(1, clips, held, width)
    normed_kept, e_expand_shard = lax.optimization_barrier((normed_kept, e_expand_shard))
    e_expand = gather(e_expand_shard)
    normed_all = exchange(jnp.broadcast_to(normed_kept, (seq_size, clips, held, width)))
    embed, p_joint, p_out = gather(embed_shard), gather(p_joint_shard), gather(p_out_shard)
    e_by_sender = by_sender(e_joint, seq_size)
    normed_all, embed, p_joint, p_out, e_by_sender = lax.optimization_barrier(
        (normed_all, embed, p_joint, p_out, e_by_sender)
    )
    queries = (mm(normed, e_joint[:, :width]) + e_vec["query_bias"]).astype(bf16)
    joined = mm(normed_all.reshape(-1, width), e_joint[:, width:])
    joined_bias = jnp.concatenate([jnp.zeros_like(e_vec["value_bias"]), e_vec["value_bias"]])
    joined = (joined + joined_bias).astype(bf16)
    joined, e_contract_shard = lax.optimization_barrier((joined, e_contract_shard))
    e_contract = gather(e_contract_shard)
    mixed = attend(
        queries.reshape(clips, slots, width),
        by_clip(joined.reshape(seq_size, clips, held, 2 * width)),
        head_size,
        bias,
    ).reshape(rows, width)
    middle = inputs + mm(mixed, e_out) + e_vec["out_bias"]
    normed_mid = norm_layer(middle, e_vec["mid_gain"], e_vec["mid_shift"])
    active = gelu(mm(normed_mid, e_expand) + e_vec["expand_bias"])
    encoded = middle + mm(active, e_contract) + e_vec["contract_bias"]
    context = encoded.astype(bf16)

    embedded = mm(context, embed) + embed_bias
    pred_input = jnp.where(own_flat, embedded, mask_token) + slot_code
    p_normed = norm_layer(pred_input, p_vec["pre_gain"], p_vec["pre_shift"])
    p_normed, rows_all, mid_rows, mixed_rows, middle_rows = lax.optimization_barrier(
        (p_normed, normed_all, normed_mid, mixed, middle)
    )
    p_queries = (mm(p_normed, p_joint[:, :small_width]) + p_vec["query_bias"]).astype(bf16)
    own_weight, own_bias = own_joint(
        e_joint, e_vec["query_bias"], e_vec["value_bias"], seq_size, shard
    )
    own_qkv = [by_clip(member) for member in own_parts(rows_all, own_weight, own_bias)]
    p_bias = jnp.concatenate([jnp.zeros_like(p_vec["value_bias"]), p_vec["value_bias"]])
    p_normed_all = []
    p_mixed = []
    everyone = [
        lax.all_gather(p_normed.reshape(clips, slots, small_width)[clip], "seq", axis=0, tiled=True)
        for clip in range(clips)
    ]
    p_expand_shard, p_contract_shard, everyone[0] = lax.optimization_barrier(
        (p_expand_shard, p_contract_shard, everyone[0])
    )
    p_expand, p_contract = gather(p_expand_shard), gather(p_contract_shard)
    for clip in range(clips):
        every = everyone[clip]
        p_joined = (mm(every, p_joint[:, small_width:]) + p_bias).astype(bf16)
        p_normed_all.append(every)
        p_mixed.append(
            attend(
                p_queries.reshape(clips, slots, small_width)[clip : clip + 1],
                p_joined.reshape(1, 1, span, 2 * small_width),
                small_head,
                None,
            )
        )
    kept_mid, kept_mixed, kept_middle, kept_inputs = (
        keep(member) for member in (mid_rows, mixed_rows, middle_rows, inputs)
    )
    p_mixed[0], kept_mid, kept_mixed, kept_middle, kept_inputs, *own_qkv = (
        lax.optimization_barrier(
            (p_mixed[0], kept_mid, kept_mixed, kept_middle, kept_inputs, *own_qkv)
        )
    )
    p_mixed = jnp.concatenate(p_mixed, axis=0).reshape(rows, small_width)
    p_middle = pred_input + mm(p_mixed, p_out) + p_vec["out_bias"]
    p_normed_mid = norm_layer(p_middle, p_vec["mid_gain"], p_vec["mid_shift"])
    p_hidden = mm(p_normed_mid, p_expand) + p_vec["expand_bias"]
    p_active = gelu(p_hidden)
    predicted = p_middle + mm(p_active, p_contract) + p_vec["contract_bias"]

    grad_middle, grad_att, grad_mixed, p_grads, p_small = feed_back(
        cotangent.reshape(rows, small_width),
        p_middle,
        p_normed_mid,
        p_hidden,
        p_active,
        (p_out, p_expand, p_contract),
        p_vec["mid_gain"],
    )
    p_grad_out = mm(p_mixed, grad_att, TN).astype(bf16)
    p_wide = jnp.concatenate([p_grad_out, p_grads[0]], axis=1)
    p_tall = p_grads[1]
    grad_mixed, p_wide, p_tall = lax.optimization_barrier((grad_mixed, p_wide, p_tall))
    p_wide, p_tall = scatter(p_wide), scatter(p_tall)
    own_weight, own_bias = own_joint(
        p_joint, p_vec["query_bias"], p_vec["value_bias"], seq_size, shard
    )
    own_width = small_width // seq_size
    grad_mixed = grad_mixed.reshape(rows, seq_size, own_width).transpose(1, 0, 2)
    grad_mixed = exchange(grad_mixed.reshape(seq_size, clips, slots, own_width))
    p_by_sender = by_sender(p_joint, seq_size)
    grad_normed = []
    p_grad_joint = 0.0
    p_columns = 0.0
    for clip in range(clips):
        every = p_normed_all[clip].reshape(1, 1, span, small_width)
        grads = attend_back(
            *own_parts(every, own_weight, own_bias),
            grad_mixed[:, clip].reshape(1, 1, span, own_width),
            0,
            small_head,
            None,
            seq_size,
        )
        if clip == 0:
            grads, p_wide, p_tall = lax.optimization_barrier((grads, p_wide, p_tall))
        flat = grads.reshape(span, 3 * own_width)
        p_grad_joint = p_grad_joint + mm(p_normed_all[clip], flat, TN)
        p_columns = p_columns + jnp.sum(flat.astype(f32), axis=0)
        grad_normed.append(joint_back(exchange(grads), p_by_sender))
    p_small.update(joint_small(p_columns, fsdp_size, seq_size, shard))
    p_own_width = own_width
    grad_norm, p_small["pre_gain"], p_small["pre_shift"] = norm_back(
        pred_input, p_vec["pre_gain"], jnp.concatenate(grad_normed, axis=0)
    )
    grad_pred_input = grad_middle + grad_norm
    grad_mask_token = jnp.sum(jnp.where(own_flat, 0.0, grad_pred_input), axis=0)
    grad_embedded = jnp.where(own_flat, grad_pred_input, 0.0).astype(bf16)
    grad_embed_bias = jnp.sum(grad_embedded.astype(f32), axis=0)

    grad_embedded, predicted = lax.optimization_barrier((grad_embedded, predicted))
    grad_context = mm(keep(grad_embedded), embed, NT)
    kept_hidden = mm(kept_mid, e_expand) + e_vec["expand_bias"]
    grad_middle, grad_att, grad_mixed, e_grads, e_small = feed_back(
        grad_context,
        kept_middle,
        kept_mid,
        kept_hidden,
        gelu(kept_hidden),
        (e_out, e_expand, e_contract),
        e_vec["mid_gain"],
    )
    expand_part, contract_part = scatter(e_grads[0]), scatter(e_grads[1])
    own_width = width // seq_size
    grad_mixed = grad_mixed.reshape(clips * held, seq_size, own_width).transpose(1, 0, 2)
    grad_mixed = by_clip(exchange(grad_mixed.reshape(seq_size, clips, held, own_width)))
    grads = [
        attend_back(*own_qkv, grad_mixed, clip, head_size, bias, seq_size) for clip in range(clips)
    ]
    grads[-1], grad_att, late_embedded = lax.optimization_barrier(
        (grads[-1], grad_att, grad_embedded)
    )
    received = [exchange(member) for member in grads]
    received[0], contract_part = lax.optimization_barrier((received[0], contract_part))
    flat = jnp.concatenate(grads, axis=1).reshape(-1, 3 * own_width)
    e_grad_joint = mm(normed_all.reshape(-1, width), flat, TN).astype(bf16)
    e_grad_out = mm(kept_mixed, grad_att, TN).astype(bf16)
    grad_embed = mm(context, late_embedded, TN).astype(bf16)
    e_small.update(joint_small(jnp.sum(flat.astype(f32), axis=0), fsdp_size, seq_size, shard))
    grad_normed = jnp.concatenate([joint_back(member, e_by_sender) for member in received], axis=0)
    grad_norm, e_small["pre_gain"], e_small["pre_shift"] = norm_back(
        kept_inputs, e_vec["pre_gain"], grad_normed
    )

    own_rows = width // fsdp_size
    p_rows = small_width // fsdp_size
    p_lanes = -(-3 * p_own_width // 128) * 128
    p_grad_joint = p_grad_joint.astype(bf16).reshape(fsdp_size, p_rows, 3 * p_own_width)
    p_grad_joint = jnp.pad(
        p_grad_joint, ((0, 0), (0, own_rows - p_rows), (0, p_lanes - 3 * p_own_width))
    ).reshape(width, p_lanes)
    small = [e_small[name] for name in ORDER] + [grad_embed_bias, grad_mask_token]
    small += [p_small[name] for name in ORDER]
    small = [member.reshape(fsdp_size, -1) for member in small]
    sizes = [member.shape[1] for member in small]
    small.append(jnp.zeros((fsdp_size, own_rows * 128 - sum(sizes)), f32))
    small = jnp.concatenate(small, axis=1).astype(bf16).reshape(width, 128)
    late = scatter(jnp.concatenate([e_grad_joint, p_grad_joint, e_grad_out, grad_embed, small], axis=1))
    grad_tokens = put_back(grad_middle + grad_norm)

    first = 0 if whole else 2
    contract_sum, expand_sum, p_wide_sum, p_contract_sum = sum_slots(
        (contract_part, expand_part, p_wide, p_tall), seq_size, first
    )
    late, expand_sum = lax.optimization_barrier((late, expand_sum))
    shared = 3 * own_width + p_lanes
    late_sum, columns = sum_slots((late[:, shared:],), seq_size, first + 1, late[:, :shared])
    e_joint_sum = columns[:, :, : 3 * own_width].reshape(seq_size, own_rows, 3, own_width)
    e_joint_sum = e_joint_sum.transpose(1, 2, 0, 3).reshape(own_rows, 3 * width)
    p_joint_sum = columns[:, :p_rows, 3 * own_width : 3 * (own_width + p_own_width)]
    p_joint_sum = p_joint_sum.reshape(seq_size, p_rows, 3, p_own_width)
    p_joint_sum = p_joint_sum.transpose(1, 2, 0, 3).reshape(p_rows, 3 * small_width)
    out_sum = late_sum[:, :width]
    embed_sum = late_sum[:, width : width + small_width]
    vector_sum = late_sum[:, width + small_width :].reshape(-1)
    small_out = []
    at = 0
    for size in sizes:
        small_out.append(vector_sum[at : at + size].astype(f32))
        at += size
    p_out_sum, p_expand_sum = p_wide_sum[:, :small_width], p_wide_sum[:, small_width:]

    def ordered(vec, joint, out, expand, contract):
        vec = dict(
            zip(ORDER, vec),
            joint=joint.astype(f32),
            out=out.astype(f32),
            expand=expand.astype(f32),
            contract=contract.astype(f32),
        )
        return tuple(vec[name] for name in BLOCK)

    return (
        encoded.reshape(tokens.shape),
        predicted.reshape(cotangent.shape),
        grad_tokens.reshape(tokens.shape),
        *ordered(small_out[:9], e_joint_sum, out_sum, expand_sum, contract_sum),
        embed_sum.astype(f32),
        small_out[9],
        small_out[10],
        *ordered(small_out[11:], p_joint_sum, p_out_sum, p_expand_sum, p_contract_sum),
    )


def solution(mesh):
    cut, rows, vec, full = P("fsdp", "seq", None), P("fsdp", None), P("fsdp"), P()
    block = (vec, vec, rows, vec, vec, rows, vec, vec, vec, rows, vec, rows, vec)
    return jax.shard_map(
        functools.partial(body, mesh.shape["fsdp"], mesh.shape["seq"]),
        mesh=mesh,
        in_specs=(cut, rows, rows, full, *block, rows, vec, vec, *block, cut),
        out_specs=(cut, cut, cut, *block, rows, vec, vec, *block),
        check_vma=False,
    )
```

```python
import functools
import math

import jax
import jax.numpy as jnp
from jax import lax
from jax.experimental import pallas as pl
from jax.experimental.pallas import tpu as pltpu
from jax.sharding import PartitionSpec as P

HEADS = 16
PHEADS = 12

f32 = jnp.float32
bf16 = jnp.bfloat16
norm_eps = 1e-06
LOG2E = math.log2(math.e)
NN = (((1,), (0,)), ((), ()))
NT = (((1,), (1,)), ((), ()))
TN = (((0,), (0,)), ((), ()))
VMEM_LIMIT = 60 * 2**20


def mm(left, right, dims=NN):
    return lax.dot_general(left, right, dims, preferred_element_type=f32)


def norm_parts(value):
    center = value - jnp.mean(value, axis=-1, keepdims=True)
    spread = jnp.mean(center * center, axis=-1, keepdims=True)
    scale = lax.rsqrt(spread + norm_eps)
    return center * scale, scale


def norm_layer(value, gain, shift):
    unit, _ = norm_parts(value)
    return (unit * gain + shift).astype(bf16)


def norm_back(value, gain, grad):
    unit, scale = norm_parts(value)
    grad_gain = jnp.sum(grad * unit, axis=0)
    grad_shift = jnp.sum(grad, axis=0)
    inner = grad * gain
    inner = inner - jnp.mean(inner, axis=-1, keepdims=True) - unit * jnp.mean(
        inner * unit, axis=-1, keepdims=True
    )
    return scale * inner, grad_gain, grad_shift


def gelu_parts(hidden):
    cdf = 0.5 * (1.0 + lax.erf(hidden * math.sqrt(0.5)))
    return cdf


def gelu(hidden):
    return (hidden * gelu_parts(hidden)).astype(bf16)


def gelu_slope(hidden):
    pdf = jnp.exp(-0.5 * hidden * hidden) * (1.0 / math.sqrt(2.0 * math.pi))
    return gelu_parts(hidden) + hidden * pdf


def forward_kernel(scale, head_size, q_ref, k_ref, v_ref, *rest):
    if len(rest) == 2:
        bias_ref, o_ref = rest
    else:
        bias_ref, o_ref = None, rest[0]
    query = q_ref[0]
    lanes = query.shape[1]
    key = k_ref[...].reshape(-1, lanes)
    value = v_ref[...].reshape(-1, lanes)
    lane = lax.broadcasted_iota(jnp.int32, query.shape, 1)
    result = None
    for head in range(lanes // head_size):
        mine = (lane // head_size) == head
        own_query = jnp.where(mine, query, jnp.zeros_like(query))
        scores = mm(own_query, key, NT) * (scale * LOG2E)
        if bias_ref is not None:
            scores = scores + bias_ref[0]
        top = jnp.max(scores, axis=1, keepdims=True)
        weight = jnp.exp2(scores - top)
        total = jnp.sum(weight, axis=1, keepdims=True)
        part = jnp.where(mine, mm(weight.astype(bf16), value) / total, 0.0)
        result = part if result is None else result + part
    o_ref[0] = result.astype(bf16)


def attend(queries, joined, head_size, bias):
    clips, rows, width = queries.shape
    major, _, length, _ = joined.shape
    keys = major * length
    groups = width // 128
    in_specs = [
        pl.BlockSpec((1, rows, 128), lambda c, g: (c, 0, g)),
        pl.BlockSpec((major, 1, length, 128), lambda c, g: (0, c, 0, g)),
        pl.BlockSpec((major, 1, length, 128), lambda c, g: (0, c, 0, g + groups)),
    ]
    operands = [queries, joined, joined]
    if bias is not None:
        in_specs.append(pl.BlockSpec((1, 1, keys), lambda c, g: (c, 0, 0)))
        operands.append(bias)
    cells = clips * rows * keys * (width // head_size)
    return pl.pallas_call(
        functools.partial(forward_kernel, 1.0 / math.sqrt(head_size), head_size),
        grid=(clips, groups),
        in_specs=in_specs,
        out_specs=pl.BlockSpec((1, rows, 128), lambda c, g: (c, 0, g)),
        out_shape=jax.ShapeDtypeStruct((clips, rows, width), bf16),
        compiler_params=pltpu.CompilerParams(vmem_limit_bytes=VMEM_LIMIT),
        cost_estimate=pl.CostEstimate(
            flops=cells * 1024, bytes_accessed=4 * clips * keys * width, transcendentals=cells
        ),
        name="attend",
    )(*operands)


def backward_kernel(scale, head_size, shards, q_ref, k_ref, v_ref, g_ref, *rest):
    if len(rest) == 4:
        bias_ref = rest[0]
        rest = rest[1:]
    else:
        bias_ref = None
    out_ref, dk_sum, dv_sum = rest
    group = pl.program_id(0)
    part = pl.program_id(1)
    lanes = q_ref.shape[-1]
    query = q_ref[...].reshape(-1, lanes)
    key = k_ref[...].reshape(-1, lanes)
    value = v_ref[...].reshape(-1, lanes)
    grad = g_ref[...].reshape(-1, lanes)
    lane = lax.broadcasted_iota(jnp.int32, query.shape, 1)
    key_lane = lax.broadcasted_iota(jnp.int32, key.shape, 1)
    sums = None
    for head in range(lanes // head_size):
        mine = (lane // head_size) == head
        own_query = jnp.where(mine, query, jnp.zeros_like(query))
        own_grad = jnp.where(mine, grad, jnp.zeros_like(grad))
        own_key = jnp.where((key_lane // head_size) == head, key, jnp.zeros_like(key))
        scores = mm(own_query, key, NT) * (scale * LOG2E)
        if bias_ref is not None:
            scores = scores + bias_ref[0]
        top = jnp.max(scores, axis=1, keepdims=True)
        weight = jnp.exp2(scores - top)
        chance = weight * (1.0 / jnp.sum(weight, axis=1, keepdims=True))
        grad_chance = mm(own_grad, value, NT)
        delta = jnp.sum(chance * grad_chance, axis=1, keepdims=True)
        grad_scores = (chance * (grad_chance - delta)).astype(bf16)
        terms = (
            mm(grad_scores, own_key),
            mm(own_query, grad_scores, TN),
            mm(own_grad, chance.astype(bf16), TN),
        )
        sums = terms if sums is None else tuple(x + y for x, y in zip(sums, terms))
    part_q, part_k, part_v = sums

    @pl.when(part == 0)
    def _():
        dk_sum[...] = part_k
        dv_sum[...] = part_v

    @pl.when(part > 0)
    def _():
        dk_sum[...] += part_k
        dv_sum[...] += part_v

    rows = out_ref.shape[2]
    width = out_ref.shape[3] // 3
    held = query.shape[0] // rows

    def place(kind):
        if width == lanes:
            return slice(kind * width, (kind + 1) * width)
        return pl.ds(pl.multiple_of(kind * width + group * lanes, 128), lanes)

    result_q = (part_q * scale).astype(bf16)
    for index in range(held):
        out_ref[part * held + index, 0, :, place(0)] = result_q[index * rows : (index + 1) * rows]

    @pl.when(part == pl.num_programs(1) - 1)
    def _():
        for kind, total_ref, factor in ((1, dk_sum, scale), (2, dv_sum, 1.0)):
            result = (total_ref[...] * factor).T.astype(bf16)
            for index in range(shards):
                out_ref[index, 0, :, place(kind)] = result[index * rows : (index + 1) * rows]


def attend_back(queries, keys, values, grad_mixed, clip, head_size, bias, shards):
    major, _, length, width = queries.shape
    lanes = min(width, 128)
    groups = width // lanes
    rows = major * length // shards
    parts = shards if major == 1 else 1
    query_rows = rows if major == 1 else length
    by_query = pl.BlockSpec((major, 1, query_rows, lanes), lambda g, r: (0, clip, r, g))
    by_key = pl.BlockSpec((major, 1, length, lanes), lambda g, r: (0, clip, 0, g))
    in_specs = [by_query, by_key, by_key, by_query]
    operands = [queries, keys, values, grad_mixed]
    total = major * length
    if bias is not None:
        in_specs.append(pl.BlockSpec((1, 1, total), lambda g, r: (clip, 0, 0)))
        operands.append(bias)
    cells = total * total * (width // head_size)
    return pl.pallas_call(
        functools.partial(backward_kernel, 1.0 / math.sqrt(head_size), head_size, shards),
        grid=(groups, parts),
        in_specs=in_specs,
        out_specs=pl.BlockSpec((shards, 1, rows, 3 * width), lambda g, r: (0, 0, 0, 0)),
        out_shape=jax.ShapeDtypeStruct((shards, 1, rows, 3 * width), bf16),
        scratch_shapes=[pltpu.VMEM((lanes, total), f32), pltpu.VMEM((lanes, total), f32)],
        compiler_params=pltpu.CompilerParams(vmem_limit_bytes=VMEM_LIMIT),
        cost_estimate=pl.CostEstimate(
            flops=cells * 2560, bytes_accessed=14 * total * width, transcendentals=cells
        ),
        name="attend_back",
    )(*operands)


def exchange(array):
    return lax.all_to_all(array, "seq", split_axis=0, concat_axis=0, tiled=True)


def gather(array):
    return lax.all_gather(array, "fsdp", axis=0, tiled=True)


def scatter(array):
    return lax.psum_scatter(array, "fsdp", scatter_dimension=0, tiled=True)


def pack_rows(vectors):
    rows = []
    for member in vectors:
        count = -(-member.shape[0] // 128)
        padded = jnp.pad(member.astype(f32), (0, count * 128 - member.shape[0]))
        rows.append(padded.reshape(count, 128))
    total = sum(member.shape[0] for member in rows)
    if total % 8:
        rows.append(jnp.zeros((8 - total % 8, 128), f32))
    return jnp.concatenate(rows, axis=0)


def unpack_rows(packed, sizes):
    out = []
    at = 0
    for size in sizes:
        count = -(-size // 128)
        piece = packed[:, at : at + count].reshape(packed.shape[0], count * 128)[:, :size]
        out.append(piece.reshape(-1))
        at += count
    return out


MESH = pl.DeviceIdType.MESH


def line_kernel(size, cuts, shares, *refs):
    count = len(cuts)
    held = count + shares
    ins, outs = refs[:count], refs[held : held + count]
    own, every = refs[count], refs[held + count]
    scratch = refs[2 * held :]
    inner, outer, partial = (scratch[i * count : (i + 1) * count] for i in range(3))
    to_inner, to_outer, from_inner, from_outer = scratch[3 * count : 3 * count + 4]
    me = lax.axis_index("seq")
    left = me < size // 2
    toward = jnp.where(left, me + 1, me - 1)
    away = jnp.where(left, me - 1, me + 1)
    end = (me == 0) | (me == size - 1)
    barrier = pltpu.get_barrier_semaphore()
    pl.semaphore_signal(barrier, inc=1, device_id={"seq": toward}, device_id_type=MESH)

    @pl.when(jnp.logical_not(end))
    def _():
        pl.semaphore_signal(barrier, inc=1, device_id={"seq": away}, device_id_type=MESH)
        pl.semaphore_wait(barrier, 2)

    @pl.when(end)
    def _():
        pl.semaphore_wait(barrier, 1)

    pieces = []
    for index, parts in enumerate(cuts):
        rows = ins[index].shape[0] // parts
        for part in range(parts):
            pieces.append((part / parts, index, slice(part * rows, (part + 1) * rows)))
    pieces.sort(key=lambda piece: piece[:2])
    pieces = [(slot, index, cut) for slot, (_, index, cut) in enumerate(pieces)]

    def inwards(slot, index, cut):
        return pltpu.make_async_remote_copy(
            src_ref=ins[index].at[cut],
            dst_ref=outer[index].at[cut],
            send_sem=to_inner.at[slot],
            recv_sem=from_outer.at[slot],
            device_id={"seq": toward},
            device_id_type=MESH,
        )

    def swap(slot, index, cut):
        return pltpu.make_async_remote_copy(
            src_ref=partial[index].at[cut],
            dst_ref=inner[index].at[cut],
            send_sem=to_inner.at[slot],
            recv_sem=from_inner.at[slot],
            device_id={"seq": toward},
            device_id_type=MESH,
        )

    def outwards(slot, index, cut):
        return pltpu.make_async_remote_copy(
            src_ref=outs[index].at[cut],
            dst_ref=outs[index].at[cut],
            send_sem=to_outer.at[slot],
            recv_sem=from_inner.at[slot],
            device_id={"seq": away},
            device_id_type=MESH,
        )

    @pl.when(end)
    def _():
        for piece in pieces:
            inwards(*piece).start()

    if shares:
        sent, arrived = scratch[3 * count + 4 :]
        every[me] = own[...]

        def passes(way, hop):
            step = 1 - 2 * way
            block = me - step * hop
            return pltpu.make_async_remote_copy(
                src_ref=own if hop == 0 else every.at[block],
                dst_ref=every.at[block],
                send_sem=sent.at[way, hop],
                recv_sem=arrived.at[way, hop],
                device_id={"seq": me + step},
                device_id_type=MESH,
            )

        def sends(way, hop):
            if way == 0:
                return (me < size - 1) & (me - hop >= 0)
            return (me > 0) & (me + hop <= size - 1)

        def receives(way, hop):
            return me - 1 - hop >= 0 if way == 0 else me + 1 + hop <= size - 1

        def landing(way, hop):
            block = me - 1 - hop if way == 0 else me + 1 + hop
            return pltpu.make_async_remote_copy(
                src_ref=every.at[block],
                dst_ref=every.at[block],
                send_sem=sent.at[way, hop],
                recv_sem=arrived.at[way, hop],
                device_id={"seq": toward},
                device_id_type=MESH,
            )

        def forward(hop):
            for way in (0, 1):
                if hop > 0:

                    @pl.when(receives(way, hop - 1))
                    def _(way=way):
                        landing(way, hop - 1).wait_recv()

                if hop < size - 1:

                    @pl.when(sends(way, hop))
                    def _(way=way):
                        passes(way, hop).start()

        forward(0)

    @pl.when(end)
    def _():
        for piece in pieces:
            outwards(*piece).wait_recv()
        for piece in pieces:
            inwards(*piece).wait_send()

    @pl.when(jnp.logical_not(end))
    def _():
        lag = min(count, len(pieces))
        steps = len(pieces) + lag
        for step in range(steps):
            if shares and step in (steps // 3, 2 * steps // 3):
                forward(1 if step == steps // 3 else 2)
            if step < len(pieces):
                piece = pieces[step]
                inwards(*piece).wait_recv()
                _, index, cut = piece
                both = ins[index][cut].astype(f32) + outer[index][cut].astype(f32)
                partial[index][cut] = both.astype(bf16)
                swap(*piece).start()
            if step >= lag:
                piece = pieces[step - lag]
                swap(*piece).wait_recv()
                _, index, cut = piece
                both = partial[index][cut].astype(f32) + inner[index][cut].astype(f32)
                outs[index][cut] = both.astype(bf16)
                outwards(*piece).start()
        for piece in pieces:
            swap(*piece).wait_send()
            outwards(*piece).wait_send()

    if shares:

        @pl.when(end)
        def _():
            for hop in range(1, size):
                forward(hop)

        @pl.when(jnp.logical_not(end))
        def _():
            for hop in range(3, size):
                forward(hop)

        for way in (0, 1):
            for hop in range(size - 1):

                @pl.when(sends(way, hop))
                def _(way=way, hop=hop):
                    passes(way, hop).wait_send()


def line_sum(arrays, size, identity, share=None):
    cuts = []
    for member in arrays:
        parts = 8
        while parts > 1 and member.shape[0] % (16 * parts):
            parts //= 2
        cuts.append(parts)
    hold = [pltpu.VMEM(member.shape, bf16) for member in arrays]
    shapes = [jax.ShapeDtypeStruct(member.shape, bf16) for member in arrays]
    semaphores = [pltpu.SemaphoreType.DMA((sum(cuts),))] * 4
    operands = list(arrays)
    if share is not None:
        operands.append(share)
        shapes.append(jax.ShapeDtypeStruct((size,) + share.shape, bf16))
        semaphores += [pltpu.SemaphoreType.DMA((2, size - 1))] * 2
    whole = pl.BlockSpec(memory_space=pltpu.VMEM)
    return pl.pallas_call(
        functools.partial(line_kernel, size, tuple(cuts), int(share is not None)),
        out_shape=shapes,
        in_specs=[whole] * len(operands),
        out_specs=[whole] * len(operands),
        scratch_shapes=hold * 3 + semaphores,
        compiler_params=pltpu.CompilerParams(
            collective_id=identity, has_side_effects=True, vmem_limit_bytes=VMEM_LIMIT
        ),
        cost_estimate=pl.CostEstimate(
            flops=0,
            bytes_accessed=40 * sum(2 * member.size for member in operands),
            transcendentals=0,
        ),
        name="line_sum",
    )(*operands)


def sum_slots(arrays, size, identity, share=None):
    if size == 4:
        return line_sum(arrays, size, identity, share)
    sums = lax.psum(tuple(arrays), "seq")
    if share is None:
        return sums
    return (*sums, lax.all_gather(share, "seq", axis=0, tiled=False))


def feed_back(grad_out, middle, normed_mid, hidden, active, weights, mid_gain):
    out, expand, contract = weights
    grad_y = grad_out.astype(bf16)
    grad_contract = mm(active, grad_y, TN).astype(bf16)
    grad_contract_bias = jnp.sum(grad_y.astype(f32), axis=0)
    grad_y, grad_contract = lax.optimization_barrier((grad_y, grad_contract))
    grad_hidden = (mm(grad_y, contract, NT) * gelu_slope(hidden)).astype(bf16)
    grad_expand = mm(normed_mid, grad_hidden, TN).astype(bf16)
    grad_expand_bias = jnp.sum(grad_hidden.astype(f32), axis=0)
    grad_normed = mm(grad_hidden, expand, NT)
    grad_normed, grad_expand = lax.optimization_barrier((grad_normed, grad_expand))
    grad_norm, grad_mid_gain, grad_mid_shift = norm_back(middle, mid_gain, grad_normed)
    grad_middle = grad_out + grad_norm
    grad_att = grad_middle.astype(bf16)
    grad_out_bias = jnp.sum(grad_att.astype(f32), axis=0)
    grad_mixed = mm(grad_att, out, NT).astype(bf16)
    small = dict(
        out_bias=grad_out_bias,
        mid_gain=grad_mid_gain,
        mid_shift=grad_mid_shift,
        expand_bias=grad_expand_bias,
        contract_bias=grad_contract_bias,
    )
    return grad_middle, grad_att, grad_mixed, (grad_expand, grad_contract), small


def own_joint(joint_weight, query_bias, value_bias, shards, shard):
    width = joint_weight.shape[0]
    own = width // shards
    weight = lax.dynamic_slice_in_dim(joint_weight.reshape(width, 3, width), shard * own, own, 2)
    bias_q = lax.dynamic_slice_in_dim(query_bias, shard * own, own, 0)
    bias_v = lax.dynamic_slice_in_dim(value_bias, shard * own, own, 0)
    return weight, (bias_q, None, bias_v)


def own_parts(normed_all, weight, biases):
    flat = normed_all.reshape(-1, normed_all.shape[3])
    out = []
    for index in range(3):
        part = mm(flat, weight[:, index])
        if biases[index] is not None:
            part = part + biases[index]
        out.append(part.astype(bf16).reshape(normed_all.shape[:3] + (weight.shape[2],)))
    return out


def by_sender(joint_weight, shards):
    width = joint_weight.shape[0]
    array = joint_weight.reshape(width, 3, shards, width // shards)
    return array.transpose(0, 2, 1, 3).reshape(width, 3 * width)


def joint_back(received, joint_by_sender):
    shards, clips, rows, width = received.shape
    flat = received.reshape(shards, clips * rows, width).transpose(1, 0, 2)
    return mm(flat.reshape(clips * rows, shards * width), joint_by_sender, NT)


def joint_small(columns, owners, shards, shard):
    own = columns.shape[0] // 3
    each = owners // shards
    mine = lax.broadcasted_iota(jnp.int32, (owners, 1), 0) // each == shard

    def full(vector):
        return jnp.where(mine, jnp.tile(vector.reshape(each, -1), (shards, 1)), 0.0)

    return dict(query_bias=full(columns[:own]), value_bias=full(columns[2 * own :]))


ORDER = (
    "pre_gain",
    "pre_shift",
    "query_bias",
    "value_bias",
    "out_bias",
    "mid_gain",
    "mid_shift",
    "expand_bias",
    "contract_bias",
)
BLOCK = (
    "pre_gain",
    "pre_shift",
    "joint",
    "query_bias",
    "value_bias",
    "out",
    "out_bias",
    "mid_gain",
    "mid_shift",
    "expand",
    "expand_bias",
    "contract",
    "contract_bias",
)
FRAMES = 8
GRID = 14
MOST_VISIBLE = FRAMES * max(
    high * wide
    for high in range(1, GRID + 1)
    for wide in range(1, GRID + 1)
    if 2 * high * wide < GRID * GRID
)


def body(fsdp_size, seq_size, tokens, visible, slot_token, positions, *rest):
    e_shard = dict(zip(BLOCK, rest[:13]))
    embed_weight, embed_bias, mask_token = rest[13:16]
    p_shard = dict(zip(BLOCK, rest[16:29]))
    cotangent = rest[29]
    shard = lax.axis_index("seq")
    clips, slots, width = tokens.shape
    span = visible.shape[1]

    e_joint = gather(e_shard["joint"])
    place = lax.broadcasted_iota(jnp.int32, (1, 1, span), 2)
    slot_visible = jnp.any(
        (slot_token[:, :, None] == place) & (visible[:, None, :] > 0), axis=2
    )
    counts = jnp.sum(slot_visible.reshape(clips, seq_size, slots).astype(jnp.int32), axis=2)
    compact = -(-MOST_VISIBLE // (16 * seq_size)) * 16
    fits = (jnp.max(counts) <= compact).astype(f32)

    vectors = [e_shard[name] for name in ORDER] + [embed_bias, mask_token]
    vectors += [p_shard[name] for name in ORDER]
    sizes = [member.shape[0] for member in vectors]
    packed = lax.all_gather(
        pack_rows(vectors + [jnp.full((1,), fits)]), "fsdp", axis=0, tiled=False
    )
    full = unpack_rows(packed, sizes + [1])
    all_fit = jnp.min(full[-1]) > 0.5
    normed = norm_layer(tokens.reshape(-1, width), full[0], full[1])

    operands = (
        tokens,
        slot_visible,
        counts,
        slot_token,
        positions,
        normed,
        e_joint,
        tuple(e_shard[name] for name in ("out", "expand", "contract")),
        embed_weight,
        tuple(p_shard[name] for name in ("joint", "out", "expand", "contract")),
        tuple(full[:-1]),
        cotangent,
    )
    whole = functools.partial(main, fsdp_size, seq_size, slots)
    if compact >= slots:
        return whole(*operands)
    return lax.cond(
        all_fit, functools.partial(main, fsdp_size, seq_size, compact), whole, *operands
    )


def main(
    fsdp_size,
    seq_size,
    held,
    tokens,
    slot_visible,
    counts,
    slot_token,
    positions,
    normed,
    e_joint,
    e_shards,
    embed_shard,
    p_shards,
    vectors,
    cotangent,
):
    shard = lax.axis_index("seq")
    clips, slots, width = tokens.shape
    span = slot_visible.shape[1]
    rows = clips * slots
    small_width = cotangent.shape[2]
    head_size = width // HEADS
    small_head = small_width // PHEADS
    whole = held == slots
    e_vec = dict(zip(ORDER, vectors[:9]))
    embed_bias, mask_token = vectors[9:11]
    p_vec = dict(zip(ORDER, vectors[11:]))

    e_out_shard, e_expand_shard, e_contract_shard = e_shards
    p_joint_shard, p_out_shard, p_expand_shard, p_contract_shard = p_shards
    e_out, e_expand = gather(e_out_shard), gather(e_expand_shard)

    own_visible = lax.dynamic_slice_in_dim(slot_visible, shard * slots, slots, 1)
    own_flat = own_visible.reshape(rows, 1)
    own_tokens = lax.dynamic_slice_in_dim(slot_token, shard * slots, slots, 1)
    slot_code = jnp.take(positions, own_tokens.reshape(rows), axis=0)

    if whole:
        kept = slot_visible.reshape(clips, 1, span)

        def keep(array):
            return array

        def put_back(array):
            return array

    else:
        kept = lax.broadcasted_iota(jnp.int32, (1, 1, held), 2) < counts[:, :, None]
        kept = kept.reshape(clips, 1, seq_size * held)
        ones = own_visible.astype(bf16)
        before = lax.broadcasted_iota(jnp.int32, (slots, slots), 0)
        after = lax.broadcasted_iota(jnp.int32, (slots, slots), 1)
        rank = mm(ones, (before < after).astype(bf16)).astype(jnp.int32)
        target = lax.broadcasted_iota(jnp.int32, (1, held, 1), 1)
        picks = ((rank[:, None, :] == target) & own_visible[:, None, :]).astype(bf16)

        def keep(array):
            precision = lax.Precision.HIGHEST if array.dtype == f32 else None
            picked = jnp.einsum(
                "crs,csw->crw",
                picks.astype(array.dtype),
                array.reshape(clips, slots, -1),
                precision=precision,
                preferred_element_type=f32,
            )
            return picked.astype(array.dtype).reshape(clips * held, -1)

        def put_back(array):
            placed = jnp.einsum(
                "crs,crw->csw",
                picks.astype(f32),
                array.reshape(clips, held, -1),
                precision=lax.Precision.HIGHEST,
                preferred_element_type=f32,
            )
            return placed.reshape(rows, -1)

    bias = jnp.where(kept, 0.0, -1e30).astype(f32)
    tiled = held % 16 == 0

    def by_clip(array):
        if tiled:
            return array
        shards, count, length, lanes = array.shape
        return array.transpose(1, 0, 2, 3).reshape(1, count, shards * length, lanes)

    inputs = tokens.reshape(rows, width)
    normed_kept = keep(normed).reshape(1, clips, held, width)
    normed_all = exchange(jnp.broadcast_to(normed_kept, (seq_size, clips, held, width)))
    embed, p_joint, p_out = gather(embed_shard), gather(p_joint_shard), gather(p_out_shard)
    e_by_sender = by_sender(e_joint, seq_size)
    normed_all, embed, p_joint, p_out, e_by_sender = lax.optimization_barrier(
        (normed_all, embed, p_joint, p_out, e_by_sender)
    )
    queries = (mm(normed, e_joint[:, :width]) + e_vec["query_bias"]).astype(bf16)
    joined = mm(normed_all.reshape(-1, width), e_joint[:, width:])
    joined_bias = jnp.concatenate([jnp.zeros_like(e_vec["value_bias"]), e_vec["value_bias"]])
    joined = (joined + joined_bias).astype(bf16)
    joined, e_contract_shard = lax.optimization_barrier((joined, e_contract_shard))
    e_contract = gather(e_contract_shard)
    mixed = attend(
        queries.reshape(clips, slots, width),
        by_clip(joined.reshape(seq_size, clips, held, 2 * width)),
        head_size,
        bias,
    ).reshape(rows, width)
    mixed, p_expand_shard = lax.optimization_barrier((mixed, p_expand_shard))
    p_expand = gather(p_expand_shard)
    middle = inputs + mm(mixed, e_out) + e_vec["out_bias"]
    normed_mid = norm_layer(middle, e_vec["mid_gain"], e_vec["mid_shift"])
    active = gelu(mm(normed_mid, e_expand) + e_vec["expand_bias"])
    encoded = middle + mm(active, e_contract) + e_vec["contract_bias"]
    context = encoded.astype(bf16)

    embedded = mm(context, embed) + embed_bias
    pred_input = jnp.where(own_flat, embedded, mask_token) + slot_code
    p_normed = norm_layer(pred_input, p_vec["pre_gain"], p_vec["pre_shift"])
    (
        p_normed,
        rows_all,
        mid_rows,
        mixed_rows,
        middle_rows,
        e_vec["query_bias"],
        e_vec["value_bias"],
        p_vec["query_bias"],
        p_vec["value_bias"],
    ) = lax.optimization_barrier(
        (
            p_normed,
            normed_all,
            normed_mid,
            mixed,
            middle,
            e_vec["query_bias"],
            e_vec["value_bias"],
            p_vec["query_bias"],
            p_vec["value_bias"],
        )
    )
    p_queries = (mm(p_normed, p_joint[:, :small_width]) + p_vec["query_bias"]).astype(bf16)
    own_weight, own_bias = own_joint(
        e_joint, e_vec["query_bias"], e_vec["value_bias"], seq_size, shard
    )
    own_qkv = [by_clip(member) for member in own_parts(rows_all, own_weight, own_bias)]
    p_bias = jnp.concatenate([jnp.zeros_like(p_vec["value_bias"]), p_vec["value_bias"]])
    p_normed_all = []
    p_mixed = []
    everyone = [
        lax.all_gather(p_normed.reshape(clips, slots, small_width)[clip], "seq", axis=0, tiled=True)
        for clip in range(clips)
    ]
    p_contract_shard, p_expand, everyone[0] = lax.optimization_barrier(
        (p_contract_shard, p_expand, everyone[0])
    )
    p_contract = gather(p_contract_shard)
    for clip in range(clips):
        every = everyone[clip]
        if clip > 0:
            every, p_mixed[-1] = lax.optimization_barrier((every, p_mixed[-1]))
        p_joined = (mm(every, p_joint[:, small_width:]) + p_bias).astype(bf16)
        p_normed_all.append(every)
        p_mixed.append(
            attend(
                p_queries.reshape(clips, slots, small_width)[clip : clip + 1],
                p_joined.reshape(1, 1, span, 2 * small_width),
                small_head,
                None,
            )
        )
    kept_mid, kept_mixed, kept_middle, kept_inputs = (
        keep(member) for member in (mid_rows, mixed_rows, middle_rows, inputs)
    )
    p_mixed[0], kept_mid, kept_mixed, kept_middle, kept_inputs, *own_qkv = (
        lax.optimization_barrier(
            (p_mixed[0], kept_mid, kept_mixed, kept_middle, kept_inputs, *own_qkv)
        )
    )
    p_mixed = jnp.concatenate(p_mixed, axis=0).reshape(rows, small_width)
    p_middle = pred_input + mm(p_mixed, p_out) + p_vec["out_bias"]
    p_normed_mid = norm_layer(p_middle, p_vec["mid_gain"], p_vec["mid_shift"])
    p_hidden = mm(p_normed_mid, p_expand) + p_vec["expand_bias"]
    p_active = gelu(p_hidden)
    predicted = p_middle + mm(p_active, p_contract) + p_vec["contract_bias"]

    grad_middle, grad_att, grad_mixed, p_grads, p_small = feed_back(
        cotangent.reshape(rows, small_width),
        p_middle,
        p_normed_mid,
        p_hidden,
        p_active,
        (p_out, p_expand, p_contract),
        p_vec["mid_gain"],
    )
    p_grad_out = mm(p_mixed, grad_att, TN).astype(bf16)
    p_wide = jnp.concatenate([p_grad_out, p_grads[0]], axis=1)
    p_tall = p_grads[1]
    grad_mixed, p_wide, p_tall = lax.optimization_barrier((grad_mixed, p_wide, p_tall))
    p_wide, p_tall = scatter(p_wide), scatter(p_tall)
    own_weight, own_bias = own_joint(
        p_joint, p_vec["query_bias"], p_vec["value_bias"], seq_size, shard
    )
    own_width = small_width // seq_size
    grad_mixed = grad_mixed.reshape(rows, seq_size, own_width).transpose(1, 0, 2)
    grad_mixed = exchange(grad_mixed.reshape(seq_size, clips, slots, own_width))
    p_by_sender = by_sender(p_joint, seq_size)
    grad_normed = []
    p_grad_joint = 0.0
    p_columns = 0.0
    for clip in range(clips):
        every = p_normed_all[clip].reshape(1, 1, span, small_width)
        grads = attend_back(
            *own_parts(every, own_weight, own_bias),
            grad_mixed[:, clip].reshape(1, 1, span, own_width),
            0,
            small_head,
            None,
            seq_size,
        )
        if clip == 0:
            grads, p_wide, p_tall = lax.optimization_barrier((grads, p_wide, p_tall))
        flat = grads.reshape(span, 3 * own_width)
        p_grad_joint = p_grad_joint + mm(p_normed_all[clip], flat, TN)
        p_columns = p_columns + jnp.sum(flat.astype(f32), axis=0)
        grad_normed.append(joint_back(exchange(grads), p_by_sender))
    p_small.update(joint_small(p_columns, fsdp_size, seq_size, shard))
    p_own_width = own_width
    grad_norm, p_small["pre_gain"], p_small["pre_shift"] = norm_back(
        pred_input, p_vec["pre_gain"], jnp.concatenate(grad_normed, axis=0)
    )
    grad_pred_input = grad_middle + grad_norm
    grad_mask_token = jnp.sum(jnp.where(own_flat, 0.0, grad_pred_input), axis=0)
    grad_embedded = jnp.where(own_flat, grad_pred_input, 0.0).astype(bf16)
    grad_embed_bias = jnp.sum(grad_embedded.astype(f32), axis=0)

    grad_embedded, predicted = lax.optimization_barrier((grad_embedded, predicted))
    grad_context = mm(keep(grad_embedded), embed, NT)
    kept_hidden = mm(kept_mid, e_expand) + e_vec["expand_bias"]
    grad_middle, grad_att, grad_mixed, e_grads, e_small = feed_back(
        grad_context,
        kept_middle,
        kept_mid,
        kept_hidden,
        gelu(kept_hidden),
        (e_out, e_expand, e_contract),
        e_vec["mid_gain"],
    )
    expand_part, contract_part = scatter(e_grads[0]), scatter(e_grads[1])
    own_width = width // seq_size
    grad_mixed = grad_mixed.reshape(clips * held, seq_size, own_width).transpose(1, 0, 2)
    grad_mixed = by_clip(exchange(grad_mixed.reshape(seq_size, clips, held, own_width)))
    grads = [
        attend_back(*own_qkv, grad_mixed, clip, head_size, bias, seq_size) for clip in range(clips)
    ]
    grads[-1], grad_att, late_embedded = lax.optimization_barrier(
        (grads[-1], grad_att, grad_embedded)
    )
    received = [exchange(member) for member in grads]
    received[0], contract_part = lax.optimization_barrier((received[0], contract_part))
    flat = jnp.concatenate(grads, axis=1).reshape(-1, 3 * own_width)
    e_grad_joint = mm(normed_all.reshape(-1, width), flat, TN).astype(bf16)
    e_grad_out = mm(kept_mixed, grad_att, TN).astype(bf16)
    grad_embed = mm(context, late_embedded, TN).astype(bf16)
    e_small.update(joint_small(jnp.sum(flat.astype(f32), axis=0), fsdp_size, seq_size, shard))
    grad_normed = jnp.concatenate([joint_back(member, e_by_sender) for member in received], axis=0)
    grad_norm, e_small["pre_gain"], e_small["pre_shift"] = norm_back(
        kept_inputs, e_vec["pre_gain"], grad_normed
    )

    own_rows = width // fsdp_size
    p_rows = small_width // fsdp_size
    p_lanes = -(-3 * p_own_width // 128) * 128
    p_grad_joint = p_grad_joint.astype(bf16).reshape(fsdp_size, p_rows, 3 * p_own_width)
    p_grad_joint = jnp.pad(
        p_grad_joint, ((0, 0), (0, own_rows - p_rows), (0, p_lanes - 3 * p_own_width))
    ).reshape(width, p_lanes)
    small = [e_small[name] for name in ORDER] + [grad_embed_bias, grad_mask_token]
    small += [p_small[name] for name in ORDER]
    small = [member.reshape(fsdp_size, -1) for member in small]
    sizes = [member.shape[1] for member in small]
    small.append(jnp.zeros((fsdp_size, own_rows * 128 - sum(sizes)), f32))
    small = jnp.concatenate(small, axis=1).astype(bf16).reshape(width, 128)
    late = scatter(jnp.concatenate([e_grad_joint, p_grad_joint, e_grad_out, grad_embed, small], axis=1))
    grad_tokens = put_back(grad_middle + grad_norm)

    first = 0 if whole else 2
    contract_sum, expand_sum, p_wide_sum, p_contract_sum = sum_slots(
        (contract_part, expand_part, p_wide, p_tall), seq_size, first
    )
    late, expand_sum = lax.optimization_barrier((late, expand_sum))
    shared = 3 * own_width + p_lanes
    late_sum, columns = sum_slots((late[:, shared:],), seq_size, first + 1, late[:, :shared])
    e_joint_sum = columns[:, :, : 3 * own_width].reshape(seq_size, own_rows, 3, own_width)
    e_joint_sum = e_joint_sum.transpose(1, 2, 0, 3).reshape(own_rows, 3 * width)
    p_joint_sum = columns[:, :p_rows, 3 * own_width : 3 * (own_width + p_own_width)]
    p_joint_sum = p_joint_sum.reshape(seq_size, p_rows, 3, p_own_width)
    p_joint_sum = p_joint_sum.transpose(1, 2, 0, 3).reshape(p_rows, 3 * small_width)
    out_sum = late_sum[:, :width]
    embed_sum = late_sum[:, width : width + small_width]
    vector_sum = late_sum[:, width + small_width :].reshape(-1)
    small_out = []
    at = 0
    for size in sizes:
        small_out.append(vector_sum[at : at + size].astype(f32))
        at += size
    p_out_sum, p_expand_sum = p_wide_sum[:, :small_width], p_wide_sum[:, small_width:]

    def ordered(vec, joint, out, expand, contract):
        vec = dict(
            zip(ORDER, vec),
            joint=joint.astype(f32),
            out=out.astype(f32),
            expand=expand.astype(f32),
            contract=contract.astype(f32),
        )
        return tuple(vec[name] for name in BLOCK)

    return (
        encoded.reshape(tokens.shape),
        predicted.reshape(cotangent.shape),
        grad_tokens.reshape(tokens.shape),
        *ordered(small_out[:9], e_joint_sum, out_sum, expand_sum, contract_sum),
        embed_sum.astype(f32),
        small_out[9],
        small_out[10],
        *ordered(small_out[11:], p_joint_sum, p_out_sum, p_expand_sum, p_contract_sum),
    )


def solution(mesh):
    cut, rows, vec, full = P("fsdp", "seq", None), P("fsdp", None), P("fsdp"), P()
    block = (vec, vec, rows, vec, vec, rows, vec, vec, vec, rows, vec, rows, vec)
    return jax.shard_map(
        functools.partial(body, mesh.shape["fsdp"], mesh.shape["seq"]),
        mesh=mesh,
        in_specs=(cut, rows, rows, full, *block, rows, vec, vec, *block, cut),
        out_specs=(cut, cut, cut, *block, rows, vec, vec, *block),
        check_vma=False,
    )
```

```python
import functools
import math

import jax
import jax.numpy as jnp
from jax import lax
from jax.experimental import pallas as pl
from jax.experimental.pallas import tpu as pltpu
from jax.sharding import PartitionSpec as P

HEADS = 16
PHEADS = 12

f32 = jnp.float32
bf16 = jnp.bfloat16
norm_eps = 1e-06
LOG2E = math.log2(math.e)
NN = (((1,), (0,)), ((), ()))
NT = (((1,), (1,)), ((), ()))
TN = (((0,), (0,)), ((), ()))
VMEM_LIMIT = 60 * 2**20


def mm(left, right, dims=NN):
    return lax.dot_general(left, right, dims, preferred_element_type=f32)


def norm_parts(value):
    center = value - jnp.mean(value, axis=-1, keepdims=True)
    spread = jnp.mean(center * center, axis=-1, keepdims=True)
    scale = lax.rsqrt(spread + norm_eps)
    return center * scale, scale


def norm_layer(value, gain, shift):
    unit, _ = norm_parts(value)
    return (unit * gain + shift).astype(bf16)


def norm_back(value, gain, grad):
    unit, scale = norm_parts(value)
    grad_gain = jnp.sum(grad * unit, axis=0)
    grad_shift = jnp.sum(grad, axis=0)
    inner = grad * gain
    inner = inner - jnp.mean(inner, axis=-1, keepdims=True) - unit * jnp.mean(
        inner * unit, axis=-1, keepdims=True
    )
    return scale * inner, grad_gain, grad_shift


def gelu_parts(hidden):
    cdf = 0.5 * (1.0 + lax.erf(hidden * math.sqrt(0.5)))
    return cdf


def gelu(hidden):
    return (hidden * gelu_parts(hidden)).astype(bf16)


def gelu_slope(hidden):
    pdf = jnp.exp(-0.5 * hidden * hidden) * (1.0 / math.sqrt(2.0 * math.pi))
    return gelu_parts(hidden) + hidden * pdf


def forward_kernel(scale, head_size, q_ref, k_ref, v_ref, *rest):
    if len(rest) == 2:
        bias_ref, o_ref = rest
    else:
        bias_ref, o_ref = None, rest[0]
    query = q_ref[0]
    lanes = query.shape[1]
    key = k_ref[...].reshape(-1, lanes)
    value = v_ref[...].reshape(-1, lanes)
    lane = lax.broadcasted_iota(jnp.int32, query.shape, 1)
    result = None
    for head in range(lanes // head_size):
        mine = (lane // head_size) == head
        own_query = jnp.where(mine, query, jnp.zeros_like(query))
        scores = mm(own_query, key, NT) * (scale * LOG2E)
        if bias_ref is not None:
            scores = scores + bias_ref[0]
        top = jnp.max(scores, axis=1, keepdims=True)
        weight = jnp.exp2(scores - top)
        total = jnp.sum(weight, axis=1, keepdims=True)
        part = jnp.where(mine, mm(weight.astype(bf16), value) / total, 0.0)
        result = part if result is None else result + part
    o_ref[0] = result.astype(bf16)


def attend(queries, joined, head_size, bias):
    clips, rows, width = queries.shape
    major, _, length, _ = joined.shape
    keys = major * length
    groups = width // 128
    in_specs = [
        pl.BlockSpec((1, rows, 128), lambda c, g: (c, 0, g)),
        pl.BlockSpec((major, 1, length, 128), lambda c, g: (0, c, 0, g)),
        pl.BlockSpec((major, 1, length, 128), lambda c, g: (0, c, 0, g + groups)),
    ]
    operands = [queries, joined, joined]
    if bias is not None:
        in_specs.append(pl.BlockSpec((1, 1, keys), lambda c, g: (c, 0, 0)))
        operands.append(bias)
    cells = clips * rows * keys * (width // head_size)
    return pl.pallas_call(
        functools.partial(forward_kernel, 1.0 / math.sqrt(head_size), head_size),
        grid=(clips, groups),
        in_specs=in_specs,
        out_specs=pl.BlockSpec((1, rows, 128), lambda c, g: (c, 0, g)),
        out_shape=jax.ShapeDtypeStruct((clips, rows, width), bf16),
        compiler_params=pltpu.CompilerParams(vmem_limit_bytes=VMEM_LIMIT),
        cost_estimate=pl.CostEstimate(
            flops=cells * 1024, bytes_accessed=4 * clips * keys * width, transcendentals=cells
        ),
        name="attend",
    )(*operands)


def backward_kernel(scale, head_size, shards, q_ref, k_ref, v_ref, g_ref, *rest):
    if len(rest) == 4:
        bias_ref = rest[0]
        rest = rest[1:]
    else:
        bias_ref = None
    out_ref, dk_sum, dv_sum = rest
    group = pl.program_id(0)
    part = pl.program_id(1)
    lanes = q_ref.shape[-1]
    query = q_ref[...].reshape(-1, lanes)
    key = k_ref[...].reshape(-1, lanes)
    value = v_ref[...].reshape(-1, lanes)
    grad = g_ref[...].reshape(-1, lanes)
    lane = lax.broadcasted_iota(jnp.int32, query.shape, 1)
    key_lane = lax.broadcasted_iota(jnp.int32, key.shape, 1)
    sums = None
    for head in range(lanes // head_size):
        mine = (lane // head_size) == head
        own_query = jnp.where(mine, query, jnp.zeros_like(query))
        own_grad = jnp.where(mine, grad, jnp.zeros_like(grad))
        own_key = jnp.where((key_lane // head_size) == head, key, jnp.zeros_like(key))
        scores = mm(own_query, key, NT) * (scale * LOG2E)
        if bias_ref is not None:
            scores = scores + bias_ref[0]
        top = jnp.max(scores, axis=1, keepdims=True)
        weight = jnp.exp2(scores - top)
        chance = weight * (1.0 / jnp.sum(weight, axis=1, keepdims=True))
        grad_chance = mm(own_grad, value, NT)
        delta = jnp.sum(chance * grad_chance, axis=1, keepdims=True)
        grad_scores = (chance * (grad_chance - delta)).astype(bf16)
        terms = (
            mm(grad_scores, own_key),
            mm(own_query, grad_scores, TN),
            mm(own_grad, chance.astype(bf16), TN),
        )
        sums = terms if sums is None else tuple(x + y for x, y in zip(sums, terms))
    part_q, part_k, part_v = sums

    @pl.when(part == 0)
    def _():
        dk_sum[...] = part_k
        dv_sum[...] = part_v

    @pl.when(part > 0)
    def _():
        dk_sum[...] += part_k
        dv_sum[...] += part_v

    rows = out_ref.shape[2]
    width = out_ref.shape[3] // 3
    held = query.shape[0] // rows

    def place(kind):
        if width == lanes:
            return slice(kind * width, (kind + 1) * width)
        return pl.ds(pl.multiple_of(kind * width + group * lanes, 128), lanes)

    result_q = (part_q * scale).astype(bf16)
    for index in range(held):
        out_ref[part * held + index, 0, :, place(0)] = result_q[index * rows : (index + 1) * rows]

    @pl.when(part == pl.num_programs(1) - 1)
    def _():
        for kind, total_ref, factor in ((1, dk_sum, scale), (2, dv_sum, 1.0)):
            result = (total_ref[...] * factor).T.astype(bf16)
            for index in range(shards):
                out_ref[index, 0, :, place(kind)] = result[index * rows : (index + 1) * rows]


def attend_back(queries, keys, values, grad_mixed, clip, head_size, bias, shards):
    major, _, length, width = queries.shape
    lanes = min(width, 128)
    groups = width // lanes
    rows = major * length // shards
    parts = shards if major == 1 else 1
    query_rows = rows if major == 1 else length
    by_query = pl.BlockSpec((major, 1, query_rows, lanes), lambda g, r: (0, clip, r, g))
    by_key = pl.BlockSpec((major, 1, length, lanes), lambda g, r: (0, clip, 0, g))
    in_specs = [by_query, by_key, by_key, by_query]
    operands = [queries, keys, values, grad_mixed]
    total = major * length
    if bias is not None:
        in_specs.append(pl.BlockSpec((1, 1, total), lambda g, r: (clip, 0, 0)))
        operands.append(bias)
    cells = total * total * (width // head_size)
    return pl.pallas_call(
        functools.partial(backward_kernel, 1.0 / math.sqrt(head_size), head_size, shards),
        grid=(groups, parts),
        in_specs=in_specs,
        out_specs=pl.BlockSpec((shards, 1, rows, 3 * width), lambda g, r: (0, 0, 0, 0)),
        out_shape=jax.ShapeDtypeStruct((shards, 1, rows, 3 * width), bf16),
        scratch_shapes=[pltpu.VMEM((lanes, total), f32), pltpu.VMEM((lanes, total), f32)],
        compiler_params=pltpu.CompilerParams(vmem_limit_bytes=VMEM_LIMIT),
        cost_estimate=pl.CostEstimate(
            flops=cells * 2560, bytes_accessed=14 * total * width, transcendentals=cells
        ),
        name="attend_back",
    )(*operands)


def exchange(array):
    return lax.all_to_all(array, "seq", split_axis=0, concat_axis=0, tiled=True)


def gather(array):
    return lax.all_gather(array, "fsdp", axis=0, tiled=True)


def scatter(array):
    return lax.psum_scatter(array, "fsdp", scatter_dimension=0, tiled=True)


def pack_rows(vectors):
    rows = []
    for member in vectors:
        count = -(-member.shape[0] // 128)
        padded = jnp.pad(member.astype(f32), (0, count * 128 - member.shape[0]))
        rows.append(padded.reshape(count, 128))
    total = sum(member.shape[0] for member in rows)
    if total % 8:
        rows.append(jnp.zeros((8 - total % 8, 128), f32))
    return jnp.concatenate(rows, axis=0)


def unpack_rows(packed, sizes):
    out = []
    at = 0
    for size in sizes:
        count = -(-size // 128)
        piece = packed[:, at : at + count].reshape(packed.shape[0], count * 128)[:, :size]
        out.append(piece.reshape(-1))
        at += count
    return out


MESH = pl.DeviceIdType.MESH


def line_kernel(size, cuts, shares, *refs):
    count = len(cuts)
    ins, outs = refs[:count], refs[count : 2 * count]
    if shares:
        ins, own, outs, every = (refs[0].at[:, shares:],), refs[0].at[:, :shares], refs[1:2], refs[2]
    scratch = refs[3 if shares else 2 * count :]
    inner, outer, partial = (scratch[i * count : (i + 1) * count] for i in range(3))
    to_inner, to_outer, from_inner, from_outer = scratch[3 * count : 3 * count + 4]
    me = lax.axis_index("seq")
    left = me < size // 2
    toward = jnp.where(left, me + 1, me - 1)
    away = jnp.where(left, me - 1, me + 1)
    end = (me == 0) | (me == size - 1)
    barrier = pltpu.get_barrier_semaphore()
    pl.semaphore_signal(barrier, inc=1, device_id={"seq": toward}, device_id_type=MESH)

    @pl.when(jnp.logical_not(end))
    def _():
        pl.semaphore_signal(barrier, inc=1, device_id={"seq": away}, device_id_type=MESH)
        pl.semaphore_wait(barrier, 2)

    @pl.when(end)
    def _():
        pl.semaphore_wait(barrier, 1)

    pieces = []
    for index, parts in enumerate(cuts):
        rows = ins[index].shape[0] // parts
        for part in range(parts):
            pieces.append((part / parts, index, slice(part * rows, (part + 1) * rows)))
    pieces.sort(key=lambda piece: piece[:2])
    pieces = [(slot, index, cut) for slot, (_, index, cut) in enumerate(pieces)]

    def inwards(slot, index, cut):
        return pltpu.make_async_remote_copy(
            src_ref=ins[index].at[cut],
            dst_ref=outer[index].at[cut],
            send_sem=to_inner.at[slot],
            recv_sem=from_outer.at[slot],
            device_id={"seq": toward},
            device_id_type=MESH,
        )

    def swap(slot, index, cut):
        return pltpu.make_async_remote_copy(
            src_ref=partial[index].at[cut],
            dst_ref=inner[index].at[cut],
            send_sem=to_inner.at[slot],
            recv_sem=from_inner.at[slot],
            device_id={"seq": toward},
            device_id_type=MESH,
        )

    def outwards(slot, index, cut):
        return pltpu.make_async_remote_copy(
            src_ref=outs[index].at[cut],
            dst_ref=outs[index].at[cut],
            send_sem=to_outer.at[slot],
            recv_sem=from_inner.at[slot],
            device_id={"seq": away},
            device_id_type=MESH,
        )

    @pl.when(end)
    def _():
        for piece in pieces:
            inwards(*piece).start()

    if shares:
        sent, arrived = scratch[3 * count + 4 :]
        every[me] = own[...]

        def passes(way, hop):
            step = 1 - 2 * way
            block = me - step * hop
            return pltpu.make_async_remote_copy(
                src_ref=own if hop == 0 else every.at[block],
                dst_ref=every.at[block],
                send_sem=sent.at[way, hop],
                recv_sem=arrived.at[way, hop],
                device_id={"seq": me + step},
                device_id_type=MESH,
            )

        def sends(way, hop):
            if way == 0:
                return (me < size - 1) & (me - hop >= 0)
            return (me > 0) & (me + hop <= size - 1)

        def receives(way, hop):
            return me - 1 - hop >= 0 if way == 0 else me + 1 + hop <= size - 1

        def landing(way, hop):
            block = me - 1 - hop if way == 0 else me + 1 + hop
            return pltpu.make_async_remote_copy(
                src_ref=every.at[block],
                dst_ref=every.at[block],
                send_sem=sent.at[way, hop],
                recv_sem=arrived.at[way, hop],
                device_id={"seq": toward},
                device_id_type=MESH,
            )

        def forward(hop):
            for way in (0, 1):
                if hop > 0:

                    @pl.when(receives(way, hop - 1))
                    def _(way=way):
                        landing(way, hop - 1).wait_recv()

                if hop < size - 1:

                    @pl.when(sends(way, hop))
                    def _(way=way):
                        passes(way, hop).start()

        forward(0)

    @pl.when(end)
    def _():
        for piece in pieces:
            outwards(*piece).wait_recv()
        for piece in pieces:
            inwards(*piece).wait_send()

    @pl.when(jnp.logical_not(end))
    def _():
        lag = min(count, len(pieces))
        steps = len(pieces) + lag
        for step in range(steps):
            if shares and step in (steps // 3, 2 * steps // 3):
                forward(1 if step == steps // 3 else 2)
            if step < len(pieces):
                piece = pieces[step]
                inwards(*piece).wait_recv()
                _, index, cut = piece
                both = ins[index][cut].astype(f32) + outer[index][cut].astype(f32)
                partial[index][cut] = both.astype(bf16)
                swap(*piece).start()
            if step >= lag:
                piece = pieces[step - lag]
                swap(*piece).wait_recv()
                _, index, cut = piece
                both = partial[index][cut].astype(f32) + inner[index][cut].astype(f32)
                outs[index][cut] = both.astype(bf16)
                outwards(*piece).start()
        for piece in pieces:
            swap(*piece).wait_send()
            outwards(*piece).wait_send()

    if shares:

        @pl.when(end)
        def _():
            for hop in range(1, size):
                forward(hop)

        @pl.when(jnp.logical_not(end))
        def _():
            for hop in range(3, size):
                forward(hop)

        for way in (0, 1):
            for hop in range(size - 1):

                @pl.when(sends(way, hop))
                def _(way=way, hop=hop):
                    passes(way, hop).wait_send()


def line_sum(arrays, size, identity, shares=0):
    cuts = []
    shapes = []
    for member in arrays:
        parts = 8
        while parts > 1 and member.shape[0] % (16 * parts):
            parts //= 2
        cuts.append(parts)
        shapes.append((member.shape[0], member.shape[1] - shares))
    hold = [pltpu.VMEM(shape, bf16) for shape in shapes]
    semaphores = [pltpu.SemaphoreType.DMA((sum(cuts),))] * 4
    if shares:
        shapes.append((size, arrays[0].shape[0], shares))
        semaphores += [pltpu.SemaphoreType.DMA((2, size - 1))] * 2
    whole = pl.BlockSpec(memory_space=pltpu.VMEM)
    return pl.pallas_call(
        functools.partial(line_kernel, size, tuple(cuts), shares),
        out_shape=[jax.ShapeDtypeStruct(shape, bf16) for shape in shapes],
        in_specs=[whole] * len(arrays),
        out_specs=[whole] * len(shapes),
        scratch_shapes=hold * 3 + semaphores,
        compiler_params=pltpu.CompilerParams(
            collective_id=identity, has_side_effects=True, vmem_limit_bytes=VMEM_LIMIT
        ),
        cost_estimate=pl.CostEstimate(
            flops=0,
            bytes_accessed=40 * sum(2 * member.size for member in arrays),
            transcendentals=0,
        ),
        name="line_sum",
    )(*arrays)


def sum_slots(arrays, size, identity, shares=0):
    if size == 4:
        return line_sum(arrays, size, identity, shares)
    if shares == 0:
        return lax.psum(tuple(arrays), "seq")
    summed = lax.psum(arrays[0][:, shares:], "seq")
    return summed, lax.all_gather(arrays[0][:, :shares], "seq", axis=0, tiled=False)


def feed_back(grad_out, middle, normed_mid, hidden, active, weights, mid_gain):
    out, expand, contract = weights
    grad_y = grad_out.astype(bf16)
    grad_contract = mm(active, grad_y, TN).astype(bf16)
    grad_contract_bias = jnp.sum(grad_y.astype(f32), axis=0)
    grad_y, grad_contract = lax.optimization_barrier((grad_y, grad_contract))
    grad_hidden = (mm(grad_y, contract, NT) * gelu_slope(hidden)).astype(bf16)
    grad_expand = mm(normed_mid, grad_hidden, TN).astype(bf16)
    grad_expand_bias = jnp.sum(grad_hidden.astype(f32), axis=0)
    grad_normed = mm(grad_hidden, expand, NT)
    grad_normed, grad_expand = lax.optimization_barrier((grad_normed, grad_expand))
    grad_norm, grad_mid_gain, grad_mid_shift = norm_back(middle, mid_gain, grad_normed)
    grad_middle = grad_out + grad_norm
    grad_att = grad_middle.astype(bf16)
    grad_out_bias = jnp.sum(grad_att.astype(f32), axis=0)
    grad_mixed = mm(grad_att, out, NT).astype(bf16)
    small = dict(
        out_bias=grad_out_bias,
        mid_gain=grad_mid_gain,
        mid_shift=grad_mid_shift,
        expand_bias=grad_expand_bias,
        contract_bias=grad_contract_bias,
    )
    return grad_middle, grad_att, grad_mixed, (grad_expand, grad_contract), small


def own_joint(joint_weight, query_bias, value_bias, shards, shard):
    width = joint_weight.shape[0]
    own = width // shards
    weight = lax.dynamic_slice_in_dim(joint_weight.reshape(width, 3, width), shard * own, own, 2)
    bias_q = lax.dynamic_slice_in_dim(query_bias, shard * own, own, 0)
    bias_v = lax.dynamic_slice_in_dim(value_bias, shard * own, own, 0)
    return weight, (bias_q, None, bias_v)


def own_parts(normed_all, weight, biases):
    flat = normed_all.reshape(-1, normed_all.shape[3])
    out = []
    for index in range(3):
        part = mm(flat, weight[:, index])
        if biases[index] is not None:
            part = part + biases[index]
        out.append(part.astype(bf16).reshape(normed_all.shape[:3] + (weight.shape[2],)))
    return out


def by_sender(joint_weight, shards):
    width = joint_weight.shape[0]
    array = joint_weight.reshape(width, 3, shards, width // shards)
    return array.transpose(0, 2, 1, 3).reshape(width, 3 * width)


def joint_back(received, joint_by_sender):
    shards, clips, rows, width = received.shape
    flat = received.reshape(shards, clips * rows, width).transpose(1, 0, 2)
    return mm(flat.reshape(clips * rows, shards * width), joint_by_sender, NT)


def joint_small(columns, owners, shards, shard):
    own = columns.shape[0] // 3
    each = owners // shards
    mine = lax.broadcasted_iota(jnp.int32, (owners, 1), 0) // each == shard

    def full(vector):
        return jnp.where(mine, jnp.tile(vector.reshape(each, -1), (shards, 1)), 0.0)

    return dict(query_bias=full(columns[:own]), value_bias=full(columns[2 * own :]))


ORDER = (
    "pre_gain",
    "pre_shift",
    "query_bias",
    "value_bias",
    "out_bias",
    "mid_gain",
    "mid_shift",
    "expand_bias",
    "contract_bias",
)
BLOCK = (
    "pre_gain",
    "pre_shift",
    "joint",
    "query_bias",
    "value_bias",
    "out",
    "out_bias",
    "mid_gain",
    "mid_shift",
    "expand",
    "expand_bias",
    "contract",
    "contract_bias",
)
FRAMES = 8
GRID = 14
MOST_VISIBLE = FRAMES * max(
    high * wide
    for high in range(1, GRID + 1)
    for wide in range(1, GRID + 1)
    if 2 * high * wide < GRID * GRID
)


def body(fsdp_size, seq_size, tokens, visible, slot_token, positions, *rest):
    e_shard = dict(zip(BLOCK, rest[:13]))
    embed_weight, embed_bias, mask_token = rest[13:16]
    p_shard = dict(zip(BLOCK, rest[16:29]))
    cotangent = rest[29]
    shard = lax.axis_index("seq")
    clips, slots, width = tokens.shape
    span = visible.shape[1]

    e_joint = gather(e_shard["joint"])
    place = lax.broadcasted_iota(jnp.int32, (1, 1, span), 2)
    slot_visible = jnp.any(
        (slot_token[:, :, None] == place) & (visible[:, None, :] > 0), axis=2
    )
    counts = jnp.sum(slot_visible.reshape(clips, seq_size, slots).astype(jnp.int32), axis=2)
    compact = -(-MOST_VISIBLE // (16 * seq_size)) * 16
    fits = (jnp.max(counts) <= compact).astype(f32)

    vectors = [e_shard[name] for name in ORDER] + [embed_bias, mask_token]
    vectors += [p_shard[name] for name in ORDER]
    sizes = [member.shape[0] for member in vectors]
    packed = lax.all_gather(
        pack_rows(vectors + [jnp.full((1,), fits)]), "fsdp", axis=0, tiled=False
    )
    full = unpack_rows(packed, sizes + [1])
    all_fit = jnp.min(full[-1]) > 0.5
    normed = norm_layer(tokens.reshape(-1, width), full[0], full[1])

    operands = (
        tokens,
        slot_visible,
        counts,
        slot_token,
        positions,
        normed,
        e_joint,
        tuple(e_shard[name] for name in ("out", "expand", "contract")),
        embed_weight,
        tuple(p_shard[name] for name in ("joint", "out", "expand", "contract")),
        tuple(full[:-1]),
        cotangent,
    )
    whole = functools.partial(main, fsdp_size, seq_size, slots)
    if compact >= slots:
        results = whole(*operands)
    else:
        results = lax.cond(
            all_fit, functools.partial(main, fsdp_size, seq_size, compact), whole, *operands
        )
    encoded, predicted, grad_tokens, e_sums, embed_sum, p_sums, vector_sum = results
    vector_sum = vector_sum.reshape(-1).astype(f32)
    small = []
    at = 0
    for size in sizes:
        small.append(vector_sum[at : at + size])
        at += size

    def ordered(vec, sums):
        vec = dict(zip(ORDER, vec))
        vec.update(zip(("joint", "out", "expand", "contract"), (x.astype(f32) for x in sums)))
        return tuple(vec[name] for name in BLOCK)

    return (
        encoded,
        predicted,
        grad_tokens,
        *ordered(small[:9], e_sums),
        embed_sum.astype(f32),
        small[9],
        small[10],
        *ordered(small[11:], p_sums),
    )


def main(
    fsdp_size,
    seq_size,
    held,
    tokens,
    slot_visible,
    counts,
    slot_token,
    positions,
    normed,
    e_joint,
    e_shards,
    embed_shard,
    p_shards,
    vectors,
    cotangent,
):
    shard = lax.axis_index("seq")
    clips, slots, width = tokens.shape
    span = slot_visible.shape[1]
    rows = clips * slots
    small_width = cotangent.shape[2]
    head_size = width // HEADS
    small_head = small_width // PHEADS
    whole = held == slots
    e_vec = dict(zip(ORDER, vectors[:9]))
    embed_bias, mask_token = vectors[9:11]
    p_vec = dict(zip(ORDER, vectors[11:]))

    e_out_shard, e_expand_shard, e_contract_shard = e_shards
    p_joint_shard, p_out_shard, p_expand_shard, p_contract_shard = p_shards
    e_out, e_expand = gather(e_out_shard), gather(e_expand_shard)

    own_visible = lax.dynamic_slice_in_dim(slot_visible, shard * slots, slots, 1)
    own_flat = own_visible.reshape(rows, 1)
    own_tokens = lax.dynamic_slice_in_dim(slot_token, shard * slots, slots, 1)
    slot_code = jnp.take(positions, own_tokens.reshape(rows), axis=0)

    if whole:
        kept = slot_visible.reshape(clips, 1, span)

        def keep(array):
            return array

        def put_back(array):
            return array

    else:
        kept = lax.broadcasted_iota(jnp.int32, (1, 1, held), 2) < counts[:, :, None]
        kept = kept.reshape(clips, 1, seq_size * held)
        ones = own_visible.astype(bf16)
        before = lax.broadcasted_iota(jnp.int32, (slots, slots), 0)
        after = lax.broadcasted_iota(jnp.int32, (slots, slots), 1)
        rank = mm(ones, (before < after).astype(bf16)).astype(jnp.int32)
        target = lax.broadcasted_iota(jnp.int32, (1, held, 1), 1)
        picks = ((rank[:, None, :] == target) & own_visible[:, None, :]).astype(bf16)

        def keep(array):
            precision = lax.Precision.HIGHEST if array.dtype == f32 else None
            picked = jnp.einsum(
                "crs,csw->crw",
                picks.astype(array.dtype),
                array.reshape(clips, slots, -1),
                precision=precision,
                preferred_element_type=f32,
            )
            return picked.astype(array.dtype).reshape(clips * held, -1)

        def put_back(array):
            placed = jnp.einsum(
                "crs,crw->csw",
                picks.astype(f32),
                array.reshape(clips, held, -1),
                precision=lax.Precision.HIGHEST,
                preferred_element_type=f32,
            )
            return placed.reshape(rows, -1)

    bias = jnp.where(kept, 0.0, -1e30).astype(f32)
    tiled = held % 16 == 0

    def by_clip(array):
        if tiled:
            return array
        shards, count, length, lanes = array.shape
        return array.transpose(1, 0, 2, 3).reshape(1, count, shards * length, lanes)

    inputs = tokens.reshape(rows, width)
    normed_kept = keep(normed).reshape(1, clips, held, width)
    normed_all = exchange(jnp.broadcast_to(normed_kept, (seq_size, clips, held, width)))
    embed, p_joint, p_out = gather(embed_shard), gather(p_joint_shard), gather(p_out_shard)
    e_by_sender = by_sender(e_joint, seq_size)
    normed_all, embed, p_joint, p_out, e_by_sender = lax.optimization_barrier(
        (normed_all, embed, p_joint, p_out, e_by_sender)
    )
    queries = (mm(normed, e_joint[:, :width]) + e_vec["query_bias"]).astype(bf16)
    joined = mm(normed_all.reshape(-1, width), e_joint[:, width:])
    joined_bias = jnp.concatenate([jnp.zeros_like(e_vec["value_bias"]), e_vec["value_bias"]])
    joined = (joined + joined_bias).astype(bf16)
    joined, e_contract_shard = lax.optimization_barrier((joined, e_contract_shard))
    e_contract = gather(e_contract_shard)
    mixed = attend(
        queries.reshape(clips, slots, width),
        by_clip(joined.reshape(seq_size, clips, held, 2 * width)),
        head_size,
        bias,
    ).reshape(rows, width)
    mixed, p_expand_shard = lax.optimization_barrier((mixed, p_expand_shard))
    p_expand = gather(p_expand_shard)
    middle = inputs + mm(mixed, e_out) + e_vec["out_bias"]
    normed_mid = norm_layer(middle, e_vec["mid_gain"], e_vec["mid_shift"])
    active = gelu(mm(normed_mid, e_expand) + e_vec["expand_bias"])
    encoded = middle + mm(active, e_contract) + e_vec["contract_bias"]
    context = encoded.astype(bf16)

    embedded = mm(context, embed) + embed_bias
    pred_input = jnp.where(own_flat, embedded, mask_token) + slot_code
    p_normed = norm_layer(pred_input, p_vec["pre_gain"], p_vec["pre_shift"])
    (
        p_normed,
        rows_all,
        mid_rows,
        mixed_rows,
        middle_rows,
        e_vec["query_bias"],
        e_vec["value_bias"],
        p_vec["query_bias"],
        p_vec["value_bias"],
    ) = lax.optimization_barrier(
        (
            p_normed,
            normed_all,
            normed_mid,
            mixed,
            middle,
            e_vec["query_bias"],
            e_vec["value_bias"],
            p_vec["query_bias"],
            p_vec["value_bias"],
        )
    )
    p_queries = (mm(p_normed, p_joint[:, :small_width]) + p_vec["query_bias"]).astype(bf16)
    own_weight, own_bias = own_joint(
        e_joint, e_vec["query_bias"], e_vec["value_bias"], seq_size, shard
    )
    own_qkv = [by_clip(member) for member in own_parts(rows_all, own_weight, own_bias)]
    p_bias = jnp.concatenate([jnp.zeros_like(p_vec["value_bias"]), p_vec["value_bias"]])
    p_normed_all = []
    p_mixed = []
    everyone = [
        lax.all_gather(p_normed.reshape(clips, slots, small_width)[clip], "seq", axis=0, tiled=True)
        for clip in range(clips)
    ]
    p_contract_shard, p_expand, everyone[0] = lax.optimization_barrier(
        (p_contract_shard, p_expand, everyone[0])
    )
    p_contract = gather(p_contract_shard)
    for clip in range(clips):
        every = everyone[clip]
        if clip > 0:
            every, p_mixed[-1] = lax.optimization_barrier((every, p_mixed[-1]))
        p_joined = (mm(every, p_joint[:, small_width:]) + p_bias).astype(bf16)
        p_normed_all.append(every)
        p_mixed.append(
            attend(
                p_queries.reshape(clips, slots, small_width)[clip : clip + 1],
                p_joined.reshape(1, 1, span, 2 * small_width),
                small_head,
                None,
            )
        )
    kept_mid, kept_mixed, kept_middle, kept_inputs = (
        keep(member) for member in (mid_rows, mixed_rows, middle_rows, inputs)
    )
    p_mixed[0], kept_mid, kept_mixed, kept_middle, kept_inputs, *own_qkv = (
        lax.optimization_barrier(
            (p_mixed[0], kept_mid, kept_mixed, kept_middle, kept_inputs, *own_qkv)
        )
    )
    p_mixed = jnp.concatenate(p_mixed, axis=0).reshape(rows, small_width)
    p_middle = pred_input + mm(p_mixed, p_out) + p_vec["out_bias"]
    p_normed_mid = norm_layer(p_middle, p_vec["mid_gain"], p_vec["mid_shift"])
    p_hidden = mm(p_normed_mid, p_expand) + p_vec["expand_bias"]
    p_active = gelu(p_hidden)
    predicted = p_middle + mm(p_active, p_contract) + p_vec["contract_bias"]

    grad_middle, grad_att, grad_mixed, p_grads, p_small = feed_back(
        cotangent.reshape(rows, small_width),
        p_middle,
        p_normed_mid,
        p_hidden,
        p_active,
        (p_out, p_expand, p_contract),
        p_vec["mid_gain"],
    )
    p_grad_out = mm(p_mixed, grad_att, TN).astype(bf16)
    p_wide = jnp.concatenate([p_grad_out, p_grads[0]], axis=1)
    p_tall = p_grads[1]
    grad_mixed, p_wide, p_tall = lax.optimization_barrier((grad_mixed, p_wide, p_tall))
    p_wide, p_tall = scatter(p_wide), scatter(p_tall)
    own_weight, own_bias = own_joint(
        p_joint, p_vec["query_bias"], p_vec["value_bias"], seq_size, shard
    )
    own_width = small_width // seq_size
    grad_mixed = grad_mixed.reshape(rows, seq_size, own_width).transpose(1, 0, 2)
    grad_mixed = exchange(grad_mixed.reshape(seq_size, clips, slots, own_width))
    p_by_sender = by_sender(p_joint, seq_size)
    grad_normed = []
    p_grad_joint = 0.0
    p_columns = 0.0
    for clip in range(clips):
        every = p_normed_all[clip].reshape(1, 1, span, small_width)
        grads = attend_back(
            *own_parts(every, own_weight, own_bias),
            grad_mixed[:, clip].reshape(1, 1, span, own_width),
            0,
            small_head,
            None,
            seq_size,
        )
        if clip == 0:
            grads, p_wide, p_tall = lax.optimization_barrier((grads, p_wide, p_tall))
        flat = grads.reshape(span, 3 * own_width)
        p_grad_joint = p_grad_joint + mm(p_normed_all[clip], flat, TN)
        p_columns = p_columns + jnp.sum(flat.astype(f32), axis=0)
        grad_normed.append(joint_back(exchange(grads), p_by_sender))
    p_small.update(joint_small(p_columns, fsdp_size, seq_size, shard))
    p_own_width = own_width
    grad_norm, p_small["pre_gain"], p_small["pre_shift"] = norm_back(
        pred_input, p_vec["pre_gain"], jnp.concatenate(grad_normed, axis=0)
    )
    grad_pred_input = grad_middle + grad_norm
    grad_mask_token = jnp.sum(jnp.where(own_flat, 0.0, grad_pred_input), axis=0)
    grad_embedded = jnp.where(own_flat, grad_pred_input, 0.0).astype(bf16)
    grad_embed_bias = jnp.sum(grad_embedded.astype(f32), axis=0)

    grad_embedded, predicted = lax.optimization_barrier((grad_embedded, predicted))
    grad_context = mm(keep(grad_embedded), embed, NT)
    kept_hidden = mm(kept_mid, e_expand) + e_vec["expand_bias"]
    grad_middle, grad_att, grad_mixed, e_grads, e_small = feed_back(
        grad_context,
        kept_middle,
        kept_mid,
        kept_hidden,
        gelu(kept_hidden),
        (e_out, e_expand, e_contract),
        e_vec["mid_gain"],
    )
    expand_part, contract_part = scatter(e_grads[0]), scatter(e_grads[1])
    own_width = width // seq_size
    grad_mixed = grad_mixed.reshape(clips * held, seq_size, own_width).transpose(1, 0, 2)
    grad_mixed = by_clip(exchange(grad_mixed.reshape(seq_size, clips, held, own_width)))
    grads = [
        attend_back(*own_qkv, grad_mixed, clip, head_size, bias, seq_size) for clip in range(clips)
    ]
    grads[-1], grad_att, late_embedded = lax.optimization_barrier(
        (grads[-1], grad_att, grad_embedded)
    )
    received = [exchange(member) for member in grads]
    received[0], contract_part = lax.optimization_barrier((received[0], contract_part))
    flat = jnp.concatenate(grads, axis=1).reshape(-1, 3 * own_width)
    e_grad_joint = mm(normed_all.reshape(-1, width), flat, TN).astype(bf16)
    e_grad_out = mm(kept_mixed, grad_att, TN).astype(bf16)
    grad_embed = mm(context, late_embedded, TN).astype(bf16)
    e_small.update(joint_small(jnp.sum(flat.astype(f32), axis=0), fsdp_size, seq_size, shard))
    grad_normed = jnp.concatenate([joint_back(member, e_by_sender) for member in received], axis=0)
    grad_norm, e_small["pre_gain"], e_small["pre_shift"] = norm_back(
        kept_inputs, e_vec["pre_gain"], grad_normed
    )

    own_rows = width // fsdp_size
    p_rows = small_width // fsdp_size
    p_lanes = -(-3 * p_own_width // 128) * 128
    p_grad_joint = p_grad_joint.astype(bf16).reshape(fsdp_size, p_rows, 3 * p_own_width)
    p_grad_joint = jnp.pad(
        p_grad_joint, ((0, 0), (0, own_rows - p_rows), (0, p_lanes - 3 * p_own_width))
    ).reshape(width, p_lanes)
    small = [e_small[name] for name in ORDER] + [grad_embed_bias, grad_mask_token]
    small += [p_small[name] for name in ORDER]
    small = [member.reshape(fsdp_size, -1) for member in small]
    sizes = [member.shape[1] for member in small]
    small.append(jnp.zeros((fsdp_size, own_rows * 128 - sum(sizes)), f32))
    small = jnp.concatenate(small, axis=1).astype(bf16).reshape(width, 128)
    late = scatter(jnp.concatenate([e_grad_joint, p_grad_joint, e_grad_out, grad_embed, small], axis=1))
    grad_tokens = put_back(grad_middle + grad_norm)

    first = 0 if whole else 2
    contract_sum, expand_sum, p_wide_sum, p_contract_sum = sum_slots(
        (contract_part, expand_part, p_wide, p_tall), seq_size, first
    )
    late, expand_sum = lax.optimization_barrier((late, expand_sum))
    shared = 3 * own_width + p_lanes
    late_sum, columns = sum_slots((late,), seq_size, first + 1, shared)
    e_joint_sum = columns[:, :, : 3 * own_width].reshape(seq_size, own_rows, 3, own_width)
    e_joint_sum = e_joint_sum.transpose(1, 2, 0, 3).reshape(own_rows, 3 * width)
    p_joint_sum = columns[:, :p_rows, 3 * own_width : 3 * (own_width + p_own_width)]
    p_joint_sum = p_joint_sum.reshape(seq_size, p_rows, 3, p_own_width)
    p_joint_sum = p_joint_sum.transpose(1, 2, 0, 3).reshape(p_rows, 3 * small_width)
    out_sum = late_sum[:, :width]
    embed_sum = late_sum[:, width : width + small_width]
    p_out_sum, p_expand_sum = p_wide_sum[:, :small_width], p_wide_sum[:, small_width:]
    return (
        encoded.reshape(tokens.shape),
        predicted.reshape(cotangent.shape),
        grad_tokens.reshape(tokens.shape),
        (e_joint_sum, out_sum, expand_sum, contract_sum),
        embed_sum,
        (p_joint_sum, p_out_sum, p_expand_sum, p_contract_sum),
        late_sum[:, width + small_width :],
    )


def solution(mesh):
    cut, rows, vec, full = P("fsdp", "seq", None), P("fsdp", None), P("fsdp"), P()
    block = (vec, vec, rows, vec, vec, rows, vec, vec, vec, rows, vec, rows, vec)
    return jax.shard_map(
        functools.partial(body, mesh.shape["fsdp"], mesh.shape["seq"]),
        mesh=mesh,
        in_specs=(cut, rows, rows, full, *block, rows, vec, vec, *block, cut),
        out_specs=(cut, cut, cut, *block, rows, vec, vec, *block),
        check_vma=False,
    )
```

```python
import functools
import math

import jax
import jax.numpy as jnp
from jax import lax
from jax.experimental import pallas as pl
from jax.experimental.pallas import tpu as pltpu
from jax.sharding import PartitionSpec as P

HEADS = 16
PHEADS = 12

f32 = jnp.float32
bf16 = jnp.bfloat16
norm_eps = 1e-06
LOG2E = math.log2(math.e)
NN = (((1,), (0,)), ((), ()))
NT = (((1,), (1,)), ((), ()))
TN = (((0,), (0,)), ((), ()))
VMEM_LIMIT = 60 * 2**20


def mm(left, right, dims=NN):
    return lax.dot_general(left, right, dims, preferred_element_type=f32)


def norm_parts(value):
    center = value - jnp.mean(value, axis=-1, keepdims=True)
    spread = jnp.mean(center * center, axis=-1, keepdims=True)
    scale = lax.rsqrt(spread + norm_eps)
    return center * scale, scale


def norm_layer(value, gain, shift):
    unit, _ = norm_parts(value)
    return (unit * gain + shift).astype(bf16)


def norm_back_kernel(grad_ref, value_ref, gain_ref, other_ref, total_ref, low_ref, sums_ref):
    grad = grad_ref[...]
    value = value_ref[...]
    center = value - jnp.mean(value, axis=1, keepdims=True)
    scale = lax.rsqrt(jnp.mean(center * center, axis=1, keepdims=True) + norm_eps)
    unit = center * scale
    inner = grad * gain_ref[...]
    inner = inner - jnp.mean(inner, axis=1, keepdims=True) - unit * jnp.mean(
        inner * unit, axis=1, keepdims=True
    )
    total = other_ref[...] + scale * inner
    low = total.astype(bf16)
    total_ref[...] = total
    low_ref[...] = low
    rows = [
        jnp.sum(grad * unit, axis=0, keepdims=True),
        jnp.sum(grad, axis=0, keepdims=True),
        jnp.sum(low.astype(f32), axis=0, keepdims=True),
    ]

    @pl.when(pl.program_id(0) == 0)
    def _():
        sums_ref[...] = jnp.zeros_like(sums_ref)

    for index, row in enumerate(rows):
        sums_ref[index : index + 1] += row


def norm_back(value, gain, grad, other):
    rows, width = value.shape
    block = max(size for size in range(8, 136, 8) if rows % size == 0)
    by_row = pl.BlockSpec((block, width), lambda i: (i, 0))
    total, low, sums = pl.pallas_call(
        norm_back_kernel,
        grid=(rows // block,),
        in_specs=[by_row, by_row, pl.BlockSpec((1, width), lambda i: (0, 0)), by_row],
        out_specs=[by_row, by_row, pl.BlockSpec((8, width), lambda i: (0, 0))],
        out_shape=[
            jax.ShapeDtypeStruct((rows, width), f32),
            jax.ShapeDtypeStruct((rows, width), bf16),
            jax.ShapeDtypeStruct((8, width), f32),
        ],
        cost_estimate=pl.CostEstimate(
            flops=20 * rows * width, bytes_accessed=18 * rows * width, transcendentals=rows
        ),
        name="norm_back",
    )(grad, value, gain.reshape(1, width), other)
    return total, low, sums[0], sums[1], sums[2]


def gelu_parts(hidden):
    cdf = 0.5 * (1.0 + lax.erf(hidden * math.sqrt(0.5)))
    return cdf


def gelu(hidden):
    return (hidden * gelu_parts(hidden)).astype(bf16)


def gelu_slope(hidden):
    pdf = jnp.exp(-0.5 * hidden * hidden) * (1.0 / math.sqrt(2.0 * math.pi))
    return gelu_parts(hidden) + hidden * pdf


def forward_kernel(scale, head_size, q_ref, k_ref, v_ref, *rest):
    if len(rest) == 2:
        bias_ref, o_ref = rest
    else:
        bias_ref, o_ref = None, rest[0]
    query = q_ref[0]
    lanes = query.shape[1]
    key = k_ref[...].reshape(-1, lanes)
    value = v_ref[...].reshape(-1, lanes)
    lane = lax.broadcasted_iota(jnp.int32, query.shape, 1)
    result = None
    for head in range(lanes // head_size):
        mine = (lane // head_size) == head
        own_query = jnp.where(mine, query, jnp.zeros_like(query))
        scores = mm(own_query, key, NT) * (scale * LOG2E)
        if bias_ref is not None:
            scores = scores + bias_ref[0]
        top = jnp.max(scores, axis=1, keepdims=True)
        weight = jnp.exp2(scores - top)
        total = jnp.sum(weight, axis=1, keepdims=True)
        part = jnp.where(mine, mm(weight.astype(bf16), value) / total, 0.0)
        result = part if result is None else result + part
    o_ref[0] = result.astype(bf16)


def attend(queries, joined, head_size, bias):
    clips, rows, width = queries.shape
    major, _, length, _ = joined.shape
    keys = major * length
    groups = width // 128
    in_specs = [
        pl.BlockSpec((1, rows, 128), lambda c, g: (c, 0, g)),
        pl.BlockSpec((major, 1, length, 128), lambda c, g: (0, c, 0, g)),
        pl.BlockSpec((major, 1, length, 128), lambda c, g: (0, c, 0, g + groups)),
    ]
    operands = [queries, joined, joined]
    if bias is not None:
        in_specs.append(pl.BlockSpec((1, 1, keys), lambda c, g: (c, 0, 0)))
        operands.append(bias)
    cells = clips * rows * keys * (width // head_size)
    return pl.pallas_call(
        functools.partial(forward_kernel, 1.0 / math.sqrt(head_size), head_size),
        grid=(clips, groups),
        in_specs=in_specs,
        out_specs=pl.BlockSpec((1, rows, 128), lambda c, g: (c, 0, g)),
        out_shape=jax.ShapeDtypeStruct((clips, rows, width), bf16),
        compiler_params=pltpu.CompilerParams(vmem_limit_bytes=VMEM_LIMIT),
        cost_estimate=pl.CostEstimate(
            flops=cells * 1024, bytes_accessed=4 * clips * keys * width, transcendentals=cells
        ),
        name="attend",
    )(*operands)


def backward_kernel(scale, head_size, shards, q_ref, k_ref, v_ref, g_ref, *rest):
    if len(rest) == 4:
        bias_ref = rest[0]
        rest = rest[1:]
    else:
        bias_ref = None
    out_ref, dk_sum, dv_sum = rest
    group = pl.program_id(0)
    part = pl.program_id(1)
    lanes = q_ref.shape[-1]
    query = q_ref[...].reshape(-1, lanes)
    key = k_ref[...].reshape(-1, lanes)
    value = v_ref[...].reshape(-1, lanes)
    grad = g_ref[...].reshape(-1, lanes)
    lane = lax.broadcasted_iota(jnp.int32, query.shape, 1)
    key_lane = lax.broadcasted_iota(jnp.int32, key.shape, 1)
    sums = None
    for head in range(lanes // head_size):
        mine = (lane // head_size) == head
        own_query = jnp.where(mine, query, jnp.zeros_like(query))
        own_grad = jnp.where(mine, grad, jnp.zeros_like(grad))
        own_key = jnp.where((key_lane // head_size) == head, key, jnp.zeros_like(key))
        scores = mm(own_query, key, NT) * (scale * LOG2E)
        if bias_ref is not None:
            scores = scores + bias_ref[0]
        top = jnp.max(scores, axis=1, keepdims=True)
        weight = jnp.exp2(scores - top)
        chance = weight * (1.0 / jnp.sum(weight, axis=1, keepdims=True))
        grad_chance = mm(own_grad, value, NT)
        delta = jnp.sum(chance * grad_chance, axis=1, keepdims=True)
        grad_scores = (chance * (grad_chance - delta)).astype(bf16)
        terms = (
            mm(grad_scores, own_key),
            mm(own_query, grad_scores, TN),
            mm(own_grad, chance.astype(bf16), TN),
        )
        sums = terms if sums is None else tuple(x + y for x, y in zip(sums, terms))
    part_q, part_k, part_v = sums

    @pl.when(part == 0)
    def _():
        dk_sum[...] = part_k
        dv_sum[...] = part_v

    @pl.when(part > 0)
    def _():
        dk_sum[...] += part_k
        dv_sum[...] += part_v

    rows = out_ref.shape[2]
    width = out_ref.shape[3] // 3
    held = query.shape[0] // rows

    def place(kind):
        if width == lanes:
            return slice(kind * width, (kind + 1) * width)
        return pl.ds(pl.multiple_of(kind * width + group * lanes, 128), lanes)

    result_q = (part_q * scale).astype(bf16)
    for index in range(held):
        out_ref[part * held + index, 0, :, place(0)] = result_q[index * rows : (index + 1) * rows]

    @pl.when(part == pl.num_programs(1) - 1)
    def _():
        for kind, total_ref, factor in ((1, dk_sum, scale), (2, dv_sum, 1.0)):
            result = (total_ref[...] * factor).T.astype(bf16)
            for index in range(shards):
                out_ref[index, 0, :, place(kind)] = result[index * rows : (index + 1) * rows]


def attend_back(queries, keys, values, grad_mixed, clip, head_size, bias, shards):
    major, _, length, width = queries.shape
    lanes = min(width, 128)
    groups = width // lanes
    rows = major * length // shards
    parts = shards if major == 1 else 1
    query_rows = rows if major == 1 else length
    by_query = pl.BlockSpec((major, 1, query_rows, lanes), lambda g, r: (0, clip, r, g))
    by_key = pl.BlockSpec((major, 1, length, lanes), lambda g, r: (0, clip, 0, g))
    in_specs = [by_query, by_key, by_key, by_query]
    operands = [queries, keys, values, grad_mixed]
    total = major * length
    if bias is not None:
        in_specs.append(pl.BlockSpec((1, 1, total), lambda g, r: (clip, 0, 0)))
        operands.append(bias)
    cells = total * total * (width // head_size)
    return pl.pallas_call(
        functools.partial(backward_kernel, 1.0 / math.sqrt(head_size), head_size, shards),
        grid=(groups, parts),
        in_specs=in_specs,
        out_specs=pl.BlockSpec((shards, 1, rows, 3 * width), lambda g, r: (0, 0, 0, 0)),
        out_shape=jax.ShapeDtypeStruct((shards, 1, rows, 3 * width), bf16),
        scratch_shapes=[pltpu.VMEM((lanes, total), f32), pltpu.VMEM((lanes, total), f32)],
        compiler_params=pltpu.CompilerParams(vmem_limit_bytes=VMEM_LIMIT),
        cost_estimate=pl.CostEstimate(
            flops=cells * 2560, bytes_accessed=14 * total * width, transcendentals=cells
        ),
        name="attend_back",
    )(*operands)


def exchange(array):
    return lax.all_to_all(array, "seq", split_axis=0, concat_axis=0, tiled=True)


def gather(array):
    return lax.all_gather(array, "fsdp", axis=0, tiled=True)


def scatter(array):
    return lax.psum_scatter(array, "fsdp", scatter_dimension=0, tiled=True)


def pack_rows(vectors):
    rows = []
    for member in vectors:
        count = -(-member.shape[0] // 128)
        padded = jnp.pad(member.astype(f32), (0, count * 128 - member.shape[0]))
        rows.append(padded.reshape(count, 128))
    total = sum(member.shape[0] for member in rows)
    if total % 8:
        rows.append(jnp.zeros((8 - total % 8, 128), f32))
    return jnp.concatenate(rows, axis=0)


def unpack_rows(packed, sizes):
    out = []
    at = 0
    for size in sizes:
        count = -(-size // 128)
        piece = packed[:, at : at + count].reshape(packed.shape[0], count * 128)[:, :size]
        out.append(piece.reshape(-1))
        at += count
    return out


MESH = pl.DeviceIdType.MESH


def line_kernel(size, cuts, shares, *refs):
    count = len(cuts)
    ins, outs = refs[:count], refs[count : 2 * count]
    if shares:
        ins, own, outs, every = (refs[0].at[:, shares:],), refs[0].at[:, :shares], refs[1:2], refs[2]
    scratch = refs[3 if shares else 2 * count :]
    inner, outer, partial = (scratch[i * count : (i + 1) * count] for i in range(3))
    to_inner, to_outer, from_inner, from_outer = scratch[3 * count : 3 * count + 4]
    me = lax.axis_index("seq")
    left = me < size // 2
    toward = jnp.where(left, me + 1, me - 1)
    away = jnp.where(left, me - 1, me + 1)
    end = (me == 0) | (me == size - 1)
    barrier = pltpu.get_barrier_semaphore()
    pl.semaphore_signal(barrier, inc=1, device_id={"seq": toward}, device_id_type=MESH)

    @pl.when(jnp.logical_not(end))
    def _():
        pl.semaphore_signal(barrier, inc=1, device_id={"seq": away}, device_id_type=MESH)
        pl.semaphore_wait(barrier, 2)

    @pl.when(end)
    def _():
        pl.semaphore_wait(barrier, 1)

    pieces = []
    for index, parts in enumerate(cuts):
        rows = ins[index].shape[0] // parts
        for part in range(parts):
            pieces.append((part / parts, index, slice(part * rows, (part + 1) * rows)))
    pieces.sort(key=lambda piece: piece[:2])
    pieces = [(slot, index, cut) for slot, (_, index, cut) in enumerate(pieces)]

    def inwards(slot, index, cut):
        return pltpu.make_async_remote_copy(
            src_ref=ins[index].at[cut],
            dst_ref=outer[index].at[cut],
            send_sem=to_inner.at[slot],
            recv_sem=from_outer.at[slot],
            device_id={"seq": toward},
            device_id_type=MESH,
        )

    def swap(slot, index, cut):
        return pltpu.make_async_remote_copy(
            src_ref=partial[index].at[cut],
            dst_ref=inner[index].at[cut],
            send_sem=to_inner.at[slot],
            recv_sem=from_inner.at[slot],
            device_id={"seq": toward},
            device_id_type=MESH,
        )

    def outwards(slot, index, cut):
        return pltpu.make_async_remote_copy(
            src_ref=outs[index].at[cut],
            dst_ref=outs[index].at[cut],
            send_sem=to_outer.at[slot],
            recv_sem=from_inner.at[slot],
            device_id={"seq": away},
            device_id_type=MESH,
        )

    @pl.when(end)
    def _():
        for piece in pieces:
            inwards(*piece).start()

    if shares:
        sent, arrived = scratch[3 * count + 4 :]
        every[me] = own[...]

        def passes(way, hop):
            step = 1 - 2 * way
            block = me - step * hop
            return pltpu.make_async_remote_copy(
                src_ref=own if hop == 0 else every.at[block],
                dst_ref=every.at[block],
                send_sem=sent.at[way, hop],
                recv_sem=arrived.at[way, hop],
                device_id={"seq": me + step},
                device_id_type=MESH,
            )

        def sends(way, hop):
            if way == 0:
                return (me < size - 1) & (me - hop >= 0)
            return (me > 0) & (me + hop <= size - 1)

        def receives(way, hop):
            return me - 1 - hop >= 0 if way == 0 else me + 1 + hop <= size - 1

        def landing(way, hop):
            block = me - 1 - hop if way == 0 else me + 1 + hop
            return pltpu.make_async_remote_copy(
                src_ref=every.at[block],
                dst_ref=every.at[block],
                send_sem=sent.at[way, hop],
                recv_sem=arrived.at[way, hop],
                device_id={"seq": toward},
                device_id_type=MESH,
            )

        def forward(hop):
            for way in (0, 1):
                if hop > 0:

                    @pl.when(receives(way, hop - 1))
                    def _(way=way):
                        landing(way, hop - 1).wait_recv()

                if hop < size - 1:

                    @pl.when(sends(way, hop))
                    def _(way=way):
                        passes(way, hop).start()

        forward(0)

    @pl.when(end)
    def _():
        for piece in pieces:
            outwards(*piece).wait_recv()
        for piece in pieces:
            inwards(*piece).wait_send()

    @pl.when(jnp.logical_not(end))
    def _():
        lag = min(count, len(pieces))
        steps = len(pieces) + lag
        for step in range(steps):
            if shares and step in (steps // 3, 2 * steps // 3):
                forward(1 if step == steps // 3 else 2)
            if step < len(pieces):
                piece = pieces[step]
                inwards(*piece).wait_recv()
                _, index, cut = piece
                both = ins[index][cut].astype(f32) + outer[index][cut].astype(f32)
                partial[index][cut] = both.astype(bf16)
                swap(*piece).start()
            if step >= lag:
                piece = pieces[step - lag]
                swap(*piece).wait_recv()
                _, index, cut = piece
                both = partial[index][cut].astype(f32) + inner[index][cut].astype(f32)
                outs[index][cut] = both.astype(bf16)
                outwards(*piece).start()
        for piece in pieces:
            swap(*piece).wait_send()
            outwards(*piece).wait_send()

    if shares:

        @pl.when(end)
        def _():
            for hop in range(1, size):
                forward(hop)

        @pl.when(jnp.logical_not(end))
        def _():
            for hop in range(3, size):
                forward(hop)

        for way in (0, 1):
            for hop in range(size - 1):

                @pl.when(sends(way, hop))
                def _(way=way, hop=hop):
                    passes(way, hop).wait_send()


def line_sum(arrays, size, identity, shares=0):
    cuts = []
    shapes = []
    for member in arrays:
        parts = 8
        while parts > 1 and member.shape[0] % (16 * parts):
            parts //= 2
        cuts.append(parts)
        shapes.append((member.shape[0], member.shape[1] - shares))
    hold = [pltpu.VMEM(shape, bf16) for shape in shapes]
    semaphores = [pltpu.SemaphoreType.DMA((sum(cuts),))] * 4
    if shares:
        shapes.append((size, arrays[0].shape[0], shares))
        semaphores += [pltpu.SemaphoreType.DMA((2, size - 1))] * 2
    whole = pl.BlockSpec(memory_space=pltpu.VMEM)
    return pl.pallas_call(
        functools.partial(line_kernel, size, tuple(cuts), shares),
        out_shape=[jax.ShapeDtypeStruct(shape, bf16) for shape in shapes],
        in_specs=[whole] * len(arrays),
        out_specs=[whole] * len(shapes),
        scratch_shapes=hold * 3 + semaphores,
        compiler_params=pltpu.CompilerParams(
            collective_id=identity, has_side_effects=True, vmem_limit_bytes=VMEM_LIMIT
        ),
        cost_estimate=pl.CostEstimate(
            flops=0,
            bytes_accessed=40 * sum(2 * member.size for member in arrays),
            transcendentals=0,
        ),
        name="line_sum",
    )(*arrays)


def sum_slots(arrays, size, identity, shares=0):
    if size == 4:
        return line_sum(arrays, size, identity, shares)
    if shares == 0:
        return lax.psum(tuple(arrays), "seq")
    summed = lax.psum(arrays[0][:, shares:], "seq")
    return summed, lax.all_gather(arrays[0][:, :shares], "seq", axis=0, tiled=False)


def feed_back(grad_out, middle, normed_mid, hidden, active, weights, mid_gain):
    out, expand, contract = weights
    grad_y = grad_out.astype(bf16)
    grad_contract = mm(active, grad_y, TN).astype(bf16)
    grad_contract_bias = jnp.sum(grad_y.astype(f32), axis=0)
    grad_y, grad_contract = lax.optimization_barrier((grad_y, grad_contract))
    grad_hidden = (mm(grad_y, contract, NT) * gelu_slope(hidden)).astype(bf16)
    grad_expand = mm(normed_mid, grad_hidden, TN).astype(bf16)
    grad_expand_bias = jnp.sum(grad_hidden.astype(f32), axis=0)
    grad_normed = mm(grad_hidden, expand, NT)
    grad_normed, grad_expand = lax.optimization_barrier((grad_normed, grad_expand))
    grad_middle, grad_att, grad_mid_gain, grad_mid_shift, grad_out_bias = norm_back(
        middle, mid_gain, grad_normed, grad_out
    )
    grad_mixed = mm(grad_att, out, NT).astype(bf16)
    small = dict(
        out_bias=grad_out_bias,
        mid_gain=grad_mid_gain,
        mid_shift=grad_mid_shift,
        expand_bias=grad_expand_bias,
        contract_bias=grad_contract_bias,
    )
    return grad_middle, grad_att, grad_mixed, (grad_expand, grad_contract), small


def own_joint(joint_weight, query_bias, value_bias, shards, shard):
    width = joint_weight.shape[0]
    own = width // shards
    weight = lax.dynamic_slice_in_dim(joint_weight.reshape(width, 3, width), shard * own, own, 2)
    bias_q = lax.dynamic_slice_in_dim(query_bias, shard * own, own, 0)
    bias_v = lax.dynamic_slice_in_dim(value_bias, shard * own, own, 0)
    return weight, (bias_q, None, bias_v)


def own_parts(normed_all, weight, biases):
    flat = normed_all.reshape(-1, normed_all.shape[3])
    out = []
    for index in range(3):
        part = mm(flat, weight[:, index])
        if biases[index] is not None:
            part = part + biases[index]
        out.append(part.astype(bf16).reshape(normed_all.shape[:3] + (weight.shape[2],)))
    return out


def by_sender(joint_weight, shards):
    width = joint_weight.shape[0]
    array = joint_weight.reshape(width, 3, shards, width // shards)
    return array.transpose(0, 2, 1, 3).reshape(width, 3 * width)


def joint_back(received, joint_by_sender):
    shards, clips, rows, width = received.shape
    flat = received.reshape(shards, clips * rows, width).transpose(1, 0, 2)
    return mm(flat.reshape(clips * rows, shards * width), joint_by_sender, NT)


def joint_small(columns, owners, shards, shard):
    own = columns.shape[0] // 3
    each = owners // shards
    mine = lax.broadcasted_iota(jnp.int32, (owners, 1), 0) // each == shard

    def full(vector):
        return jnp.where(mine, jnp.tile(vector.reshape(each, -1), (shards, 1)), 0.0)

    return dict(query_bias=full(columns[:own]), value_bias=full(columns[2 * own :]))


ORDER = (
    "pre_gain",
    "pre_shift",
    "query_bias",
    "value_bias",
    "out_bias",
    "mid_gain",
    "mid_shift",
    "expand_bias",
    "contract_bias",
)
BLOCK = (
    "pre_gain",
    "pre_shift",
    "joint",
    "query_bias",
    "value_bias",
    "out",
    "out_bias",
    "mid_gain",
    "mid_shift",
    "expand",
    "expand_bias",
    "contract",
    "contract_bias",
)
FRAMES = 8
GRID = 14
MOST_VISIBLE = FRAMES * max(
    high * wide
    for high in range(1, GRID + 1)
    for wide in range(1, GRID + 1)
    if 2 * high * wide < GRID * GRID
)


def body(fsdp_size, seq_size, tokens, visible, slot_token, positions, *rest):
    e_shard = dict(zip(BLOCK, rest[:13]))
    embed_weight, embed_bias, mask_token = rest[13:16]
    p_shard = dict(zip(BLOCK, rest[16:29]))
    cotangent = rest[29]
    shard = lax.axis_index("seq")
    clips, slots, width = tokens.shape
    span = visible.shape[1]

    e_joint = gather(e_shard["joint"])
    place = lax.broadcasted_iota(jnp.int32, (1, 1, span), 2)
    slot_visible = jnp.any(
        (slot_token[:, :, None] == place) & (visible[:, None, :] > 0), axis=2
    )
    counts = jnp.sum(slot_visible.reshape(clips, seq_size, slots).astype(jnp.int32), axis=2)
    compact = -(-MOST_VISIBLE // (16 * seq_size)) * 16
    fits = (jnp.max(counts) <= compact).astype(f32)

    vectors = [e_shard[name] for name in ORDER] + [embed_bias, mask_token]
    vectors += [p_shard[name] for name in ORDER]
    sizes = [member.shape[0] for member in vectors]
    packed = lax.all_gather(
        pack_rows(vectors + [jnp.full((1,), fits)]), "fsdp", axis=0, tiled=False
    )
    full = unpack_rows(packed, sizes + [1])
    all_fit = jnp.min(full[-1]) > 0.5
    normed = norm_layer(tokens.reshape(-1, width), full[0], full[1])

    operands = (
        tokens,
        slot_visible,
        counts,
        slot_token,
        positions,
        normed,
        e_joint,
        tuple(e_shard[name] for name in ("out", "expand", "contract")),
        embed_weight,
        tuple(p_shard[name] for name in ("joint", "out", "expand", "contract")),
        tuple(full[:-1]),
        cotangent,
    )
    whole = functools.partial(main, fsdp_size, seq_size, slots)
    if compact >= slots:
        results = whole(*operands)
    else:
        results = lax.cond(
            all_fit, functools.partial(main, fsdp_size, seq_size, compact), whole, *operands
        )
    encoded, predicted, grad_tokens, e_sums, embed_sum, p_sums, vector_sum = results
    vector_sum = vector_sum.reshape(-1).astype(f32)
    small = []
    at = 0
    for size in sizes:
        small.append(vector_sum[at : at + size])
        at += size

    def ordered(vec, sums):
        vec = dict(zip(ORDER, vec))
        vec.update(zip(("joint", "out", "expand", "contract"), (x.astype(f32) for x in sums)))
        return tuple(vec[name] for name in BLOCK)

    return (
        encoded,
        predicted,
        grad_tokens,
        *ordered(small[:9], e_sums),
        embed_sum.astype(f32),
        small[9],
        small[10],
        *ordered(small[11:], p_sums),
    )


def main(
    fsdp_size,
    seq_size,
    held,
    tokens,
    slot_visible,
    counts,
    slot_token,
    positions,
    normed,
    e_joint,
    e_shards,
    embed_shard,
    p_shards,
    vectors,
    cotangent,
):
    shard = lax.axis_index("seq")
    clips, slots, width = tokens.shape
    span = slot_visible.shape[1]
    rows = clips * slots
    small_width = cotangent.shape[2]
    head_size = width // HEADS
    small_head = small_width // PHEADS
    whole = held == slots
    e_vec = dict(zip(ORDER, vectors[:9]))
    embed_bias, mask_token = vectors[9:11]
    p_vec = dict(zip(ORDER, vectors[11:]))

    e_out_shard, e_expand_shard, e_contract_shard = e_shards
    p_joint_shard, p_out_shard, p_expand_shard, p_contract_shard = p_shards
    e_out, e_expand = gather(e_out_shard), gather(e_expand_shard)

    own_visible = lax.dynamic_slice_in_dim(slot_visible, shard * slots, slots, 1)
    own_flat = own_visible.reshape(rows, 1)
    own_tokens = lax.dynamic_slice_in_dim(slot_token, shard * slots, slots, 1)
    slot_code = jnp.take(positions, own_tokens.reshape(rows), axis=0)

    if whole:
        kept = slot_visible.reshape(clips, 1, span)

        def keep(array):
            return array

        def put_back(array):
            return array

    else:
        kept = lax.broadcasted_iota(jnp.int32, (1, 1, held), 2) < counts[:, :, None]
        kept = kept.reshape(clips, 1, seq_size * held)
        ones = own_visible.astype(bf16)
        before = lax.broadcasted_iota(jnp.int32, (slots, slots), 0)
        after = lax.broadcasted_iota(jnp.int32, (slots, slots), 1)
        rank = mm(ones, (before < after).astype(bf16)).astype(jnp.int32)
        target = lax.broadcasted_iota(jnp.int32, (1, held, 1), 1)
        picks = ((rank[:, None, :] == target) & own_visible[:, None, :]).astype(bf16)

        def keep(array):
            precision = lax.Precision.HIGHEST if array.dtype == f32 else None
            picked = jnp.einsum(
                "crs,csw->crw",
                picks.astype(array.dtype),
                array.reshape(clips, slots, -1),
                precision=precision,
                preferred_element_type=f32,
            )
            return picked.astype(array.dtype).reshape(clips * held, -1)

        def put_back(array):
            placed = jnp.einsum(
                "crs,crw->csw",
                picks.astype(f32),
                array.reshape(clips, held, -1),
                precision=lax.Precision.HIGHEST,
                preferred_element_type=f32,
            )
            return placed.reshape(rows, -1)

    bias = jnp.where(kept, 0.0, -1e30).astype(f32)
    tiled = held % 16 == 0

    def by_clip(array):
        if tiled:
            return array
        shards, count, length, lanes = array.shape
        return array.transpose(1, 0, 2, 3).reshape(1, count, shards * length, lanes)

    inputs = tokens.reshape(rows, width)
    normed_kept = keep(normed).reshape(1, clips, held, width)
    normed_all = exchange(jnp.broadcast_to(normed_kept, (seq_size, clips, held, width)))
    embed, p_joint, p_out = gather(embed_shard), gather(p_joint_shard), gather(p_out_shard)
    e_by_sender = by_sender(e_joint, seq_size)
    normed_all, embed, p_joint, p_out, e_by_sender = lax.optimization_barrier(
        (normed_all, embed, p_joint, p_out, e_by_sender)
    )
    queries = (mm(normed, e_joint[:, :width]) + e_vec["query_bias"]).astype(bf16)
    joined = mm(normed_all.reshape(-1, width), e_joint[:, width:])
    joined_bias = jnp.concatenate([jnp.zeros_like(e_vec["value_bias"]), e_vec["value_bias"]])
    joined = (joined + joined_bias).astype(bf16)
    joined, e_contract_shard = lax.optimization_barrier((joined, e_contract_shard))
    e_contract = gather(e_contract_shard)
    mixed = attend(
        queries.reshape(clips, slots, width),
        by_clip(joined.reshape(seq_size, clips, held, 2 * width)),
        head_size,
        bias,
    ).reshape(rows, width)
    mixed, p_expand_shard = lax.optimization_barrier((mixed, p_expand_shard))
    p_expand = gather(p_expand_shard)
    middle = inputs + mm(mixed, e_out) + e_vec["out_bias"]
    normed_mid = norm_layer(middle, e_vec["mid_gain"], e_vec["mid_shift"])
    active = gelu(mm(normed_mid, e_expand) + e_vec["expand_bias"])
    encoded = middle + mm(active, e_contract) + e_vec["contract_bias"]
    context = encoded.astype(bf16)

    embedded = mm(context, embed) + embed_bias
    pred_input = jnp.where(own_flat, embedded, mask_token) + slot_code
    p_normed = norm_layer(pred_input, p_vec["pre_gain"], p_vec["pre_shift"])
    (
        p_normed,
        rows_all,
        mid_rows,
        mixed_rows,
        middle_rows,
        e_vec["query_bias"],
        e_vec["value_bias"],
        p_vec["query_bias"],
        p_vec["value_bias"],
    ) = lax.optimization_barrier(
        (
            p_normed,
            normed_all,
            normed_mid,
            mixed,
            middle,
            e_vec["query_bias"],
            e_vec["value_bias"],
            p_vec["query_bias"],
            p_vec["value_bias"],
        )
    )
    p_queries = (mm(p_normed, p_joint[:, :small_width]) + p_vec["query_bias"]).astype(bf16)
    own_weight, own_bias = own_joint(
        e_joint, e_vec["query_bias"], e_vec["value_bias"], seq_size, shard
    )
    own_qkv = [by_clip(member) for member in own_parts(rows_all, own_weight, own_bias)]
    p_bias = jnp.concatenate([jnp.zeros_like(p_vec["value_bias"]), p_vec["value_bias"]])
    p_normed_all = []
    p_mixed = []
    everyone = [
        lax.all_gather(p_normed.reshape(clips, slots, small_width)[clip], "seq", axis=0, tiled=True)
        for clip in range(clips)
    ]
    p_contract_shard, p_expand, everyone[0] = lax.optimization_barrier(
        (p_contract_shard, p_expand, everyone[0])
    )
    p_contract = gather(p_contract_shard)
    for clip in range(clips):
        every = everyone[clip]
        if clip > 0:
            every, p_mixed[-1] = lax.optimization_barrier((every, p_mixed[-1]))
        p_joined = (mm(every, p_joint[:, small_width:]) + p_bias).astype(bf16)
        p_normed_all.append(every)
        p_mixed.append(
            attend(
                p_queries.reshape(clips, slots, small_width)[clip : clip + 1],
                p_joined.reshape(1, 1, span, 2 * small_width),
                small_head,
                None,
            )
        )
    kept_mid, kept_mixed, kept_middle, kept_inputs = (
        keep(member) for member in (mid_rows, mixed_rows, middle_rows, inputs)
    )
    p_mixed[0], kept_mid, kept_mixed, kept_middle, kept_inputs, *own_qkv = (
        lax.optimization_barrier(
            (p_mixed[0], kept_mid, kept_mixed, kept_middle, kept_inputs, *own_qkv)
        )
    )
    p_mixed = jnp.concatenate(p_mixed, axis=0).reshape(rows, small_width)
    p_middle = pred_input + mm(p_mixed, p_out) + p_vec["out_bias"]
    p_normed_mid = norm_layer(p_middle, p_vec["mid_gain"], p_vec["mid_shift"])
    p_hidden = mm(p_normed_mid, p_expand) + p_vec["expand_bias"]
    p_active = gelu(p_hidden)
    predicted = p_middle + mm(p_active, p_contract) + p_vec["contract_bias"]

    grad_middle, grad_att, grad_mixed, p_grads, p_small = feed_back(
        cotangent.reshape(rows, small_width),
        p_middle,
        p_normed_mid,
        p_hidden,
        p_active,
        (p_out, p_expand, p_contract),
        p_vec["mid_gain"],
    )
    p_grad_out = mm(p_mixed, grad_att, TN).astype(bf16)
    p_wide = jnp.concatenate([p_grad_out, p_grads[0]], axis=1)
    p_tall = p_grads[1]
    grad_mixed, p_wide, p_tall = lax.optimization_barrier((grad_mixed, p_wide, p_tall))
    p_wide, p_tall = scatter(p_wide), scatter(p_tall)
    own_weight, own_bias = own_joint(
        p_joint, p_vec["query_bias"], p_vec["value_bias"], seq_size, shard
    )
    own_width = small_width // seq_size
    grad_mixed = grad_mixed.reshape(rows, seq_size, own_width).transpose(1, 0, 2)
    grad_mixed = exchange(grad_mixed.reshape(seq_size, clips, slots, own_width))
    p_by_sender = by_sender(p_joint, seq_size)
    grad_normed = []
    p_grad_joint = 0.0
    p_columns = 0.0
    for clip in range(clips):
        every = p_normed_all[clip].reshape(1, 1, span, small_width)
        grads = attend_back(
            *own_parts(every, own_weight, own_bias),
            grad_mixed[:, clip].reshape(1, 1, span, own_width),
            0,
            small_head,
            None,
            seq_size,
        )
        if clip == 0:
            grads, p_wide, p_tall = lax.optimization_barrier((grads, p_wide, p_tall))
        flat = grads.reshape(span, 3 * own_width)
        p_grad_joint = p_grad_joint + mm(p_normed_all[clip], flat, TN)
        p_columns = p_columns + jnp.sum(flat.astype(f32), axis=0)
        grad_normed.append(joint_back(exchange(grads), p_by_sender))
    p_small.update(joint_small(p_columns, fsdp_size, seq_size, shard))
    p_own_width = own_width
    grad_pred_input, _, p_small["pre_gain"], p_small["pre_shift"], _ = norm_back(
        pred_input, p_vec["pre_gain"], jnp.concatenate(grad_normed, axis=0), grad_middle
    )
    grad_mask_token = jnp.sum(jnp.where(own_flat, 0.0, grad_pred_input), axis=0)
    grad_embedded = jnp.where(own_flat, grad_pred_input, 0.0).astype(bf16)
    grad_embed_bias = jnp.sum(grad_embedded.astype(f32), axis=0)

    grad_embedded, predicted = lax.optimization_barrier((grad_embedded, predicted))
    grad_context = mm(keep(grad_embedded), embed, NT)
    kept_hidden = mm(kept_mid, e_expand) + e_vec["expand_bias"]
    grad_middle, grad_att, grad_mixed, e_grads, e_small = feed_back(
        grad_context,
        kept_middle,
        kept_mid,
        kept_hidden,
        gelu(kept_hidden),
        (e_out, e_expand, e_contract),
        e_vec["mid_gain"],
    )
    expand_part, contract_part = scatter(e_grads[0]), scatter(e_grads[1])
    own_width = width // seq_size
    grad_mixed = grad_mixed.reshape(clips * held, seq_size, own_width).transpose(1, 0, 2)
    grad_mixed = by_clip(exchange(grad_mixed.reshape(seq_size, clips, held, own_width)))
    grads = [
        attend_back(*own_qkv, grad_mixed, clip, head_size, bias, seq_size) for clip in range(clips)
    ]
    grads[-1], grad_att, late_embedded = lax.optimization_barrier(
        (grads[-1], grad_att, grad_embedded)
    )
    received = [exchange(member) for member in grads]
    received[0], contract_part = lax.optimization_barrier((received[0], contract_part))
    flat = jnp.concatenate(grads, axis=1).reshape(-1, 3 * own_width)
    e_grad_joint = mm(normed_all.reshape(-1, width), flat, TN).astype(bf16)
    e_grad_out = mm(kept_mixed, grad_att, TN).astype(bf16)
    grad_embed = mm(context, late_embedded, TN).astype(bf16)
    e_small.update(joint_small(jnp.sum(flat.astype(f32), axis=0), fsdp_size, seq_size, shard))
    grad_normed = jnp.concatenate([joint_back(member, e_by_sender) for member in received], axis=0)
    grad_inputs, _, e_small["pre_gain"], e_small["pre_shift"], _ = norm_back(
        kept_inputs, e_vec["pre_gain"], grad_normed, grad_middle
    )

    own_rows = width // fsdp_size
    p_rows = small_width // fsdp_size
    p_lanes = -(-3 * p_own_width // 128) * 128
    p_grad_joint = p_grad_joint.astype(bf16).reshape(fsdp_size, p_rows, 3 * p_own_width)
    p_grad_joint = jnp.pad(
        p_grad_joint, ((0, 0), (0, own_rows - p_rows), (0, p_lanes - 3 * p_own_width))
    ).reshape(width, p_lanes)
    small = [e_small[name] for name in ORDER] + [grad_embed_bias, grad_mask_token]
    small += [p_small[name] for name in ORDER]
    small = [member.reshape(fsdp_size, -1) for member in small]
    sizes = [member.shape[1] for member in small]
    small.append(jnp.zeros((fsdp_size, own_rows * 128 - sum(sizes)), f32))
    small = jnp.concatenate(small, axis=1).astype(bf16).reshape(width, 128)
    late = scatter(jnp.concatenate([e_grad_joint, p_grad_joint, e_grad_out, grad_embed, small], axis=1))
    grad_tokens = put_back(grad_inputs)

    first = 0 if whole else 2
    contract_sum, expand_sum, p_wide_sum, p_contract_sum = sum_slots(
        (contract_part, expand_part, p_wide, p_tall), seq_size, first
    )
    late, expand_sum = lax.optimization_barrier((late, expand_sum))
    shared = 3 * own_width + p_lanes
    late_sum, columns = sum_slots((late,), seq_size, first + 1, shared)
    e_joint_sum = columns[:, :, : 3 * own_width].reshape(seq_size, own_rows, 3, own_width)
    e_joint_sum = e_joint_sum.transpose(1, 2, 0, 3).reshape(own_rows, 3 * width)
    p_joint_sum = columns[:, :p_rows, 3 * own_width : 3 * (own_width + p_own_width)]
    p_joint_sum = p_joint_sum.reshape(seq_size, p_rows, 3, p_own_width)
    p_joint_sum = p_joint_sum.transpose(1, 2, 0, 3).reshape(p_rows, 3 * small_width)
    out_sum = late_sum[:, :width]
    embed_sum = late_sum[:, width : width + small_width]
    p_out_sum, p_expand_sum = p_wide_sum[:, :small_width], p_wide_sum[:, small_width:]
    return (
        encoded.reshape(tokens.shape),
        predicted.reshape(cotangent.shape),
        grad_tokens.reshape(tokens.shape),
        (e_joint_sum, out_sum, expand_sum, contract_sum),
        embed_sum,
        (p_joint_sum, p_out_sum, p_expand_sum, p_contract_sum),
        late_sum[:, width + small_width :],
    )


def solution(mesh):
    cut, rows, vec, full = P("fsdp", "seq", None), P("fsdp", None), P("fsdp"), P()
    block = (vec, vec, rows, vec, vec, rows, vec, vec, vec, rows, vec, rows, vec)
    return jax.shard_map(
        functools.partial(body, mesh.shape["fsdp"], mesh.shape["seq"]),
        mesh=mesh,
        in_specs=(cut, rows, rows, full, *block, rows, vec, vec, *block, cut),
        out_specs=(cut, cut, cut, *block, rows, vec, vec, *block),
        check_vma=False,
    )
```

```python
import functools
import math

import jax
import jax.numpy as jnp
from jax import lax
from jax.experimental import pallas as pl
from jax.experimental.pallas import tpu as pltpu
from jax.sharding import PartitionSpec as P

HEADS = 16
PHEADS = 12

f32 = jnp.float32
bf16 = jnp.bfloat16
norm_eps = 1e-06
LOG2E = math.log2(math.e)
NN = (((1,), (0,)), ((), ()))
NT = (((1,), (1,)), ((), ()))
TN = (((0,), (0,)), ((), ()))
VMEM_LIMIT = 60 * 2**20


def mm(left, right, dims=NN):
    return lax.dot_general(left, right, dims, preferred_element_type=f32)


def norm_parts(value):
    center = value - jnp.mean(value, axis=-1, keepdims=True)
    spread = jnp.mean(center * center, axis=-1, keepdims=True)
    scale = lax.rsqrt(spread + norm_eps)
    return center * scale, scale


def norm_layer(value, gain, shift):
    unit, _ = norm_parts(value)
    return (unit * gain + shift).astype(bf16)


def norm_back(value, gain, grad):
    unit, scale = norm_parts(value)
    grad_gain = jnp.sum(grad * unit, axis=0)
    grad_shift = jnp.sum(grad, axis=0)
    inner = grad * gain
    inner = inner - jnp.mean(inner, axis=-1, keepdims=True) - unit * jnp.mean(
        inner * unit, axis=-1, keepdims=True
    )
    return scale * inner, grad_gain, grad_shift


def gelu_parts(hidden):
    cdf = 0.5 * (1.0 + lax.erf(hidden * math.sqrt(0.5)))
    return cdf


def gelu(hidden):
    return (hidden * gelu_parts(hidden)).astype(bf16)


def gelu_slope(hidden):
    pdf = jnp.exp(-0.5 * hidden * hidden) * (1.0 / math.sqrt(2.0 * math.pi))
    return gelu_parts(hidden) + hidden * pdf


def forward_kernel(scale, head_size, q_ref, k_ref, v_ref, *rest):
    if len(rest) == 2:
        bias_ref, o_ref = rest
    else:
        bias_ref, o_ref = None, rest[0]
    query = q_ref[0]
    lanes = query.shape[1]
    key = k_ref[...].reshape(-1, lanes)
    value = v_ref[...].reshape(-1, lanes)
    lane = lax.broadcasted_iota(jnp.int32, query.shape, 1)
    result = None
    for head in range(lanes // head_size):
        mine = (lane // head_size) == head
        own_query = jnp.where(mine, query, jnp.zeros_like(query))
        scores = mm(own_query, key, NT) * (scale * LOG2E)
        if bias_ref is not None:
            scores = scores + bias_ref[0]
        top = jnp.max(scores, axis=1, keepdims=True)
        weight = jnp.exp2(scores - top)
        total = jnp.sum(weight, axis=1, keepdims=True)
        part = jnp.where(mine, mm(weight.astype(bf16), value) / total, 0.0)
        result = part if result is None else result + part
    o_ref[0] = result.astype(bf16)


def attend(queries, joined, head_size, bias):
    clips, rows, width = queries.shape
    major, _, length, _ = joined.shape
    keys = major * length
    groups = width // 128
    in_specs = [
        pl.BlockSpec((1, rows, 128), lambda c, g: (c, 0, g)),
        pl.BlockSpec((major, 1, length, 128), lambda c, g: (0, c, 0, g)),
        pl.BlockSpec((major, 1, length, 128), lambda c, g: (0, c, 0, g + groups)),
    ]
    operands = [queries, joined, joined]
    if bias is not None:
        in_specs.append(pl.BlockSpec((1, 1, keys), lambda c, g: (c, 0, 0)))
        operands.append(bias)
    cells = clips * rows * keys * (width // head_size)
    return pl.pallas_call(
        functools.partial(forward_kernel, 1.0 / math.sqrt(head_size), head_size),
        grid=(clips, groups),
        in_specs=in_specs,
        out_specs=pl.BlockSpec((1, rows, 128), lambda c, g: (c, 0, g)),
        out_shape=jax.ShapeDtypeStruct((clips, rows, width), bf16),
        compiler_params=pltpu.CompilerParams(vmem_limit_bytes=VMEM_LIMIT),
        cost_estimate=pl.CostEstimate(
            flops=cells * 1024, bytes_accessed=4 * clips * keys * width, transcendentals=cells
        ),
        name="attend",
    )(*operands)


def backward_kernel(scale, head_size, shards, q_ref, k_ref, v_ref, g_ref, *rest):
    if len(rest) == 4:
        bias_ref = rest[0]
        rest = rest[1:]
    else:
        bias_ref = None
    out_ref, dk_sum, dv_sum = rest
    group = pl.program_id(0)
    part = pl.program_id(1)
    lanes = q_ref.shape[-1]
    query = q_ref[...].reshape(-1, lanes)
    key = k_ref[...].reshape(-1, lanes)
    value = v_ref[...].reshape(-1, lanes)
    grad = g_ref[...].reshape(-1, lanes)
    lane = lax.broadcasted_iota(jnp.int32, query.shape, 1)
    key_lane = lax.broadcasted_iota(jnp.int32, key.shape, 1)
    sums = None
    for head in range(lanes // head_size):
        mine = (lane // head_size) == head
        own_query = jnp.where(mine, query, jnp.zeros_like(query))
        own_grad = jnp.where(mine, grad, jnp.zeros_like(grad))
        own_key = jnp.where((key_lane // head_size) == head, key, jnp.zeros_like(key))
        scores = mm(own_query, key, NT) * (scale * LOG2E)
        if bias_ref is not None:
            scores = scores + bias_ref[0]
        top = jnp.max(scores, axis=1, keepdims=True)
        weight = jnp.exp2(scores - top)
        chance = weight * (1.0 / jnp.sum(weight, axis=1, keepdims=True))
        grad_chance = mm(own_grad, value, NT)
        delta = jnp.sum(chance * grad_chance, axis=1, keepdims=True)
        grad_scores = (chance * (grad_chance - delta)).astype(bf16)
        terms = (
            mm(grad_scores, own_key),
            mm(own_query, grad_scores, TN),
            mm(own_grad, chance.astype(bf16), TN),
        )
        sums = terms if sums is None else tuple(x + y for x, y in zip(sums, terms))
    part_q, part_k, part_v = sums

    @pl.when(part == 0)
    def _():
        dk_sum[...] = part_k
        dv_sum[...] = part_v

    @pl.when(part > 0)
    def _():
        dk_sum[...] += part_k
        dv_sum[...] += part_v

    rows = out_ref.shape[2]
    width = out_ref.shape[3] // 3
    held = query.shape[0] // rows

    def place(kind):
        if width == lanes:
            return slice(kind * width, (kind + 1) * width)
        return pl.ds(pl.multiple_of(kind * width + group * lanes, 128), lanes)

    result_q = (part_q * scale).astype(bf16)
    for index in range(held):
        out_ref[part * held + index, 0, :, place(0)] = result_q[index * rows : (index + 1) * rows]

    @pl.when(part == pl.num_programs(1) - 1)
    def _():
        for kind, total_ref, factor in ((1, dk_sum, scale), (2, dv_sum, 1.0)):
            result = (total_ref[...] * factor).T.astype(bf16)
            for index in range(shards):
                out_ref[index, 0, :, place(kind)] = result[index * rows : (index + 1) * rows]


def attend_back(queries, keys, values, grad_mixed, clip, head_size, bias, shards):
    major, _, length, width = queries.shape
    lanes = min(width, 128)
    groups = width // lanes
    rows = major * length // shards
    parts = shards if major == 1 else 1
    query_rows = rows if major == 1 else length
    by_query = pl.BlockSpec((major, 1, query_rows, lanes), lambda g, r: (0, clip, r, g))
    by_key = pl.BlockSpec((major, 1, length, lanes), lambda g, r: (0, clip, 0, g))
    in_specs = [by_query, by_key, by_key, by_query]
    operands = [queries, keys, values, grad_mixed]
    total = major * length
    if bias is not None:
        in_specs.append(pl.BlockSpec((1, 1, total), lambda g, r: (clip, 0, 0)))
        operands.append(bias)
    cells = total * total * (width // head_size)
    return pl.pallas_call(
        functools.partial(backward_kernel, 1.0 / math.sqrt(head_size), head_size, shards),
        grid=(groups, parts),
        in_specs=in_specs,
        out_specs=pl.BlockSpec((shards, 1, rows, 3 * width), lambda g, r: (0, 0, 0, 0)),
        out_shape=jax.ShapeDtypeStruct((shards, 1, rows, 3 * width), bf16),
        scratch_shapes=[pltpu.VMEM((lanes, total), f32), pltpu.VMEM((lanes, total), f32)],
        compiler_params=pltpu.CompilerParams(vmem_limit_bytes=VMEM_LIMIT),
        cost_estimate=pl.CostEstimate(
            flops=cells * 2560, bytes_accessed=14 * total * width, transcendentals=cells
        ),
        name="attend_back",
    )(*operands)


def exchange(array):
    return lax.all_to_all(array, "seq", split_axis=0, concat_axis=0, tiled=True)


def gather(array):
    return lax.all_gather(array, "fsdp", axis=0, tiled=True)


def scatter(array):
    return lax.psum_scatter(array, "fsdp", scatter_dimension=0, tiled=True)


def pack_rows(vectors):
    rows = []
    for member in vectors:
        count = -(-member.shape[0] // 128)
        padded = jnp.pad(member.astype(f32), (0, count * 128 - member.shape[0]))
        rows.append(padded.reshape(count, 128))
    total = sum(member.shape[0] for member in rows)
    if total % 8:
        rows.append(jnp.zeros((8 - total % 8, 128), f32))
    return jnp.concatenate(rows, axis=0)


def unpack_rows(packed, sizes):
    out = []
    at = 0
    for size in sizes:
        count = -(-size // 128)
        piece = packed[:, at : at + count].reshape(packed.shape[0], count * 128)[:, :size]
        out.append(piece.reshape(-1))
        at += count
    return out


MESH = pl.DeviceIdType.MESH


def line_kernel(size, cuts, shares, *refs):
    count = len(cuts)
    ins, outs = refs[:count], refs[count : 2 * count]
    if shares:
        ins, own, outs, every = (refs[0].at[:, shares:],), refs[0].at[:, :shares], refs[1:2], refs[2]
    scratch = refs[3 if shares else 2 * count :]
    inner, outer, partial = (scratch[i * count : (i + 1) * count] for i in range(3))
    to_inner, to_outer, from_inner, from_outer = scratch[3 * count : 3 * count + 4]
    me = lax.axis_index("seq")
    left = me < size // 2
    toward = jnp.where(left, me + 1, me - 1)
    away = jnp.where(left, me - 1, me + 1)
    end = (me == 0) | (me == size - 1)
    barrier = pltpu.get_barrier_semaphore()
    pl.semaphore_signal(barrier, inc=1, device_id={"seq": toward}, device_id_type=MESH)

    @pl.when(jnp.logical_not(end))
    def _():
        pl.semaphore_signal(barrier, inc=1, device_id={"seq": away}, device_id_type=MESH)
        pl.semaphore_wait(barrier, 2)

    @pl.when(end)
    def _():
        pl.semaphore_wait(barrier, 1)

    pieces = []
    for index, parts in enumerate(cuts):
        rows = ins[index].shape[0] // parts
        for part in range(parts):
            pieces.append((part / parts, index, slice(part * rows, (part + 1) * rows)))
    pieces.sort(key=lambda piece: piece[:2])
    pieces = [(slot, index, cut) for slot, (_, index, cut) in enumerate(pieces)]

    def inwards(slot, index, cut):
        return pltpu.make_async_remote_copy(
            src_ref=ins[index].at[cut],
            dst_ref=outer[index].at[cut],
            send_sem=to_inner.at[slot],
            recv_sem=from_outer.at[slot],
            device_id={"seq": toward},
            device_id_type=MESH,
        )

    def swap(slot, index, cut):
        return pltpu.make_async_remote_copy(
            src_ref=partial[index].at[cut],
            dst_ref=inner[index].at[cut],
            send_sem=to_inner.at[slot],
            recv_sem=from_inner.at[slot],
            device_id={"seq": toward},
            device_id_type=MESH,
        )

    def outwards(slot, index, cut):
        return pltpu.make_async_remote_copy(
            src_ref=outs[index].at[cut],
            dst_ref=outs[index].at[cut],
            send_sem=to_outer.at[slot],
            recv_sem=from_inner.at[slot],
            device_id={"seq": away},
            device_id_type=MESH,
        )

    @pl.when(end)
    def _():
        for piece in pieces:
            inwards(*piece).start()

    if shares:
        sent, arrived = scratch[3 * count + 4 :]
        every[me] = own[...]

        def passes(way, hop):
            step = 1 - 2 * way
            block = me - step * hop
            return pltpu.make_async_remote_copy(
                src_ref=own if hop == 0 else every.at[block],
                dst_ref=every.at[block],
                send_sem=sent.at[way, hop],
                recv_sem=arrived.at[way, hop],
                device_id={"seq": me + step},
                device_id_type=MESH,
            )

        def sends(way, hop):
            if way == 0:
                return (me < size - 1) & (me - hop >= 0)
            return (me > 0) & (me + hop <= size - 1)

        def receives(way, hop):
            return me - 1 - hop >= 0 if way == 0 else me + 1 + hop <= size - 1

        def landing(way, hop):
            block = me - 1 - hop if way == 0 else me + 1 + hop
            return pltpu.make_async_remote_copy(
                src_ref=every.at[block],
                dst_ref=every.at[block],
                send_sem=sent.at[way, hop],
                recv_sem=arrived.at[way, hop],
                device_id={"seq": toward},
                device_id_type=MESH,
            )

        def forward(hop):
            for way in (0, 1):
                if hop > 0:

                    @pl.when(receives(way, hop - 1))
                    def _(way=way):
                        landing(way, hop - 1).wait_recv()

                if hop < size - 1:

                    @pl.when(sends(way, hop))
                    def _(way=way):
                        passes(way, hop).start()

        forward(0)

    @pl.when(end)
    def _():
        for piece in pieces:
            outwards(*piece).wait_recv()
        for piece in pieces:
            inwards(*piece).wait_send()

    @pl.when(jnp.logical_not(end))
    def _():
        lag = min(count, len(pieces))
        steps = len(pieces) + lag
        for step in range(steps):
            if shares and step in (steps // 3, 2 * steps // 3):
                forward(1 if step == steps // 3 else 2)
            if step < len(pieces):
                piece = pieces[step]
                inwards(*piece).wait_recv()
                _, index, cut = piece
                both = ins[index][cut].astype(f32) + outer[index][cut].astype(f32)
                partial[index][cut] = both.astype(bf16)
                swap(*piece).start()
            if step >= lag:
                piece = pieces[step - lag]
                swap(*piece).wait_recv()
                _, index, cut = piece
                both = partial[index][cut].astype(f32) + inner[index][cut].astype(f32)
                outs[index][cut] = both.astype(bf16)
                outwards(*piece).start()
        for piece in pieces:
            swap(*piece).wait_send()
            outwards(*piece).wait_send()

    if shares:

        @pl.when(end)
        def _():
            for hop in range(1, size):
                forward(hop)

        @pl.when(jnp.logical_not(end))
        def _():
            for hop in range(3, size):
                forward(hop)

        for way in (0, 1):
            for hop in range(size - 1):

                @pl.when(sends(way, hop))
                def _(way=way, hop=hop):
                    passes(way, hop).wait_send()


def line_sum(arrays, size, identity, shares=0):
    cuts = []
    shapes = []
    for member in arrays:
        parts = 8
        while parts > 1 and member.shape[0] % (16 * parts):
            parts //= 2
        cuts.append(parts)
        shapes.append((member.shape[0], member.shape[1] - shares))
    hold = [pltpu.VMEM(shape, bf16) for shape in shapes]
    semaphores = [pltpu.SemaphoreType.DMA((sum(cuts),))] * 4
    if shares:
        shapes.append((size, arrays[0].shape[0], shares))
        semaphores += [pltpu.SemaphoreType.DMA((2, size - 1))] * 2
    whole = pl.BlockSpec(memory_space=pltpu.VMEM)
    return pl.pallas_call(
        functools.partial(line_kernel, size, tuple(cuts), shares),
        out_shape=[jax.ShapeDtypeStruct(shape, bf16) for shape in shapes],
        in_specs=[whole] * len(arrays),
        out_specs=[whole] * len(shapes),
        scratch_shapes=hold * 3 + semaphores,
        compiler_params=pltpu.CompilerParams(
            collective_id=identity, has_side_effects=True, vmem_limit_bytes=VMEM_LIMIT
        ),
        cost_estimate=pl.CostEstimate(
            flops=0,
            bytes_accessed=40 * sum(2 * member.size for member in arrays),
            transcendentals=0,
        ),
        name="line_sum",
    )(*arrays)


def sum_slots(arrays, size, identity, shares=0):
    if size == 4:
        return line_sum(arrays, size, identity, shares)
    if shares == 0:
        return lax.psum(tuple(arrays), "seq")
    summed = lax.psum(arrays[0][:, shares:], "seq")
    return summed, lax.all_gather(arrays[0][:, :shares], "seq", axis=0, tiled=False)


def feed_back(grad_out, middle, normed_mid, hidden, active, weights, mid_gain):
    out, expand, contract = weights
    grad_y = grad_out.astype(bf16)
    grad_contract = mm(active, grad_y, TN).astype(bf16)
    grad_contract_bias = jnp.sum(grad_y.astype(f32), axis=0)
    grad_y, grad_contract = lax.optimization_barrier((grad_y, grad_contract))
    grad_hidden = (mm(grad_y, contract, NT) * gelu_slope(hidden)).astype(bf16)
    grad_expand = mm(normed_mid, grad_hidden, TN).astype(bf16)
    grad_expand_bias = jnp.sum(grad_hidden.astype(f32), axis=0)
    grad_normed = mm(grad_hidden, expand, NT)
    grad_normed, grad_expand = lax.optimization_barrier((grad_normed, grad_expand))
    grad_norm, grad_mid_gain, grad_mid_shift = norm_back(middle, mid_gain, grad_normed)
    grad_middle = grad_out + grad_norm
    grad_att = grad_middle.astype(bf16)
    grad_out_bias = jnp.sum(grad_att.astype(f32), axis=0)
    grad_mixed = mm(grad_att, out, NT).astype(bf16)
    small = dict(
        out_bias=grad_out_bias,
        mid_gain=grad_mid_gain,
        mid_shift=grad_mid_shift,
        expand_bias=grad_expand_bias,
        contract_bias=grad_contract_bias,
    )
    return grad_middle, grad_att, grad_mixed, (grad_expand, grad_contract), small


def own_joint(joint_weight, query_bias, value_bias, shards, shard):
    width = joint_weight.shape[0]
    own = width // shards
    weight = lax.dynamic_slice_in_dim(joint_weight.reshape(width, 3, width), shard * own, own, 2)
    bias_q = lax.dynamic_slice_in_dim(query_bias, shard * own, own, 0)
    bias_v = lax.dynamic_slice_in_dim(value_bias, shard * own, own, 0)
    return weight, (bias_q, None, bias_v)


def own_parts(normed_all, weight, biases):
    flat = normed_all.reshape(-1, normed_all.shape[3])
    out = []
    for index in range(3):
        part = mm(flat, weight[:, index])
        if biases[index] is not None:
            part = part + biases[index]
        out.append(part.astype(bf16).reshape(normed_all.shape[:3] + (weight.shape[2],)))
    return out


def by_sender(joint_weight, shards):
    width = joint_weight.shape[0]
    array = joint_weight.reshape(width, 3, shards, width // shards)
    return array.transpose(0, 2, 1, 3).reshape(width, 3 * width)


def joint_back(received, joint_by_sender):
    shards, clips, rows, width = received.shape
    flat = received.reshape(shards, clips * rows, width).transpose(1, 0, 2)
    return mm(flat.reshape(clips * rows, shards * width), joint_by_sender, NT)


def joint_small(columns, owners, shards, shard):
    own = columns.shape[0] // 3
    each = owners // shards
    mine = lax.broadcasted_iota(jnp.int32, (owners, 1), 0) // each == shard

    def full(vector):
        return jnp.where(mine, jnp.tile(vector.reshape(each, -1), (shards, 1)), 0.0)

    return dict(query_bias=full(columns[:own]), value_bias=full(columns[2 * own :]))


ORDER = (
    "pre_gain",
    "pre_shift",
    "query_bias",
    "value_bias",
    "out_bias",
    "mid_gain",
    "mid_shift",
    "expand_bias",
    "contract_bias",
)
BLOCK = (
    "pre_gain",
    "pre_shift",
    "joint",
    "query_bias",
    "value_bias",
    "out",
    "out_bias",
    "mid_gain",
    "mid_shift",
    "expand",
    "expand_bias",
    "contract",
    "contract_bias",
)
FRAMES = 8
GRID = 14
MOST_VISIBLE = FRAMES * max(
    high * wide
    for high in range(1, GRID + 1)
    for wide in range(1, GRID + 1)
    if 2 * high * wide < GRID * GRID
)


def body(fsdp_size, seq_size, tokens, visible, slot_token, positions, *rest):
    e_shard = dict(zip(BLOCK, rest[:13]))
    embed_weight, embed_bias, mask_token = rest[13:16]
    p_shard = dict(zip(BLOCK, rest[16:29]))
    cotangent = rest[29]
    shard = lax.axis_index("seq")
    clips, slots, width = tokens.shape
    span = visible.shape[1]

    e_joint = gather(e_shard["joint"])
    place = lax.broadcasted_iota(jnp.int32, (1, 1, span), 2)
    slot_visible = jnp.any(
        (slot_token[:, :, None] == place) & (visible[:, None, :] > 0), axis=2
    )
    counts = jnp.sum(slot_visible.reshape(clips, seq_size, slots).astype(jnp.int32), axis=2)
    compact = -(-MOST_VISIBLE // (16 * seq_size)) * 16
    fits = (jnp.max(counts) <= compact).astype(f32)

    vectors = [e_shard[name] for name in ORDER] + [embed_bias, mask_token]
    vectors += [p_shard[name] for name in ORDER]
    sizes = [member.shape[0] for member in vectors]
    packed = lax.all_gather(
        pack_rows(vectors + [jnp.full((1,), fits)]), "fsdp", axis=0, tiled=False
    )
    full = unpack_rows(packed, sizes + [1])
    all_fit = jnp.min(full[-1]) > 0.5
    normed = norm_layer(tokens.reshape(-1, width), full[0], full[1])

    operands = (
        tokens,
        slot_visible,
        counts,
        slot_token,
        positions,
        normed,
        e_joint,
        tuple(e_shard[name] for name in ("out", "expand", "contract")),
        embed_weight,
        tuple(p_shard[name] for name in ("joint", "out", "expand", "contract")),
        tuple(full[:-1]),
        cotangent,
    )
    whole = functools.partial(main, fsdp_size, seq_size, slots)
    if compact >= slots:
        results = whole(*operands)
    else:
        results = lax.cond(
            all_fit, functools.partial(main, fsdp_size, seq_size, compact), whole, *operands
        )
    encoded, predicted, grad_tokens, e_sums, embed_sum, p_sums, vector_sum = results
    vector_sum = vector_sum.reshape(-1).astype(f32)
    small = []
    at = 0
    for size in sizes:
        small.append(vector_sum[at : at + size])
        at += size

    def ordered(vec, sums):
        vec = dict(zip(ORDER, vec))
        vec.update(zip(("joint", "out", "expand", "contract"), (x.astype(f32) for x in sums)))
        return tuple(vec[name] for name in BLOCK)

    return (
        encoded,
        predicted,
        grad_tokens,
        *ordered(small[:9], e_sums),
        embed_sum.astype(f32),
        small[9],
        small[10],
        *ordered(small[11:], p_sums),
    )


def main(
    fsdp_size,
    seq_size,
    held,
    tokens,
    slot_visible,
    counts,
    slot_token,
    positions,
    normed,
    e_joint,
    e_shards,
    embed_shard,
    p_shards,
    vectors,
    cotangent,
):
    shard = lax.axis_index("seq")
    clips, slots, width = tokens.shape
    span = slot_visible.shape[1]
    rows = clips * slots
    small_width = cotangent.shape[2]
    head_size = width // HEADS
    small_head = small_width // PHEADS
    whole = held == slots
    e_vec = dict(zip(ORDER, vectors[:9]))
    embed_bias, mask_token = vectors[9:11]
    p_vec = dict(zip(ORDER, vectors[11:]))

    e_out_shard, e_expand_shard, e_contract_shard = e_shards
    p_joint_shard, p_out_shard, p_expand_shard, p_contract_shard = p_shards
    e_out, e_expand = gather(e_out_shard), gather(e_expand_shard)

    own_visible = lax.dynamic_slice_in_dim(slot_visible, shard * slots, slots, 1)
    own_flat = own_visible.reshape(rows, 1)
    own_tokens = lax.dynamic_slice_in_dim(slot_token, shard * slots, slots, 1)
    slot_code = jnp.take(positions, own_tokens.reshape(rows), axis=0)

    if whole:
        kept = slot_visible.reshape(clips, 1, span)

        def keep(array):
            return array

        def put_back(array):
            return array

    else:
        kept = lax.broadcasted_iota(jnp.int32, (1, 1, held), 2) < counts[:, :, None]
        kept = kept.reshape(clips, 1, seq_size * held)
        ones = own_visible.astype(bf16)
        before = lax.broadcasted_iota(jnp.int32, (slots, slots), 0)
        after = lax.broadcasted_iota(jnp.int32, (slots, slots), 1)
        rank = mm(ones, (before < after).astype(bf16)).astype(jnp.int32)
        target = lax.broadcasted_iota(jnp.int32, (1, held, 1), 1)
        picks = ((rank[:, None, :] == target) & own_visible[:, None, :]).astype(bf16)

        def keep(array):
            precision = lax.Precision.HIGHEST if array.dtype == f32 else None
            picked = jnp.einsum(
                "crs,csw->crw",
                picks.astype(array.dtype),
                array.reshape(clips, slots, -1),
                precision=precision,
                preferred_element_type=f32,
            )
            return picked.astype(array.dtype).reshape(clips * held, -1)

        def put_back(array):
            placed = jnp.einsum(
                "crs,crw->csw",
                picks.astype(f32),
                array.reshape(clips, held, -1),
                precision=lax.Precision.HIGHEST,
                preferred_element_type=f32,
            )
            return placed.reshape(rows, -1)

    bias = jnp.where(kept, 0.0, -1e30).astype(f32)
    tiled = held % 16 == 0

    def by_clip(array):
        if tiled:
            return array
        shards, count, length, lanes = array.shape
        return array.transpose(1, 0, 2, 3).reshape(1, count, shards * length, lanes)

    inputs = tokens.reshape(rows, width)
    normed_kept = keep(normed).reshape(1, clips, held, width)
    normed_all = exchange(jnp.broadcast_to(normed_kept, (seq_size, clips, held, width)))
    embed, p_joint, p_out = gather(embed_shard), gather(p_joint_shard), gather(p_out_shard)
    e_by_sender = by_sender(e_joint, seq_size)
    p_by_sender = by_sender(p_joint, seq_size)
    p_own_weight = own_joint(
        p_joint, p_vec["query_bias"], p_vec["value_bias"], seq_size, shard
    )[0]
    normed_all, embed, p_joint, p_out, e_by_sender, p_by_sender, p_own_weight = (
        lax.optimization_barrier(
            (normed_all, embed, p_joint, p_out, e_by_sender, p_by_sender, p_own_weight)
        )
    )
    queries = (mm(normed, e_joint[:, :width]) + e_vec["query_bias"]).astype(bf16)
    joined = mm(normed_all.reshape(-1, width), e_joint[:, width:])
    joined_bias = jnp.concatenate([jnp.zeros_like(e_vec["value_bias"]), e_vec["value_bias"]])
    joined = (joined + joined_bias).astype(bf16)
    joined, e_contract_shard = lax.optimization_barrier((joined, e_contract_shard))
    e_contract = gather(e_contract_shard)
    mixed = attend(
        queries.reshape(clips, slots, width),
        by_clip(joined.reshape(seq_size, clips, held, 2 * width)),
        head_size,
        bias,
    ).reshape(rows, width)
    mixed, p_expand_shard = lax.optimization_barrier((mixed, p_expand_shard))
    p_expand = gather(p_expand_shard)
    middle = inputs + mm(mixed, e_out) + e_vec["out_bias"]
    normed_mid = norm_layer(middle, e_vec["mid_gain"], e_vec["mid_shift"])
    active = gelu(mm(normed_mid, e_expand) + e_vec["expand_bias"])
    encoded = middle + mm(active, e_contract) + e_vec["contract_bias"]
    context = encoded.astype(bf16)

    embedded = mm(context, embed) + embed_bias
    pred_input = jnp.where(own_flat, embedded, mask_token) + slot_code
    p_normed = norm_layer(pred_input, p_vec["pre_gain"], p_vec["pre_shift"])
    (
        p_normed,
        rows_all,
        mid_rows,
        mixed_rows,
        middle_rows,
        e_vec["query_bias"],
        e_vec["value_bias"],
        p_vec["query_bias"],
        p_vec["value_bias"],
    ) = lax.optimization_barrier(
        (
            p_normed,
            normed_all,
            normed_mid,
            mixed,
            middle,
            e_vec["query_bias"],
            e_vec["value_bias"],
            p_vec["query_bias"],
            p_vec["value_bias"],
        )
    )
    p_queries = (mm(p_normed, p_joint[:, :small_width]) + p_vec["query_bias"]).astype(bf16)
    own_weight, own_bias = own_joint(
        e_joint, e_vec["query_bias"], e_vec["value_bias"], seq_size, shard
    )
    own_qkv = [by_clip(member) for member in own_parts(rows_all, own_weight, own_bias)]
    p_bias = jnp.concatenate([jnp.zeros_like(p_vec["value_bias"]), p_vec["value_bias"]])
    p_normed_all = []
    p_mixed = []
    everyone = [
        lax.all_gather(p_normed.reshape(clips, slots, small_width)[clip], "seq", axis=0, tiled=True)
        for clip in range(clips)
    ]
    p_contract_shard, p_expand, everyone[0] = lax.optimization_barrier(
        (p_contract_shard, p_expand, everyone[0])
    )
    p_contract = gather(p_contract_shard)
    for clip in range(clips):
        every = everyone[clip]
        if clip > 0:
            every, p_mixed[-1] = lax.optimization_barrier((every, p_mixed[-1]))
        p_joined = (mm(every, p_joint[:, small_width:]) + p_bias).astype(bf16)
        p_normed_all.append(every)
        p_mixed.append(
            attend(
                p_queries.reshape(clips, slots, small_width)[clip : clip + 1],
                p_joined.reshape(1, 1, span, 2 * small_width),
                small_head,
                None,
            )
        )
    kept_mid, kept_mixed, kept_middle, kept_inputs = (
        keep(member) for member in (mid_rows, mixed_rows, middle_rows, inputs)
    )
    p_mixed[0], kept_mid, kept_mixed, kept_middle, kept_inputs, *own_qkv = (
        lax.optimization_barrier(
            (p_mixed[0], kept_mid, kept_mixed, kept_middle, kept_inputs, *own_qkv)
        )
    )
    p_mixed = jnp.concatenate(p_mixed, axis=0).reshape(rows, small_width)
    p_middle = pred_input + mm(p_mixed, p_out) + p_vec["out_bias"]
    p_normed_mid = norm_layer(p_middle, p_vec["mid_gain"], p_vec["mid_shift"])
    p_hidden = mm(p_normed_mid, p_expand) + p_vec["expand_bias"]
    p_active = gelu(p_hidden)
    predicted = p_middle + mm(p_active, p_contract) + p_vec["contract_bias"]

    grad_middle, grad_att, grad_mixed, p_grads, p_small = feed_back(
        cotangent.reshape(rows, small_width),
        p_middle,
        p_normed_mid,
        p_hidden,
        p_active,
        (p_out, p_expand, p_contract),
        p_vec["mid_gain"],
    )
    p_grad_out = mm(p_mixed, grad_att, TN).astype(bf16)
    p_wide = jnp.concatenate([p_grad_out, p_grads[0]], axis=1)
    p_tall = p_grads[1]
    grad_mixed, p_wide, p_tall = lax.optimization_barrier((grad_mixed, p_wide, p_tall))
    p_wide, p_tall = scatter(p_wide), scatter(p_tall)
    own_weight = p_own_weight
    _, own_bias = own_joint(p_joint, p_vec["query_bias"], p_vec["value_bias"], seq_size, shard)
    own_width = small_width // seq_size
    grad_mixed = grad_mixed.reshape(rows, seq_size, own_width).transpose(1, 0, 2)
    grad_mixed = exchange(grad_mixed.reshape(seq_size, clips, slots, own_width))
    grad_normed = []
    p_grad_joint = 0.0
    p_columns = 0.0
    for clip in range(clips):
        every = p_normed_all[clip].reshape(1, 1, span, small_width)
        grads = attend_back(
            *own_parts(every, own_weight, own_bias),
            grad_mixed[:, clip].reshape(1, 1, span, own_width),
            0,
            small_head,
            None,
            seq_size,
        )
        if clip == 0:
            grads, p_wide, p_tall = lax.optimization_barrier((grads, p_wide, p_tall))
        flat = grads.reshape(span, 3 * own_width)
        p_grad_joint = p_grad_joint + mm(p_normed_all[clip], flat, TN)
        p_columns = p_columns + jnp.sum(flat.astype(f32), axis=0)
        grad_normed.append(joint_back(exchange(grads), p_by_sender))
    p_small.update(joint_small(p_columns, fsdp_size, seq_size, shard))
    p_own_width = own_width
    grad_norm, p_small["pre_gain"], p_small["pre_shift"] = norm_back(
        pred_input, p_vec["pre_gain"], jnp.concatenate(grad_normed, axis=0)
    )
    grad_pred_input = grad_middle + grad_norm
    grad_mask_token = jnp.sum(jnp.where(own_flat, 0.0, grad_pred_input), axis=0)
    grad_embedded = jnp.where(own_flat, grad_pred_input, 0.0).astype(bf16)
    grad_embed_bias = jnp.sum(grad_embedded.astype(f32), axis=0)

    grad_embedded, predicted = lax.optimization_barrier((grad_embedded, predicted))
    grad_context = mm(keep(grad_embedded), embed, NT)
    kept_hidden = mm(kept_mid, e_expand) + e_vec["expand_bias"]
    grad_middle, grad_att, grad_mixed, e_grads, e_small = feed_back(
        grad_context,
        kept_middle,
        kept_mid,
        kept_hidden,
        gelu(kept_hidden),
        (e_out, e_expand, e_contract),
        e_vec["mid_gain"],
    )
    expand_part, contract_part = scatter(e_grads[0]), scatter(e_grads[1])
    own_width = width // seq_size
    grad_mixed = grad_mixed.reshape(clips * held, seq_size, own_width).transpose(1, 0, 2)
    grad_mixed = by_clip(exchange(grad_mixed.reshape(seq_size, clips, held, own_width)))
    grads = [
        attend_back(*own_qkv, grad_mixed, clip, head_size, bias, seq_size) for clip in range(clips)
    ]
    grads[-1], grad_att, late_embedded = lax.optimization_barrier(
        (grads[-1], grad_att, grad_embedded)
    )
    received = [exchange(member) for member in grads]
    received[0], contract_part = lax.optimization_barrier((received[0], contract_part))
    flat = jnp.concatenate(grads, axis=1).reshape(-1, 3 * own_width)
    e_grad_joint = mm(normed_all.reshape(-1, width), flat, TN).astype(bf16)
    e_grad_out = mm(kept_mixed, grad_att, TN).astype(bf16)
    grad_embed = mm(context, late_embedded, TN).astype(bf16)
    e_small.update(joint_small(jnp.sum(flat.astype(f32), axis=0), fsdp_size, seq_size, shard))
    grad_normed = jnp.concatenate([joint_back(member, e_by_sender) for member in received], axis=0)
    grad_norm, e_small["pre_gain"], e_small["pre_shift"] = norm_back(
        kept_inputs, e_vec["pre_gain"], grad_normed
    )

    own_rows = width // fsdp_size
    p_rows = small_width // fsdp_size
    p_lanes = -(-3 * p_own_width // 128) * 128
    p_grad_joint = p_grad_joint.astype(bf16).reshape(fsdp_size, p_rows, 3 * p_own_width)
    p_grad_joint = jnp.pad(
        p_grad_joint, ((0, 0), (0, own_rows - p_rows), (0, p_lanes - 3 * p_own_width))
    ).reshape(width, p_lanes)
    small = [e_small[name] for name in ORDER] + [grad_embed_bias, grad_mask_token]
    small += [p_small[name] for name in ORDER]
    small = [member.reshape(fsdp_size, -1) for member in small]
    sizes = [member.shape[1] for member in small]
    small.append(jnp.zeros((fsdp_size, own_rows * 128 - sum(sizes)), f32))
    small = jnp.concatenate(small, axis=1).astype(bf16).reshape(width, 128)
    late = scatter(jnp.concatenate([e_grad_joint, p_grad_joint, e_grad_out, grad_embed, small], axis=1))
    grad_tokens = put_back(grad_middle + grad_norm)

    first = 0 if whole else 2
    contract_sum, expand_sum, p_wide_sum, p_contract_sum = sum_slots(
        (contract_part, expand_part, p_wide, p_tall), seq_size, first
    )
    late, expand_sum = lax.optimization_barrier((late, expand_sum))
    shared = 3 * own_width + p_lanes
    late_sum, columns = sum_slots((late,), seq_size, first + 1, shared)
    e_joint_sum = columns[:, :, : 3 * own_width].reshape(seq_size, own_rows, 3, own_width)
    e_joint_sum = e_joint_sum.transpose(1, 2, 0, 3).reshape(own_rows, 3 * width)
    p_joint_sum = columns[:, :p_rows, 3 * own_width : 3 * (own_width + p_own_width)]
    p_joint_sum = p_joint_sum.reshape(seq_size, p_rows, 3, p_own_width)
    p_joint_sum = p_joint_sum.transpose(1, 2, 0, 3).reshape(p_rows, 3 * small_width)
    out_sum = late_sum[:, :width]
    embed_sum = late_sum[:, width : width + small_width]
    p_out_sum, p_expand_sum = p_wide_sum[:, :small_width], p_wide_sum[:, small_width:]
    return (
        encoded.reshape(tokens.shape),
        predicted.reshape(cotangent.shape),
        grad_tokens.reshape(tokens.shape),
        (e_joint_sum, out_sum, expand_sum, contract_sum),
        embed_sum,
        (p_joint_sum, p_out_sum, p_expand_sum, p_contract_sum),
        late_sum[:, width + small_width :],
    )


def solution(mesh):
    cut, rows, vec, full = P("fsdp", "seq", None), P("fsdp", None), P("fsdp"), P()
    block = (vec, vec, rows, vec, vec, rows, vec, vec, vec, rows, vec, rows, vec)
    return jax.shard_map(
        functools.partial(body, mesh.shape["fsdp"], mesh.shape["seq"]),
        mesh=mesh,
        in_specs=(cut, rows, rows, full, *block, rows, vec, vec, *block, cut),
        out_specs=(cut, cut, cut, *block, rows, vec, vec, *block),
        check_vma=False,
    )
```
